32 devices in a mesh: dp: 16 (over z, y, core), mlp: 2 (over x).
Axes of the slice: x: 2, y: 2, z: 4, core: 2. Of those that a mesh axis runs over, the one named last changes fastest.
Arguments:
- tokens: bfloat16 [2, 2048, 2048], P(None, ('dp', 'mlp')), may hold values from -6 to 6
- cotangent: bfloat16 [2, 2048, 2048], P(None, ('dp', 'mlp')), may hold values from -6 to 6
- group_start: int32 [2, 32], P(None, ('dp', 'mlp')), may hold values from 0 to 1, as said below
- pad_mask: int32 [2, 2048], P(None, ('dp', 'mlp')), may hold values from 0 to 1, as said below
- query_weight: bfloat16 [2048, 2048], P(('dp', 'mlp')), may hold values from -0.125 to 0.125
- key_weight: bfloat16 [2048, 2048], P(('dp', 'mlp')), may hold values from -0.125 to 0.125
- value_weight: bfloat16 [2048, 2048], P(('dp', 'mlp')), may hold values from -0.125 to 0.125
- gate_weight: bfloat16 [2048, 2048], P(('dp', 'mlp')), may hold values from -0.125 to 0.125
- beta_weight: bfloat16 [2048, 16], P(('dp', 'mlp')), may hold values from -0.25 to 0.25
- out_weight: bfloat16 [2048, 2048], P(('dp', 'mlp')), may hold values from -0.1875 to 0.1875
- conv_weight: bfloat16 [3, 4, 2048], P(None, None, ('dp', 'mlp')), may hold values from -3 to 3
- mixer_gain: bfloat16 [2048], P(('dp', 'mlp')), may hold values from 0.25 to 1.75
- head_gain: bfloat16 [128], replicated, may hold values from 0.25 to 1.75
- swiglu_gain: bfloat16 [2048], P(('dp', 'mlp')), may hold values from 0.25 to 1.75
- swiglu_gate: bfloat16 [2048, 5632], P('dp', 'mlp'), may hold values from -0.125 to 0.125
- swiglu_up: bfloat16 [2048, 5632], P('dp', 'mlp'), may hold values from -0.125 to 0.125
- swiglu_down: bfloat16 [5632, 2048], P('mlp', 'dp'), may hold values from -0.15625 to 0.15625
Outputs:
- block_out: bfloat16 [2, 2048, 2048], P(None, ('dp', 'mlp'))
- tokens_grad: float32 [2, 2048, 2048], P(None, ('dp', 'mlp'))
- query_grad: float32 [2048, 2048], P(('dp', 'mlp'))
- key_grad: float32 [2048, 2048], P(('dp', 'mlp'))
- value_grad: float32 [2048, 2048], P(('dp', 'mlp'))
- gate_grad: float32 [2048, 2048], P(('dp', 'mlp'))
- beta_grad: float32 [2048, 16], P(('dp', 'mlp'))
- out_grad: float32 [2048, 2048], P(('dp', 'mlp'))
- conv_grad: float32 [3, 4, 2048], P(None, None, ('dp', 'mlp'))
- mixer_gain_grad: float32 [2048], P(('dp', 'mlp'))
- head_gain_grad: float32 [128], replicated
- swiglu_gain_grad: float32 [2048], P(('dp', 'mlp'))
- swiglu_gate_grad: float32 [2048, 5632], P('dp', 'mlp')
- swiglu_up_grad: float32 [2048, 5632], P('dp', 'mlp')
- swiglu_down_grad: float32 [5632, 2048], P('mlp', 'dp')
The draws below stay inside these ranges and needn't reach their ends.
Inputs may be any that keep to these rules, and one draw needn't show every extreme that they name: group_start is 1 at the first block of 64 tokens of every device's share of a micro-batch, so a document never spans two devices. `pad_mask`: each document's padding lies at its end, within its last block of 64 tokens, and holds 1 to 63 tokens.
All inputs are finite; a program needn't handle non-finite values.
Results may differ from the reference program's by a relative error of at most 0.013.
Values may be sent and summed in bfloat16 or wider, within the bound.
A program may use at most 384 MiB of HBM per device.

```python
import jax
import jax.numpy as jnp
from jax import lax

D = 2048
H = 16
DK = 128
FF = 5632
CONV = 4
GROUP = 64
MICRO = 2
SLOT = 64
TOKENS = 2048
N_DP = 16
N_MLP = 2


def starts_of(key):
    per_slot = SLOT // GROUP
    coins = jax.random.randint(jax.random.fold_in(key, 7), (MICRO, TOKENS // GROUP), 0, 3)
    place = jnp.arange(TOKENS // GROUP) % per_slot
    return jnp.where((place[None, :] == 0) | (coins == 0), 1, 0).astype(jnp.int32)


def draw_group_start(key, part):
    return starts_of(key)


def draw_pad_mask(key, part):
    starts = starts_of(key)
    following = jnp.concatenate([starts[:, 1:], jnp.ones((MICRO, 1), jnp.int32)], axis=1)
    kept_count = jax.random.randint(jax.random.fold_in(key, 9), (MICRO, TOKENS // GROUP), 1, GROUP)
    limit = jnp.where(following == 1, kept_count, GROUP)
    position = jnp.arange(GROUP)
    masked = (position[None, None, :] < limit[:, :, None]).astype(jnp.int32)
    return masked.reshape(MICRO, TOKENS)


def raised(entries, key, source, target, blocks, factor):
    owner, partner = [(jnp.arange(entries.shape[dim]) // (entries.shape[dim] // blocks)).reshape([-1 if axis == dim else 1 for axis in range(entries.ndim)]) for dim in (source, target)]
    chosen = jax.random.permutation(key, blocks)[partner]
    strong = (owner == chosen) | (owner == (partner + blocks // 2) % blocks)
    return jnp.where(strong, factor * entries, entries)


def block_levels(key, shape, pieces, least, high):
    gain, own = 1.0, jax.random.fold_in(key, 6)
    for dim, shards_of in pieces:
        heights = jnp.exp(jax.random.uniform(jax.random.fold_in(own, dim), (shards_of,), jnp.float32, least / len(pieces), high / len(pieces)))
        gain = gain * jnp.repeat(heights, shape[dim] // shards_of).reshape([-1 if axis == dim else 1 for axis in range(len(shape))])
    return gain


def normal_values(key, dims, deviation, most, cuts=(), held_as=jnp.bfloat16):
    factor_of = block_levels(key, dims, cuts, -0.22, 0.18) if cuts else 1.0
    drawn = jax.random.normal(key, dims, jnp.float32) * deviation * factor_of
    return jnp.minimum(jnp.maximum(drawn, -most), most).astype(held_as)


def gaussian_with(stream_key, dims, width, bound, shards, heavy, held_as=jnp.bfloat16):
    values = width * jax.random.normal(stream_key, dims, jnp.float32)
    if shards:
        values = values * block_levels(stream_key, dims, shards, -0.22, 0.18)
    return jnp.clip(raised(values, jax.random.fold_in(stream_key, 3), *heavy), -bound, bound).astype(held_as)


def setup_inputs(seed: int = 0) -> dict:
    splits = jax.random.split(jax.random.key(seed), 18)
    return {
        "tokens": gaussian_with(splits[0], (MICRO, TOKENS, D), 1.0, 6.0, ((1, 32),), (1, 2, 32, 2.75)),
        "cotangent": gaussian_with(splits[1], (MICRO, TOKENS, D), 1.0, 6.0, ((1, 32),), (1, 2, 32, 2.75)),
        "group_start": draw_group_start(jax.random.fold_in(splits[17], 71), 0),
        "pad_mask": draw_pad_mask(jax.random.fold_in(splits[17], 71), 0),
        "query_weight": normal_values(splits[4], (D, D), D ** -0.5, 0.125, ((0, 32),)),
        "key_weight": normal_values(splits[5], (D, D), D ** -0.5, 0.125, ((0, 32),)),
        "value_weight": normal_values(splits[6], (D, D), D ** -0.5, 0.125, ((0, 32),)),
        "gate_weight": normal_values(splits[7], (D, D), D ** -0.5, 0.125, ((0, 32),)),
        "beta_weight": normal_values(splits[8], (D, H), (D // 4) ** -0.5, 0.25, ((0, 32),)),
        "out_weight": normal_values(splits[9], (D, D), (D // 2) ** -0.5, 0.1875, ((0, 32),)),
        "conv_weight": normal_values(splits[10], (3, CONV, D), CONV ** -0.5, 3.0, ((2, 32),)),
        "mixer_gain": jnp.clip(1.0 + 0.15 * jax.random.normal(splits[11], (D,), jnp.float32), 0.25, 1.75).astype(jnp.bfloat16),
        "head_gain": jnp.clip(1.0 + 0.15 * jax.random.normal(splits[12], (DK,), jnp.float32), 0.25, 1.75).astype(jnp.bfloat16),
        "swiglu_gain": jnp.clip(1.0 + 0.15 * jax.random.normal(splits[13], (D,), jnp.float32), 0.25, 1.75).astype(jnp.bfloat16),
        "swiglu_gate": normal_values(splits[14], (D, FF), D ** -0.5, 0.125, ((0, 16), (1, 2))),
        "swiglu_up": normal_values(splits[15], (D, FF), D ** -0.5, 0.125, ((0, 16), (1, 2))),
        "swiglu_down": normal_values(splits[16], (FF, D), (FF // 4) ** -0.5, 0.15625, ((0, 2), (1, 16))),
    }


@jax.custom_vjp
def low(v):
    return lax.optimization_barrier(v.astype(jnp.bfloat16)).astype(jnp.float32)

@jax.custom_vjp
def low_back(v):
    return v

def low_keep(v):
    return (low(v), None)

def low_pass(kept, grad):
    return (grad,)

def back_keep(v):
    return (v, None)

def back_low(kept, grad):
    return (low(grad),)
low.defvjp(low_keep, low_pass)
low_back.defvjp(back_keep, back_low)

def rms_norm(values, scale_gain):
    return values * lax.rsqrt(lax.optimization_barrier(jnp.mean(values * values, axis=-1, keepdims=True)) + 1e-06) * scale_gain

def short_conv(linear, tap_weights, starts):
    length = linear.shape[0]
    position = jnp.arange(length)
    restart = jnp.repeat(starts, GROUP)
    summed = linear * tap_weights[0]
    for offset in range(1, CONV):
        shifted = jnp.concatenate([jnp.zeros((offset, linear.shape[1]), linear.dtype), linear[:length - offset]], axis=0)
        usable = ((position % GROUP >= offset) | (restart == 0)).astype(linear.dtype)
        summed = summed + shifted * tap_weights[offset] * usable[:, None]
    return summed

def outer_product_result(form, first, second):
    return jnp.einsum(form, first, second, precision=lax.Precision.HIGHEST)

def delta_core(queries, keys, values, betas, starts):
    length, head_count, head_width = queries.shape
    value_width = values.shape[2]
    block_count = length // GROUP

    def blocked(array):
        return array.reshape(block_count, GROUP, head_count, -1).transpose(0, 2, 1, 3)
    query_blocks = blocked(queries)
    key_blocks = blocked(keys)
    value_blocks = blocked(values)
    beta_blocks = betas.reshape(block_count, GROUP, head_count).transpose(0, 2, 1)[..., None]
    position = jnp.arange(GROUP)
    strict = (position[:, None] > position[None, :]).astype(queries.dtype)
    causal = (position[:, None] >= position[None, :]).astype(queries.dtype)
    weighted = key_blocks * beta_blocks
    negative = -outer_product_result('nhik,nhjk->nhij', weighted, key_blocks) * strict
    inverse = jnp.eye(GROUP, dtype=queries.dtype) + negative
    power_term = negative
    for doubling in range(5):
        power_term = outer_product_result('nhij,nhjk->nhik', power_term, power_term)
        inverse = inverse + outer_product_result('nhij,nhjk->nhik', inverse, power_term)
    key_mix = outer_product_result('nhij,nhjk->nhik', inverse, weighted)
    value_mix = outer_product_result('nhij,nhjk->nhik', inverse, value_blocks * beta_blocks)
    scores = outer_product_result('nhik,nhjk->nhij', query_blocks, key_blocks) * causal

    def advance(current_state, block_items):
        query_slice, key_slice, key_mixture_slice, value_mixture_slice, attention_score_slice, restart = block_items
        current_state = current_state * (1 - restart).astype(current_state.dtype)
        adjusted_result = value_mixture_slice - outer_product_result('pzd,pde->pze', key_mixture_slice, current_state)
        produced_output = outer_product_result('pzd,pde->pze', query_slice, current_state) + outer_product_result('lqz,lzr->lqr', attention_score_slice, adjusted_result)
        current_state = current_state + outer_product_result('ixl,ixr->ilr', key_slice, adjusted_result)
        return (current_state, produced_output)
    initial = jnp.zeros((head_count, head_width, value_width), queries.dtype)
    final_state, produced_output = lax.scan(advance, initial, (query_blocks, key_blocks, key_mix, value_mix, scores, starts))
    return produced_output.transpose(0, 2, 1, 3).reshape(length, head_count, value_width)

def mixer_core(query_lin, key_lin, value_lin, gate_lin, beta_lin, conv_taps, head_scale, starts):
    length = query_lin.shape[0]
    head_count = beta_lin.shape[1]
    head_width = query_lin.shape[1] // head_count
    queries = jax.nn.silu(short_conv(query_lin, conv_taps[0], starts)).reshape(length, head_count, head_width)
    keys = jax.nn.silu(short_conv(key_lin, conv_taps[1], starts)).reshape(length, head_count, head_width)
    values = jax.nn.silu(short_conv(value_lin, conv_taps[2], starts)).reshape(length, head_count, head_width)
    queries = queries * lax.rsqrt(lax.optimization_barrier(jnp.sum(queries * queries, axis=-1, keepdims=True)) + 1e-06) * head_width ** (-0.5)
    keys = keys * lax.rsqrt(lax.optimization_barrier(jnp.sum(keys * keys, axis=-1, keepdims=True)) + 1e-06)
    recurrent = delta_core(queries, keys, values, jax.nn.sigmoid(beta_lin), starts)
    normed = recurrent * lax.rsqrt(lax.optimization_barrier(jnp.mean(recurrent * recurrent, axis=-1, keepdims=True)) + 1e-05) * head_scale
    gated_out = normed * jax.nn.silu(gate_lin.reshape(length, head_count, head_width))
    return gated_out.reshape(length, head_count * head_width)

def dense_product(left, right):
    return jnp.dot(left, right, preferred_element_type=jnp.float32, precision=lax.Precision.HIGHEST)

def layer_forward(inputs, query_weight, key_weight, value_weight, gate_weight, beta_weight, out_weight, conv_weight, mixer_gain, head_gain, swiglu_gain, swiglu_gate, swiglu_up, swiglu_down, starts):
    normed = low(rms_norm(inputs, mixer_gain))
    query_lin = low_back(dense_product(normed, query_weight))
    key_lin = low_back(dense_product(normed, key_weight))
    value_lin = low_back(dense_product(normed, value_weight))
    gate_lin = low_back(dense_product(normed, gate_weight))
    beta_lin = low_back(dense_product(normed, beta_weight))
    gated_out = low(mixer_core(query_lin, key_lin, value_lin, gate_lin, beta_lin, conv_weight, head_gain, starts))
    residual = inputs + low_back(dense_product(gated_out, out_weight))
    inner = low(rms_norm(residual, swiglu_gain))
    gate_act = low_back(dense_product(inner, swiglu_gate))
    up_act = low_back(dense_product(inner, swiglu_up))
    hidden = low(jax.nn.silu(gate_act) * up_act)
    return residual + low_back(dense_product(hidden, swiglu_down))

def reference(tokens, cotangent, group_start, pad_mask, query_weight, key_weight, value_weight, gate_weight, beta_weight, out_weight, conv_weight, mixer_gain, head_gain, swiglu_gain, swiglu_gate, swiglu_up, swiglu_down):
    weights = tuple((member.astype(jnp.float32) for member in (query_weight, key_weight, value_weight, gate_weight, beta_weight, out_weight, conv_weight, mixer_gain, head_gain, swiglu_gain, swiglu_gate, swiglu_up, swiglu_down)))
    slot_count = MICRO * N_DP * N_MLP

    def visit_slot(totals, slot_items):
        slot_inputs, upstream, starts, kept_mask = slot_items

        def forward(inputs, *params):
            return layer_forward(inputs, *params, starts)
        result, pullback = jax.vjp(forward, slot_inputs.astype(jnp.float32), *weights)
        gradients = pullback(upstream.astype(jnp.float32) * kept_mask.astype(jnp.float32)[:, None])
        totals = tuple((running + gradient for running, gradient in zip(totals, gradients[1:])))
        return (totals, (result.astype(jnp.bfloat16), gradients[0]))
    empty_sums = tuple((jnp.zeros(member.shape, jnp.float32) for member in weights))
    totals, (results, input_grads) = lax.scan(visit_slot, empty_sums, (tokens.reshape(slot_count, SLOT, D), cotangent.reshape(slot_count, SLOT, D), group_start.reshape(slot_count, SLOT // GROUP), pad_mask.reshape(slot_count, SLOT)))
    return (results.reshape(MICRO, TOKENS, D), input_grads.reshape(MICRO, TOKENS, D), totals[0], totals[1], totals[2], totals[3], totals[4], totals[5], totals[6], totals[7], totals[8], totals[9], totals[10], totals[11], totals[12])
```

```python
import jax
import jax.numpy as jnp
from jax import lax
from jax.sharding import PartitionSpec as P


def rms_norm(values, scale_gain):
    return (
        values * lax.rsqrt(jnp.mean(values * values, axis=-1, keepdims=True) + 1e-06) * scale_gain
    )


def short_conv(linear, tap_weights, starts):
    length = linear.shape[0]
    block_len = length // starts.shape[0]
    position = jnp.arange(length)
    restart = jnp.repeat(starts, block_len)
    summed = linear * tap_weights[0]
    for offset in range(1, tap_weights.shape[0]):
        shifted = jnp.concatenate(
            [jnp.zeros((offset, linear.shape[1]), linear.dtype), linear[: length - offset]], axis=0
        )
        usable = ((position % block_len >= offset) | (restart == 0)).astype(linear.dtype)
        summed = summed + shifted * tap_weights[offset] * usable[:, None]
    return summed


def outer_product_result(form, first, second):
    return jnp.einsum(form, first, second, precision=lax.Precision.HIGHEST)


def delta_core(queries, keys, values, betas, starts):
    length, head_count, head_width = queries.shape
    value_width = values.shape[2]
    block_count = starts.shape[0]
    block_len = length // block_count

    def blocked(array):
        return array.reshape(block_count, block_len, head_count, -1).transpose(0, 2, 1, 3)

    query_blocks = blocked(queries)
    key_blocks = blocked(keys)
    value_blocks = blocked(values)
    beta_blocks = betas.reshape(block_count, block_len, head_count).transpose(0, 2, 1)[..., None]
    position = jnp.arange(block_len)
    strict = (position[:, None] > position[None, :]).astype(queries.dtype)
    causal = (position[:, None] >= position[None, :]).astype(queries.dtype)
    weighted = key_blocks * beta_blocks
    negative = -outer_product_result("nhik,nhjk->nhij", weighted, key_blocks) * strict
    inverse = jnp.eye(block_len, dtype=queries.dtype) + negative
    power_term = negative
    for doubling in range(5):
        power_term = outer_product_result("nhij,nhjk->nhik", power_term, power_term)
        inverse = inverse + outer_product_result("nhij,nhjk->nhik", inverse, power_term)
    key_mix = outer_product_result("nhij,nhjk->nhik", inverse, weighted)
    value_mix = outer_product_result("nhij,nhjk->nhik", inverse, value_blocks * beta_blocks)
    scores = outer_product_result("nhik,nhjk->nhij", query_blocks, key_blocks) * causal

    def advance(current_state, block_items):
        (
            query_slice,
            key_slice,
            key_mixture_slice,
            value_mixture_slice,
            attention_score_slice,
            restart,
        ) = block_items
        current_state = current_state * (1 - restart).astype(current_state.dtype)
        adjusted_result = value_mixture_slice - outer_product_result(
            "pzd,pde->pze", key_mixture_slice, current_state
        )
        produced_output = outer_product_result(
            "pzd,pde->pze", query_slice, current_state
        ) + outer_product_result("lqz,lzr->lqr", attention_score_slice, adjusted_result)
        current_state = current_state + outer_product_result(
            "ixl,ixr->ilr", key_slice, adjusted_result
        )
        return (current_state, produced_output)

    initial = jnp.zeros((head_count, head_width, value_width), queries.dtype)
    final_state, produced_output = lax.scan(
        advance, initial, (query_blocks, key_blocks, key_mix, value_mix, scores, starts)
    )
    return produced_output.transpose(0, 2, 1, 3).reshape(length, head_count, value_width)


def mixer_core(query_lin, key_lin, value_lin, gate_lin, beta_lin, conv_taps, head_scale, starts):
    length = query_lin.shape[0]
    head_count = beta_lin.shape[1]
    head_width = query_lin.shape[1] // head_count
    queries = jax.nn.silu(short_conv(query_lin, conv_taps[0], starts)).reshape(
        length, head_count, head_width
    )
    keys = jax.nn.silu(short_conv(key_lin, conv_taps[1], starts)).reshape(
        length, head_count, head_width
    )
    values = jax.nn.silu(short_conv(value_lin, conv_taps[2], starts)).reshape(
        length, head_count, head_width
    )
    queries = (
        queries
        * lax.rsqrt(jnp.sum(queries * queries, axis=-1, keepdims=True) + 1e-06)
        * head_width ** (-0.5)
    )
    keys = keys * lax.rsqrt(jnp.sum(keys * keys, axis=-1, keepdims=True) + 1e-06)
    recurrent = delta_core(queries, keys, values, jax.nn.sigmoid(beta_lin), starts)
    normed = (
        recurrent
        * lax.rsqrt(jnp.mean(recurrent * recurrent, axis=-1, keepdims=True) + 1e-05)
        * head_scale
    )
    gated_out = normed * jax.nn.silu(gate_lin.reshape(length, head_count, head_width))
    return gated_out.reshape(length, head_count * head_width)


def swiglu_mix(gate_act, up_act):
    return jax.nn.silu(gate_act) * up_act


def matmul_rows(left, right):
    return jnp.dot(left, right, preferred_element_type=jnp.float32)


def left_product(first, second):
    return jnp.einsum("tf,tg->fg", first, second, preferred_element_type=jnp.float32)


def back_product(gradient, weight):
    return jnp.einsum("tg,fg->tf", gradient, weight, preferred_element_type=jnp.float32)


def add_terms(running, fresh_terms):
    if running is None:
        return fresh_terms
    return tuple((left_term + right_term for left_term, right_term in zip(running, fresh_terms)))


def scatter_low(term, axes, dimension):
    return lax.psum_scatter(
        term.astype(jnp.bfloat16), axes, scatter_dimension=dimension, tiled=True
    ).astype(jnp.float32)


def joined(pieces):
    return jnp.concatenate(pieces, axis=0)


def on_device(
    tokens,
    cotangent,
    group_start,
    pad_mask,
    query_weight,
    key_weight,
    value_weight,
    gate_weight,
    beta_weight,
    out_weight,
    conv_weight,
    mixer_gain,
    head_gain,
    swiglu_gain,
    swiglu_gate,
    swiglu_up,
    swiglu_down,
):
    micro_count = tokens.shape[0]
    n_all = tokens.shape[2] // query_weight.shape[0]
    head_scale = head_gain.astype(jnp.float32)
    mixer_set = (
        lax.all_gather(query_weight, ("dp", "mlp"), axis=0, tiled=True),
        lax.all_gather(key_weight, ("dp", "mlp"), axis=0, tiled=True),
        lax.all_gather(value_weight, ("dp", "mlp"), axis=0, tiled=True),
        lax.all_gather(gate_weight, ("dp", "mlp"), axis=0, tiled=True),
        lax.all_gather(out_weight, ("dp", "mlp"), axis=0, tiled=True),
    )
    rows = beta_weight.shape[0]
    small_pack = jnp.concatenate(
        [
            conv_weight.reshape(-1),
            beta_weight.reshape(-1),
            mixer_gain.reshape(-1),
            swiglu_gain.reshape(-1),
        ]
    )
    small_all = lax.all_gather(small_pack, ("dp", "mlp"), axis=0, tiled=False)
    conv_size = conv_weight.size
    beta_size = beta_weight.size
    conv_full = (
        small_all[:, :conv_size]
        .reshape((n_all,) + conv_weight.shape)
        .transpose(1, 2, 0, 3)
        .reshape(conv_weight.shape[0], conv_weight.shape[1], -1)
    )
    beta_full = small_all[:, conv_size : conv_size + beta_size].reshape(-1, beta_weight.shape[1])
    gain_mixer = small_all[:, conv_size + beta_size : conv_size + beta_size + rows].reshape(-1)
    gain_swiglu = small_all[:, conv_size + beta_size + rows :].reshape(-1)
    swiglu_set = (
        lax.all_gather(swiglu_gate, "dp", axis=0, tiled=True),
        lax.all_gather(swiglu_up, "dp", axis=0, tiled=True),
        lax.all_gather(swiglu_down, "dp", axis=1, tiled=True),
    )
    mixer_sums = None
    swiglu_sums = None
    small_sums = None
    kept_rows = []
    head_sums = jnp.zeros(head_gain.shape, jnp.float32)
    outputs = []
    input_grads = []
    for micro_index in range(micro_count):
        query_full, key_full, value_full, gate_full, out_full = mixer_set
        gate_half, up_half, down_half = swiglu_set
        inputs = tokens[micro_index].astype(jnp.float32)
        starts = group_start[micro_index]
        normed, norm_back = jax.vjp(rms_norm, inputs, gain_mixer.astype(jnp.float32))
        normed_low = normed.astype(jnp.bfloat16)
        query_lin = matmul_rows(normed_low, query_full)
        key_lin = matmul_rows(normed_low, key_full)
        value_lin = matmul_rows(normed_low, value_full)
        gate_lin = matmul_rows(normed_low, gate_full)
        beta_lin = matmul_rows(normed_low, beta_full)

        def core_at(query_in, key_in, value_in, gate_in, beta_in, conv_in, head_in):
            return mixer_core(
                query_in, key_in, value_in, gate_in, beta_in, conv_in, head_in, starts
            )

        gated_out, core_back = jax.vjp(
            core_at,
            query_lin,
            key_lin,
            value_lin,
            gate_lin,
            beta_lin,
            conv_full.astype(jnp.float32),
            head_scale,
        )
        gated_low = gated_out.astype(jnp.bfloat16)
        residual = inputs + matmul_rows(gated_low, out_full)
        inner, inner_norm_back = jax.vjp(rms_norm, residual, gain_swiglu.astype(jnp.float32))
        inner_low = inner.astype(jnp.bfloat16)
        inner_pair = lax.all_gather(inner_low, "mlp", axis=0, tiled=True)
        gate_act = matmul_rows(inner_pair, gate_half)
        up_act = matmul_rows(inner_pair, up_half)
        hidden, hidden_back = jax.vjp(swiglu_mix, gate_act, up_act)
        hidden_low = hidden.astype(jnp.bfloat16)
        partial_rows = matmul_rows(hidden_low, down_half)
        branch_rows = lax.psum_scatter(
            partial_rows.astype(jnp.bfloat16), "mlp", scatter_dimension=0, tiled=True
        ).astype(jnp.float32)
        outputs.append((residual + branch_rows).astype(jnp.bfloat16))
        out_back = (
            cotangent[micro_index].astype(jnp.float32)
            * pad_mask[micro_index].astype(jnp.float32)[:, None]
        )
        out_back_low = out_back.astype(jnp.bfloat16)
        upstream_pair = lax.all_gather(out_back_low, "mlp", axis=0, tiled=True)
        gate_back, up_back = hidden_back(back_product(upstream_pair, down_half))
        gate_back_low = gate_back.astype(jnp.bfloat16)
        up_back_low = up_back.astype(jnp.bfloat16)
        inner_part = back_product(gate_back_low, gate_half) + back_product(up_back_low, up_half)
        inner_back = lax.psum_scatter(
            inner_part.astype(jnp.bfloat16), "mlp", scatter_dimension=0, tiled=True
        ).astype(jnp.float32)
        residual_part, swiglu_gain_term = inner_norm_back(inner_back)
        residual_back = out_back + residual_part
        mixed_back = residual_back.astype(jnp.bfloat16)
        gated_back = back_product(mixed_back, out_full)
        query_back, key_back, value_back, gate_lin_back, beta_back, conv_term, head_term = (
            core_back(gated_back)
        )
        query_low = query_back.astype(jnp.bfloat16)
        key_low = key_back.astype(jnp.bfloat16)
        value_low = value_back.astype(jnp.bfloat16)
        gate_low = gate_lin_back.astype(jnp.bfloat16)
        beta_low = beta_back.astype(jnp.bfloat16)
        normed_back = (
            back_product(query_low, query_full)
            + back_product(key_low, key_full)
            + back_product(value_low, value_full)
            + back_product(gate_low, gate_full)
            + back_product(beta_low, beta_full)
        )
        input_part, mixer_gain_term = norm_back(normed_back)
        input_grads.append(residual_back + input_part)
        kept_rows.append(
            (
                normed_low,
                query_low,
                key_low,
                value_low,
                gate_low,
                beta_low,
                gated_low,
                mixed_back,
                inner_pair,
                gate_back_low,
                up_back_low,
                hidden_low,
                upstream_pair,
            )
        )
        small_sums = add_terms(small_sums, (conv_term, mixer_gain_term, swiglu_gain_term))
        head_sums = head_sums + head_term
    columns = [joined([row[position] for row in kept_rows]) for position in range(13)]
    normed_all = columns[0]
    gate_term = left_product(columns[8], columns[9])
    up_term = left_product(columns[8], columns[10])
    down_term = left_product(columns[11], columns[12])
    swiglu_sums = (
        scatter_low(gate_term, "dp", 0),
        scatter_low(up_term, "dp", 0),
        scatter_low(down_term, "dp", 1),
    )
    query_term = left_product(normed_all, columns[1])
    key_term = left_product(normed_all, columns[2])
    value_term = left_product(normed_all, columns[3])
    gate_term_mix = left_product(normed_all, columns[4])
    beta_term = left_product(normed_all, columns[5])
    out_term = left_product(columns[6], columns[7])
    big_sums = tuple(
        scatter_low(term, ("dp", "mlp"), 0)
        for term in (query_term, key_term, value_term, gate_term_mix, out_term)
    )
    conv_sum, mixer_gain_sum, swiglu_gain_sum = small_sums
    taps = conv_sum.shape[0] * conv_sum.shape[1]
    small_rows = jnp.concatenate(
        [
            conv_sum.reshape(taps, n_all, -1).transpose(1, 0, 2).reshape(n_all, -1),
            beta_term.reshape(n_all, -1),
            mixer_gain_sum.reshape(n_all, -1),
            swiglu_gain_sum.reshape(n_all, -1),
            jnp.broadcast_to(head_sums[None, :], (n_all, head_sums.shape[0])),
        ],
        axis=1,
    )
    small_out = lax.psum_scatter(small_rows, ("dp", "mlp"), scatter_dimension=0, tiled=False)
    conv_owned = small_out[: conv_size].reshape(conv_weight.shape)
    beta_owned = small_out[conv_size : conv_size + beta_size].reshape(beta_weight.shape)
    mixer_gain_owned = small_out[conv_size + beta_size : conv_size + beta_size + rows]
    swiglu_gain_owned = small_out[conv_size + beta_size + rows : conv_size + beta_size + 2 * rows]
    head_total = small_out[conv_size + beta_size + 2 * rows :]
    mixer_sums = (
        big_sums[0],
        big_sums[1],
        big_sums[2],
        big_sums[3],
        beta_owned,
        big_sums[4],
        conv_owned,
        mixer_gain_owned,
        swiglu_gain_owned,
    )
    return (
        jnp.stack(outputs),
        jnp.stack(input_grads),
        mixer_sums[0],
        mixer_sums[1],
        mixer_sums[2],
        mixer_sums[3],
        mixer_sums[4],
        mixer_sums[5],
        mixer_sums[6],
        mixer_sums[7],
        head_total,
        mixer_sums[8],
        swiglu_sums[0],
        swiglu_sums[1],
        swiglu_sums[2],
    )


def solution(mesh):
    placed = (
        P(None, ("dp", "mlp"), None),
        P(None, ("dp", "mlp"), None),
        P(None, ("dp", "mlp")),
        P(None, ("dp", "mlp")),
        P(("dp", "mlp"), None),
        P(("dp", "mlp"), None),
        P(("dp", "mlp"), None),
        P(("dp", "mlp"), None),
        P(("dp", "mlp"), None),
        P(("dp", "mlp"), None),
        P(None, None, ("dp", "mlp")),
        P(("dp", "mlp")),
        P(),
        P(("dp", "mlp")),
        P("dp", "mlp"),
        P("dp", "mlp"),
        P("mlp", "dp"),
    )
    return jax.shard_map(
        on_device,
        mesh=mesh,
        in_specs=placed,
        out_specs=(
            P(None, ("dp", "mlp"), None),
            P(None, ("dp", "mlp"), None),
            P(("dp", "mlp"), None),
            P(("dp", "mlp"), None),
            P(("dp", "mlp"), None),
            P(("dp", "mlp"), None),
            P(("dp", "mlp"), None),
            P(("dp", "mlp"), None),
            P(None, None, ("dp", "mlp")),
            P(("dp", "mlp")),
            P(),
            P(("dp", "mlp")),
            P("dp", "mlp"),
            P("dp", "mlp"),
            P("mlp", "dp"),
        ),
        check_vma=False,
    )
```

```python
import jax
import jax.numpy as jnp
import numpy as np
from jax import lax
from jax.sharding import Mesh
from jax.sharding import PartitionSpec as P

TP_AXES = ("core", "mlp")
ALL_AXES = ("dq", "core", "mlp")
FSDP_AXES = tuple(name for name in ALL_AXES if name not in TP_AXES)
INNER_AXES = tuple(name for name in TP_AXES if name != "mlp")


def rms_norm(values, scale_gain):
    return (
        values * lax.rsqrt(jnp.mean(values * values, axis=-1, keepdims=True) + 1e-06) * scale_gain
    )


def short_conv(linear, tap_weights, starts):
    length = linear.shape[0]
    block_len = length // starts.shape[0]
    position = jnp.arange(length)
    restart = jnp.repeat(starts, block_len)
    summed = linear * tap_weights[0]
    for offset in range(1, tap_weights.shape[0]):
        shifted = jnp.concatenate(
            [jnp.zeros((offset, linear.shape[1]), linear.dtype), linear[: length - offset]], axis=0
        )
        usable = ((position % block_len >= offset) | (restart == 0)).astype(linear.dtype)
        summed = summed + shifted * tap_weights[offset] * usable[:, None]
    return summed


def outer_product_result(form, first, second):
    return jnp.einsum(form, first, second, precision=lax.Precision.HIGHEST)


def delta_core(queries, keys, values, betas, starts):
    length, head_count, head_width = queries.shape
    value_width = values.shape[2]
    block_count = starts.shape[0]
    block_len = length // block_count

    def blocked(array):
        return array.reshape(block_count, block_len, head_count, -1).transpose(0, 2, 1, 3)

    query_blocks = blocked(queries)
    key_blocks = blocked(keys)
    value_blocks = blocked(values)
    beta_blocks = betas.reshape(block_count, block_len, head_count).transpose(0, 2, 1)[..., None]
    position = jnp.arange(block_len)
    strict = (position[:, None] > position[None, :]).astype(queries.dtype)
    causal = (position[:, None] >= position[None, :]).astype(queries.dtype)
    weighted = key_blocks * beta_blocks
    negative = -outer_product_result("nhik,nhjk->nhij", weighted, key_blocks) * strict
    inverse = jnp.eye(block_len, dtype=queries.dtype) + negative
    power_term = negative
    for doubling in range(5):
        power_term = outer_product_result("nhij,nhjk->nhik", power_term, power_term)
        inverse = inverse + outer_product_result("nhij,nhjk->nhik", inverse, power_term)
    key_mix = outer_product_result("nhij,nhjk->nhik", inverse, weighted)
    value_mix = outer_product_result("nhij,nhjk->nhik", inverse, value_blocks * beta_blocks)
    scores = outer_product_result("nhik,nhjk->nhij", query_blocks, key_blocks) * causal

    def advance(current_state, block_items):
        (
            query_slice,
            key_slice,
            key_mixture_slice,
            value_mixture_slice,
            attention_score_slice,
            restart,
        ) = block_items
        current_state = current_state * (1 - restart).astype(current_state.dtype)
        adjusted_result = value_mixture_slice - outer_product_result(
            "pzd,pde->pze", key_mixture_slice, current_state
        )
        produced_output = outer_product_result(
            "pzd,pde->pze", query_slice, current_state
        ) + outer_product_result("lqz,lzr->lqr", attention_score_slice, adjusted_result)
        current_state = current_state + outer_product_result(
            "ixl,ixr->ilr", key_slice, adjusted_result
        )
        return (current_state, produced_output)

    initial = jnp.zeros((head_count, head_width, value_width), queries.dtype)
    final_state, produced_output = lax.scan(
        advance, initial, (query_blocks, key_blocks, key_mix, value_mix, scores, starts)
    )
    return produced_output.transpose(0, 2, 1, 3).reshape(length, head_count, value_width)


def mixer_core(query_lin, key_lin, value_lin, gate_lin, beta_lin, conv_taps, head_scale, starts):
    length = query_lin.shape[0]
    head_count = beta_lin.shape[1]
    head_width = query_lin.shape[1] // head_count
    queries = jax.nn.silu(short_conv(query_lin, conv_taps[0], starts)).reshape(
        length, head_count, head_width
    )
    keys = jax.nn.silu(short_conv(key_lin, conv_taps[1], starts)).reshape(
        length, head_count, head_width
    )
    values = jax.nn.silu(short_conv(value_lin, conv_taps[2], starts)).reshape(
        length, head_count, head_width
    )
    queries = (
        queries
        * lax.rsqrt(jnp.sum(queries * queries, axis=-1, keepdims=True) + 1e-06)
        * head_width ** (-0.5)
    )
    keys = keys * lax.rsqrt(jnp.sum(keys * keys, axis=-1, keepdims=True) + 1e-06)
    recurrent = delta_core(queries, keys, values, jax.nn.sigmoid(beta_lin), starts)
    normed = (
        recurrent
        * lax.rsqrt(jnp.mean(recurrent * recurrent, axis=-1, keepdims=True) + 1e-05)
        * head_scale
    )
    gated_out = normed * jax.nn.silu(gate_lin.reshape(length, head_count, head_width))
    return gated_out.reshape(length, head_count * head_width)


def swiglu_mix(gate_act, up_act):
    return jax.nn.silu(gate_act) * up_act


def matmul_rows(left, right):
    return jnp.dot(left, right, preferred_element_type=jnp.float32)


def left_product(first, second):
    return jnp.einsum("tf,tg->fg", first, second, preferred_element_type=jnp.float32)


def back_product(gradient, weight):
    return jnp.einsum("tg,fg->tf", gradient, weight, preferred_element_type=jnp.float32)


def tp_gather(value, axis):
    return lax.all_gather(value, TP_AXES, axis=axis, tiled=True)


def tp_scatter_low(value, axis):
    return lax.psum_scatter(
        value.astype(jnp.bfloat16), TP_AXES, scatter_dimension=axis, tiled=True
    ).astype(jnp.float32)


def fsdp_gather(value, axis):
    return lax.all_gather(value, FSDP_AXES, axis=axis, tiled=True)


def fsdp_scatter_low(value, axis):
    return lax.psum_scatter(
        value.astype(jnp.bfloat16), FSDP_AXES, scatter_dimension=axis, tiled=True
    ).astype(jnp.float32)


def exchange(value, axes, split_axis, concat_axis):
    if not axes:
        return value
    return lax.all_to_all(value, axes, split_axis, concat_axis, tiled=True)


def column_weight(owned, tp):
    rows, width = owned.shape
    swapped = exchange(owned.reshape(rows, tp, width // tp), TP_AXES, 1, 0)
    return fsdp_gather(swapped.reshape(rows * tp, width // tp), 0)


def column_grad(partial, tp):
    reduced = fsdp_scatter_low(partial, 0)
    group_rows, cols = reduced.shape
    swapped = exchange(reduced.reshape(tp, group_rows // tp, cols), TP_AXES, 0, 2)
    return swapped.reshape(group_rows // tp, cols * tp)


def heads_to_rows(values, tp, fsdp, rows):
    count = values.shape[0]
    staged = values.reshape(count, 1, fsdp // tp, tp, rows)
    moved = exchange(staged, TP_AXES, 3, 1)
    return moved.reshape(count, fsdp * rows)


def rows_to_heads(values, tp, fsdp, rows):
    count = values.shape[0]
    staged = values.reshape(count, tp, fsdp // tp, 1, rows)
    moved = exchange(staged, TP_AXES, 1, 3)
    return moved.reshape(count, fsdp * rows)


def make_on_device(tp, fsdp, inner):
    def on_device(
        tokens,
        cotangent,
        group_start,
        pad_mask,
        query_weight,
        key_weight,
        value_weight,
        gate_weight,
        beta_weight,
        out_weight,
        conv_weight,
        mixer_gain,
        head_gain,
        swiglu_gain,
        swiglu_gate,
        swiglu_up,
        swiglu_down,
    ):
        micro_count, slot, width = tokens.shape
        n_all = tp * fsdp
        rows = query_weight.shape[0]
        head_count = beta_weight.shape[1]
        heads_here = head_count // tp
        cols_here = width // tp
        position = lax.axis_index(TP_AXES)
        head_scale = head_gain.astype(jnp.float32)

        query_cols = column_weight(query_weight, tp)
        key_cols = column_weight(key_weight, tp)
        value_cols = column_weight(value_weight, tp)
        gate_cols = column_weight(gate_weight, tp)
        out_rows = fsdp_gather(out_weight, 0)

        small_pack = jnp.concatenate(
            [
                conv_weight.reshape(-1),
                beta_weight.reshape(-1),
                mixer_gain.reshape(-1),
                swiglu_gain.reshape(-1),
            ]
        )
        small_all = lax.all_gather(small_pack, ALL_AXES, axis=0, tiled=False)
        conv_size = conv_weight.size
        beta_size = beta_weight.size
        conv_full = (
            small_all[:, :conv_size]
            .reshape((n_all,) + conv_weight.shape)
            .transpose(1, 2, 0, 3)
            .reshape(conv_weight.shape[0], conv_weight.shape[1], -1)
        )
        beta_full = small_all[:, conv_size : conv_size + beta_size].reshape(-1, head_count)
        gain_mixer = small_all[:, conv_size + beta_size : conv_size + beta_size + rows].reshape(-1)
        gain_swiglu = small_all[:, conv_size + beta_size + rows :].reshape(-1)
        conv_here = lax.dynamic_slice_in_dim(
            conv_full.astype(jnp.float32), position * cols_here, cols_here, axis=2
        )
        beta_here = lax.dynamic_slice_in_dim(beta_full, position * heads_here, heads_here, axis=1)

        owned_rows, hidden_half = swiglu_gate.shape
        gate_half = fsdp_gather(
            exchange(swiglu_gate.reshape(owned_rows, inner, hidden_half // inner), INNER_AXES, 1, 0)
            .reshape(owned_rows * inner, hidden_half // inner),
            0,
        )
        up_half = fsdp_gather(
            exchange(swiglu_up.reshape(owned_rows, inner, hidden_half // inner), INNER_AXES, 1, 0)
            .reshape(owned_rows * inner, hidden_half // inner),
            0,
        )
        down_half = fsdp_gather(
            exchange(swiglu_down.reshape(inner, hidden_half // inner, owned_rows), INNER_AXES, 0, 2)
            .reshape(hidden_half // inner, inner * owned_rows),
            1,
        )

        inputs = tokens.astype(jnp.float32).reshape(micro_count * slot, width)
        normed, norm_back = jax.vjp(rms_norm, inputs, gain_mixer.astype(jnp.float32))
        normed_low = normed.astype(jnp.bfloat16)
        group_tokens = micro_count * slot * tp
        normed_group = tp_gather(normed_low.reshape(micro_count, slot, width), 1).reshape(
            group_tokens, width
        )
        starts = tp_gather(group_start, 1).reshape(-1)

        query_lin = matmul_rows(normed_group, query_cols)
        key_lin = matmul_rows(normed_group, key_cols)
        value_lin = matmul_rows(normed_group, value_cols)
        gate_lin = matmul_rows(normed_group, gate_cols)
        beta_lin = matmul_rows(normed_group, beta_here)

        def core_at(query_in, key_in, value_in, gate_in, beta_in, conv_in, head_in):
            return mixer_core(
                query_in, key_in, value_in, gate_in, beta_in, conv_in, head_in, starts
            )

        gated_out, core_back = jax.vjp(
            core_at, query_lin, key_lin, value_lin, gate_lin, beta_lin, conv_here, head_scale
        )
        gated_low = gated_out.astype(jnp.bfloat16)
        gated_rows = heads_to_rows(gated_low, tp, fsdp, rows)
        mixed_partial = matmul_rows(gated_rows, out_rows)
        residual = inputs + tp_scatter_low(
            mixed_partial.reshape(micro_count, slot * tp, width), 1
        ).reshape(micro_count * slot, width)

        inner_norm, inner_norm_back = jax.vjp(rms_norm, residual, gain_swiglu.astype(jnp.float32))
        inner_low = inner_norm.astype(jnp.bfloat16)
        inner_group = tp_gather(inner_low.reshape(micro_count, slot, width), 1).reshape(
            group_tokens, width
        )
        gate_act = matmul_rows(inner_group, gate_half)
        up_act = matmul_rows(inner_group, up_half)
        hidden, hidden_back = jax.vjp(swiglu_mix, gate_act, up_act)
        hidden_low = hidden.astype(jnp.bfloat16)
        partial_rows = matmul_rows(hidden_low, down_half)
        branch_rows = tp_scatter_low(partial_rows.reshape(micro_count, slot * tp, width), 1)
        block_out = (residual.reshape(micro_count, slot, width) + branch_rows).astype(jnp.bfloat16)

        out_back = cotangent.astype(jnp.float32) * pad_mask.astype(jnp.float32)[:, :, None]
        out_back_low = out_back.astype(jnp.bfloat16)
        upstream_group = tp_gather(out_back_low, 1).reshape(group_tokens, width)
        gate_back, up_back = hidden_back(back_product(upstream_group, down_half))
        gate_back_low = gate_back.astype(jnp.bfloat16)
        up_back_low = up_back.astype(jnp.bfloat16)
        inner_part = back_product(gate_back_low, gate_half) + back_product(up_back_low, up_half)
        inner_back = tp_scatter_low(inner_part.reshape(micro_count, slot * tp, width), 1)
        residual_part, swiglu_gain_term = inner_norm_back(
            inner_back.reshape(micro_count * slot, width)
        )
        residual_back = out_back.reshape(micro_count * slot, width) + residual_part
        mixed_back = residual_back.astype(jnp.bfloat16)
        mixed_group = tp_gather(mixed_back.reshape(micro_count, slot, width), 1).reshape(
            group_tokens, width
        )
        gated_back_rows = back_product(mixed_group, out_rows)
        gated_back = rows_to_heads(gated_back_rows, tp, fsdp, rows)
        query_back, key_back, value_back, gate_lin_back, beta_back, conv_term, head_term = (
            core_back(gated_back)
        )
        query_low = query_back.astype(jnp.bfloat16)
        key_low = key_back.astype(jnp.bfloat16)
        value_low = value_back.astype(jnp.bfloat16)
        gate_low = gate_lin_back.astype(jnp.bfloat16)
        beta_low = beta_back.astype(jnp.bfloat16)
        normed_part = (
            back_product(query_low, query_cols)
            + back_product(key_low, key_cols)
            + back_product(value_low, value_cols)
            + back_product(gate_low, gate_cols)
            + back_product(beta_low, beta_here)
        )
        normed_back = tp_scatter_low(normed_part.reshape(micro_count, slot * tp, width), 1)
        input_part, mixer_gain_term = norm_back(normed_back.reshape(micro_count * slot, width))
        tokens_grad = (residual_back + input_part).reshape(micro_count, slot, width)

        swiglu_gate_sum = left_product(inner_group, gate_back_low)
        swiglu_up_sum = left_product(inner_group, up_back_low)
        swiglu_down_sum = left_product(hidden_low, upstream_group)
        gate_grad_rows = fsdp_scatter_low(swiglu_gate_sum, 0)
        swiglu_gate_grad = exchange(
            gate_grad_rows.reshape(inner, owned_rows, hidden_half // inner), INNER_AXES, 0, 2
        ).reshape(owned_rows, hidden_half)
        up_grad_rows = fsdp_scatter_low(swiglu_up_sum, 0)
        swiglu_up_grad = exchange(
            up_grad_rows.reshape(inner, owned_rows, hidden_half // inner), INNER_AXES, 0, 2
        ).reshape(owned_rows, hidden_half)
        down_grad_cols = fsdp_scatter_low(swiglu_down_sum, 1)
        swiglu_down_grad = exchange(
            down_grad_cols.reshape(hidden_half // inner, inner, owned_rows), INNER_AXES, 1, 0
        ).reshape(hidden_half, owned_rows)

        out_grad = fsdp_scatter_low(left_product(gated_rows, mixed_group), 0)
        query_grad = column_grad(left_product(normed_group, query_low), tp)
        key_grad = column_grad(left_product(normed_group, key_low), tp)
        value_grad = column_grad(left_product(normed_group, value_low), tp)
        gate_grad = column_grad(left_product(normed_group, gate_low), tp)
        beta_sum = left_product(normed_group, beta_low)
        beta_wide = lax.dynamic_update_slice_in_dim(
            jnp.zeros((width, head_count), jnp.float32), beta_sum, position * heads_here, axis=1
        )
        conv_wide = lax.dynamic_update_slice_in_dim(
            jnp.zeros(conv_full.shape, jnp.float32), conv_term, position * cols_here, axis=2
        )
        taps = conv_wide.shape[0] * conv_wide.shape[1]
        small_rows = jnp.concatenate(
            [
                conv_wide.reshape(taps, n_all, -1).transpose(1, 0, 2).reshape(n_all, -1),
                beta_wide.reshape(n_all, -1),
                mixer_gain_term.reshape(n_all, -1),
                swiglu_gain_term.reshape(n_all, -1),
                jnp.broadcast_to(head_term[None, :], (n_all, head_term.shape[0])),
            ],
            axis=1,
        )
        small_out = lax.psum_scatter(small_rows, ALL_AXES, scatter_dimension=0, tiled=False)
        conv_grad = small_out[:conv_size].reshape(conv_weight.shape)
        beta_grad = small_out[conv_size : conv_size + beta_size].reshape(beta_weight.shape)
        mixer_gain_grad = small_out[conv_size + beta_size : conv_size + beta_size + rows]
        swiglu_gain_grad = small_out[conv_size + beta_size + rows : conv_size + beta_size + 2 * rows]
        head_total = small_out[conv_size + beta_size + 2 * rows :]
        return (
            block_out,
            tokens_grad,
            query_grad,
            key_grad,
            value_grad,
            gate_grad,
            beta_grad,
            out_grad,
            conv_grad,
            mixer_gain_grad,
            head_total,
            swiglu_gain_grad,
            swiglu_gate_grad,
            swiglu_up_grad,
            swiglu_down_grad,
        )

    return on_device


def solution(mesh):
    n_dp = mesh.shape["dp"]
    n_mlp = mesh.shape["mlp"]
    devices = np.asarray(mesh.devices).reshape(n_dp // 2, 2, n_mlp)
    split_mesh = Mesh(devices, ALL_AXES)
    sizes = dict(zip(ALL_AXES, devices.shape))
    tp = int(np.prod([sizes[name] for name in TP_AXES]))
    fsdp = int(np.prod([sizes[name] for name in FSDP_AXES]))
    inner = int(np.prod([sizes[name] for name in INNER_AXES]))
    rows_axes = ALL_AXES
    swiglu_rows = ("dq", "core")
    placed = (
        P(None, rows_axes, None),
        P(None, rows_axes, None),
        P(None, rows_axes),
        P(None, rows_axes),
        P(rows_axes, None),
        P(rows_axes, None),
        P(rows_axes, None),
        P(rows_axes, None),
        P(rows_axes, None),
        P(rows_axes, None),
        P(None, None, rows_axes),
        P(rows_axes),
        P(),
        P(rows_axes),
        P(swiglu_rows, "mlp"),
        P(swiglu_rows, "mlp"),
        P("mlp", swiglu_rows),
    )
    return jax.shard_map(
        make_on_device(tp, fsdp, inner),
        mesh=split_mesh,
        in_specs=placed,
        out_specs=(
            P(None, rows_axes, None),
            P(None, rows_axes, None),
            P(rows_axes, None),
            P(rows_axes, None),
            P(rows_axes, None),
            P(rows_axes, None),
            P(rows_axes, None),
            P(rows_axes, None),
            P(None, None, rows_axes),
            P(rows_axes),
            P(),
            P(rows_axes),
            P(swiglu_rows, "mlp"),
            P(swiglu_rows, "mlp"),
            P("mlp", swiglu_rows),
        ),
        check_vma=False,
    )
```

```python
import jax
import jax.numpy as jnp
import numpy as np
from jax import lax
from jax.sharding import Mesh
from jax.sharding import PartitionSpec as P

TP_AXES = ("core", "mlp")
ALL_AXES = ("dq", "core", "mlp")
FSDP_AXES = tuple(name for name in ALL_AXES if name not in TP_AXES)
INNER_AXES = tuple(name for name in TP_AXES if name != "mlp")


def rms_norm(values, scale_gain):
    return (
        values * lax.rsqrt(jnp.mean(values * values, axis=-1, keepdims=True) + 1e-06) * scale_gain
    )


def short_conv(linear, tap_weights, starts):
    length = linear.shape[0]
    block_len = length // starts.shape[0]
    position = jnp.arange(length)
    restart = jnp.repeat(starts, block_len)
    summed = linear * tap_weights[0]
    for offset in range(1, tap_weights.shape[0]):
        shifted = jnp.concatenate(
            [jnp.zeros((offset, linear.shape[1]), linear.dtype), linear[: length - offset]], axis=0
        )
        usable = ((position % block_len >= offset) | (restart == 0)).astype(linear.dtype)
        summed = summed + shifted * tap_weights[offset] * usable[:, None]
    return summed


def outer_product_result(form, first, second):
    return jnp.einsum(form, first, second, precision=lax.Precision.HIGHEST)


def delta_core(queries, keys, values, betas, starts):
    length, head_count, head_width = queries.shape
    value_width = values.shape[2]
    block_count = starts.shape[0]
    block_len = length // block_count

    def blocked(array):
        return array.reshape(block_count, block_len, head_count, -1).transpose(0, 2, 1, 3)

    query_blocks = blocked(queries)
    key_blocks = blocked(keys)
    value_blocks = blocked(values)
    beta_blocks = betas.reshape(block_count, block_len, head_count).transpose(0, 2, 1)[..., None]
    position = jnp.arange(block_len)
    strict = (position[:, None] > position[None, :]).astype(queries.dtype)
    causal = (position[:, None] >= position[None, :]).astype(queries.dtype)
    weighted = key_blocks * beta_blocks
    negative = -outer_product_result("nhik,nhjk->nhij", weighted, key_blocks) * strict
    inverse = jnp.eye(block_len, dtype=queries.dtype) + negative
    power_term = negative
    for doubling in range(5):
        power_term = outer_product_result("nhij,nhjk->nhik", power_term, power_term)
        inverse = inverse + outer_product_result("nhij,nhjk->nhik", inverse, power_term)
    key_mix = outer_product_result("nhij,nhjk->nhik", inverse, weighted)
    value_mix = outer_product_result("nhij,nhjk->nhik", inverse, value_blocks * beta_blocks)
    scores = outer_product_result("nhik,nhjk->nhij", query_blocks, key_blocks) * causal

    def advance(current_state, block_items):
        (
            query_slice,
            key_slice,
            key_mixture_slice,
            value_mixture_slice,
            attention_score_slice,
            restart,
        ) = block_items
        current_state = current_state * (1 - restart).astype(current_state.dtype)
        adjusted_result = value_mixture_slice - outer_product_result(
            "pzd,pde->pze", key_mixture_slice, current_state
        )
        produced_output = outer_product_result(
            "pzd,pde->pze", query_slice, current_state
        ) + outer_product_result("lqz,lzr->lqr", attention_score_slice, adjusted_result)
        current_state = current_state + outer_product_result(
            "ixl,ixr->ilr", key_slice, adjusted_result
        )
        return (current_state, produced_output)

    initial = jnp.zeros((head_count, head_width, value_width), queries.dtype)
    final_state, produced_output = lax.scan(
        advance, initial, (query_blocks, key_blocks, key_mix, value_mix, scores, starts)
    )
    return produced_output.transpose(0, 2, 1, 3).reshape(length, head_count, value_width)


def delta_core_reset(queries, keys, values, betas, block_len):
    length, head_count, head_width = queries.shape
    block_count = length // block_len

    def blocked(array):
        return array.reshape(block_count, block_len, head_count, -1).transpose(0, 2, 1, 3)

    query_blocks = blocked(queries)
    key_blocks = blocked(keys)
    value_blocks = blocked(values)
    beta_blocks = betas.reshape(block_count, block_len, head_count).transpose(0, 2, 1)[..., None]
    position = jnp.arange(block_len)
    strict = (position[:, None] > position[None, :]).astype(queries.dtype)
    causal = (position[:, None] >= position[None, :]).astype(queries.dtype)
    weighted = key_blocks * beta_blocks
    negative = -outer_product_result("nhik,nhjk->nhij", weighted, key_blocks) * strict
    inverse = jnp.eye(block_len, dtype=queries.dtype) + negative
    power_term = negative
    for doubling in range(5):
        power_term = outer_product_result("nhij,nhjk->nhik", power_term, power_term)
        inverse = inverse + outer_product_result("nhij,nhjk->nhik", inverse, power_term)
    value_mix = outer_product_result("nhij,nhjk->nhik", inverse, value_blocks * beta_blocks)
    scores = outer_product_result("nhik,nhjk->nhij", query_blocks, key_blocks) * causal
    produced_output = outer_product_result("nhqz,nhzr->nhqr", scores, value_mix)
    return produced_output.transpose(0, 2, 1, 3).reshape(length, head_count, -1)


def mixer_core(
    query_lin, key_lin, value_lin, gate_lin, beta_lin, conv_taps, head_scale, starts, reset_len
):
    length = query_lin.shape[0]
    head_count = beta_lin.shape[1]
    head_width = query_lin.shape[1] // head_count
    queries = jax.nn.silu(short_conv(query_lin, conv_taps[0], starts)).reshape(
        length, head_count, head_width
    )
    keys = jax.nn.silu(short_conv(key_lin, conv_taps[1], starts)).reshape(
        length, head_count, head_width
    )
    values = jax.nn.silu(short_conv(value_lin, conv_taps[2], starts)).reshape(
        length, head_count, head_width
    )
    queries = (
        queries
        * lax.rsqrt(jnp.sum(queries * queries, axis=-1, keepdims=True) + 1e-06)
        * head_width ** (-0.5)
    )
    keys = keys * lax.rsqrt(jnp.sum(keys * keys, axis=-1, keepdims=True) + 1e-06)
    if reset_len:
        recurrent = delta_core_reset(queries, keys, values, jax.nn.sigmoid(beta_lin), reset_len)
    else:
        recurrent = delta_core(queries, keys, values, jax.nn.sigmoid(beta_lin), starts)
    normed = (
        recurrent
        * lax.rsqrt(jnp.mean(recurrent * recurrent, axis=-1, keepdims=True) + 1e-05)
        * head_scale
    )
    gated_out = normed * jax.nn.silu(gate_lin.reshape(length, head_count, head_width))
    return gated_out.reshape(length, head_count * head_width)


def swiglu_mix(gate_act, up_act):
    return jax.nn.silu(gate_act) * up_act


def matmul_rows(left, right):
    return jnp.dot(left, right, preferred_element_type=jnp.float32)


def left_product(first, second):
    return jnp.einsum("tf,tg->fg", first, second, preferred_element_type=jnp.float32)


def back_product(gradient, weight):
    return jnp.einsum("tg,fg->tf", gradient, weight, preferred_element_type=jnp.float32)


def exchange(value, axes, split_axis, concat_axis):
    if not axes:
        return value
    return lax.all_to_all(value, axes, split_axis, concat_axis, tiled=True)


def tp_gather(value, tp):
    spread = jnp.broadcast_to(value[:, None], (value.shape[0], tp) + value.shape[1:])
    moved = exchange(spread, TP_AXES, 1, 1)
    return moved.reshape((value.shape[0], tp * value.shape[1]) + value.shape[2:])


def tp_scatter_sum(value, tp):
    micro, group, width = value.shape
    staged = value.astype(jnp.bfloat16).reshape(micro, tp, group // tp, width)
    moved = exchange(staged, TP_AXES, 1, 1)
    return jnp.sum(moved.astype(jnp.float32), axis=1)


def fsdp_gather_flat(value):
    return lax.all_gather(value, FSDP_AXES, axis=0, tiled=False)


def fsdp_scatter_flat(value, fsdp):
    length = value.shape[1]
    pieces = 16 if length % 16 == 0 else 1
    reduced = lax.psum_scatter(
        value.astype(jnp.bfloat16).reshape(fsdp * pieces, length // pieces),
        FSDP_AXES,
        scatter_dimension=0,
        tiled=True,
    )
    return reduced.reshape(length).astype(jnp.float32)


def heads_to_rows(values, tp, fsdp, rows):
    count = values.shape[0]
    staged = values.reshape(count, 1, fsdp // tp, tp, rows)
    moved = exchange(staged, TP_AXES, 3, 1)
    return moved.reshape(count, fsdp * rows)


def rows_to_heads(values, tp, fsdp, rows):
    count = values.shape[0]
    staged = values.reshape(count, tp, fsdp // tp, 1, rows)
    moved = exchange(staged, TP_AXES, 1, 3)
    return moved.reshape(count, fsdp * rows)


def make_on_device(tp, fsdp, inner):
    def on_device(
        tokens,
        cotangent,
        group_start,
        pad_mask,
        query_weight,
        key_weight,
        value_weight,
        gate_weight,
        beta_weight,
        out_weight,
        conv_weight,
        mixer_gain,
        head_gain,
        swiglu_gain,
        swiglu_gate,
        swiglu_up,
        swiglu_down,
    ):
        micro_count, slot, width = tokens.shape
        n_all = tp * fsdp
        rows = query_weight.shape[0]
        head_count = beta_weight.shape[1]
        heads_here = head_count // tp
        cols_here = width // tp
        position = lax.axis_index(TP_AXES)
        head_scale = head_gain.astype(jnp.float32)
        reset_len = slot if group_start.shape[1] == 1 else 0

        column_owned = jnp.stack([query_weight, key_weight, value_weight, gate_weight])
        column_chunks = column_owned.reshape(4, rows, tp, cols_here).transpose(2, 0, 1, 3)
        small_pack = jnp.concatenate(
            [
                conv_weight.reshape(-1),
                beta_weight.reshape(-1),
                mixer_gain.reshape(-1),
                swiglu_gain.reshape(-1),
            ]
        )
        small_size = small_pack.shape[0]
        swap_in = jnp.concatenate(
            [
                column_chunks.reshape(tp, -1),
                jnp.broadcast_to(small_pack[None, :], (tp, small_size)),
            ],
            axis=1,
        )
        swap_out = exchange(swap_in, TP_AXES, 0, 0)
        column_size = 4 * rows * cols_here
        column_group = (
            swap_out[:, :column_size].reshape(tp, 4, rows, cols_here).transpose(1, 0, 2, 3)
        )
        mixer_flat = jnp.concatenate(
            [
                column_group.reshape(-1),
                out_weight.reshape(-1),
                swap_out[:, column_size:].reshape(-1),
            ]
        )
        mixer_all = fsdp_gather_flat(mixer_flat)
        group_size = tp * column_size
        column_all = (
            mixer_all[:, :group_size]
            .reshape(fsdp, 4, tp * rows, cols_here)
            .transpose(1, 0, 2, 3)
            .reshape(4, width, cols_here)
        )
        query_cols, key_cols, value_cols, gate_cols = (column_all[index] for index in range(4))
        out_size = rows * width
        out_rows = mixer_all[:, group_size : group_size + out_size].reshape(fsdp * rows, width)
        small_all = mixer_all[:, group_size + out_size :].reshape(n_all, small_size)
        conv_size = conv_weight.size
        beta_size = beta_weight.size
        conv_full = (
            small_all[:, :conv_size]
            .reshape((n_all,) + conv_weight.shape)
            .transpose(1, 2, 0, 3)
            .reshape(conv_weight.shape[0], conv_weight.shape[1], -1)
        )
        beta_full = small_all[:, conv_size : conv_size + beta_size].reshape(-1, head_count)
        gain_mixer = small_all[:, conv_size + beta_size : conv_size + beta_size + rows].reshape(-1)
        gain_swiglu = small_all[:, conv_size + beta_size + rows :].reshape(-1)
        conv_here = lax.dynamic_slice_in_dim(
            conv_full.astype(jnp.float32), position * cols_here, cols_here, axis=2
        )
        beta_here = lax.dynamic_slice_in_dim(beta_full, position * heads_here, heads_here, axis=1)

        owned_rows, hidden_half = swiglu_gate.shape
        hidden_here = hidden_half // inner
        gate_chunks = swiglu_gate.reshape(owned_rows, inner, hidden_here).transpose(1, 0, 2)
        up_chunks = swiglu_up.reshape(owned_rows, inner, hidden_here).transpose(1, 0, 2)
        down_chunks = swiglu_down.reshape(inner, hidden_here, owned_rows)
        ff_in = jnp.concatenate(
            [
                gate_chunks.reshape(inner, -1),
                up_chunks.reshape(inner, -1),
                down_chunks.reshape(inner, -1),
            ],
            axis=1,
        )
        ff_out = exchange(ff_in, INNER_AXES, 0, 0)
        ff_all = fsdp_gather_flat(ff_out.reshape(-1)).reshape(fsdp, inner, 3, -1)
        piece = owned_rows * hidden_here
        gate_half = ff_all[:, :, 0, :piece].reshape(width, hidden_here)
        up_half = ff_all[:, :, 1, :piece].reshape(width, hidden_here)
        down_half = (
            ff_all[:, :, 2, :piece]
            .reshape(fsdp, inner, hidden_here, owned_rows)
            .transpose(2, 0, 1, 3)
            .reshape(hidden_here, width)
        )

        inputs = tokens.astype(jnp.float32).reshape(micro_count * slot, width)
        normed, norm_back = jax.vjp(rms_norm, inputs, gain_mixer.astype(jnp.float32))
        normed_low = normed.astype(jnp.bfloat16)
        group_tokens = micro_count * slot * tp
        normed_group = tp_gather(normed_low.reshape(micro_count, slot, width), tp).reshape(
            group_tokens, width
        )
        starts = tp_gather(group_start, tp).reshape(-1)
        out_back = cotangent.astype(jnp.float32) * pad_mask.astype(jnp.float32)[:, :, None]
        out_back_low = out_back.astype(jnp.bfloat16)
        upstream_group = tp_gather(out_back_low, tp).reshape(group_tokens, width)

        query_lin = matmul_rows(normed_group, query_cols)
        key_lin = matmul_rows(normed_group, key_cols)
        value_lin = matmul_rows(normed_group, value_cols)
        gate_lin = matmul_rows(normed_group, gate_cols)
        beta_lin = matmul_rows(normed_group, beta_here)

        def core_at(query_in, key_in, value_in, gate_in, beta_in, conv_in, head_in):
            return mixer_core(
                query_in, key_in, value_in, gate_in, beta_in, conv_in, head_in, starts, reset_len
            )

        gated_out, core_back = jax.vjp(
            core_at, query_lin, key_lin, value_lin, gate_lin, beta_lin, conv_here, head_scale
        )
        gated_low = gated_out.astype(jnp.bfloat16)
        gated_rows = heads_to_rows(gated_low, tp, fsdp, rows)
        mixed_partial = matmul_rows(gated_rows, out_rows)
        residual = inputs + tp_scatter_sum(
            mixed_partial.reshape(micro_count, slot * tp, width), tp
        ).reshape(micro_count * slot, width)

        inner_norm, inner_norm_back = jax.vjp(rms_norm, residual, gain_swiglu.astype(jnp.float32))
        inner_low = inner_norm.astype(jnp.bfloat16)
        inner_group = tp_gather(inner_low.reshape(micro_count, slot, width), tp).reshape(
            group_tokens, width
        )
        gate_act = matmul_rows(inner_group, gate_half)
        up_act = matmul_rows(inner_group, up_half)
        hidden, hidden_back = jax.vjp(swiglu_mix, gate_act, up_act)
        hidden_low = hidden.astype(jnp.bfloat16)
        partial_rows = matmul_rows(hidden_low, down_half)
        branch_rows = tp_scatter_sum(partial_rows.reshape(micro_count, slot * tp, width), tp)
        block_out = (residual.reshape(micro_count, slot, width) + branch_rows).astype(jnp.bfloat16)

        gate_back, up_back = hidden_back(back_product(upstream_group, down_half))
        gate_back_low = gate_back.astype(jnp.bfloat16)
        up_back_low = up_back.astype(jnp.bfloat16)
        inner_part = back_product(gate_back_low, gate_half) + back_product(up_back_low, up_half)
        inner_back = tp_scatter_sum(inner_part.reshape(micro_count, slot * tp, width), tp)

        gate_sum = left_product(inner_group, gate_back_low).reshape(fsdp, -1)
        up_sum = left_product(inner_group, up_back_low).reshape(fsdp, -1)
        down_sum = (
            left_product(hidden_low, upstream_group)
            .reshape(hidden_here, fsdp, inner * owned_rows)
            .transpose(1, 0, 2)
            .reshape(fsdp, -1)
        )
        ff_reduced = fsdp_scatter_flat(
            jnp.concatenate([gate_sum, up_sum, down_sum], axis=1), fsdp
        ).reshape(3, inner, -1)
        down_for_swap = (
            ff_reduced[2]
            .reshape(hidden_here, inner, owned_rows)
            .transpose(1, 0, 2)
            .reshape(inner, -1)
        )
        ff_back = exchange(
            jnp.concatenate([ff_reduced[0], ff_reduced[1], down_for_swap], axis=1),
            INNER_AXES,
            0,
            0,
        ).reshape(inner, 3, -1)
        swiglu_gate_grad = (
            ff_back[:, 0].reshape(inner, owned_rows, hidden_here).transpose(1, 0, 2)
        ).reshape(owned_rows, hidden_half)
        swiglu_up_grad = (
            ff_back[:, 1].reshape(inner, owned_rows, hidden_here).transpose(1, 0, 2)
        ).reshape(owned_rows, hidden_half)
        swiglu_down_grad = ff_back[:, 2].reshape(hidden_half, owned_rows)

        residual_part, swiglu_gain_term = inner_norm_back(
            inner_back.reshape(micro_count * slot, width)
        )
        residual_back = out_back.reshape(micro_count * slot, width) + residual_part
        mixed_back = residual_back.astype(jnp.bfloat16)
        mixed_group = tp_gather(mixed_back.reshape(micro_count, slot, width), tp).reshape(
            group_tokens, width
        )
        gated_back_rows = back_product(mixed_group, out_rows)
        gated_back = rows_to_heads(gated_back_rows, tp, fsdp, rows)
        query_back, key_back, value_back, gate_lin_back, beta_back, conv_term, head_term = (
            core_back(gated_back)
        )
        query_low = query_back.astype(jnp.bfloat16)
        key_low = key_back.astype(jnp.bfloat16)
        value_low = value_back.astype(jnp.bfloat16)
        gate_low = gate_lin_back.astype(jnp.bfloat16)
        beta_low = beta_back.astype(jnp.bfloat16)
        normed_part = (
            back_product(query_low, query_cols)
            + back_product(key_low, key_cols)
            + back_product(value_low, value_cols)
            + back_product(gate_low, gate_cols)
            + back_product(beta_low, beta_here)
        )
        normed_back = tp_scatter_sum(normed_part.reshape(micro_count, slot * tp, width), tp)
        input_part, mixer_gain_term = norm_back(normed_back.reshape(micro_count * slot, width))
        tokens_grad = (residual_back + input_part).reshape(micro_count, slot, width)

        column_sums = jnp.stack(
            [
                left_product(normed_group, query_low),
                left_product(normed_group, key_low),
                left_product(normed_group, value_low),
                left_product(normed_group, gate_low),
            ]
        )
        column_flat = column_sums.reshape(4, fsdp, -1).transpose(1, 0, 2).reshape(fsdp, -1)
        out_flat = left_product(gated_rows, mixed_group).reshape(fsdp, -1)
        beta_sum = left_product(normed_group, beta_low)
        beta_wide = lax.dynamic_update_slice_in_dim(
            jnp.zeros((width, head_count), jnp.float32), beta_sum, position * heads_here, axis=1
        )
        conv_wide = lax.dynamic_update_slice_in_dim(
            jnp.zeros(conv_full.shape, jnp.float32), conv_term, position * cols_here, axis=2
        )
        taps = conv_wide.shape[0] * conv_wide.shape[1]
        small_rows = jnp.concatenate(
            [
                conv_wide.reshape(taps, n_all, -1).transpose(1, 0, 2).reshape(n_all, -1),
                beta_wide.reshape(n_all, -1),
                mixer_gain_term.reshape(n_all, -1),
                swiglu_gain_term.reshape(n_all, -1),
                jnp.broadcast_to(head_term[None, :], (n_all, head_term.shape[0])),
            ],
            axis=1,
        )
        small_width = small_rows.shape[1]
        small_tp = jnp.sum(
            exchange(small_rows.reshape(fsdp, tp, small_width), TP_AXES, 1, 1), axis=1
        )
        mixer_reduced = fsdp_scatter_flat(
            jnp.concatenate([column_flat, out_flat, small_tp], axis=1), fsdp
        )
        column_red = mixer_reduced[:group_size].reshape(4, tp, rows, 1, cols_here)
        column_back = exchange(column_red, TP_AXES, 1, 3).reshape(4, rows, width)
        query_grad, key_grad, value_grad, gate_grad = (column_back[index] for index in range(4))
        out_grad = mixer_reduced[group_size : group_size + out_size].reshape(rows, width)
        small_out = mixer_reduced[group_size + out_size :]
        conv_grad = small_out[:conv_size].reshape(conv_weight.shape)
        beta_grad = small_out[conv_size : conv_size + beta_size].reshape(beta_weight.shape)
        mixer_gain_grad = small_out[conv_size + beta_size : conv_size + beta_size + rows]
        swiglu_gain_grad = small_out[conv_size + beta_size + rows : conv_size + beta_size + 2 * rows]
        head_total = small_out[conv_size + beta_size + 2 * rows :]
        return (
            block_out,
            tokens_grad,
            query_grad,
            key_grad,
            value_grad,
            gate_grad,
            beta_grad,
            out_grad,
            conv_grad,
            mixer_gain_grad,
            head_total,
            swiglu_gain_grad,
            swiglu_gate_grad,
            swiglu_up_grad,
            swiglu_down_grad,
        )

    return on_device


def solution(mesh):
    n_dp = mesh.shape["dp"]
    n_mlp = mesh.shape["mlp"]
    devices = np.asarray(mesh.devices).reshape(n_dp // 2, 2, n_mlp)
    split_mesh = Mesh(devices, ALL_AXES)
    sizes = dict(zip(ALL_AXES, devices.shape))
    tp = int(np.prod([sizes[name] for name in TP_AXES]))
    fsdp = int(np.prod([sizes[name] for name in FSDP_AXES]))
    inner = int(np.prod([sizes[name] for name in INNER_AXES]))
    rows_axes = ALL_AXES
    swiglu_rows = ("dq", "core")
    placed = (
        P(None, rows_axes, None),
        P(None, rows_axes, None),
        P(None, rows_axes),
        P(None, rows_axes),
        P(rows_axes, None),
        P(rows_axes, None),
        P(rows_axes, None),
        P(rows_axes, None),
        P(rows_axes, None),
        P(rows_axes, None),
        P(None, None, rows_axes),
        P(rows_axes),
        P(),
        P(rows_axes),
        P(swiglu_rows, "mlp"),
        P(swiglu_rows, "mlp"),
        P("mlp", swiglu_rows),
    )
    return jax.shard_map(
        make_on_device(tp, fsdp, inner),
        mesh=split_mesh,
        in_specs=placed,
        out_specs=(
            P(None, rows_axes, None),
            P(None, rows_axes, None),
            P(rows_axes, None),
            P(rows_axes, None),
            P(rows_axes, None),
            P(rows_axes, None),
            P(rows_axes, None),
            P(rows_axes, None),
            P(None, None, rows_axes),
            P(rows_axes),
            P(),
            P(rows_axes),
            P(swiglu_rows, "mlp"),
            P(swiglu_rows, "mlp"),
            P("mlp", swiglu_rows),
        ),
        check_vma=False,
    )
```

```python
import jax
import jax.numpy as jnp
import numpy as np
from jax import lax
from jax.sharding import Mesh
from jax.sharding import PartitionSpec as P

TP_AXES = ("core", "mlp")
ALL_AXES = ("dq", "core", "mlp")
FSDP_AXES = tuple(name for name in ALL_AXES if name not in TP_AXES)
INNER_AXES = tuple(name for name in TP_AXES if name != "mlp")


def rms_norm(values, scale_gain):
    return (
        values * lax.rsqrt(jnp.mean(values * values, axis=-1, keepdims=True) + 1e-06) * scale_gain
    )


def short_conv(linear, tap_weights, starts):
    length = linear.shape[0]
    block_len = length // starts.shape[0]
    position = jnp.arange(length)
    restart = jnp.repeat(starts, block_len)
    summed = linear * tap_weights[0]
    for offset in range(1, tap_weights.shape[0]):
        shifted = jnp.concatenate(
            [jnp.zeros((offset, linear.shape[1]), linear.dtype), linear[: length - offset]], axis=0
        )
        usable = ((position % block_len >= offset) | (restart == 0)).astype(linear.dtype)
        summed = summed + shifted * tap_weights[offset] * usable[:, None]
    return summed


def outer_product_result(form, first, second):
    return jnp.einsum(form, first, second, precision=lax.Precision.HIGHEST)


def delta_core(queries, keys, values, betas, starts):
    length, head_count, head_width = queries.shape
    value_width = values.shape[2]
    block_count = starts.shape[0]
    block_len = length // block_count

    def blocked(array):
        return array.reshape(block_count, block_len, head_count, -1).transpose(0, 2, 1, 3)

    query_blocks = blocked(queries)
    key_blocks = blocked(keys)
    value_blocks = blocked(values)
    beta_blocks = betas.reshape(block_count, block_len, head_count).transpose(0, 2, 1)[..., None]
    position = jnp.arange(block_len)
    strict = (position[:, None] > position[None, :]).astype(queries.dtype)
    causal = (position[:, None] >= position[None, :]).astype(queries.dtype)
    weighted = key_blocks * beta_blocks
    negative = -outer_product_result("nhik,nhjk->nhij", weighted, key_blocks) * strict
    inverse = jnp.eye(block_len, dtype=queries.dtype) + negative
    power_term = negative
    for doubling in range(5):
        power_term = outer_product_result("nhij,nhjk->nhik", power_term, power_term)
        inverse = inverse + outer_product_result("nhij,nhjk->nhik", inverse, power_term)
    key_mix = outer_product_result("nhij,nhjk->nhik", inverse, weighted)
    value_mix = outer_product_result("nhij,nhjk->nhik", inverse, value_blocks * beta_blocks)
    scores = outer_product_result("nhik,nhjk->nhij", query_blocks, key_blocks) * causal

    def advance(current_state, block_items):
        (
            query_slice,
            key_slice,
            key_mixture_slice,
            value_mixture_slice,
            attention_score_slice,
            restart,
        ) = block_items
        current_state = current_state * (1 - restart).astype(current_state.dtype)
        adjusted_result = value_mixture_slice - outer_product_result(
            "pzd,pde->pze", key_mixture_slice, current_state
        )
        produced_output = outer_product_result(
            "pzd,pde->pze", query_slice, current_state
        ) + outer_product_result("lqz,lzr->lqr", attention_score_slice, adjusted_result)
        current_state = current_state + outer_product_result(
            "ixl,ixr->ilr", key_slice, adjusted_result
        )
        return (current_state, produced_output)

    initial = jnp.zeros((head_count, head_width, value_width), queries.dtype)
    final_state, produced_output = lax.scan(
        advance, initial, (query_blocks, key_blocks, key_mix, value_mix, scores, starts)
    )
    return produced_output.transpose(0, 2, 1, 3).reshape(length, head_count, value_width)


def delta_core_reset(queries, keys, values, betas, block_len):
    length, head_count, head_width = queries.shape
    block_count = length // block_len

    def blocked(array):
        return array.reshape(block_count, block_len, head_count, -1).transpose(0, 2, 1, 3)

    query_blocks = blocked(queries)
    key_blocks = blocked(keys)
    value_blocks = blocked(values)
    beta_blocks = betas.reshape(block_count, block_len, head_count).transpose(0, 2, 1)[..., None]
    position = jnp.arange(block_len)
    strict = (position[:, None] > position[None, :]).astype(queries.dtype)
    causal = (position[:, None] >= position[None, :]).astype(queries.dtype)
    weighted = key_blocks * beta_blocks
    negative = -outer_product_result("nhik,nhjk->nhij", weighted, key_blocks) * strict
    inverse = jnp.eye(block_len, dtype=queries.dtype) + negative
    power_term = negative
    for doubling in range(5):
        power_term = outer_product_result("nhij,nhjk->nhik", power_term, power_term)
        inverse = inverse + outer_product_result("nhij,nhjk->nhik", inverse, power_term)
    value_mix = outer_product_result("nhij,nhjk->nhik", inverse, value_blocks * beta_blocks)
    scores = outer_product_result("nhik,nhjk->nhij", query_blocks, key_blocks) * causal
    produced_output = outer_product_result("nhqz,nhzr->nhqr", scores, value_mix)
    return produced_output.transpose(0, 2, 1, 3).reshape(length, head_count, -1)


def mixer_core(
    query_lin, key_lin, value_lin, gate_lin, beta_lin, conv_taps, head_scale, starts, reset_len
):
    length = query_lin.shape[0]
    head_count = beta_lin.shape[1]
    head_width = query_lin.shape[1] // head_count
    queries = jax.nn.silu(short_conv(query_lin, conv_taps[0], starts)).reshape(
        length, head_count, head_width
    )
    keys = jax.nn.silu(short_conv(key_lin, conv_taps[1], starts)).reshape(
        length, head_count, head_width
    )
    values = jax.nn.silu(short_conv(value_lin, conv_taps[2], starts)).reshape(
        length, head_count, head_width
    )
    queries = (
        queries
        * lax.rsqrt(jnp.sum(queries * queries, axis=-1, keepdims=True) + 1e-06)
        * head_width ** (-0.5)
    )
    keys = keys * lax.rsqrt(jnp.sum(keys * keys, axis=-1, keepdims=True) + 1e-06)
    if reset_len:
        recurrent = delta_core_reset(queries, keys, values, jax.nn.sigmoid(beta_lin), reset_len)
    else:
        recurrent = delta_core(queries, keys, values, jax.nn.sigmoid(beta_lin), starts)
    normed = (
        recurrent
        * lax.rsqrt(jnp.mean(recurrent * recurrent, axis=-1, keepdims=True) + 1e-05)
        * head_scale
    )
    gated_out = normed * jax.nn.silu(gate_lin.reshape(length, head_count, head_width))
    return gated_out.reshape(length, head_count * head_width)


def swiglu_mix(gate_act, up_act):
    return jax.nn.silu(gate_act) * up_act


def matmul_rows(left, right):
    return jnp.dot(left, right, preferred_element_type=jnp.float32)


def left_product(first, second):
    return jnp.einsum("tf,tg->fg", first, second, preferred_element_type=jnp.float32)


def back_product(gradient, weight):
    return jnp.einsum("tg,fg->tf", gradient, weight, preferred_element_type=jnp.float32)


def tp_gather(value, axis):
    return lax.all_gather(value, TP_AXES, axis=axis, tiled=True)


def tp_scatter_low(value, axis):
    return lax.psum_scatter(
        value.astype(jnp.bfloat16), TP_AXES, scatter_dimension=axis, tiled=True
    ).astype(jnp.float32)


def fsdp_gather(value, axis):
    return lax.all_gather(value, FSDP_AXES, axis=axis, tiled=True)


def fsdp_scatter_low(value, axis):
    return lax.psum_scatter(
        value.astype(jnp.bfloat16), FSDP_AXES, scatter_dimension=axis, tiled=True
    ).astype(jnp.float32)


def exchange(value, axes, split_axis, concat_axis):
    if not axes:
        return value
    return lax.all_to_all(value, axes, split_axis, concat_axis, tiled=True)


def heads_to_rows(values, tp, fsdp, rows):
    count = values.shape[0]
    staged = values.reshape(count, 1, fsdp // tp, tp, rows)
    moved = exchange(staged, TP_AXES, 3, 1)
    return moved.reshape(count, fsdp * rows)


def rows_to_heads(values, tp, fsdp, rows):
    count = values.shape[0]
    staged = values.reshape(count, tp, fsdp // tp, 1, rows)
    moved = exchange(staged, TP_AXES, 1, 3)
    return moved.reshape(count, fsdp * rows)


def padded_rows(flat, slices, width):
    extra = -(-flat.shape[0] // (slices * width))
    extra = -(-extra // 16) * 16
    filled = jnp.pad(flat, (0, slices * extra * width - flat.shape[0]))
    return filled.reshape(slices, extra, width)


def make_on_device(tp, fsdp, inner):
    def on_device(
        tokens,
        cotangent,
        group_start,
        pad_mask,
        query_weight,
        key_weight,
        value_weight,
        gate_weight,
        beta_weight,
        out_weight,
        conv_weight,
        mixer_gain,
        head_gain,
        swiglu_gain,
        swiglu_gate,
        swiglu_up,
        swiglu_down,
    ):
        micro_count, slot, width = tokens.shape
        n_all = tp * fsdp
        rows = query_weight.shape[0]
        head_count = beta_weight.shape[1]
        heads_here = head_count // tp
        cols_here = width // tp
        group_rows = tp * rows
        position = lax.axis_index(TP_AXES)
        head_scale = head_gain.astype(jnp.float32)
        reset_len = slot if group_start.shape[1] == 1 else 0

        column_owned = jnp.stack([query_weight, key_weight, value_weight, gate_weight])
        column_swapped = exchange(
            column_owned.reshape(4, rows, tp, cols_here), TP_AXES, 2, 1
        ).reshape(4, group_rows, cols_here)
        small_pack = jnp.concatenate(
            [
                conv_weight.reshape(-1),
                beta_weight.reshape(-1),
                mixer_gain.reshape(-1),
                swiglu_gain.reshape(-1),
            ]
        )
        small_size = small_pack.shape[0]
        small_group = exchange(
            jnp.broadcast_to(small_pack[None, :], (tp, small_size)), TP_AXES, 0, 0
        )
        small_rows_in = padded_rows(small_group.reshape(-1), 5, cols_here)
        extra_in = small_rows_in.shape[1]
        mixer_stack = jnp.concatenate(
            [
                jnp.concatenate(
                    [column_swapped, out_weight.reshape(1, group_rows, cols_here)], axis=0
                ),
                small_rows_in,
            ],
            axis=1,
        )
        mixer_all = fsdp_gather(mixer_stack, 1).reshape(5, fsdp, group_rows + extra_in, cols_here)
        weight_all = mixer_all[:, :, :group_rows].reshape(5, width, cols_here)
        query_cols, key_cols, value_cols, gate_cols = (weight_all[index] for index in range(4))
        out_rows = weight_all[4].reshape(fsdp * rows, width)
        small_all = (
            mixer_all[:, :, group_rows:]
            .transpose(1, 0, 2, 3)
            .reshape(fsdp, -1)[:, : tp * small_size]
            .reshape(n_all, small_size)
        )
        conv_size = conv_weight.size
        beta_size = beta_weight.size
        conv_full = (
            small_all[:, :conv_size]
            .reshape((n_all,) + conv_weight.shape)
            .transpose(1, 2, 0, 3)
            .reshape(conv_weight.shape[0], conv_weight.shape[1], -1)
        )
        beta_full = small_all[:, conv_size : conv_size + beta_size].reshape(-1, head_count)
        gain_mixer = small_all[:, conv_size + beta_size : conv_size + beta_size + rows].reshape(-1)
        gain_swiglu = small_all[:, conv_size + beta_size + rows :].reshape(-1)
        conv_here = lax.dynamic_slice_in_dim(
            conv_full.astype(jnp.float32), position * cols_here, cols_here, axis=2
        )
        beta_here = lax.dynamic_slice_in_dim(beta_full, position * heads_here, heads_here, axis=1)

        owned_rows, hidden_half = swiglu_gate.shape
        hidden_here = hidden_half // inner
        ff_owned = jnp.stack([swiglu_gate, swiglu_up, swiglu_down.T])
        ff_swapped = exchange(
            ff_owned.reshape(3, owned_rows, inner, hidden_here), INNER_AXES, 2, 1
        ).reshape(3, inner * owned_rows, hidden_here)
        ff_all = fsdp_gather(ff_swapped, 1)
        gate_half = ff_all[0]
        up_half = ff_all[1]
        down_half_t = ff_all[2]

        inputs = tokens.astype(jnp.float32).reshape(micro_count * slot, width)
        normed, norm_back = jax.vjp(rms_norm, inputs, gain_mixer.astype(jnp.float32))
        normed_low = normed.astype(jnp.bfloat16)
        group_tokens = micro_count * slot * tp
        normed_group = tp_gather(normed_low.reshape(micro_count, slot, width), 1).reshape(
            group_tokens, width
        )
        starts = tp_gather(group_start, 1).reshape(-1)

        query_lin = matmul_rows(normed_group, query_cols)
        key_lin = matmul_rows(normed_group, key_cols)
        value_lin = matmul_rows(normed_group, value_cols)
        gate_lin = matmul_rows(normed_group, gate_cols)
        beta_lin = matmul_rows(normed_group, beta_here)

        def core_at(query_in, key_in, value_in, gate_in, beta_in, conv_in, head_in):
            return mixer_core(
                query_in, key_in, value_in, gate_in, beta_in, conv_in, head_in, starts, reset_len
            )

        gated_out, core_back = jax.vjp(
            core_at, query_lin, key_lin, value_lin, gate_lin, beta_lin, conv_here, head_scale
        )
        gated_low = gated_out.astype(jnp.bfloat16)
        gated_rows = heads_to_rows(gated_low, tp, fsdp, rows)
        mixed_partial = matmul_rows(gated_rows, out_rows)
        residual = inputs + tp_scatter_low(
            mixed_partial.reshape(micro_count, slot * tp, width), 1
        ).reshape(micro_count * slot, width)

        inner_norm, inner_norm_back = jax.vjp(rms_norm, residual, gain_swiglu.astype(jnp.float32))
        inner_low = inner_norm.astype(jnp.bfloat16)
        inner_group = tp_gather(inner_low.reshape(micro_count, slot, width), 1).reshape(
            group_tokens, width
        )
        gate_act = matmul_rows(inner_group, gate_half)
        up_act = matmul_rows(inner_group, up_half)
        hidden, hidden_back = jax.vjp(swiglu_mix, gate_act, up_act)
        hidden_low = hidden.astype(jnp.bfloat16)
        partial_rows = back_product(hidden_low, down_half_t)
        branch_rows = tp_scatter_low(partial_rows.reshape(micro_count, slot * tp, width), 1)
        block_out = (residual.reshape(micro_count, slot, width) + branch_rows).astype(jnp.bfloat16)

        out_back = cotangent.astype(jnp.float32) * pad_mask.astype(jnp.float32)[:, :, None]
        out_back_low = out_back.astype(jnp.bfloat16)
        upstream_group = tp_gather(out_back_low, 1).reshape(group_tokens, width)
        gate_back, up_back = hidden_back(matmul_rows(upstream_group, down_half_t))
        gate_back_low = gate_back.astype(jnp.bfloat16)
        up_back_low = up_back.astype(jnp.bfloat16)
        inner_part = back_product(gate_back_low, gate_half) + back_product(up_back_low, up_half)
        inner_back = tp_scatter_low(inner_part.reshape(micro_count, slot * tp, width), 1)

        ff_sums = jnp.stack(
            [
                left_product(inner_group, gate_back_low),
                left_product(inner_group, up_back_low),
                left_product(upstream_group, hidden_low),
            ]
        )
        ff_reduced = fsdp_scatter_low(ff_sums, 1)
        ff_back = exchange(
            ff_reduced.reshape(3, inner, owned_rows, 1, hidden_here), INNER_AXES, 1, 3
        ).reshape(3, owned_rows, hidden_half)
        swiglu_gate_grad = ff_back[0]
        swiglu_up_grad = ff_back[1]
        swiglu_down_grad = ff_back[2].T

        residual_part, swiglu_gain_term = inner_norm_back(
            inner_back.reshape(micro_count * slot, width)
        )
        residual_back = out_back.reshape(micro_count * slot, width) + residual_part
        mixed_back = residual_back.astype(jnp.bfloat16)
        mixed_group = tp_gather(mixed_back.reshape(micro_count, slot, width), 1).reshape(
            group_tokens, width
        )
        gated_back_rows = back_product(mixed_group, out_rows)
        gated_back = rows_to_heads(gated_back_rows, tp, fsdp, rows)
        query_back, key_back, value_back, gate_lin_back, beta_back, conv_term, head_term = (
            core_back(gated_back)
        )
        query_low = query_back.astype(jnp.bfloat16)
        key_low = key_back.astype(jnp.bfloat16)
        value_low = value_back.astype(jnp.bfloat16)
        gate_low = gate_lin_back.astype(jnp.bfloat16)
        beta_low = beta_back.astype(jnp.bfloat16)
        normed_part = (
            back_product(query_low, query_cols)
            + back_product(key_low, key_cols)
            + back_product(value_low, value_cols)
            + back_product(gate_low, gate_cols)
            + back_product(beta_low, beta_here)
        )
        normed_back = tp_scatter_low(normed_part.reshape(micro_count, slot * tp, width), 1)
        input_part, mixer_gain_term = norm_back(normed_back.reshape(micro_count * slot, width))
        tokens_grad = (residual_back + input_part).reshape(micro_count, slot, width)

        mixer_sums = jnp.stack(
            [
                left_product(normed_group, query_low),
                left_product(normed_group, key_low),
                left_product(normed_group, value_low),
                left_product(normed_group, gate_low),
                left_product(gated_rows, mixed_group).reshape(width, cols_here),
            ]
        ).reshape(5, fsdp, group_rows, cols_here)
        beta_sum = left_product(normed_group, beta_low)
        beta_wide = lax.dynamic_update_slice_in_dim(
            jnp.zeros((width, head_count), jnp.float32), beta_sum, position * heads_here, axis=1
        )
        conv_wide = lax.dynamic_update_slice_in_dim(
            jnp.zeros(conv_full.shape, jnp.float32), conv_term, position * cols_here, axis=2
        )
        taps = conv_wide.shape[0] * conv_wide.shape[1]
        small_terms = jnp.concatenate(
            [
                conv_wide.reshape(taps, n_all, -1).transpose(1, 0, 2).reshape(n_all, -1),
                beta_wide.reshape(n_all, -1),
                mixer_gain_term.reshape(n_all, -1),
                swiglu_gain_term.reshape(n_all, -1),
                jnp.broadcast_to(head_term[None, :], (n_all, head_term.shape[0])),
            ],
            axis=1,
        )
        small_width = small_terms.shape[1]
        small_tp = jnp.sum(
            exchange(small_terms.reshape(fsdp, tp, small_width), TP_AXES, 1, 1), axis=1
        )
        small_block = jax.vmap(lambda flat: padded_rows(flat, 5, cols_here))(small_tp)
        extra_out = small_block.shape[2]
        reduce_in = jnp.concatenate([mixer_sums, small_block.transpose(1, 0, 2, 3)], axis=2)
        mixer_reduced = fsdp_scatter_low(
            reduce_in.reshape(5, fsdp * (group_rows + extra_out), cols_here), 1
        )
        column_back = exchange(
            mixer_reduced[:4, :group_rows].reshape(4, tp, rows, 1, cols_here), TP_AXES, 1, 3
        ).reshape(4, rows, width)
        query_grad, key_grad, value_grad, gate_grad = (column_back[index] for index in range(4))
        out_grad = mixer_reduced[4, :group_rows].reshape(rows, width)
        small_out = mixer_reduced[:, group_rows:].reshape(-1)[:small_width]
        conv_grad = small_out[:conv_size].reshape(conv_weight.shape)
        beta_grad = small_out[conv_size : conv_size + beta_size].reshape(beta_weight.shape)
        mixer_gain_grad = small_out[conv_size + beta_size : conv_size + beta_size + rows]
        swiglu_gain_grad = small_out[conv_size + beta_size + rows : conv_size + beta_size + 2 * rows]
        head_total = small_out[conv_size + beta_size + 2 * rows :]
        return (
            block_out,
            tokens_grad,
            query_grad,
            key_grad,
            value_grad,
            gate_grad,
            beta_grad,
            out_grad,
            conv_grad,
            mixer_gain_grad,
            head_total,
            swiglu_gain_grad,
            swiglu_gate_grad,
            swiglu_up_grad,
            swiglu_down_grad,
        )

    return on_device


def solution(mesh):
    n_dp = mesh.shape["dp"]
    n_mlp = mesh.shape["mlp"]
    devices = np.asarray(mesh.devices).reshape(n_dp // 2, 2, n_mlp)
    split_mesh = Mesh(devices, ALL_AXES)
    sizes = dict(zip(ALL_AXES, devices.shape))
    tp = int(np.prod([sizes[name] for name in TP_AXES]))
    fsdp = int(np.prod([sizes[name] for name in FSDP_AXES]))
    inner = int(np.prod([sizes[name] for name in INNER_AXES]))
    rows_axes = ALL_AXES
    swiglu_rows = ("dq", "core")
    placed = (
        P(None, rows_axes, None),
        P(None, rows_axes, None),
        P(None, rows_axes),
        P(None, rows_axes),
        P(rows_axes, None),
        P(rows_axes, None),
        P(rows_axes, None),
        P(rows_axes, None),
        P(rows_axes, None),
        P(rows_axes, None),
        P(None, None, rows_axes),
        P(rows_axes),
        P(),
        P(rows_axes),
        P(swiglu_rows, "mlp"),
        P(swiglu_rows, "mlp"),
        P("mlp", swiglu_rows),
    )
    return jax.shard_map(
        make_on_device(tp, fsdp, inner),
        mesh=split_mesh,
        in_specs=placed,
        out_specs=(
            P(None, rows_axes, None),
            P(None, rows_axes, None),
            P(rows_axes, None),
            P(rows_axes, None),
            P(rows_axes, None),
            P(rows_axes, None),
            P(rows_axes, None),
            P(rows_axes, None),
            P(None, None, rows_axes),
            P(rows_axes),
            P(),
            P(rows_axes),
            P(swiglu_rows, "mlp"),
            P(swiglu_rows, "mlp"),
            P("mlp", swiglu_rows),
        ),
        check_vma=False,
    )
```

```python
import jax
import jax.numpy as jnp
import numpy as np
from jax import lax
from jax.sharding import Mesh
from jax.sharding import PartitionSpec as P

TP_AXES = ("core", "mlp")
ALL_AXES = ("dq", "core", "mlp")
FSDP_AXES = tuple(name for name in ALL_AXES if name not in TP_AXES)
INNER_AXES = tuple(name for name in TP_AXES if name != "mlp")


def rms_norm(values, scale_gain):
    return (
        values * lax.rsqrt(jnp.mean(values * values, axis=-1, keepdims=True) + 1e-06) * scale_gain
    )


def short_conv(linear, tap_weights, starts):
    length = linear.shape[0]
    block_len = length // starts.shape[0]
    position = jnp.arange(length)
    restart = jnp.repeat(starts, block_len)
    summed = linear * tap_weights[0]
    for offset in range(1, tap_weights.shape[0]):
        shifted = jnp.concatenate(
            [jnp.zeros((offset, linear.shape[1]), linear.dtype), linear[: length - offset]], axis=0
        )
        usable = ((position % block_len >= offset) | (restart == 0)).astype(linear.dtype)
        summed = summed + shifted * tap_weights[offset] * usable[:, None]
    return summed


def outer_product_result(form, first, second):
    return jnp.einsum(form, first, second, precision=lax.Precision.HIGHEST)


def delta_core(queries, keys, values, betas, starts):
    length, head_count, head_width = queries.shape
    value_width = values.shape[2]
    block_count = starts.shape[0]
    block_len = length // block_count

    def blocked(array):
        return array.reshape(block_count, block_len, head_count, -1).transpose(0, 2, 1, 3)

    query_blocks = blocked(queries)
    key_blocks = blocked(keys)
    value_blocks = blocked(values)
    beta_blocks = betas.reshape(block_count, block_len, head_count).transpose(0, 2, 1)[..., None]
    position = jnp.arange(block_len)
    strict = (position[:, None] > position[None, :]).astype(queries.dtype)
    causal = (position[:, None] >= position[None, :]).astype(queries.dtype)
    weighted = key_blocks * beta_blocks
    negative = -outer_product_result("nhik,nhjk->nhij", weighted, key_blocks) * strict
    inverse = jnp.eye(block_len, dtype=queries.dtype) + negative
    power_term = negative
    for doubling in range(5):
        power_term = outer_product_result("nhij,nhjk->nhik", power_term, power_term)
        inverse = inverse + outer_product_result("nhij,nhjk->nhik", inverse, power_term)
    key_mix = outer_product_result("nhij,nhjk->nhik", inverse, weighted)
    value_mix = outer_product_result("nhij,nhjk->nhik", inverse, value_blocks * beta_blocks)
    scores = outer_product_result("nhik,nhjk->nhij", query_blocks, key_blocks) * causal

    def advance(current_state, block_items):
        (
            query_slice,
            key_slice,
            key_mixture_slice,
            value_mixture_slice,
            attention_score_slice,
            restart,
        ) = block_items
        current_state = current_state * (1 - restart).astype(current_state.dtype)
        adjusted_result = value_mixture_slice - outer_product_result(
            "pzd,pde->pze", key_mixture_slice, current_state
        )
        produced_output = outer_product_result(
            "pzd,pde->pze", query_slice, current_state
        ) + outer_product_result("lqz,lzr->lqr", attention_score_slice, adjusted_result)
        current_state = current_state + outer_product_result(
            "ixl,ixr->ilr", key_slice, adjusted_result
        )
        return (current_state, produced_output)

    initial = jnp.zeros((head_count, head_width, value_width), queries.dtype)
    final_state, produced_output = lax.scan(
        advance, initial, (query_blocks, key_blocks, key_mix, value_mix, scores, starts)
    )
    return produced_output.transpose(0, 2, 1, 3).reshape(length, head_count, value_width)


def delta_core_reset(queries, keys, values, betas, block_len):
    length, head_count, head_width = queries.shape
    block_count = length // block_len

    def blocked(array):
        return array.reshape(block_count, block_len, head_count, -1).transpose(0, 2, 1, 3)

    query_blocks = blocked(queries)
    key_blocks = blocked(keys)
    value_blocks = blocked(values)
    beta_blocks = betas.reshape(block_count, block_len, head_count).transpose(0, 2, 1)[..., None]
    position = jnp.arange(block_len)
    strict = (position[:, None] > position[None, :]).astype(queries.dtype)
    causal = (position[:, None] >= position[None, :]).astype(queries.dtype)
    weighted = key_blocks * beta_blocks
    negative = -outer_product_result("nhik,nhjk->nhij", weighted, key_blocks) * strict
    inverse = jnp.eye(block_len, dtype=queries.dtype) + negative
    power_term = negative
    for doubling in range(5):
        power_term = outer_product_result("nhij,nhjk->nhik", power_term, power_term)
        inverse = inverse + outer_product_result("nhij,nhjk->nhik", inverse, power_term)
    value_mix = outer_product_result("nhij,nhjk->nhik", inverse, value_blocks * beta_blocks)
    scores = outer_product_result("nhik,nhjk->nhij", query_blocks, key_blocks) * causal
    produced_output = outer_product_result("nhqz,nhzr->nhqr", scores, value_mix)
    return produced_output.transpose(0, 2, 1, 3).reshape(length, head_count, -1)


def mixer_core(
    query_lin, key_lin, value_lin, gate_lin, beta_lin, conv_taps, head_scale, starts, reset_len
):
    length = query_lin.shape[0]
    head_count = beta_lin.shape[1]
    head_width = query_lin.shape[1] // head_count
    queries = jax.nn.silu(short_conv(query_lin, conv_taps[0], starts)).reshape(
        length, head_count, head_width
    )
    keys = jax.nn.silu(short_conv(key_lin, conv_taps[1], starts)).reshape(
        length, head_count, head_width
    )
    values = jax.nn.silu(short_conv(value_lin, conv_taps[2], starts)).reshape(
        length, head_count, head_width
    )
    queries = (
        queries
        * lax.rsqrt(jnp.sum(queries * queries, axis=-1, keepdims=True) + 1e-06)
        * head_width ** (-0.5)
    )
    keys = keys * lax.rsqrt(jnp.sum(keys * keys, axis=-1, keepdims=True) + 1e-06)
    if reset_len:
        recurrent = delta_core_reset(queries, keys, values, jax.nn.sigmoid(beta_lin), reset_len)
    else:
        recurrent = delta_core(queries, keys, values, jax.nn.sigmoid(beta_lin), starts)
    normed = (
        recurrent
        * lax.rsqrt(jnp.mean(recurrent * recurrent, axis=-1, keepdims=True) + 1e-05)
        * head_scale
    )
    gated_out = normed * jax.nn.silu(gate_lin.reshape(length, head_count, head_width))
    return gated_out.reshape(length, head_count * head_width)


def swiglu_mix(gate_act, up_act):
    return jax.nn.silu(gate_act) * up_act


def matmul_rows(left, right):
    return jnp.dot(left, right, preferred_element_type=jnp.float32)


def left_product(first, second):
    return jnp.einsum("tf,tg->fg", first, second, preferred_element_type=jnp.float32)


def back_product(gradient, weight):
    return jnp.einsum("tg,fg->tf", gradient, weight, preferred_element_type=jnp.float32)


def tp_gather(value, axis):
    return lax.all_gather(value, TP_AXES, axis=axis, tiled=True)


def tp_scatter_low(value, axis):
    return lax.psum_scatter(
        value.astype(jnp.bfloat16), TP_AXES, scatter_dimension=axis, tiled=True
    ).astype(jnp.float32)


def fsdp_gather(value, axis):
    return lax.all_gather(value, FSDP_AXES, axis=axis, tiled=True)


def fsdp_scatter_low(value, axis):
    return lax.psum_scatter(
        value.astype(jnp.bfloat16), FSDP_AXES, scatter_dimension=axis, tiled=True
    ).astype(jnp.float32)


def fsdp_gather_direct(value, fsdp, axis):
    spread = jnp.broadcast_to(
        jnp.expand_dims(value, axis + 1), value.shape[: axis + 1] + (fsdp,) + value.shape[axis + 1 :]
    )
    spread = jnp.moveaxis(spread, axis + 1, axis)
    moved = lax.all_to_all(spread, FSDP_AXES, axis, axis, tiled=True)
    shape = list(value.shape)
    shape[axis] *= fsdp
    return moved.reshape(shape)


def fsdp_scatter_direct(value, fsdp, axis):
    shape = list(value.shape)
    staged = value.astype(jnp.bfloat16).reshape(
        shape[:axis] + [fsdp, shape[axis] // fsdp] + shape[axis + 1 :]
    )
    moved = lax.all_to_all(staged, FSDP_AXES, axis, axis, tiled=True)
    return jnp.sum(moved.astype(jnp.float32), axis=axis)


def exchange(value, axes, split_axis, concat_axis):
    if not axes:
        return value
    return lax.all_to_all(value, axes, split_axis, concat_axis, tiled=True)


def heads_to_rows(values, tp, fsdp, rows):
    count = values.shape[0]
    staged = values.reshape(count, 1, fsdp // tp, tp, rows)
    moved = exchange(staged, TP_AXES, 3, 1)
    return moved.reshape(count, fsdp * rows)


def rows_to_heads(values, tp, fsdp, rows):
    count = values.shape[0]
    staged = values.reshape(count, tp, fsdp // tp, 1, rows)
    moved = exchange(staged, TP_AXES, 1, 3)
    return moved.reshape(count, fsdp * rows)


def padded_rows(flat, slices, width):
    extra = -(-flat.shape[0] // (slices * width))
    extra = -(-extra // 16) * 16
    filled = jnp.pad(flat, (0, slices * extra * width - flat.shape[0]))
    return filled.reshape(slices, extra, width)


def make_on_device(tp, fsdp, inner):
    def on_device(
        tokens,
        cotangent,
        group_start,
        pad_mask,
        query_weight,
        key_weight,
        value_weight,
        gate_weight,
        beta_weight,
        out_weight,
        conv_weight,
        mixer_gain,
        head_gain,
        swiglu_gain,
        swiglu_gate,
        swiglu_up,
        swiglu_down,
    ):
        micro_count, slot, width = tokens.shape
        n_all = tp * fsdp
        rows = query_weight.shape[0]
        head_count = beta_weight.shape[1]
        heads_here = head_count // tp
        cols_here = width // tp
        group_rows = tp * rows
        position = lax.axis_index(TP_AXES)
        head_scale = head_gain.astype(jnp.float32)
        reset_len = slot if group_start.shape[1] == 1 else 0

        column_owned = jnp.stack([query_weight, key_weight, value_weight, gate_weight])
        column_swapped = exchange(
            column_owned.reshape(4, rows, tp, cols_here), TP_AXES, 2, 1
        ).reshape(4, group_rows, cols_here)
        small_pack = jnp.concatenate(
            [
                conv_weight.reshape(-1),
                beta_weight.reshape(-1),
                mixer_gain.reshape(-1),
                swiglu_gain.reshape(-1),
            ]
        )
        small_size = small_pack.shape[0]
        small_group = exchange(
            jnp.broadcast_to(small_pack[None, :], (tp, small_size)), TP_AXES, 0, 0
        )
        small_rows_in = padded_rows(small_group.reshape(-1), 5, cols_here)
        extra_in = small_rows_in.shape[1]
        mixer_stack = jnp.concatenate(
            [
                jnp.concatenate(
                    [column_swapped, out_weight.reshape(1, group_rows, cols_here)], axis=0
                ),
                small_rows_in,
            ],
            axis=1,
        )
        mixer_all = fsdp_gather(mixer_stack, 1).reshape(5, fsdp, group_rows + extra_in, cols_here)
        weight_all = mixer_all[:, :, :group_rows].reshape(5, width, cols_here)
        query_cols, key_cols, value_cols, gate_cols = (weight_all[index] for index in range(4))
        out_rows = weight_all[4].reshape(fsdp * rows, width)
        small_all = (
            mixer_all[:, :, group_rows:]
            .transpose(1, 0, 2, 3)
            .reshape(fsdp, -1)[:, : tp * small_size]
            .reshape(n_all, small_size)
        )
        conv_size = conv_weight.size
        beta_size = beta_weight.size
        conv_full = (
            small_all[:, :conv_size]
            .reshape((n_all,) + conv_weight.shape)
            .transpose(1, 2, 0, 3)
            .reshape(conv_weight.shape[0], conv_weight.shape[1], -1)
        )
        beta_full = small_all[:, conv_size : conv_size + beta_size].reshape(-1, head_count)
        gain_mixer = small_all[:, conv_size + beta_size : conv_size + beta_size + rows].reshape(-1)
        gain_swiglu = small_all[:, conv_size + beta_size + rows :].reshape(-1)
        conv_here = lax.dynamic_slice_in_dim(
            conv_full.astype(jnp.float32), position * cols_here, cols_here, axis=2
        )
        beta_here = lax.dynamic_slice_in_dim(beta_full, position * heads_here, heads_here, axis=1)

        owned_rows, hidden_half = swiglu_gate.shape
        hidden_here = hidden_half // inner
        ff_owned = jnp.stack([swiglu_gate, swiglu_up, swiglu_down.T])
        ff_rows = fsdp_gather_direct(ff_owned, fsdp, 1)
        ff_all = exchange(
            ff_rows.reshape(3, fsdp, 1, owned_rows, inner, hidden_here), INNER_AXES, 4, 2
        ).reshape(3, width, hidden_here)
        gate_half = ff_all[0]
        up_half = ff_all[1]
        down_half_t = ff_all[2]

        inputs = tokens.astype(jnp.float32).reshape(micro_count * slot, width)
        normed, norm_back = jax.vjp(rms_norm, inputs, gain_mixer.astype(jnp.float32))
        normed_low = normed.astype(jnp.bfloat16)
        group_tokens = micro_count * slot * tp
        normed_group = tp_gather(normed_low.reshape(micro_count, slot, width), 1).reshape(
            group_tokens, width
        )
        starts = tp_gather(group_start, 1).reshape(-1)

        query_lin = matmul_rows(normed_group, query_cols)
        key_lin = matmul_rows(normed_group, key_cols)
        value_lin = matmul_rows(normed_group, value_cols)
        gate_lin = matmul_rows(normed_group, gate_cols)
        beta_lin = matmul_rows(normed_group, beta_here)

        def core_at(query_in, key_in, value_in, gate_in, beta_in, conv_in, head_in):
            return mixer_core(
                query_in, key_in, value_in, gate_in, beta_in, conv_in, head_in, starts, reset_len
            )

        gated_out, core_back = jax.vjp(
            core_at, query_lin, key_lin, value_lin, gate_lin, beta_lin, conv_here, head_scale
        )
        gated_low = gated_out.astype(jnp.bfloat16)
        gated_rows = heads_to_rows(gated_low, tp, fsdp, rows)
        mixed_partial = matmul_rows(gated_rows, out_rows)
        residual = inputs + tp_scatter_low(
            mixed_partial.reshape(micro_count, slot * tp, width), 1
        ).reshape(micro_count * slot, width)

        inner_norm, inner_norm_back = jax.vjp(rms_norm, residual, gain_swiglu.astype(jnp.float32))
        inner_low = inner_norm.astype(jnp.bfloat16)
        inner_group = tp_gather(inner_low.reshape(micro_count, slot, width), 1).reshape(
            group_tokens, width
        )
        gate_act = matmul_rows(inner_group, gate_half)
        up_act = matmul_rows(inner_group, up_half)
        hidden, hidden_back = jax.vjp(swiglu_mix, gate_act, up_act)
        hidden_low = hidden.astype(jnp.bfloat16)
        partial_rows = back_product(hidden_low, down_half_t)
        branch_rows = tp_scatter_low(partial_rows.reshape(micro_count, slot * tp, width), 1)
        block_out = (residual.reshape(micro_count, slot, width) + branch_rows).astype(jnp.bfloat16)

        out_back = cotangent.astype(jnp.float32) * pad_mask.astype(jnp.float32)[:, :, None]
        out_back_low = out_back.astype(jnp.bfloat16)
        upstream_group = tp_gather(out_back_low, 1).reshape(group_tokens, width)
        block_out, upstream_group = lax.optimization_barrier((block_out, upstream_group))
        gate_back, up_back = hidden_back(matmul_rows(upstream_group, down_half_t))
        gate_back_low = gate_back.astype(jnp.bfloat16)
        up_back_low = up_back.astype(jnp.bfloat16)
        inner_part = back_product(gate_back_low, gate_half) + back_product(up_back_low, up_half)
        inner_back = tp_scatter_low(inner_part.reshape(micro_count, slot * tp, width), 1)

        ff_sums = jnp.stack(
            [
                left_product(inner_group, gate_back_low),
                left_product(inner_group, up_back_low),
                left_product(upstream_group, hidden_low),
            ]
        )
        ff_reduced = fsdp_scatter_direct(ff_sums, fsdp, 1)
        ff_back = exchange(
            ff_reduced.reshape(3, inner, owned_rows, 1, hidden_here), INNER_AXES, 1, 3
        ).reshape(3, owned_rows, hidden_half)
        swiglu_gate_grad = ff_back[0]
        swiglu_up_grad = ff_back[1]
        swiglu_down_grad = ff_back[2].T

        residual_part, swiglu_gain_term = inner_norm_back(
            inner_back.reshape(micro_count * slot, width)
        )
        residual_back = out_back.reshape(micro_count * slot, width) + residual_part
        mixed_back = residual_back.astype(jnp.bfloat16)
        mixed_group = tp_gather(mixed_back.reshape(micro_count, slot, width), 1).reshape(
            group_tokens, width
        )
        gated_back_rows = back_product(mixed_group, out_rows)
        gated_back = rows_to_heads(gated_back_rows, tp, fsdp, rows)
        query_back, key_back, value_back, gate_lin_back, beta_back, conv_term, head_term = (
            core_back(gated_back)
        )
        query_low = query_back.astype(jnp.bfloat16)
        key_low = key_back.astype(jnp.bfloat16)
        value_low = value_back.astype(jnp.bfloat16)
        gate_low = gate_lin_back.astype(jnp.bfloat16)
        beta_low = beta_back.astype(jnp.bfloat16)
        normed_part = (
            back_product(query_low, query_cols)
            + back_product(key_low, key_cols)
            + back_product(value_low, value_cols)
            + back_product(gate_low, gate_cols)
            + back_product(beta_low, beta_here)
        )
        normed_back = tp_scatter_low(normed_part.reshape(micro_count, slot * tp, width), 1)
        input_part, mixer_gain_term = norm_back(normed_back.reshape(micro_count * slot, width))
        tokens_grad = (residual_back + input_part).reshape(micro_count, slot, width)

        mixer_sums = jnp.stack(
            [
                left_product(normed_group, query_low),
                left_product(normed_group, key_low),
                left_product(normed_group, value_low),
                left_product(normed_group, gate_low),
                left_product(gated_rows, mixed_group).reshape(width, cols_here),
            ]
        ).reshape(5, fsdp, group_rows, cols_here)
        beta_sum = left_product(normed_group, beta_low)
        beta_wide = lax.dynamic_update_slice_in_dim(
            jnp.zeros((width, head_count), jnp.float32), beta_sum, position * heads_here, axis=1
        )
        conv_wide = lax.dynamic_update_slice_in_dim(
            jnp.zeros(conv_full.shape, jnp.float32), conv_term, position * cols_here, axis=2
        )
        taps = conv_wide.shape[0] * conv_wide.shape[1]
        small_terms = jnp.concatenate(
            [
                conv_wide.reshape(taps, n_all, -1).transpose(1, 0, 2).reshape(n_all, -1),
                beta_wide.reshape(n_all, -1),
                mixer_gain_term.reshape(n_all, -1),
                swiglu_gain_term.reshape(n_all, -1),
                jnp.broadcast_to(head_term[None, :], (n_all, head_term.shape[0])),
            ],
            axis=1,
        )
        small_width = small_terms.shape[1]
        small_tp = jnp.sum(
            exchange(small_terms.reshape(fsdp, tp, small_width), TP_AXES, 1, 1), axis=1
        )
        small_block = jax.vmap(lambda flat: padded_rows(flat, 5, cols_here))(small_tp)
        extra_out = small_block.shape[2]
        reduce_in = jnp.concatenate([mixer_sums, small_block.transpose(1, 0, 2, 3)], axis=2)
        mixer_reduced = fsdp_scatter_low(
            reduce_in.reshape(5, fsdp * (group_rows + extra_out), cols_here), 1
        )
        column_back = exchange(
            mixer_reduced[:4, :group_rows].reshape(4, tp, rows, 1, cols_here), TP_AXES, 1, 3
        ).reshape(4, rows, width)
        query_grad, key_grad, value_grad, gate_grad = (column_back[index] for index in range(4))
        out_grad = mixer_reduced[4, :group_rows].reshape(rows, width)
        small_out = mixer_reduced[:, group_rows:].reshape(-1)[:small_width]
        conv_grad = small_out[:conv_size].reshape(conv_weight.shape)
        beta_grad = small_out[conv_size : conv_size + beta_size].reshape(beta_weight.shape)
        mixer_gain_grad = small_out[conv_size + beta_size : conv_size + beta_size + rows]
        swiglu_gain_grad = small_out[conv_size + beta_size + rows : conv_size + beta_size + 2 * rows]
        head_total = small_out[conv_size + beta_size + 2 * rows :]
        return (
            block_out,
            tokens_grad,
            query_grad,
            key_grad,
            value_grad,
            gate_grad,
            beta_grad,
            out_grad,
            conv_grad,
            mixer_gain_grad,
            head_total,
            swiglu_gain_grad,
            swiglu_gate_grad,
            swiglu_up_grad,
            swiglu_down_grad,
        )

    return on_device


def solution(mesh):
    n_dp = mesh.shape["dp"]
    n_mlp = mesh.shape["mlp"]
    devices = np.asarray(mesh.devices).reshape(n_dp // 2, 2, n_mlp)
    split_mesh = Mesh(devices, ALL_AXES)
    sizes = dict(zip(ALL_AXES, devices.shape))
    tp = int(np.prod([sizes[name] for name in TP_AXES]))
    fsdp = int(np.prod([sizes[name] for name in FSDP_AXES]))
    inner = int(np.prod([sizes[name] for name in INNER_AXES]))
    rows_axes = ALL_AXES
    swiglu_rows = ("dq", "core")
    placed = (
        P(None, rows_axes, None),
        P(None, rows_axes, None),
        P(None, rows_axes),
        P(None, rows_axes),
        P(rows_axes, None),
        P(rows_axes, None),
        P(rows_axes, None),
        P(rows_axes, None),
        P(rows_axes, None),
        P(rows_axes, None),
        P(None, None, rows_axes),
        P(rows_axes),
        P(),
        P(rows_axes),
        P(swiglu_rows, "mlp"),
        P(swiglu_rows, "mlp"),
        P("mlp", swiglu_rows),
    )
    return jax.shard_map(
        make_on_device(tp, fsdp, inner),
        mesh=split_mesh,
        in_specs=placed,
        out_specs=(
            P(None, rows_axes, None),
            P(None, rows_axes, None),
            P(rows_axes, None),
            P(rows_axes, None),
            P(rows_axes, None),
            P(rows_axes, None),
            P(rows_axes, None),
            P(rows_axes, None),
            P(None, None, rows_axes),
            P(rows_axes),
            P(),
            P(rows_axes),
            P(swiglu_rows, "mlp"),
            P(swiglu_rows, "mlp"),
            P("mlp", swiglu_rows),
        ),
        check_vma=False,
    )
```

```python
import jax
import jax.numpy as jnp
import numpy as np
from jax import lax
from jax.sharding import Mesh
from jax.sharding import PartitionSpec as P

TP_AXES = ("core", "mlp")
ALL_AXES = ("dq", "core", "mlp")
FSDP_AXES = tuple(name for name in ALL_AXES if name not in TP_AXES)
INNER_AXES = tuple(name for name in TP_AXES if name != "mlp")


def rms_norm(values, scale_gain):
    return (
        values * lax.rsqrt(jnp.mean(values * values, axis=-1, keepdims=True) + 1e-06) * scale_gain
    )


def short_conv(linear, tap_weights, starts):
    length = linear.shape[0]
    block_len = length // starts.shape[0]
    position = jnp.arange(length)
    restart = jnp.repeat(starts, block_len)
    summed = linear * tap_weights[0]
    for offset in range(1, tap_weights.shape[0]):
        shifted = jnp.concatenate(
            [jnp.zeros((offset, linear.shape[1]), linear.dtype), linear[: length - offset]], axis=0
        )
        usable = ((position % block_len >= offset) | (restart == 0)).astype(linear.dtype)
        summed = summed + shifted * tap_weights[offset] * usable[:, None]
    return summed


def outer_product_result(form, first, second):
    return jnp.einsum(form, first, second, precision=lax.Precision.HIGHEST)


def delta_core(queries, keys, values, betas, starts):
    length, head_count, head_width = queries.shape
    value_width = values.shape[2]
    block_count = starts.shape[0]
    block_len = length // block_count

    def blocked(array):
        return array.reshape(block_count, block_len, head_count, -1).transpose(0, 2, 1, 3)

    query_blocks = blocked(queries)
    key_blocks = blocked(keys)
    value_blocks = blocked(values)
    beta_blocks = betas.reshape(block_count, block_len, head_count).transpose(0, 2, 1)[..., None]
    position = jnp.arange(block_len)
    strict = (position[:, None] > position[None, :]).astype(queries.dtype)
    causal = (position[:, None] >= position[None, :]).astype(queries.dtype)
    weighted = key_blocks * beta_blocks
    negative = -outer_product_result("nhik,nhjk->nhij", weighted, key_blocks) * strict
    inverse = jnp.eye(block_len, dtype=queries.dtype) + negative
    power_term = negative
    for doubling in range(5):
        power_term = outer_product_result("nhij,nhjk->nhik", power_term, power_term)
        inverse = inverse + outer_product_result("nhij,nhjk->nhik", inverse, power_term)
    key_mix = outer_product_result("nhij,nhjk->nhik", inverse, weighted)
    value_mix = outer_product_result("nhij,nhjk->nhik", inverse, value_blocks * beta_blocks)
    scores = outer_product_result("nhik,nhjk->nhij", query_blocks, key_blocks) * causal

    def advance(current_state, block_items):
        (
            query_slice,
            key_slice,
            key_mixture_slice,
            value_mixture_slice,
            attention_score_slice,
            restart,
        ) = block_items
        current_state = current_state * (1 - restart).astype(current_state.dtype)
        adjusted_result = value_mixture_slice - outer_product_result(
            "pzd,pde->pze", key_mixture_slice, current_state
        )
        produced_output = outer_product_result(
            "pzd,pde->pze", query_slice, current_state
        ) + outer_product_result("lqz,lzr->lqr", attention_score_slice, adjusted_result)
        current_state = current_state + outer_product_result(
            "ixl,ixr->ilr", key_slice, adjusted_result
        )
        return (current_state, produced_output)

    initial = jnp.zeros((head_count, head_width, value_width), queries.dtype)
    final_state, produced_output = lax.scan(
        advance, initial, (query_blocks, key_blocks, key_mix, value_mix, scores, starts)
    )
    return produced_output.transpose(0, 2, 1, 3).reshape(length, head_count, value_width)


def delta_core_reset(queries, keys, values, betas, block_len):
    length, head_count, head_width = queries.shape
    block_count = length // block_len

    def blocked(array):
        return array.reshape(block_count, block_len, head_count, -1).transpose(0, 2, 1, 3)

    query_blocks = blocked(queries)
    key_blocks = blocked(keys)
    value_blocks = blocked(values)
    beta_blocks = betas.reshape(block_count, block_len, head_count).transpose(0, 2, 1)[..., None]
    position = jnp.arange(block_len)
    strict = (position[:, None] > position[None, :]).astype(queries.dtype)
    causal = (position[:, None] >= position[None, :]).astype(queries.dtype)
    weighted = key_blocks * beta_blocks
    negative = -outer_product_result("nhik,nhjk->nhij", weighted, key_blocks) * strict
    inverse = jnp.eye(block_len, dtype=queries.dtype) + negative
    power_term = negative
    for doubling in range(5):
        power_term = outer_product_result("nhij,nhjk->nhik", power_term, power_term)
        inverse = inverse + outer_product_result("nhij,nhjk->nhik", inverse, power_term)
    value_mix = outer_product_result("nhij,nhjk->nhik", inverse, value_blocks * beta_blocks)
    scores = outer_product_result("nhik,nhjk->nhij", query_blocks, key_blocks) * causal
    produced_output = outer_product_result("nhqz,nhzr->nhqr", scores, value_mix)
    return produced_output.transpose(0, 2, 1, 3).reshape(length, head_count, -1)


def mixer_core(
    query_lin, key_lin, value_lin, gate_lin, beta_lin, conv_taps, head_scale, starts, reset_len
):
    length = query_lin.shape[0]
    head_count = beta_lin.shape[1]
    head_width = query_lin.shape[1] // head_count
    queries = jax.nn.silu(short_conv(query_lin, conv_taps[0], starts)).reshape(
        length, head_count, head_width
    )
    keys = jax.nn.silu(short_conv(key_lin, conv_taps[1], starts)).reshape(
        length, head_count, head_width
    )
    values = jax.nn.silu(short_conv(value_lin, conv_taps[2], starts)).reshape(
        length, head_count, head_width
    )
    queries = (
        queries
        * lax.rsqrt(jnp.sum(queries * queries, axis=-1, keepdims=True) + 1e-06)
        * head_width ** (-0.5)
    )
    keys = keys * lax.rsqrt(jnp.sum(keys * keys, axis=-1, keepdims=True) + 1e-06)
    if reset_len:
        recurrent = delta_core_reset(queries, keys, values, jax.nn.sigmoid(beta_lin), reset_len)
    else:
        recurrent = delta_core(queries, keys, values, jax.nn.sigmoid(beta_lin), starts)
    normed = (
        recurrent
        * lax.rsqrt(jnp.mean(recurrent * recurrent, axis=-1, keepdims=True) + 1e-05)
        * head_scale
    )
    gated_out = normed * jax.nn.silu(gate_lin.reshape(length, head_count, head_width))
    return gated_out.reshape(length, head_count * head_width)


def swiglu_mix(gate_act, up_act):
    return jax.nn.silu(gate_act) * up_act


def matmul_rows(left, right):
    return jnp.dot(left, right, preferred_element_type=jnp.float32)


def left_product(first, second):
    return jnp.einsum("tf,tg->fg", first, second, preferred_element_type=jnp.float32)


def back_product(gradient, weight):
    return jnp.einsum("tg,fg->tf", gradient, weight, preferred_element_type=jnp.float32)


def tp_gather(value, axis):
    tp = lax.psum(1, TP_AXES)
    spread = jnp.broadcast_to(
        jnp.expand_dims(value, axis), value.shape[:axis] + (tp,) + value.shape[axis:]
    )
    moved = lax.all_to_all(spread, TP_AXES, axis, axis, tiled=True)
    shape = list(value.shape)
    shape[axis] *= tp
    return moved.reshape(shape)


def tp_scatter_low(value, axis):
    tp = lax.psum(1, TP_AXES)
    shape = list(value.shape)
    staged = value.astype(jnp.bfloat16).reshape(
        shape[:axis] + [tp, shape[axis] // tp] + shape[axis + 1 :]
    )
    moved = lax.all_to_all(staged, TP_AXES, axis, axis, tiled=True)
    return jnp.sum(moved.astype(jnp.float32), axis=axis)


def fsdp_gather(value, axis):
    return lax.all_gather(value, FSDP_AXES, axis=axis, tiled=True)


def fsdp_scatter_low(value, axis):
    return lax.psum_scatter(
        value.astype(jnp.bfloat16), FSDP_AXES, scatter_dimension=axis, tiled=True
    ).astype(jnp.float32)


def exchange(value, axes, split_axis, concat_axis):
    if not axes:
        return value
    return lax.all_to_all(value, axes, split_axis, concat_axis, tiled=True)


def heads_to_rows(values, tp, fsdp, rows):
    count = values.shape[0]
    staged = values.reshape(count, 1, fsdp // tp, tp, rows)
    moved = exchange(staged, TP_AXES, 3, 1)
    return moved.reshape(count, fsdp * rows)


def rows_to_heads(values, tp, fsdp, rows):
    count = values.shape[0]
    staged = values.reshape(count, tp, fsdp // tp, 1, rows)
    moved = exchange(staged, TP_AXES, 1, 3)
    return moved.reshape(count, fsdp * rows)


def padded_rows(flat, slices, width):
    extra = -(-flat.shape[0] // (slices * width))
    extra = -(-extra // 16) * 16
    filled = jnp.pad(flat, (0, slices * extra * width - flat.shape[0]))
    return filled.reshape(slices, extra, width)


def make_on_device(tp, fsdp, inner):
    def on_device(
        tokens,
        cotangent,
        group_start,
        pad_mask,
        query_weight,
        key_weight,
        value_weight,
        gate_weight,
        beta_weight,
        out_weight,
        conv_weight,
        mixer_gain,
        head_gain,
        swiglu_gain,
        swiglu_gate,
        swiglu_up,
        swiglu_down,
    ):
        micro_count, slot, width = tokens.shape
        n_all = tp * fsdp
        rows = query_weight.shape[0]
        head_count = beta_weight.shape[1]
        heads_here = head_count // tp
        cols_here = width // tp
        group_rows = tp * rows
        position = lax.axis_index(TP_AXES)
        head_scale = head_gain.astype(jnp.float32)
        reset_len = slot if group_start.shape[1] == 1 else 0

        column_owned = jnp.stack([query_weight, key_weight, value_weight, gate_weight])
        column_swapped = exchange(
            column_owned.reshape(4, rows, tp, cols_here), TP_AXES, 2, 1
        ).reshape(4, group_rows, cols_here)
        small_pack = jnp.concatenate(
            [
                conv_weight.reshape(-1),
                beta_weight.reshape(-1),
                mixer_gain.reshape(-1),
                swiglu_gain.reshape(-1),
            ]
        )
        small_size = small_pack.shape[0]
        small_group = exchange(
            jnp.broadcast_to(small_pack[None, :], (tp, small_size)), TP_AXES, 0, 0
        )
        small_rows_in = padded_rows(small_group.reshape(-1), 5, cols_here)
        extra_in = small_rows_in.shape[1]
        mixer_stack = jnp.concatenate(
            [
                jnp.concatenate(
                    [column_swapped, out_weight.reshape(1, group_rows, cols_here)], axis=0
                ),
                small_rows_in,
            ],
            axis=1,
        )
        mixer_all = fsdp_gather(mixer_stack, 1).reshape(5, fsdp, group_rows + extra_in, cols_here)
        weight_all = mixer_all[:, :, :group_rows].reshape(5, width, cols_here)
        query_cols, key_cols, value_cols, gate_cols = (weight_all[index] for index in range(4))
        out_rows = weight_all[4].reshape(fsdp * rows, width)
        small_all = (
            mixer_all[:, :, group_rows:]
            .transpose(1, 0, 2, 3)
            .reshape(fsdp, -1)[:, : tp * small_size]
            .reshape(n_all, small_size)
        )
        conv_size = conv_weight.size
        beta_size = beta_weight.size
        conv_full = (
            small_all[:, :conv_size]
            .reshape((n_all,) + conv_weight.shape)
            .transpose(1, 2, 0, 3)
            .reshape(conv_weight.shape[0], conv_weight.shape[1], -1)
        )
        beta_full = small_all[:, conv_size : conv_size + beta_size].reshape(-1, head_count)
        gain_mixer = small_all[:, conv_size + beta_size : conv_size + beta_size + rows].reshape(-1)
        gain_swiglu = small_all[:, conv_size + beta_size + rows :].reshape(-1)
        conv_here = lax.dynamic_slice_in_dim(
            conv_full.astype(jnp.float32), position * cols_here, cols_here, axis=2
        )
        beta_here = lax.dynamic_slice_in_dim(beta_full, position * heads_here, heads_here, axis=1)

        owned_rows, hidden_half = swiglu_gate.shape
        hidden_here = hidden_half // inner
        ff_owned = jnp.stack([swiglu_gate, swiglu_up, swiglu_down.T])
        ff_swapped = exchange(
            ff_owned.reshape(3, owned_rows, inner, hidden_here), INNER_AXES, 2, 1
        ).reshape(3, inner * owned_rows, hidden_here)
        ff_all = fsdp_gather(ff_swapped, 1)
        gate_half = ff_all[0]
        up_half = ff_all[1]
        down_half_t = ff_all[2]

        inputs = tokens.astype(jnp.float32).reshape(micro_count * slot, width)
        normed, norm_back = jax.vjp(rms_norm, inputs, gain_mixer.astype(jnp.float32))
        normed_low = normed.astype(jnp.bfloat16)
        group_tokens = micro_count * slot * tp
        normed_group = tp_gather(normed_low.reshape(micro_count, slot, width), 1).reshape(
            group_tokens, width
        )
        starts = tp_gather(group_start, 1).reshape(-1)

        query_lin = matmul_rows(normed_group, query_cols)
        key_lin = matmul_rows(normed_group, key_cols)
        value_lin = matmul_rows(normed_group, value_cols)
        gate_lin = matmul_rows(normed_group, gate_cols)
        beta_lin = matmul_rows(normed_group, beta_here)

        def core_at(query_in, key_in, value_in, gate_in, beta_in, conv_in, head_in):
            return mixer_core(
                query_in, key_in, value_in, gate_in, beta_in, conv_in, head_in, starts, reset_len
            )

        gated_out, core_back = jax.vjp(
            core_at, query_lin, key_lin, value_lin, gate_lin, beta_lin, conv_here, head_scale
        )
        gated_low = gated_out.astype(jnp.bfloat16)
        gated_rows = heads_to_rows(gated_low, tp, fsdp, rows)
        mixed_partial = matmul_rows(gated_rows, out_rows)
        residual = inputs + tp_scatter_low(
            mixed_partial.reshape(micro_count, slot * tp, width), 1
        ).reshape(micro_count * slot, width)

        inner_norm, inner_norm_back = jax.vjp(rms_norm, residual, gain_swiglu.astype(jnp.float32))
        inner_low = inner_norm.astype(jnp.bfloat16)
        inner_group = tp_gather(inner_low.reshape(micro_count, slot, width), 1).reshape(
            group_tokens, width
        )
        gate_act = matmul_rows(inner_group, gate_half)
        up_act = matmul_rows(inner_group, up_half)
        hidden, hidden_back = jax.vjp(swiglu_mix, gate_act, up_act)
        hidden_low = hidden.astype(jnp.bfloat16)
        partial_rows = back_product(hidden_low, down_half_t)
        branch_rows = tp_scatter_low(partial_rows.reshape(micro_count, slot * tp, width), 1)
        block_out = (residual.reshape(micro_count, slot, width) + branch_rows).astype(jnp.bfloat16)

        out_back = cotangent.astype(jnp.float32) * pad_mask.astype(jnp.float32)[:, :, None]
        out_back_low = out_back.astype(jnp.bfloat16)
        upstream_group = tp_gather(out_back_low, 1).reshape(group_tokens, width)
        block_out, upstream_group = lax.optimization_barrier((block_out, upstream_group))
        gate_back, up_back = hidden_back(matmul_rows(upstream_group, down_half_t))
        gate_back_low = gate_back.astype(jnp.bfloat16)
        up_back_low = up_back.astype(jnp.bfloat16)
        inner_part = back_product(gate_back_low, gate_half) + back_product(up_back_low, up_half)
        inner_back = tp_scatter_low(inner_part.reshape(micro_count, slot * tp, width), 1)

        ff_sums = jnp.stack(
            [
                left_product(inner_group, gate_back_low),
                left_product(inner_group, up_back_low),
                left_product(upstream_group, hidden_low),
            ]
        )
        ff_reduced = fsdp_scatter_low(ff_sums, 1)
        ff_back = exchange(
            ff_reduced.reshape(3, inner, owned_rows, 1, hidden_here), INNER_AXES, 1, 3
        ).reshape(3, owned_rows, hidden_half)
        swiglu_gate_grad = ff_back[0]
        swiglu_up_grad = ff_back[1]
        swiglu_down_grad = ff_back[2].T

        residual_part, swiglu_gain_term = inner_norm_back(
            inner_back.reshape(micro_count * slot, width)
        )
        residual_back = out_back.reshape(micro_count * slot, width) + residual_part
        mixed_back = residual_back.astype(jnp.bfloat16)
        mixed_group = tp_gather(mixed_back.reshape(micro_count, slot, width), 1).reshape(
            group_tokens, width
        )
        gated_back_rows = back_product(mixed_group, out_rows)
        gated_back = rows_to_heads(gated_back_rows, tp, fsdp, rows)
        query_back, key_back, value_back, gate_lin_back, beta_back, conv_term, head_term = (
            core_back(gated_back)
        )
        query_low = query_back.astype(jnp.bfloat16)
        key_low = key_back.astype(jnp.bfloat16)
        value_low = value_back.astype(jnp.bfloat16)
        gate_low = gate_lin_back.astype(jnp.bfloat16)
        beta_low = beta_back.astype(jnp.bfloat16)
        normed_part = (
            back_product(query_low, query_cols)
            + back_product(key_low, key_cols)
            + back_product(value_low, value_cols)
            + back_product(gate_low, gate_cols)
            + back_product(beta_low, beta_here)
        )
        normed_back = tp_scatter_low(normed_part.reshape(micro_count, slot * tp, width), 1)
        input_part, mixer_gain_term = norm_back(normed_back.reshape(micro_count * slot, width))
        tokens_grad = (residual_back + input_part).reshape(micro_count, slot, width)

        mixer_sums = jnp.stack(
            [
                left_product(normed_group, query_low),
                left_product(normed_group, key_low),
                left_product(normed_group, value_low),
                left_product(normed_group, gate_low),
                left_product(gated_rows, mixed_group).reshape(width, cols_here),
            ]
        ).reshape(5, fsdp, group_rows, cols_here)
        beta_sum = left_product(normed_group, beta_low)
        beta_wide = lax.dynamic_update_slice_in_dim(
            jnp.zeros((width, head_count), jnp.float32), beta_sum, position * heads_here, axis=1
        )
        conv_wide = lax.dynamic_update_slice_in_dim(
            jnp.zeros(conv_full.shape, jnp.float32), conv_term, position * cols_here, axis=2
        )
        taps = conv_wide.shape[0] * conv_wide.shape[1]
        small_terms = jnp.concatenate(
            [
                conv_wide.reshape(taps, n_all, -1).transpose(1, 0, 2).reshape(n_all, -1),
                beta_wide.reshape(n_all, -1),
                mixer_gain_term.reshape(n_all, -1),
                swiglu_gain_term.reshape(n_all, -1),
                jnp.broadcast_to(head_term[None, :], (n_all, head_term.shape[0])),
            ],
            axis=1,
        )
        small_width = small_terms.shape[1]
        small_tp = jnp.sum(
            exchange(small_terms.reshape(fsdp, tp, small_width), TP_AXES, 1, 1), axis=1
        )
        small_block = jax.vmap(lambda flat: padded_rows(flat, 5, cols_here))(small_tp)
        extra_out = small_block.shape[2]
        reduce_in = jnp.concatenate([mixer_sums, small_block.transpose(1, 0, 2, 3)], axis=2)
        mixer_reduced = fsdp_scatter_low(
            reduce_in.reshape(5, fsdp * (group_rows + extra_out), cols_here), 1
        )
        column_back = exchange(
            mixer_reduced[:4, :group_rows].reshape(4, tp, rows, 1, cols_here), TP_AXES, 1, 3
        ).reshape(4, rows, width)
        query_grad, key_grad, value_grad, gate_grad = (column_back[index] for index in range(4))
        out_grad = mixer_reduced[4, :group_rows].reshape(rows, width)
        small_out = mixer_reduced[:, group_rows:].reshape(-1)[:small_width]
        conv_grad = small_out[:conv_size].reshape(conv_weight.shape)
        beta_grad = small_out[conv_size : conv_size + beta_size].reshape(beta_weight.shape)
        mixer_gain_grad = small_out[conv_size + beta_size : conv_size + beta_size + rows]
        swiglu_gain_grad = small_out[conv_size + beta_size + rows : conv_size + beta_size + 2 * rows]
        head_total = small_out[conv_size + beta_size + 2 * rows :]
        return (
            block_out,
            tokens_grad,
            query_grad,
            key_grad,
            value_grad,
            gate_grad,
            beta_grad,
            out_grad,
            conv_grad,
            mixer_gain_grad,
            head_total,
            swiglu_gain_grad,
            swiglu_gate_grad,
            swiglu_up_grad,
            swiglu_down_grad,
        )

    return on_device


def solution(mesh):
    n_dp = mesh.shape["dp"]
    n_mlp = mesh.shape["mlp"]
    devices = np.asarray(mesh.devices).reshape(n_dp // 2, 2, n_mlp)
    split_mesh = Mesh(devices, ALL_AXES)
    sizes = dict(zip(ALL_AXES, devices.shape))
    tp = int(np.prod([sizes[name] for name in TP_AXES]))
    fsdp = int(np.prod([sizes[name] for name in FSDP_AXES]))
    inner = int(np.prod([sizes[name] for name in INNER_AXES]))
    rows_axes = ALL_AXES
    swiglu_rows = ("dq", "core")
    placed = (
        P(None, rows_axes, None),
        P(None, rows_axes, None),
        P(None, rows_axes),
        P(None, rows_axes),
        P(rows_axes, None),
        P(rows_axes, None),
        P(rows_axes, None),
        P(rows_axes, None),
        P(rows_axes, None),
        P(rows_axes, None),
        P(None, None, rows_axes),
        P(rows_axes),
        P(),
        P(rows_axes),
        P(swiglu_rows, "mlp"),
        P(swiglu_rows, "mlp"),
        P("mlp", swiglu_rows),
    )
    return jax.shard_map(
        make_on_device(tp, fsdp, inner),
        mesh=split_mesh,
        in_specs=placed,
        out_specs=(
            P(None, rows_axes, None),
            P(None, rows_axes, None),
            P(rows_axes, None),
            P(rows_axes, None),
            P(rows_axes, None),
            P(rows_axes, None),
            P(rows_axes, None),
            P(rows_axes, None),
            P(None, None, rows_axes),
            P(rows_axes),
            P(),
            P(rows_axes),
            P(swiglu_rows, "mlp"),
            P(swiglu_rows, "mlp"),
            P("mlp", swiglu_rows),
        ),
        check_vma=False,
    )
```

```python
import jax
import jax.numpy as jnp
import numpy as np
from jax import lax
from jax.sharding import Mesh
from jax.sharding import PartitionSpec as P

TP_AXES = ("core", "mlp")
ALL_AXES = ("dq", "core", "mlp")
FSDP_AXES = tuple(name for name in ALL_AXES if name not in TP_AXES)
INNER_AXES = tuple(name for name in TP_AXES if name != "mlp")


def rms_norm(values, scale_gain):
    return (
        values * lax.rsqrt(jnp.mean(values * values, axis=-1, keepdims=True) + 1e-06) * scale_gain
    )


def short_conv(linear, tap_weights, starts):
    length = linear.shape[0]
    block_len = length // starts.shape[0]
    position = jnp.arange(length)
    restart = jnp.repeat(starts, block_len)
    summed = linear * tap_weights[0]
    for offset in range(1, tap_weights.shape[0]):
        shifted = jnp.concatenate(
            [jnp.zeros((offset, linear.shape[1]), linear.dtype), linear[: length - offset]], axis=0
        )
        usable = ((position % block_len >= offset) | (restart == 0)).astype(linear.dtype)
        summed = summed + shifted * tap_weights[offset] * usable[:, None]
    return summed


def outer_product_result(form, first, second):
    return jnp.einsum(form, first, second, precision=lax.Precision.HIGHEST)


def delta_core(queries, keys, values, betas, starts):
    length, head_count, head_width = queries.shape
    value_width = values.shape[2]
    block_count = starts.shape[0]
    block_len = length // block_count

    def blocked(array):
        return array.reshape(block_count, block_len, head_count, -1).transpose(0, 2, 1, 3)

    query_blocks = blocked(queries)
    key_blocks = blocked(keys)
    value_blocks = blocked(values)
    beta_blocks = betas.reshape(block_count, block_len, head_count).transpose(0, 2, 1)[..., None]
    position = jnp.arange(block_len)
    strict = (position[:, None] > position[None, :]).astype(queries.dtype)
    causal = (position[:, None] >= position[None, :]).astype(queries.dtype)
    weighted = key_blocks * beta_blocks
    negative = -outer_product_result("nhik,nhjk->nhij", weighted, key_blocks) * strict
    inverse = jnp.eye(block_len, dtype=queries.dtype) + negative
    power_term = negative
    for doubling in range(5):
        power_term = outer_product_result("nhij,nhjk->nhik", power_term, power_term)
        inverse = inverse + outer_product_result("nhij,nhjk->nhik", inverse, power_term)
    key_mix = outer_product_result("nhij,nhjk->nhik", inverse, weighted)
    value_mix = outer_product_result("nhij,nhjk->nhik", inverse, value_blocks * beta_blocks)
    scores = outer_product_result("nhik,nhjk->nhij", query_blocks, key_blocks) * causal

    def advance(current_state, block_items):
        (
            query_slice,
            key_slice,
            key_mixture_slice,
            value_mixture_slice,
            attention_score_slice,
            restart,
        ) = block_items
        current_state = current_state * (1 - restart).astype(current_state.dtype)
        adjusted_result = value_mixture_slice - outer_product_result(
            "pzd,pde->pze", key_mixture_slice, current_state
        )
        produced_output = outer_product_result(
            "pzd,pde->pze", query_slice, current_state
        ) + outer_product_result("lqz,lzr->lqr", attention_score_slice, adjusted_result)
        current_state = current_state + outer_product_result(
            "ixl,ixr->ilr", key_slice, adjusted_result
        )
        return (current_state, produced_output)

    initial = jnp.zeros((head_count, head_width, value_width), queries.dtype)
    final_state, produced_output = lax.scan(
        advance, initial, (query_blocks, key_blocks, key_mix, value_mix, scores, starts)
    )
    return produced_output.transpose(0, 2, 1, 3).reshape(length, head_count, value_width)


def delta_core_reset(queries, keys, values, betas, block_len):
    length, head_count, head_width = queries.shape
    block_count = length // block_len

    def blocked(array):
        return array.reshape(block_count, block_len, head_count, -1).transpose(0, 2, 1, 3)

    query_blocks = blocked(queries)
    key_blocks = blocked(keys)
    value_blocks = blocked(values)
    beta_blocks = betas.reshape(block_count, block_len, head_count).transpose(0, 2, 1)[..., None]
    position = jnp.arange(block_len)
    strict = (position[:, None] > position[None, :]).astype(queries.dtype)
    causal = (position[:, None] >= position[None, :]).astype(queries.dtype)
    weighted = key_blocks * beta_blocks
    negative = -outer_product_result("nhik,nhjk->nhij", weighted, key_blocks) * strict
    inverse = jnp.eye(block_len, dtype=queries.dtype) + negative
    power_term = negative
    for doubling in range(5):
        power_term = outer_product_result("nhij,nhjk->nhik", power_term, power_term)
        inverse = inverse + outer_product_result("nhij,nhjk->nhik", inverse, power_term)
    value_mix = outer_product_result("nhij,nhjk->nhik", inverse, value_blocks * beta_blocks)
    scores = outer_product_result("nhik,nhjk->nhij", query_blocks, key_blocks) * causal
    produced_output = outer_product_result("nhqz,nhzr->nhqr", scores, value_mix)
    return produced_output.transpose(0, 2, 1, 3).reshape(length, head_count, -1)


def mixer_core(
    query_lin, key_lin, value_lin, gate_lin, beta_lin, conv_taps, head_scale, starts, reset_len
):
    length = query_lin.shape[0]
    head_count = beta_lin.shape[1]
    head_width = query_lin.shape[1] // head_count
    queries = jax.nn.silu(short_conv(query_lin, conv_taps[0], starts)).reshape(
        length, head_count, head_width
    )
    keys = jax.nn.silu(short_conv(key_lin, conv_taps[1], starts)).reshape(
        length, head_count, head_width
    )
    values = jax.nn.silu(short_conv(value_lin, conv_taps[2], starts)).reshape(
        length, head_count, head_width
    )
    queries = (
        queries
        * lax.rsqrt(jnp.sum(queries * queries, axis=-1, keepdims=True) + 1e-06)
        * head_width ** (-0.5)
    )
    keys = keys * lax.rsqrt(jnp.sum(keys * keys, axis=-1, keepdims=True) + 1e-06)
    if reset_len:
        recurrent = delta_core_reset(queries, keys, values, jax.nn.sigmoid(beta_lin), reset_len)
    else:
        recurrent = delta_core(queries, keys, values, jax.nn.sigmoid(beta_lin), starts)
    normed = (
        recurrent
        * lax.rsqrt(jnp.mean(recurrent * recurrent, axis=-1, keepdims=True) + 1e-05)
        * head_scale
    )
    gated_out = normed * jax.nn.silu(gate_lin.reshape(length, head_count, head_width))
    return gated_out.reshape(length, head_count * head_width)


def swiglu_mix(gate_act, up_act):
    return jax.nn.silu(gate_act) * up_act


def matmul_rows(left, right):
    return jnp.dot(left, right, preferred_element_type=jnp.float32)


def left_product(first, second):
    return jnp.einsum("tf,tg->fg", first, second, preferred_element_type=jnp.float32)


def back_product(gradient, weight):
    return jnp.einsum("tg,fg->tf", gradient, weight, preferred_element_type=jnp.float32)


def tp_gather(value, axis):
    tp = lax.psum(1, TP_AXES)
    spread = jnp.broadcast_to(
        jnp.expand_dims(value, axis), value.shape[:axis] + (tp,) + value.shape[axis:]
    )
    moved = lax.all_to_all(spread, TP_AXES, axis, axis, tiled=True)
    shape = list(value.shape)
    shape[axis] *= tp
    return moved.reshape(shape)


def tp_scatter_low(value, axis):
    tp = lax.psum(1, TP_AXES)
    shape = list(value.shape)
    staged = value.astype(jnp.bfloat16).reshape(
        shape[:axis] + [tp, shape[axis] // tp] + shape[axis + 1 :]
    )
    moved = lax.all_to_all(staged, TP_AXES, axis, axis, tiled=True)
    return jnp.sum(moved.astype(jnp.float32), axis=axis)


def fsdp_gather(value, axis):
    return lax.all_gather(value, FSDP_AXES, axis=axis, tiled=True)


def fsdp_scatter_low(value, axis):
    return lax.psum_scatter(
        value.astype(jnp.bfloat16), FSDP_AXES, scatter_dimension=axis, tiled=True
    ).astype(jnp.float32)


def exchange(value, axes, split_axis, concat_axis):
    if not axes:
        return value
    return lax.all_to_all(value, axes, split_axis, concat_axis, tiled=True)


def heads_to_rows(values, tp, fsdp, rows):
    count = values.shape[0]
    staged = values.reshape(count, 1, fsdp // tp, tp, rows)
    moved = exchange(staged, TP_AXES, 3, 1)
    return moved.reshape(count, fsdp * rows)


def rows_to_heads(values, tp, fsdp, rows):
    count = values.shape[0]
    staged = values.reshape(count, tp, fsdp // tp, 1, rows)
    moved = exchange(staged, TP_AXES, 1, 3)
    return moved.reshape(count, fsdp * rows)


def padded_rows(flat, slices, width):
    extra = -(-flat.shape[0] // (slices * width))
    extra = -(-extra // 16) * 16
    filled = jnp.pad(flat, (0, slices * extra * width - flat.shape[0]))
    return filled.reshape(slices, extra, width)


def make_on_device(tp, fsdp, inner):
    def on_device(
        tokens,
        cotangent,
        group_start,
        pad_mask,
        query_weight,
        key_weight,
        value_weight,
        gate_weight,
        beta_weight,
        out_weight,
        conv_weight,
        mixer_gain,
        head_gain,
        swiglu_gain,
        swiglu_gate,
        swiglu_up,
        swiglu_down,
    ):
        micro_count, slot, width = tokens.shape
        n_all = tp * fsdp
        rows = query_weight.shape[0]
        head_count = beta_weight.shape[1]
        heads_here = head_count // tp
        cols_here = width // tp
        group_rows = tp * rows
        position = lax.axis_index(TP_AXES)
        head_scale = head_gain.astype(jnp.float32)
        reset_len = slot if group_start.shape[1] == 1 else 0

        column_owned = jnp.stack([query_weight, key_weight, value_weight, gate_weight])
        column_swapped = exchange(
            column_owned.reshape(4, rows, tp, cols_here), TP_AXES, 2, 1
        ).reshape(4, group_rows, cols_here)
        small_pack = jnp.concatenate(
            [
                conv_weight.reshape(-1),
                beta_weight.reshape(-1),
                mixer_gain.reshape(-1),
                swiglu_gain.reshape(-1),
            ]
        )
        small_size = small_pack.shape[0]
        small_group = exchange(
            jnp.broadcast_to(small_pack[None, :], (tp, small_size)), TP_AXES, 0, 0
        )
        small_rows_in = padded_rows(small_group.reshape(-1), 5, cols_here)
        extra_in = small_rows_in.shape[1]
        mixer_stack = jnp.concatenate(
            [
                jnp.concatenate(
                    [column_swapped, out_weight.reshape(1, group_rows, cols_here)], axis=0
                ),
                small_rows_in,
            ],
            axis=1,
        )
        mixer_all = fsdp_gather(mixer_stack, 1).reshape(5, fsdp, group_rows + extra_in, cols_here)
        weight_all = mixer_all[:, :, :group_rows].reshape(5, width, cols_here)
        query_cols, key_cols, value_cols, gate_cols = (weight_all[index] for index in range(4))
        out_rows = weight_all[4].reshape(fsdp * rows, width)
        small_all = (
            mixer_all[:, :, group_rows:]
            .transpose(1, 0, 2, 3)
            .reshape(fsdp, -1)[:, : tp * small_size]
            .reshape(n_all, small_size)
        )
        conv_size = conv_weight.size
        beta_size = beta_weight.size
        conv_full = (
            small_all[:, :conv_size]
            .reshape((n_all,) + conv_weight.shape)
            .transpose(1, 2, 0, 3)
            .reshape(conv_weight.shape[0], conv_weight.shape[1], -1)
        )
        beta_full = small_all[:, conv_size : conv_size + beta_size].reshape(-1, head_count)
        gain_mixer = small_all[:, conv_size + beta_size : conv_size + beta_size + rows].reshape(-1)
        gain_swiglu = small_all[:, conv_size + beta_size + rows :].reshape(-1)
        conv_here = lax.dynamic_slice_in_dim(
            conv_full.astype(jnp.float32), position * cols_here, cols_here, axis=2
        )
        beta_here = lax.dynamic_slice_in_dim(beta_full, position * heads_here, heads_here, axis=1)

        owned_rows, hidden_half = swiglu_gate.shape
        hidden_here = hidden_half // inner
        ff_owned = jnp.stack([swiglu_gate, swiglu_up, swiglu_down.T])
        ff_swapped = exchange(
            ff_owned.reshape(3, owned_rows, inner, hidden_here), INNER_AXES, 2, 1
        ).reshape(3, inner * owned_rows, hidden_here)
        ff_all = fsdp_gather(ff_swapped, 1)
        gate_half = ff_all[0]
        up_half = ff_all[1]
        down_half_t = ff_all[2]

        inputs = tokens.astype(jnp.float32).reshape(micro_count * slot, width)
        normed, norm_back = jax.vjp(rms_norm, inputs, gain_mixer.astype(jnp.float32))
        normed_low = normed.astype(jnp.bfloat16)
        group_tokens = micro_count * slot * tp
        normed_group = tp_gather(normed_low.reshape(micro_count, slot, width), 1).reshape(
            group_tokens, width
        )
        starts = tp_gather(group_start, 1).reshape(-1)

        query_lin = matmul_rows(normed_group, query_cols)
        key_lin = matmul_rows(normed_group, key_cols)
        value_lin = matmul_rows(normed_group, value_cols)
        gate_lin = matmul_rows(normed_group, gate_cols)
        beta_lin = matmul_rows(normed_group, beta_here)

        def core_at(query_in, key_in, value_in, gate_in, beta_in, conv_in, head_in):
            return mixer_core(
                query_in, key_in, value_in, gate_in, beta_in, conv_in, head_in, starts, reset_len
            )

        gated_out, core_back = jax.vjp(
            core_at, query_lin, key_lin, value_lin, gate_lin, beta_lin, conv_here, head_scale
        )
        gated_low = gated_out.astype(jnp.bfloat16)
        gated_rows = heads_to_rows(gated_low, tp, fsdp, rows)
        mixed_partial = matmul_rows(gated_rows, out_rows)
        residual = inputs + tp_scatter_low(
            mixed_partial.reshape(micro_count, slot * tp, width), 1
        ).reshape(micro_count * slot, width)

        inner_norm, inner_norm_back = jax.vjp(rms_norm, residual, gain_swiglu.astype(jnp.float32))
        inner_low = inner_norm.astype(jnp.bfloat16)
        inner_group = tp_gather(inner_low.reshape(micro_count, slot, width), 1).reshape(
            group_tokens, width
        )
        gate_act = matmul_rows(inner_group, gate_half)
        up_act = matmul_rows(inner_group, up_half)
        hidden, hidden_back = jax.vjp(swiglu_mix, gate_act, up_act)
        hidden_low = hidden.astype(jnp.bfloat16)
        partial_rows = back_product(hidden_low, down_half_t)
        branch_rows = tp_scatter_low(partial_rows.reshape(micro_count, slot * tp, width), 1)
        block_out = (residual.reshape(micro_count, slot, width) + branch_rows).astype(jnp.bfloat16)

        out_back = cotangent.astype(jnp.float32) * pad_mask.astype(jnp.float32)[:, :, None]
        out_back_low = out_back.astype(jnp.bfloat16)
        upstream_group = tp_gather(out_back_low, 1).reshape(group_tokens, width)
        block_out, upstream_group = lax.optimization_barrier((block_out, upstream_group))
        gate_back, up_back = hidden_back(matmul_rows(upstream_group, down_half_t))
        gate_back_low = gate_back.astype(jnp.bfloat16)
        up_back_low = up_back.astype(jnp.bfloat16)
        inner_part = back_product(gate_back_low, gate_half) + back_product(up_back_low, up_half)
        inner_back = tp_scatter_low(inner_part.reshape(micro_count, slot * tp, width), 1)

        ff_sums = jnp.stack(
            [
                left_product(inner_group, gate_back_low),
                left_product(inner_group, up_back_low),
                left_product(upstream_group, hidden_low),
            ]
        )
        ff_sums_low = ff_sums.astype(jnp.bfloat16)
        ff_sums_low, inner_back = lax.optimization_barrier((ff_sums_low, inner_back))
        ff_reduced = fsdp_scatter_low(ff_sums_low, 1)

        residual_part, swiglu_gain_term = inner_norm_back(
            inner_back.reshape(micro_count * slot, width)
        )
        residual_back = out_back.reshape(micro_count * slot, width) + residual_part
        mixed_back = residual_back.astype(jnp.bfloat16)
        mixed_group = tp_gather(mixed_back.reshape(micro_count, slot, width), 1).reshape(
            group_tokens, width
        )
        gated_back_rows = back_product(mixed_group, out_rows)
        gated_back = rows_to_heads(gated_back_rows, tp, fsdp, rows)
        query_back, key_back, value_back, gate_lin_back, beta_back, conv_term, head_term = (
            core_back(gated_back)
        )
        query_low = query_back.astype(jnp.bfloat16)
        key_low = key_back.astype(jnp.bfloat16)
        value_low = value_back.astype(jnp.bfloat16)
        gate_low = gate_lin_back.astype(jnp.bfloat16)
        beta_low = beta_back.astype(jnp.bfloat16)
        normed_part = (
            back_product(query_low, query_cols)
            + back_product(key_low, key_cols)
            + back_product(value_low, value_cols)
            + back_product(gate_low, gate_cols)
            + back_product(beta_low, beta_here)
        )
        normed_back = tp_scatter_low(normed_part.reshape(micro_count, slot * tp, width), 1)
        input_part, mixer_gain_term = norm_back(normed_back.reshape(micro_count * slot, width))
        tokens_grad = (residual_back + input_part).reshape(micro_count, slot, width)

        mixer_sums = jnp.stack(
            [
                left_product(normed_group, query_low),
                left_product(normed_group, key_low),
                left_product(normed_group, value_low),
                left_product(normed_group, gate_low),
                left_product(gated_rows, mixed_group).reshape(width, cols_here),
            ]
        ).reshape(5, fsdp, group_rows, cols_here)
        beta_sum = left_product(normed_group, beta_low)
        beta_wide = lax.dynamic_update_slice_in_dim(
            jnp.zeros((width, head_count), jnp.float32), beta_sum, position * heads_here, axis=1
        )
        conv_wide = lax.dynamic_update_slice_in_dim(
            jnp.zeros(conv_full.shape, jnp.float32), conv_term, position * cols_here, axis=2
        )
        taps = conv_wide.shape[0] * conv_wide.shape[1]
        small_terms = jnp.concatenate(
            [
                conv_wide.reshape(taps, n_all, -1).transpose(1, 0, 2).reshape(n_all, -1),
                beta_wide.reshape(n_all, -1),
                mixer_gain_term.reshape(n_all, -1),
                swiglu_gain_term.reshape(n_all, -1),
                jnp.broadcast_to(head_term[None, :], (n_all, head_term.shape[0])),
            ],
            axis=1,
        )
        small_width = small_terms.shape[1]
        small_tp = jnp.sum(
            exchange(small_terms.reshape(fsdp, tp, small_width), TP_AXES, 1, 1), axis=1
        )
        small_block = jax.vmap(lambda flat: padded_rows(flat, 5, cols_here))(small_tp)
        extra_out = small_block.shape[2]
        reduce_in = jnp.concatenate([mixer_sums, small_block.transpose(1, 0, 2, 3)], axis=2)
        ff_reduced, reduce_in = lax.optimization_barrier((ff_reduced, reduce_in))
        ff_back = exchange(
            ff_reduced.reshape(3, inner, owned_rows, 1, hidden_here), INNER_AXES, 1, 3
        ).reshape(3, owned_rows, hidden_half)
        swiglu_gate_grad = ff_back[0]
        swiglu_up_grad = ff_back[1]
        swiglu_down_grad = ff_back[2].T
        mixer_reduced = fsdp_scatter_low(
            reduce_in.reshape(5, fsdp * (group_rows + extra_out), cols_here), 1
        )
        column_back = exchange(
            mixer_reduced[:4, :group_rows].reshape(4, tp, rows, 1, cols_here), TP_AXES, 1, 3
        ).reshape(4, rows, width)
        query_grad, key_grad, value_grad, gate_grad = (column_back[index] for index in range(4))
        out_grad = mixer_reduced[4, :group_rows].reshape(rows, width)
        small_out = mixer_reduced[:, group_rows:].reshape(-1)[:small_width]
        conv_grad = small_out[:conv_size].reshape(conv_weight.shape)
        beta_grad = small_out[conv_size : conv_size + beta_size].reshape(beta_weight.shape)
        mixer_gain_grad = small_out[conv_size + beta_size : conv_size + beta_size + rows]
        swiglu_gain_grad = small_out[conv_size + beta_size + rows : conv_size + beta_size + 2 * rows]
        head_total = small_out[conv_size + beta_size + 2 * rows :]
        return (
            block_out,
            tokens_grad,
            query_grad,
            key_grad,
            value_grad,
            gate_grad,
            beta_grad,
            out_grad,
            conv_grad,
            mixer_gain_grad,
            head_total,
            swiglu_gain_grad,
            swiglu_gate_grad,
            swiglu_up_grad,
            swiglu_down_grad,
        )

    return on_device


def solution(mesh):
    n_dp = mesh.shape["dp"]
    n_mlp = mesh.shape["mlp"]
    devices = np.asarray(mesh.devices).reshape(n_dp // 2, 2, n_mlp)
    split_mesh = Mesh(devices, ALL_AXES)
    sizes = dict(zip(ALL_AXES, devices.shape))
    tp = int(np.prod([sizes[name] for name in TP_AXES]))
    fsdp = int(np.prod([sizes[name] for name in FSDP_AXES]))
    inner = int(np.prod([sizes[name] for name in INNER_AXES]))
    rows_axes = ALL_AXES
    swiglu_rows = ("dq", "core")
    placed = (
        P(None, rows_axes, None),
        P(None, rows_axes, None),
        P(None, rows_axes),
        P(None, rows_axes),
        P(rows_axes, None),
        P(rows_axes, None),
        P(rows_axes, None),
        P(rows_axes, None),
        P(rows_axes, None),
        P(rows_axes, None),
        P(None, None, rows_axes),
        P(rows_axes),
        P(),
        P(rows_axes),
        P(swiglu_rows, "mlp"),
        P(swiglu_rows, "mlp"),
        P("mlp", swiglu_rows),
    )
    return jax.shard_map(
        make_on_device(tp, fsdp, inner),
        mesh=split_mesh,
        in_specs=placed,
        out_specs=(
            P(None, rows_axes, None),
            P(None, rows_axes, None),
            P(rows_axes, None),
            P(rows_axes, None),
            P(rows_axes, None),
            P(rows_axes, None),
            P(rows_axes, None),
            P(rows_axes, None),
            P(None, None, rows_axes),
            P(rows_axes),
            P(),
            P(rows_axes),
            P(swiglu_rows, "mlp"),
            P(swiglu_rows, "mlp"),
            P("mlp", swiglu_rows),
        ),
        check_vma=False,
    )
```

```python
import jax
import jax.numpy as jnp
import numpy as np
from jax import lax
from jax.sharding import Mesh
from jax.sharding import PartitionSpec as P

TP_AXES = ("core", "mlp")
ALL_AXES = ("dq", "core", "mlp")
FSDP_AXES = tuple(name for name in ALL_AXES if name not in TP_AXES)
INNER_AXES = tuple(name for name in TP_AXES if name != "mlp")


def rms_norm(values, scale_gain):
    return (
        values * lax.rsqrt(jnp.mean(values * values, axis=-1, keepdims=True) + 1e-06) * scale_gain
    )


def short_conv(linear, tap_weights, starts):
    length = linear.shape[0]
    block_len = length // starts.shape[0]
    position = jnp.arange(length)
    restart = jnp.repeat(starts, block_len)
    summed = linear * tap_weights[0]
    for offset in range(1, tap_weights.shape[0]):
        shifted = jnp.concatenate(
            [jnp.zeros((offset, linear.shape[1]), linear.dtype), linear[: length - offset]], axis=0
        )
        usable = ((position % block_len >= offset) | (restart == 0)).astype(linear.dtype)
        summed = summed + shifted * tap_weights[offset] * usable[:, None]
    return summed


def outer_product_result(form, first, second):
    return jnp.einsum(form, first, second, precision=lax.Precision.HIGHEST)


def delta_core(queries, keys, values, betas, starts):
    length, head_count, head_width = queries.shape
    value_width = values.shape[2]
    block_count = starts.shape[0]
    block_len = length // block_count

    def blocked(array):
        return array.reshape(block_count, block_len, head_count, -1).transpose(0, 2, 1, 3)

    query_blocks = blocked(queries)
    key_blocks = blocked(keys)
    value_blocks = blocked(values)
    beta_blocks = betas.reshape(block_count, block_len, head_count).transpose(0, 2, 1)[..., None]
    position = jnp.arange(block_len)
    strict = (position[:, None] > position[None, :]).astype(queries.dtype)
    causal = (position[:, None] >= position[None, :]).astype(queries.dtype)
    weighted = key_blocks * beta_blocks
    negative = -outer_product_result("nhik,nhjk->nhij", weighted, key_blocks) * strict
    inverse = jnp.eye(block_len, dtype=queries.dtype) + negative
    power_term = negative
    for doubling in range(5):
        power_term = outer_product_result("nhij,nhjk->nhik", power_term, power_term)
        inverse = inverse + outer_product_result("nhij,nhjk->nhik", inverse, power_term)
    key_mix = outer_product_result("nhij,nhjk->nhik", inverse, weighted)
    value_mix = outer_product_result("nhij,nhjk->nhik", inverse, value_blocks * beta_blocks)
    scores = outer_product_result("nhik,nhjk->nhij", query_blocks, key_blocks) * causal

    def advance(current_state, block_items):
        (
            query_slice,
            key_slice,
            key_mixture_slice,
            value_mixture_slice,
            attention_score_slice,
            restart,
        ) = block_items
        current_state = current_state * (1 - restart).astype(current_state.dtype)
        adjusted_result = value_mixture_slice - outer_product_result(
            "pzd,pde->pze", key_mixture_slice, current_state
        )
        produced_output = outer_product_result(
            "pzd,pde->pze", query_slice, current_state
        ) + outer_product_result("lqz,lzr->lqr", attention_score_slice, adjusted_result)
        current_state = current_state + outer_product_result(
            "ixl,ixr->ilr", key_slice, adjusted_result
        )
        return (current_state, produced_output)

    initial = jnp.zeros((head_count, head_width, value_width), queries.dtype)
    final_state, produced_output = lax.scan(
        advance, initial, (query_blocks, key_blocks, key_mix, value_mix, scores, starts)
    )
    return produced_output.transpose(0, 2, 1, 3).reshape(length, head_count, value_width)


def delta_core_reset(queries, keys, values, betas, block_len):
    length, head_count, head_width = queries.shape
    block_count = length // block_len

    def blocked(array):
        return array.reshape(block_count, block_len, head_count, -1).transpose(0, 2, 1, 3)

    query_blocks = blocked(queries)
    key_blocks = blocked(keys)
    value_blocks = blocked(values)
    beta_blocks = betas.reshape(block_count, block_len, head_count).transpose(0, 2, 1)[..., None]
    position = jnp.arange(block_len)
    strict = (position[:, None] > position[None, :]).astype(queries.dtype)
    causal = (position[:, None] >= position[None, :]).astype(queries.dtype)
    weighted = key_blocks * beta_blocks
    negative = -outer_product_result("nhik,nhjk->nhij", weighted, key_blocks) * strict
    inverse = jnp.eye(block_len, dtype=queries.dtype) + negative
    power_term = negative
    for doubling in range(5):
        power_term = outer_product_result("nhij,nhjk->nhik", power_term, power_term)
        inverse = inverse + outer_product_result("nhij,nhjk->nhik", inverse, power_term)
    value_mix = outer_product_result("nhij,nhjk->nhik", inverse, value_blocks * beta_blocks)
    scores = outer_product_result("nhik,nhjk->nhij", query_blocks, key_blocks) * causal
    produced_output = outer_product_result("nhqz,nhzr->nhqr", scores, value_mix)
    return produced_output.transpose(0, 2, 1, 3).reshape(length, head_count, -1)


def mixer_core(
    query_lin, key_lin, value_lin, gate_lin, beta_lin, conv_taps, head_scale, starts, reset_len
):
    length = query_lin.shape[0]
    head_count = beta_lin.shape[1]
    head_width = query_lin.shape[1] // head_count
    queries = jax.nn.silu(short_conv(query_lin, conv_taps[0], starts)).reshape(
        length, head_count, head_width
    )
    keys = jax.nn.silu(short_conv(key_lin, conv_taps[1], starts)).reshape(
        length, head_count, head_width
    )
    values = jax.nn.silu(short_conv(value_lin, conv_taps[2], starts)).reshape(
        length, head_count, head_width
    )
    queries = (
        queries
        * lax.rsqrt(jnp.sum(queries * queries, axis=-1, keepdims=True) + 1e-06)
        * head_width ** (-0.5)
    )
    keys = keys * lax.rsqrt(jnp.sum(keys * keys, axis=-1, keepdims=True) + 1e-06)
    if reset_len:
        recurrent = delta_core_reset(queries, keys, values, jax.nn.sigmoid(beta_lin), reset_len)
    else:
        recurrent = delta_core(queries, keys, values, jax.nn.sigmoid(beta_lin), starts)
    normed = (
        recurrent
        * lax.rsqrt(jnp.mean(recurrent * recurrent, axis=-1, keepdims=True) + 1e-05)
        * head_scale
    )
    gated_out = normed * jax.nn.silu(gate_lin.reshape(length, head_count, head_width))
    return gated_out.reshape(length, head_count * head_width)


def swiglu_mix(gate_act, up_act):
    return jax.nn.silu(gate_act) * up_act


def matmul_rows(left, right):
    return jnp.dot(left, right, preferred_element_type=jnp.float32)


def left_product(first, second):
    return jnp.einsum("tf,tg->fg", first, second, preferred_element_type=jnp.float32)


def back_product(gradient, weight):
    return jnp.einsum("tg,fg->tf", gradient, weight, preferred_element_type=jnp.float32)


def tp_gather(value, axis):
    tp = lax.psum(1, TP_AXES)
    spread = jnp.broadcast_to(
        jnp.expand_dims(value, axis), value.shape[:axis] + (tp,) + value.shape[axis:]
    )
    moved = lax.all_to_all(spread, TP_AXES, axis, axis, tiled=True)
    shape = list(value.shape)
    shape[axis] *= tp
    return moved.reshape(shape)


def tp_scatter_low(value, axis):
    tp = lax.psum(1, TP_AXES)
    shape = list(value.shape)
    staged = value.astype(jnp.bfloat16).reshape(
        shape[:axis] + [tp, shape[axis] // tp] + shape[axis + 1 :]
    )
    moved = lax.all_to_all(staged, TP_AXES, axis, axis, tiled=True)
    return jnp.sum(moved.astype(jnp.float32), axis=axis)


def fsdp_gather(value, axis):
    return lax.all_gather(value, FSDP_AXES, axis=axis, tiled=True)


def fsdp_scatter_low(value, axis):
    return lax.psum_scatter(
        value.astype(jnp.bfloat16), FSDP_AXES, scatter_dimension=axis, tiled=True
    ).astype(jnp.float32)


def exchange(value, axes, split_axis, concat_axis):
    if not axes:
        return value
    return lax.all_to_all(value, axes, split_axis, concat_axis, tiled=True)


def heads_to_rows(values, tp, fsdp, rows):
    count = values.shape[0]
    staged = values.reshape(count, 1, fsdp // tp, tp, rows)
    moved = exchange(staged, TP_AXES, 3, 1)
    return moved.reshape(count, fsdp * rows)


def rows_to_heads(values, tp, fsdp, rows):
    count = values.shape[0]
    staged = values.reshape(count, tp, fsdp // tp, 1, rows)
    moved = exchange(staged, TP_AXES, 1, 3)
    return moved.reshape(count, fsdp * rows)


def padded_rows(flat, slices, width):
    extra = -(-flat.shape[0] // (slices * width))
    extra = -(-extra // 16) * 16
    filled = jnp.pad(flat, (0, slices * extra * width - flat.shape[0]))
    return filled.reshape(slices, extra, width)


def make_on_device(tp, fsdp, inner):
    def on_device(
        tokens,
        cotangent,
        group_start,
        pad_mask,
        query_weight,
        key_weight,
        value_weight,
        gate_weight,
        beta_weight,
        out_weight,
        conv_weight,
        mixer_gain,
        head_gain,
        swiglu_gain,
        swiglu_gate,
        swiglu_up,
        swiglu_down,
    ):
        micro_count, slot, width = tokens.shape
        n_all = tp * fsdp
        rows = query_weight.shape[0]
        head_count = beta_weight.shape[1]
        heads_here = head_count // tp
        cols_here = width // tp
        group_rows = tp * rows
        position = lax.axis_index(TP_AXES)
        head_scale = head_gain.astype(jnp.float32)
        reset_len = slot if group_start.shape[1] == 1 else 0

        column_owned = jnp.stack([query_weight, key_weight, value_weight, gate_weight])
        column_swapped = exchange(
            column_owned.reshape(4, rows, tp, cols_here), TP_AXES, 2, 1
        ).reshape(4, group_rows, cols_here)
        small_pack = jnp.concatenate(
            [
                conv_weight.reshape(-1),
                beta_weight.reshape(-1),
                mixer_gain.reshape(-1),
                swiglu_gain.reshape(-1),
            ]
        )
        small_size = small_pack.shape[0]
        small_group = exchange(
            jnp.broadcast_to(small_pack[None, :], (tp, small_size)), TP_AXES, 0, 0
        )
        small_rows_in = padded_rows(small_group.reshape(-1), 5, cols_here)
        extra_in = small_rows_in.shape[1]
        mixer_stack = jnp.concatenate(
            [
                jnp.concatenate(
                    [column_swapped, out_weight.reshape(1, group_rows, cols_here)], axis=0
                ),
                small_rows_in,
            ],
            axis=1,
        )
        mixer_all = fsdp_gather(mixer_stack, 1).reshape(5, fsdp, group_rows + extra_in, cols_here)
        weight_all = mixer_all[:, :, :group_rows].reshape(5, width, cols_here)
        query_cols, key_cols, value_cols, gate_cols = (weight_all[index] for index in range(4))
        out_rows = weight_all[4].reshape(fsdp * rows, width)
        small_all = (
            mixer_all[:, :, group_rows:]
            .transpose(1, 0, 2, 3)
            .reshape(fsdp, -1)[:, : tp * small_size]
            .reshape(n_all, small_size)
        )
        conv_size = conv_weight.size
        beta_size = beta_weight.size
        conv_full = (
            small_all[:, :conv_size]
            .reshape((n_all,) + conv_weight.shape)
            .transpose(1, 2, 0, 3)
            .reshape(conv_weight.shape[0], conv_weight.shape[1], -1)
        )
        beta_full = small_all[:, conv_size : conv_size + beta_size].reshape(-1, head_count)
        gain_mixer = small_all[:, conv_size + beta_size : conv_size + beta_size + rows].reshape(-1)
        gain_swiglu = small_all[:, conv_size + beta_size + rows :].reshape(-1)
        conv_here = lax.dynamic_slice_in_dim(
            conv_full.astype(jnp.float32), position * cols_here, cols_here, axis=2
        )
        beta_here = lax.dynamic_slice_in_dim(beta_full, position * heads_here, heads_here, axis=1)

        owned_rows, hidden_half = swiglu_gate.shape
        hidden_here = hidden_half // inner
        ff_owned = jnp.stack([swiglu_gate, swiglu_up, swiglu_down.T]).reshape(
            3, owned_rows, inner, hidden_here
        )
        lanes = hidden_here // 128 if hidden_here % 128 == 0 else 0
        first = (lanes + 1) // 2 * 128 if lanes > 1 else hidden_here // 2
        bounds = ((0, first), (first, hidden_here - first))
        ff_chunks = []
        for offset, size in bounds:
            swapped = exchange(ff_owned[..., offset : offset + size], INNER_AXES, 2, 1)
            ff_chunks.append(fsdp_gather(swapped.reshape(3, inner * owned_rows, size), 1))

        inputs = tokens.astype(jnp.float32).reshape(micro_count * slot, width)
        normed, norm_back = jax.vjp(rms_norm, inputs, gain_mixer.astype(jnp.float32))
        normed_low = normed.astype(jnp.bfloat16)
        group_tokens = micro_count * slot * tp
        normed_group = tp_gather(normed_low.reshape(micro_count, slot, width), 1).reshape(
            group_tokens, width
        )
        starts = tp_gather(group_start, 1).reshape(-1)

        query_lin = matmul_rows(normed_group, query_cols)
        key_lin = matmul_rows(normed_group, key_cols)
        value_lin = matmul_rows(normed_group, value_cols)
        gate_lin = matmul_rows(normed_group, gate_cols)
        beta_lin = matmul_rows(normed_group, beta_here)

        def core_at(query_in, key_in, value_in, gate_in, beta_in, conv_in, head_in):
            return mixer_core(
                query_in, key_in, value_in, gate_in, beta_in, conv_in, head_in, starts, reset_len
            )

        gated_out, core_back = jax.vjp(
            core_at, query_lin, key_lin, value_lin, gate_lin, beta_lin, conv_here, head_scale
        )
        gated_low = gated_out.astype(jnp.bfloat16)
        gated_rows = heads_to_rows(gated_low, tp, fsdp, rows)
        mixed_partial = matmul_rows(gated_rows, out_rows)
        residual = inputs + tp_scatter_low(
            mixed_partial.reshape(micro_count, slot * tp, width), 1
        ).reshape(micro_count * slot, width)

        inner_norm, inner_norm_back = jax.vjp(rms_norm, residual, gain_swiglu.astype(jnp.float32))
        inner_low = inner_norm.astype(jnp.bfloat16)
        inner_group = tp_gather(inner_low.reshape(micro_count, slot, width), 1).reshape(
            group_tokens, width
        )
        out_back = cotangent.astype(jnp.float32) * pad_mask.astype(jnp.float32)[:, :, None]
        out_back_low = out_back.astype(jnp.bfloat16)
        upstream_group = tp_gather(out_back_low, 1).reshape(group_tokens, width)
        partial_rows = None
        inner_part = None
        ff_reduced = []
        for index, chunk_weights in enumerate(ff_chunks):
            if index > 0:
                sums_low, chunk_weights = lax.optimization_barrier((sums_low, chunk_weights))
            gate_piece, up_piece, down_piece_t = chunk_weights[0], chunk_weights[1], chunk_weights[2]
            gate_act = matmul_rows(inner_group, gate_piece)
            up_act = matmul_rows(inner_group, up_piece)
            hidden, hidden_back = jax.vjp(swiglu_mix, gate_act, up_act)
            hidden_low = hidden.astype(jnp.bfloat16)
            piece_rows = back_product(hidden_low, down_piece_t)
            partial_rows = piece_rows if partial_rows is None else partial_rows + piece_rows
            gate_back, up_back = hidden_back(matmul_rows(upstream_group, down_piece_t))
            gate_back_low = gate_back.astype(jnp.bfloat16)
            up_back_low = up_back.astype(jnp.bfloat16)
            piece_part = back_product(gate_back_low, gate_piece) + back_product(up_back_low, up_piece)
            inner_part = piece_part if inner_part is None else inner_part + piece_part
            sums_low = jnp.stack(
                [
                    left_product(inner_group, gate_back_low),
                    left_product(inner_group, up_back_low),
                    left_product(upstream_group, hidden_low),
                ]
            ).astype(jnp.bfloat16)
            ff_reduced.append(fsdp_scatter_low(sums_low, 1))
        branch_rows = tp_scatter_low(partial_rows.reshape(micro_count, slot * tp, width), 1)
        block_out = (residual.reshape(micro_count, slot, width) + branch_rows).astype(jnp.bfloat16)
        inner_back = tp_scatter_low(inner_part.reshape(micro_count, slot * tp, width), 1)
        block_out, inner_back = lax.optimization_barrier((block_out, inner_back))

        residual_part, swiglu_gain_term = inner_norm_back(
            inner_back.reshape(micro_count * slot, width)
        )
        residual_back = out_back.reshape(micro_count * slot, width) + residual_part
        mixed_back = residual_back.astype(jnp.bfloat16)
        mixed_group = tp_gather(mixed_back.reshape(micro_count, slot, width), 1).reshape(
            group_tokens, width
        )
        gated_back_rows = back_product(mixed_group, out_rows)
        gated_back = rows_to_heads(gated_back_rows, tp, fsdp, rows)
        query_back, key_back, value_back, gate_lin_back, beta_back, conv_term, head_term = (
            core_back(gated_back)
        )
        query_low = query_back.astype(jnp.bfloat16)
        key_low = key_back.astype(jnp.bfloat16)
        value_low = value_back.astype(jnp.bfloat16)
        gate_low = gate_lin_back.astype(jnp.bfloat16)
        beta_low = beta_back.astype(jnp.bfloat16)
        normed_part = (
            back_product(query_low, query_cols)
            + back_product(key_low, key_cols)
            + back_product(value_low, value_cols)
            + back_product(gate_low, gate_cols)
            + back_product(beta_low, beta_here)
        )
        normed_back = tp_scatter_low(normed_part.reshape(micro_count, slot * tp, width), 1)
        input_part, mixer_gain_term = norm_back(normed_back.reshape(micro_count * slot, width))
        tokens_grad = (residual_back + input_part).reshape(micro_count, slot, width)

        mixer_sums = jnp.stack(
            [
                left_product(normed_group, query_low),
                left_product(normed_group, key_low),
                left_product(normed_group, value_low),
                left_product(normed_group, gate_low),
                left_product(gated_rows, mixed_group).reshape(width, cols_here),
            ]
        ).reshape(5, fsdp, group_rows, cols_here)
        beta_sum = left_product(normed_group, beta_low)
        beta_wide = lax.dynamic_update_slice_in_dim(
            jnp.zeros((width, head_count), jnp.float32), beta_sum, position * heads_here, axis=1
        )
        conv_wide = lax.dynamic_update_slice_in_dim(
            jnp.zeros(conv_full.shape, jnp.float32), conv_term, position * cols_here, axis=2
        )
        taps = conv_wide.shape[0] * conv_wide.shape[1]
        small_terms = jnp.concatenate(
            [
                conv_wide.reshape(taps, n_all, -1).transpose(1, 0, 2).reshape(n_all, -1),
                beta_wide.reshape(n_all, -1),
                mixer_gain_term.reshape(n_all, -1),
                swiglu_gain_term.reshape(n_all, -1),
                jnp.broadcast_to(head_term[None, :], (n_all, head_term.shape[0])),
            ],
            axis=1,
        )
        small_width = small_terms.shape[1]
        small_tp = jnp.sum(
            exchange(small_terms.reshape(fsdp, tp, small_width), TP_AXES, 1, 1), axis=1
        )
        small_block = jax.vmap(lambda flat: padded_rows(flat, 5, cols_here))(small_tp)
        extra_out = small_block.shape[2]
        reduce_in = jnp.concatenate([mixer_sums, small_block.transpose(1, 0, 2, 3)], axis=2)
        ff_reduced, reduce_in = lax.optimization_barrier((ff_reduced, reduce_in))
        ff_back = jnp.concatenate(
            [
                exchange(
                    piece.reshape(3, inner, owned_rows, 1, size), INNER_AXES, 1, 3
                ).reshape(3, owned_rows, inner, size)
                for piece, (offset, size) in zip(ff_reduced, bounds)
            ],
            axis=3,
        ).reshape(3, owned_rows, hidden_half)
        swiglu_gate_grad = ff_back[0]
        swiglu_up_grad = ff_back[1]
        swiglu_down_grad = ff_back[2].T
        mixer_reduced = fsdp_scatter_low(
            reduce_in.reshape(5, fsdp * (group_rows + extra_out), cols_here), 1
        )
        column_back = exchange(
            mixer_reduced[:4, :group_rows].reshape(4, tp, rows, 1, cols_here), TP_AXES, 1, 3
        ).reshape(4, rows, width)
        query_grad, key_grad, value_grad, gate_grad = (column_back[index] for index in range(4))
        out_grad = mixer_reduced[4, :group_rows].reshape(rows, width)
        small_out = mixer_reduced[:, group_rows:].reshape(-1)[:small_width]
        conv_grad = small_out[:conv_size].reshape(conv_weight.shape)
        beta_grad = small_out[conv_size : conv_size + beta_size].reshape(beta_weight.shape)
        mixer_gain_grad = small_out[conv_size + beta_size : conv_size + beta_size + rows]
        swiglu_gain_grad = small_out[conv_size + beta_size + rows : conv_size + beta_size + 2 * rows]
        head_total = small_out[conv_size + beta_size + 2 * rows :]
        return (
            block_out,
            tokens_grad,
            query_grad,
            key_grad,
            value_grad,
            gate_grad,
            beta_grad,
            out_grad,
            conv_grad,
            mixer_gain_grad,
            head_total,
            swiglu_gain_grad,
            swiglu_gate_grad,
            swiglu_up_grad,
            swiglu_down_grad,
        )

    return on_device


def solution(mesh):
    n_dp = mesh.shape["dp"]
    n_mlp = mesh.shape["mlp"]
    devices = np.asarray(mesh.devices).reshape(n_dp // 2, 2, n_mlp)
    split_mesh = Mesh(devices, ALL_AXES)
    sizes = dict(zip(ALL_AXES, devices.shape))
    tp = int(np.prod([sizes[name] for name in TP_AXES]))
    fsdp = int(np.prod([sizes[name] for name in FSDP_AXES]))
    inner = int(np.prod([sizes[name] for name in INNER_AXES]))
    rows_axes = ALL_AXES
    swiglu_rows = ("dq", "core")
    placed = (
        P(None, rows_axes, None),
        P(None, rows_axes, None),
        P(None, rows_axes),
        P(None, rows_axes),
        P(rows_axes, None),
        P(rows_axes, None),
        P(rows_axes, None),
        P(rows_axes, None),
        P(rows_axes, None),
        P(rows_axes, None),
        P(None, None, rows_axes),
        P(rows_axes),
        P(),
        P(rows_axes),
        P(swiglu_rows, "mlp"),
        P(swiglu_rows, "mlp"),
        P("mlp", swiglu_rows),
    )
    return jax.shard_map(
        make_on_device(tp, fsdp, inner),
        mesh=split_mesh,
        in_specs=placed,
        out_specs=(
            P(None, rows_axes, None),
            P(None, rows_axes, None),
            P(rows_axes, None),
            P(rows_axes, None),
            P(rows_axes, None),
            P(rows_axes, None),
            P(rows_axes, None),
            P(rows_axes, None),
            P(None, None, rows_axes),
            P(rows_axes),
            P(),
            P(rows_axes),
            P(swiglu_rows, "mlp"),
            P(swiglu_rows, "mlp"),
            P("mlp", swiglu_rows),
        ),
        check_vma=False,
    )
```

```python
import jax
import jax.numpy as jnp
import numpy as np
from jax import lax
from jax.sharding import Mesh
from jax.sharding import PartitionSpec as P

TP_AXES = ("core", "mlp")
ALL_AXES = ("dq", "core", "mlp")
FSDP_AXES = tuple(name for name in ALL_AXES if name not in TP_AXES)
INNER_AXES = tuple(name for name in TP_AXES if name != "mlp")


def rms_norm(values, scale_gain):
    return (
        values * lax.rsqrt(jnp.mean(values * values, axis=-1, keepdims=True) + 1e-06) * scale_gain
    )


def short_conv(linear, tap_weights, starts):
    length = linear.shape[0]
    block_len = length // starts.shape[0]
    position = jnp.arange(length)
    restart = jnp.repeat(starts, block_len)
    summed = linear * tap_weights[0]
    for offset in range(1, tap_weights.shape[0]):
        shifted = jnp.concatenate(
            [jnp.zeros((offset, linear.shape[1]), linear.dtype), linear[: length - offset]], axis=0
        )
        usable = ((position % block_len >= offset) | (restart == 0)).astype(linear.dtype)
        summed = summed + shifted * tap_weights[offset] * usable[:, None]
    return summed


def outer_product_result(form, first, second):
    return jnp.einsum(form, first, second, precision=lax.Precision.HIGHEST)


def delta_core(queries, keys, values, betas, starts):
    length, head_count, head_width = queries.shape
    value_width = values.shape[2]
    block_count = starts.shape[0]
    block_len = length // block_count

    def blocked(array):
        return array.reshape(block_count, block_len, head_count, -1).transpose(0, 2, 1, 3)

    query_blocks = blocked(queries)
    key_blocks = blocked(keys)
    value_blocks = blocked(values)
    beta_blocks = betas.reshape(block_count, block_len, head_count).transpose(0, 2, 1)[..., None]
    position = jnp.arange(block_len)
    strict = (position[:, None] > position[None, :]).astype(queries.dtype)
    causal = (position[:, None] >= position[None, :]).astype(queries.dtype)
    weighted = key_blocks * beta_blocks
    negative = -outer_product_result("nhik,nhjk->nhij", weighted, key_blocks) * strict
    inverse = jnp.eye(block_len, dtype=queries.dtype) + negative
    power_term = negative
    for doubling in range(5):
        power_term = outer_product_result("nhij,nhjk->nhik", power_term, power_term)
        inverse = inverse + outer_product_result("nhij,nhjk->nhik", inverse, power_term)
    key_mix = outer_product_result("nhij,nhjk->nhik", inverse, weighted)
    value_mix = outer_product_result("nhij,nhjk->nhik", inverse, value_blocks * beta_blocks)
    scores = outer_product_result("nhik,nhjk->nhij", query_blocks, key_blocks) * causal

    def advance(current_state, block_items):
        (
            query_slice,
            key_slice,
            key_mixture_slice,
            value_mixture_slice,
            attention_score_slice,
            restart,
        ) = block_items
        current_state = current_state * (1 - restart).astype(current_state.dtype)
        adjusted_result = value_mixture_slice - outer_product_result(
            "pzd,pde->pze", key_mixture_slice, current_state
        )
        produced_output = outer_product_result(
            "pzd,pde->pze", query_slice, current_state
        ) + outer_product_result("lqz,lzr->lqr", attention_score_slice, adjusted_result)
        current_state = current_state + outer_product_result(
            "ixl,ixr->ilr", key_slice, adjusted_result
        )
        return (current_state, produced_output)

    initial = jnp.zeros((head_count, head_width, value_width), queries.dtype)
    final_state, produced_output = lax.scan(
        advance, initial, (query_blocks, key_blocks, key_mix, value_mix, scores, starts)
    )
    return produced_output.transpose(0, 2, 1, 3).reshape(length, head_count, value_width)


def delta_core_reset(queries, keys, values, betas, block_len):
    length, head_count, head_width = queries.shape
    block_count = length // block_len

    def blocked(array):
        return array.reshape(block_count, block_len, head_count, -1).transpose(0, 2, 1, 3)

    query_blocks = blocked(queries)
    key_blocks = blocked(keys)
    value_blocks = blocked(values)
    beta_blocks = betas.reshape(block_count, block_len, head_count).transpose(0, 2, 1)[..., None]
    position = jnp.arange(block_len)
    strict = (position[:, None] > position[None, :]).astype(queries.dtype)
    causal = (position[:, None] >= position[None, :]).astype(queries.dtype)
    weighted = key_blocks * beta_blocks
    negative = -outer_product_result("nhik,nhjk->nhij", weighted, key_blocks) * strict
    inverse = jnp.eye(block_len, dtype=queries.dtype) + negative
    power_term = negative
    for doubling in range(5):
        power_term = outer_product_result("nhij,nhjk->nhik", power_term, power_term)
        inverse = inverse + outer_product_result("nhij,nhjk->nhik", inverse, power_term)
    value_mix = outer_product_result("nhij,nhjk->nhik", inverse, value_blocks * beta_blocks)
    scores = outer_product_result("nhik,nhjk->nhij", query_blocks, key_blocks) * causal
    produced_output = outer_product_result("nhqz,nhzr->nhqr", scores, value_mix)
    return produced_output.transpose(0, 2, 1, 3).reshape(length, head_count, -1)


def mixer_core(
    query_lin, key_lin, value_lin, gate_lin, beta_lin, conv_taps, head_scale, starts, reset_len
):
    length = query_lin.shape[0]
    head_count = beta_lin.shape[1]
    head_width = query_lin.shape[1] // head_count
    queries = jax.nn.silu(short_conv(query_lin, conv_taps[0], starts)).reshape(
        length, head_count, head_width
    )
    keys = jax.nn.silu(short_conv(key_lin, conv_taps[1], starts)).reshape(
        length, head_count, head_width
    )
    values = jax.nn.silu(short_conv(value_lin, conv_taps[2], starts)).reshape(
        length, head_count, head_width
    )
    queries = (
        queries
        * lax.rsqrt(jnp.sum(queries * queries, axis=-1, keepdims=True) + 1e-06)
        * head_width ** (-0.5)
    )
    keys = keys * lax.rsqrt(jnp.sum(keys * keys, axis=-1, keepdims=True) + 1e-06)
    if reset_len:
        recurrent = delta_core_reset(queries, keys, values, jax.nn.sigmoid(beta_lin), reset_len)
    else:
        recurrent = delta_core(queries, keys, values, jax.nn.sigmoid(beta_lin), starts)
    normed = (
        recurrent
        * lax.rsqrt(jnp.mean(recurrent * recurrent, axis=-1, keepdims=True) + 1e-05)
        * head_scale
    )
    gated_out = normed * jax.nn.silu(gate_lin.reshape(length, head_count, head_width))
    return gated_out.reshape(length, head_count * head_width)


def swiglu_mix(gate_act, up_act):
    return jax.nn.silu(gate_act) * up_act


def matmul_rows(left, right):
    return jnp.dot(left, right, preferred_element_type=jnp.float32)


def left_product(first, second):
    return jnp.einsum("tf,tg->fg", first, second, preferred_element_type=jnp.float32)


def back_product(gradient, weight):
    return jnp.einsum("tg,fg->tf", gradient, weight, preferred_element_type=jnp.float32)


def tp_gather(value, axis):
    tp = lax.psum(1, TP_AXES)
    spread = jnp.broadcast_to(
        jnp.expand_dims(value, axis), value.shape[:axis] + (tp,) + value.shape[axis:]
    )
    moved = lax.all_to_all(spread, TP_AXES, axis, axis, tiled=True)
    shape = list(value.shape)
    shape[axis] *= tp
    return moved.reshape(shape)


def tp_scatter_low(value, axis):
    tp = lax.psum(1, TP_AXES)
    shape = list(value.shape)
    staged = value.astype(jnp.bfloat16).reshape(
        shape[:axis] + [tp, shape[axis] // tp] + shape[axis + 1 :]
    )
    moved = lax.all_to_all(staged, TP_AXES, axis, axis, tiled=True)
    return jnp.sum(moved.astype(jnp.float32), axis=axis)


def fsdp_gather(value, axis):
    return lax.all_gather(value, FSDP_AXES, axis=axis, tiled=True)


def fsdp_scatter_low(value, axis):
    return lax.psum_scatter(
        value.astype(jnp.bfloat16), FSDP_AXES, scatter_dimension=axis, tiled=True
    )


def exchange(value, axes, split_axis, concat_axis):
    if not axes:
        return value
    return lax.all_to_all(value, axes, split_axis, concat_axis, tiled=True)


def heads_to_rows(values, tp, fsdp, rows):
    count = values.shape[0]
    staged = values.reshape(count, 1, fsdp // tp, tp, rows)
    moved = exchange(staged, TP_AXES, 3, 1)
    return moved.reshape(count, fsdp * rows)


def rows_to_heads(values, tp, fsdp, rows):
    count = values.shape[0]
    staged = values.reshape(count, tp, fsdp // tp, 1, rows)
    moved = exchange(staged, TP_AXES, 1, 3)
    return moved.reshape(count, fsdp * rows)


def padded_rows(flat, slices, width):
    extra = -(-flat.shape[0] // (slices * width))
    extra = -(-extra // 16) * 16
    filled = jnp.pad(flat, (0, slices * extra * width - flat.shape[0]))
    return filled.reshape(slices, extra, width)


def make_on_device(tp, fsdp, inner):
    def on_device(
        tokens,
        cotangent,
        group_start,
        pad_mask,
        query_weight,
        key_weight,
        value_weight,
        gate_weight,
        beta_weight,
        out_weight,
        conv_weight,
        mixer_gain,
        head_gain,
        swiglu_gain,
        swiglu_gate,
        swiglu_up,
        swiglu_down,
    ):
        micro_count, slot, width = tokens.shape
        n_all = tp * fsdp
        rows = query_weight.shape[0]
        head_count = beta_weight.shape[1]
        heads_here = head_count // tp
        cols_here = width // tp
        group_rows = tp * rows
        position = lax.axis_index(TP_AXES)
        head_scale = head_gain.astype(jnp.float32)
        reset_len = slot if group_start.shape[1] == 1 else 0

        small_pack = jnp.concatenate(
            [
                conv_weight.reshape(-1),
                beta_weight.reshape(-1),
                mixer_gain.reshape(-1),
                swiglu_gain.reshape(-1),
            ]
        )
        small_size = small_pack.shape[0]
        small_lines = -(-small_size // (4 * cols_here))
        small_copy = jnp.pad(small_pack, (0, 4 * small_lines * cols_here - small_size))
        small_copy = jnp.broadcast_to(
            small_copy.reshape(4, small_lines, 1, cols_here), (4, small_lines, tp, cols_here)
        )
        column_owned = jnp.stack([query_weight, key_weight, value_weight, gate_weight])
        swap_in = jnp.concatenate(
            [column_owned.reshape(4, rows, tp, cols_here), small_copy], axis=1
        )
        swap_out = exchange(swap_in, TP_AXES, 2, 1).reshape(4, tp, rows + small_lines, cols_here)
        column_swapped = swap_out[:, :, :rows].reshape(4, group_rows, cols_here)
        small_group = (
            swap_out[:, :, rows:]
            .transpose(1, 0, 2, 3)
            .reshape(tp, -1)[:, :small_size]
        )
        small_rows_in = padded_rows(small_group.reshape(-1), 5, cols_here)
        extra_in = small_rows_in.shape[1]
        mixer_stack = jnp.concatenate(
            [
                jnp.concatenate(
                    [column_swapped, out_weight.reshape(1, group_rows, cols_here)], axis=0
                ),
                small_rows_in,
            ],
            axis=1,
        )
        mixer_all = fsdp_gather(mixer_stack, 1).reshape(5, fsdp, group_rows + extra_in, cols_here)
        weight_all = mixer_all[:, :, :group_rows].reshape(5, width, cols_here)
        query_cols, key_cols, value_cols, gate_cols = (weight_all[index] for index in range(4))
        out_rows = weight_all[4].reshape(fsdp * rows, width)
        small_all = (
            mixer_all[:, :, group_rows:]
            .transpose(1, 0, 2, 3)
            .reshape(fsdp, -1)[:, : tp * small_size]
            .reshape(n_all, small_size)
        )
        conv_size = conv_weight.size
        beta_size = beta_weight.size
        conv_full = (
            small_all[:, :conv_size]
            .reshape((n_all,) + conv_weight.shape)
            .transpose(1, 2, 0, 3)
            .reshape(conv_weight.shape[0], conv_weight.shape[1], -1)
        )
        beta_full = small_all[:, conv_size : conv_size + beta_size].reshape(-1, head_count)
        gain_mixer = small_all[:, conv_size + beta_size : conv_size + beta_size + rows].reshape(-1)
        gain_swiglu = small_all[:, conv_size + beta_size + rows :].reshape(-1)
        conv_here = lax.dynamic_slice_in_dim(
            conv_full.astype(jnp.float32), position * cols_here, cols_here, axis=2
        )
        beta_here = lax.dynamic_slice_in_dim(beta_full, position * heads_here, heads_here, axis=1)

        owned_rows, hidden_half = swiglu_gate.shape
        hidden_here = hidden_half // inner
        ff_owned = jnp.stack([swiglu_gate, swiglu_up, swiglu_down.T]).reshape(
            3, owned_rows, inner, hidden_here
        )
        lanes = hidden_here // 128 if hidden_here % 128 == 0 else 0
        first = (lanes + 1) // 2 * 128 if lanes > 1 else hidden_here // 2
        bounds = ((0, first), (first, hidden_here - first))
        ff_chunks = []
        for offset, size in bounds:
            swapped = exchange(ff_owned[..., offset : offset + size], INNER_AXES, 2, 1)
            ff_chunks.append(fsdp_gather(swapped.reshape(3, inner * owned_rows, size), 1))

        inputs = tokens.astype(jnp.float32).reshape(micro_count * slot, width)
        normed, norm_back = jax.vjp(rms_norm, inputs, gain_mixer.astype(jnp.float32))
        normed_low = normed.astype(jnp.bfloat16)
        group_tokens = micro_count * slot * tp
        normed_group = tp_gather(normed_low.reshape(micro_count, slot, width), 1).reshape(
            group_tokens, width
        )
        starts = tp_gather(group_start, 1).reshape(-1)

        query_lin = matmul_rows(normed_group, query_cols)
        key_lin = matmul_rows(normed_group, key_cols)
        value_lin = matmul_rows(normed_group, value_cols)
        gate_lin = matmul_rows(normed_group, gate_cols)
        beta_lin = matmul_rows(normed_group, beta_here)

        def core_at(query_in, key_in, value_in, gate_in, beta_in, conv_in, head_in):
            return mixer_core(
                query_in, key_in, value_in, gate_in, beta_in, conv_in, head_in, starts, reset_len
            )

        gated_out, core_back = jax.vjp(
            core_at, query_lin, key_lin, value_lin, gate_lin, beta_lin, conv_here, head_scale
        )
        gated_low = gated_out.astype(jnp.bfloat16)
        gated_rows = heads_to_rows(gated_low, tp, fsdp, rows)
        mixed_partial = matmul_rows(gated_rows, out_rows)
        residual = inputs + tp_scatter_low(
            mixed_partial.reshape(micro_count, slot * tp, width), 1
        ).reshape(micro_count * slot, width)

        inner_norm, inner_norm_back = jax.vjp(rms_norm, residual, gain_swiglu.astype(jnp.float32))
        inner_low = inner_norm.astype(jnp.bfloat16)
        inner_group = tp_gather(inner_low.reshape(micro_count, slot, width), 1).reshape(
            group_tokens, width
        )
        out_back = cotangent.astype(jnp.float32) * pad_mask.astype(jnp.float32)[:, :, None]
        out_back_low = out_back.astype(jnp.bfloat16)
        upstream_group = tp_gather(out_back_low, 1).reshape(group_tokens, width)
        partial_rows = None
        inner_part = None
        ff_reduced = []
        for index, chunk_weights in enumerate(ff_chunks):
            if index > 0:
                sums_low, chunk_weights = lax.optimization_barrier((sums_low, chunk_weights))
            gate_piece, up_piece, down_piece_t = chunk_weights[0], chunk_weights[1], chunk_weights[2]
            gate_act = matmul_rows(inner_group, gate_piece)
            up_act = matmul_rows(inner_group, up_piece)
            hidden, hidden_back = jax.vjp(swiglu_mix, gate_act, up_act)
            hidden_low = hidden.astype(jnp.bfloat16)
            piece_rows = back_product(hidden_low, down_piece_t)
            partial_rows = piece_rows if partial_rows is None else partial_rows + piece_rows
            gate_back, up_back = hidden_back(matmul_rows(upstream_group, down_piece_t))
            gate_back_low = gate_back.astype(jnp.bfloat16)
            up_back_low = up_back.astype(jnp.bfloat16)
            piece_part = back_product(gate_back_low, gate_piece) + back_product(up_back_low, up_piece)
            inner_part = piece_part if inner_part is None else inner_part + piece_part
            sums_low = jnp.stack(
                [
                    left_product(inner_group, gate_back_low),
                    left_product(inner_group, up_back_low),
                    left_product(upstream_group, hidden_low),
                ]
            ).astype(jnp.bfloat16)
            ff_reduced.append(fsdp_scatter_low(sums_low, 1))
        branch_rows = tp_scatter_low(partial_rows.reshape(micro_count, slot * tp, width), 1)
        block_out = (residual.reshape(micro_count, slot, width) + branch_rows).astype(jnp.bfloat16)
        inner_back = tp_scatter_low(inner_part.reshape(micro_count, slot * tp, width), 1)
        block_out, inner_back = lax.optimization_barrier((block_out, inner_back))

        residual_part, swiglu_gain_term = inner_norm_back(
            inner_back.reshape(micro_count * slot, width)
        )
        residual_back = out_back.reshape(micro_count * slot, width) + residual_part
        mixed_back = residual_back.astype(jnp.bfloat16)
        mixed_group = tp_gather(mixed_back.reshape(micro_count, slot, width), 1).reshape(
            group_tokens, width
        )
        gated_back_rows = back_product(mixed_group, out_rows)
        gated_back = rows_to_heads(gated_back_rows, tp, fsdp, rows)
        query_back, key_back, value_back, gate_lin_back, beta_back, conv_term, head_term = (
            core_back(gated_back)
        )
        query_low = query_back.astype(jnp.bfloat16)
        key_low = key_back.astype(jnp.bfloat16)
        value_low = value_back.astype(jnp.bfloat16)
        gate_low = gate_lin_back.astype(jnp.bfloat16)
        beta_low = beta_back.astype(jnp.bfloat16)
        normed_part = (
            back_product(query_low, query_cols)
            + back_product(key_low, key_cols)
            + back_product(value_low, value_cols)
            + back_product(gate_low, gate_cols)
            + back_product(beta_low, beta_here)
        )
        ff_back = jnp.concatenate(
            [
                exchange(
                    piece.reshape(3, inner, owned_rows, 1, size), INNER_AXES, 1, 3
                ).reshape(3, owned_rows, inner, size)
                for piece, (offset, size) in zip(ff_reduced, bounds)
            ],
            axis=3,
        ).reshape(3, owned_rows, hidden_half).astype(jnp.float32)
        ff_back, normed_part = lax.optimization_barrier((ff_back, normed_part))
        normed_back = tp_scatter_low(normed_part.reshape(micro_count, slot * tp, width), 1)
        input_part, mixer_gain_term = norm_back(normed_back.reshape(micro_count * slot, width))
        tokens_grad = (residual_back + input_part).reshape(micro_count, slot, width)

        mixer_sums = jnp.stack(
            [
                left_product(normed_group, query_low),
                left_product(normed_group, key_low),
                left_product(normed_group, value_low),
                left_product(normed_group, gate_low),
                left_product(gated_rows, mixed_group).reshape(width, cols_here),
            ]
        ).reshape(5, fsdp, group_rows, cols_here)
        beta_sum = left_product(normed_group, beta_low)
        beta_wide = lax.dynamic_update_slice_in_dim(
            jnp.zeros((width, head_count), jnp.float32), beta_sum, position * heads_here, axis=1
        )
        conv_wide = lax.dynamic_update_slice_in_dim(
            jnp.zeros(conv_full.shape, jnp.float32), conv_term, position * cols_here, axis=2
        )
        taps = conv_wide.shape[0] * conv_wide.shape[1]
        small_terms = jnp.concatenate(
            [
                conv_wide.reshape(taps, n_all, -1).transpose(1, 0, 2).reshape(n_all, -1),
                beta_wide.reshape(n_all, -1),
                mixer_gain_term.reshape(n_all, -1),
                swiglu_gain_term.reshape(n_all, -1),
                jnp.broadcast_to(head_term[None, :], (n_all, head_term.shape[0])),
            ],
            axis=1,
        )
        small_width = small_terms.shape[1]
        small_tp = jnp.sum(
            exchange(small_terms.reshape(fsdp, tp, small_width), TP_AXES, 1, 1), axis=1
        )
        small_block = jax.vmap(lambda flat: padded_rows(flat, 5, cols_here))(small_tp)
        extra_out = small_block.shape[2]
        reduce_in = jnp.concatenate([mixer_sums, small_block.transpose(1, 0, 2, 3)], axis=2)
        ff_back, reduce_in = lax.optimization_barrier((ff_back, reduce_in))
        swiglu_gate_grad = ff_back[0]
        swiglu_up_grad = ff_back[1]
        swiglu_down_grad = ff_back[2].T
        mixer_reduced = fsdp_scatter_low(
            reduce_in.reshape(5, fsdp * (group_rows + extra_out), cols_here), 1
        )
        column_back = exchange(
            mixer_reduced[:4, :group_rows].reshape(4, tp, rows, 1, cols_here), TP_AXES, 1, 3
        ).reshape(4, rows, width).astype(jnp.float32)
        query_grad, key_grad, value_grad, gate_grad = (column_back[index] for index in range(4))
        out_grad = mixer_reduced[4, :group_rows].reshape(rows, width).astype(jnp.float32)
        small_out = mixer_reduced[:, group_rows:].reshape(-1)[:small_width].astype(jnp.float32)
        conv_grad = small_out[:conv_size].reshape(conv_weight.shape)
        beta_grad = small_out[conv_size : conv_size + beta_size].reshape(beta_weight.shape)
        mixer_gain_grad = small_out[conv_size + beta_size : conv_size + beta_size + rows]
        swiglu_gain_grad = small_out[conv_size + beta_size + rows : conv_size + beta_size + 2 * rows]
        head_total = small_out[conv_size + beta_size + 2 * rows :]
        return (
            block_out,
            tokens_grad,
            query_grad,
            key_grad,
            value_grad,
            gate_grad,
            beta_grad,
            out_grad,
            conv_grad,
            mixer_gain_grad,
            head_total,
            swiglu_gain_grad,
            swiglu_gate_grad,
            swiglu_up_grad,
            swiglu_down_grad,
        )

    return on_device


def solution(mesh):
    n_dp = mesh.shape["dp"]
    n_mlp = mesh.shape["mlp"]
    devices = np.asarray(mesh.devices).reshape(n_dp // 2, 2, n_mlp)
    split_mesh = Mesh(devices, ALL_AXES)
    sizes = dict(zip(ALL_AXES, devices.shape))
    tp = int(np.prod([sizes[name] for name in TP_AXES]))
    fsdp = int(np.prod([sizes[name] for name in FSDP_AXES]))
    inner = int(np.prod([sizes[name] for name in INNER_AXES]))
    rows_axes = ALL_AXES
    swiglu_rows = ("dq", "core")
    placed = (
        P(None, rows_axes, None),
        P(None, rows_axes, None),
        P(None, rows_axes),
        P(None, rows_axes),
        P(rows_axes, None),
        P(rows_axes, None),
        P(rows_axes, None),
        P(rows_axes, None),
        P(rows_axes, None),
        P(rows_axes, None),
        P(None, None, rows_axes),
        P(rows_axes),
        P(),
        P(rows_axes),
        P(swiglu_rows, "mlp"),
        P(swiglu_rows, "mlp"),
        P("mlp", swiglu_rows),
    )
    return jax.shard_map(
        make_on_device(tp, fsdp, inner),
        mesh=split_mesh,
        in_specs=placed,
        out_specs=(
            P(None, rows_axes, None),
            P(None, rows_axes, None),
            P(rows_axes, None),
            P(rows_axes, None),
            P(rows_axes, None),
            P(rows_axes, None),
            P(rows_axes, None),
            P(rows_axes, None),
            P(None, None, rows_axes),
            P(rows_axes),
            P(),
            P(rows_axes),
            P(swiglu_rows, "mlp"),
            P(swiglu_rows, "mlp"),
            P("mlp", swiglu_rows),
        ),
        check_vma=False,
    )
```

```python
import jax
import jax.numpy as jnp
import numpy as np
from jax import lax
from jax.sharding import Mesh
from jax.sharding import PartitionSpec as P

TP_AXES = ("core", "mlp")
ALL_AXES = ("dq", "core", "mlp")
FSDP_AXES = tuple(name for name in ALL_AXES if name not in TP_AXES)
INNER_AXES = tuple(name for name in TP_AXES if name != "mlp")


def rms_norm(values, scale_gain):
    return (
        values * lax.rsqrt(jnp.mean(values * values, axis=-1, keepdims=True) + 1e-06) * scale_gain
    )


def short_conv(linear, tap_weights, starts):
    length = linear.shape[0]
    block_len = length // starts.shape[0]
    position = jnp.arange(length)
    restart = jnp.repeat(starts, block_len)
    summed = linear * tap_weights[0]
    for offset in range(1, tap_weights.shape[0]):
        shifted = jnp.concatenate(
            [jnp.zeros((offset, linear.shape[1]), linear.dtype), linear[: length - offset]], axis=0
        )
        usable = ((position % block_len >= offset) | (restart == 0)).astype(linear.dtype)
        summed = summed + shifted * tap_weights[offset] * usable[:, None]
    return summed


def outer_product_result(form, first, second):
    return jnp.einsum(form, first, second, precision=lax.Precision.HIGHEST)


def delta_core(queries, keys, values, betas, starts):
    length, head_count, head_width = queries.shape
    value_width = values.shape[2]
    block_count = starts.shape[0]
    block_len = length // block_count

    def blocked(array):
        return array.reshape(block_count, block_len, head_count, -1).transpose(0, 2, 1, 3)

    query_blocks = blocked(queries)
    key_blocks = blocked(keys)
    value_blocks = blocked(values)
    beta_blocks = betas.reshape(block_count, block_len, head_count).transpose(0, 2, 1)[..., None]
    position = jnp.arange(block_len)
    strict = (position[:, None] > position[None, :]).astype(queries.dtype)
    causal = (position[:, None] >= position[None, :]).astype(queries.dtype)
    weighted = key_blocks * beta_blocks
    negative = -outer_product_result("nhik,nhjk->nhij", weighted, key_blocks) * strict
    inverse = jnp.eye(block_len, dtype=queries.dtype) + negative
    power_term = negative
    for doubling in range(5):
        power_term = outer_product_result("nhij,nhjk->nhik", power_term, power_term)
        inverse = inverse + outer_product_result("nhij,nhjk->nhik", inverse, power_term)
    key_mix = outer_product_result("nhij,nhjk->nhik", inverse, weighted)
    value_mix = outer_product_result("nhij,nhjk->nhik", inverse, value_blocks * beta_blocks)
    scores = outer_product_result("nhik,nhjk->nhij", query_blocks, key_blocks) * causal

    def advance(current_state, block_items):
        (
            query_slice,
            key_slice,
            key_mixture_slice,
            value_mixture_slice,
            attention_score_slice,
            restart,
        ) = block_items
        current_state = current_state * (1 - restart).astype(current_state.dtype)
        adjusted_result = value_mixture_slice - outer_product_result(
            "pzd,pde->pze", key_mixture_slice, current_state
        )
        produced_output = outer_product_result(
            "pzd,pde->pze", query_slice, current_state
        ) + outer_product_result("lqz,lzr->lqr", attention_score_slice, adjusted_result)
        current_state = current_state + outer_product_result(
            "ixl,ixr->ilr", key_slice, adjusted_result
        )
        return (current_state, produced_output)

    initial = jnp.zeros((head_count, head_width, value_width), queries.dtype)
    final_state, produced_output = lax.scan(
        advance, initial, (query_blocks, key_blocks, key_mix, value_mix, scores, starts)
    )
    return produced_output.transpose(0, 2, 1, 3).reshape(length, head_count, value_width)


def delta_core_reset(queries, keys, values, betas, block_len):
    length, head_count, head_width = queries.shape
    block_count = length // block_len

    def blocked(array):
        return array.reshape(block_count, block_len, head_count, -1).transpose(0, 2, 1, 3)

    query_blocks = blocked(queries)
    key_blocks = blocked(keys)
    value_blocks = blocked(values)
    beta_blocks = betas.reshape(block_count, block_len, head_count).transpose(0, 2, 1)[..., None]
    position = jnp.arange(block_len)
    strict = (position[:, None] > position[None, :]).astype(queries.dtype)
    causal = (position[:, None] >= position[None, :]).astype(queries.dtype)
    weighted = key_blocks * beta_blocks
    negative = -outer_product_result("nhik,nhjk->nhij", weighted, key_blocks) * strict
    inverse = jnp.eye(block_len, dtype=queries.dtype) + negative
    power_term = negative
    for doubling in range(5):
        power_term = outer_product_result("nhij,nhjk->nhik", power_term, power_term)
        inverse = inverse + outer_product_result("nhij,nhjk->nhik", inverse, power_term)
    value_mix = outer_product_result("nhij,nhjk->nhik", inverse, value_blocks * beta_blocks)
    scores = outer_product_result("nhik,nhjk->nhij", query_blocks, key_blocks) * causal
    produced_output = outer_product_result("nhqz,nhzr->nhqr", scores, value_mix)
    return produced_output.transpose(0, 2, 1, 3).reshape(length, head_count, -1)


def mixer_core(
    query_lin, key_lin, value_lin, gate_lin, beta_lin, conv_taps, head_scale, starts, reset_len
):
    length = query_lin.shape[0]
    head_count = beta_lin.shape[1]
    head_width = query_lin.shape[1] // head_count
    queries = jax.nn.silu(short_conv(query_lin, conv_taps[0], starts)).reshape(
        length, head_count, head_width
    )
    keys = jax.nn.silu(short_conv(key_lin, conv_taps[1], starts)).reshape(
        length, head_count, head_width
    )
    values = jax.nn.silu(short_conv(value_lin, conv_taps[2], starts)).reshape(
        length, head_count, head_width
    )
    queries = (
        queries
        * lax.rsqrt(jnp.sum(queries * queries, axis=-1, keepdims=True) + 1e-06)
        * head_width ** (-0.5)
    )
    keys = keys * lax.rsqrt(jnp.sum(keys * keys, axis=-1, keepdims=True) + 1e-06)
    if reset_len:
        recurrent = delta_core_reset(queries, keys, values, jax.nn.sigmoid(beta_lin), reset_len)
    else:
        recurrent = delta_core(queries, keys, values, jax.nn.sigmoid(beta_lin), starts)
    normed = (
        recurrent
        * lax.rsqrt(jnp.mean(recurrent * recurrent, axis=-1, keepdims=True) + 1e-05)
        * head_scale
    )
    gated_out = normed * jax.nn.silu(gate_lin.reshape(length, head_count, head_width))
    return gated_out.reshape(length, head_count * head_width)


def swiglu_mix(gate_act, up_act):
    return jax.nn.silu(gate_act) * up_act


def matmul_rows(left, right):
    return jnp.dot(left, right, preferred_element_type=jnp.float32)


def left_product(first, second):
    return jnp.einsum("tf,tg->fg", first, second, preferred_element_type=jnp.float32)


def back_product(gradient, weight):
    return jnp.einsum("tg,fg->tf", gradient, weight, preferred_element_type=jnp.float32)


def tp_gather(value, axis):
    tp = lax.psum(1, TP_AXES)
    spread = jnp.broadcast_to(
        jnp.expand_dims(value, axis), value.shape[:axis] + (tp,) + value.shape[axis:]
    )
    moved = lax.all_to_all(spread, TP_AXES, axis, axis, tiled=True)
    shape = list(value.shape)
    shape[axis] *= tp
    return moved.reshape(shape)


def tp_scatter_low(value, axis):
    tp = lax.psum(1, TP_AXES)
    shape = list(value.shape)
    staged = value.astype(jnp.bfloat16).reshape(
        shape[:axis] + [tp, shape[axis] // tp] + shape[axis + 1 :]
    )
    moved = lax.all_to_all(staged, TP_AXES, axis, axis, tiled=True)
    return jnp.sum(moved.astype(jnp.float32), axis=axis)


def fsdp_gather(value, axis):
    return lax.all_gather(value, FSDP_AXES, axis=axis, tiled=True)


def fsdp_scatter_low(value, axis):
    return lax.psum_scatter(
        value.astype(jnp.bfloat16), FSDP_AXES, scatter_dimension=axis, tiled=True
    )


def exchange(value, axes, split_axis, concat_axis):
    if not axes:
        return value
    return lax.all_to_all(value, axes, split_axis, concat_axis, tiled=True)


def heads_to_rows(values, tp, fsdp, rows):
    count = values.shape[0]
    staged = values.reshape(count, 1, fsdp // tp, tp, rows)
    moved = exchange(staged, TP_AXES, 3, 1)
    return moved.reshape(count, fsdp * rows)


def rows_to_heads(values, tp, fsdp, rows):
    count = values.shape[0]
    staged = values.reshape(count, tp, fsdp // tp, 1, rows)
    moved = exchange(staged, TP_AXES, 1, 3)
    return moved.reshape(count, fsdp * rows)


def padded_rows(flat, slices, width):
    extra = -(-flat.shape[0] // (slices * width))
    extra = -(-extra // 16) * 16
    filled = jnp.pad(flat, (0, slices * extra * width - flat.shape[0]))
    return filled.reshape(slices, extra, width)


def make_on_device(tp, fsdp, inner):
    def on_device(
        tokens,
        cotangent,
        group_start,
        pad_mask,
        query_weight,
        key_weight,
        value_weight,
        gate_weight,
        beta_weight,
        out_weight,
        conv_weight,
        mixer_gain,
        head_gain,
        swiglu_gain,
        swiglu_gate,
        swiglu_up,
        swiglu_down,
    ):
        micro_count, slot, width = tokens.shape
        n_all = tp * fsdp
        rows = query_weight.shape[0]
        head_count = beta_weight.shape[1]
        heads_here = head_count // tp
        cols_here = width // tp
        group_rows = tp * rows
        position = lax.axis_index(TP_AXES)
        head_scale = head_gain.astype(jnp.float32)
        reset_len = slot if group_start.shape[1] == 1 else 0

        small_pack = jnp.concatenate(
            [
                conv_weight.reshape(-1),
                beta_weight.reshape(-1),
                mixer_gain.reshape(-1),
                swiglu_gain.reshape(-1),
            ]
        )
        small_size = small_pack.shape[0]
        small_lines = -(-small_size // (4 * cols_here))
        small_copy = jnp.pad(small_pack, (0, 4 * small_lines * cols_here - small_size))
        small_copy = jnp.broadcast_to(
            small_copy.reshape(4, small_lines, 1, cols_here), (4, small_lines, tp, cols_here)
        )
        column_owned = jnp.stack([query_weight, key_weight, value_weight, gate_weight])
        swap_in = jnp.concatenate(
            [column_owned.reshape(4, rows, tp, cols_here), small_copy], axis=1
        )
        swap_out = exchange(swap_in, TP_AXES, 2, 1).reshape(4, tp, rows + small_lines, cols_here)
        column_swapped = swap_out[:, :, :rows].reshape(4, group_rows, cols_here)
        small_group = (
            swap_out[:, :, rows:]
            .transpose(1, 0, 2, 3)
            .reshape(tp, -1)[:, :small_size]
        )
        small_rows_in = padded_rows(small_group.reshape(-1), 5, cols_here)
        extra_in = small_rows_in.shape[1]
        mixer_stack = jnp.concatenate(
            [
                jnp.concatenate(
                    [column_swapped, out_weight.reshape(1, group_rows, cols_here)], axis=0
                ),
                small_rows_in,
            ],
            axis=1,
        )
        mixer_all = fsdp_gather(mixer_stack, 1).reshape(5, fsdp, group_rows + extra_in, cols_here)
        weight_all = mixer_all[:, :, :group_rows].reshape(5, width, cols_here)
        query_cols, key_cols, value_cols, gate_cols = (weight_all[index] for index in range(4))
        out_rows = weight_all[4].reshape(fsdp * rows, width)
        small_all = (
            mixer_all[:, :, group_rows:]
            .transpose(1, 0, 2, 3)
            .reshape(fsdp, -1)[:, : tp * small_size]
            .reshape(n_all, small_size)
        )
        conv_size = conv_weight.size
        beta_size = beta_weight.size
        conv_full = (
            small_all[:, :conv_size]
            .reshape((n_all,) + conv_weight.shape)
            .transpose(1, 2, 0, 3)
            .reshape(conv_weight.shape[0], conv_weight.shape[1], -1)
        )
        beta_full = small_all[:, conv_size : conv_size + beta_size].reshape(-1, head_count)
        gain_mixer = small_all[:, conv_size + beta_size : conv_size + beta_size + rows].reshape(-1)
        gain_swiglu = small_all[:, conv_size + beta_size + rows :].reshape(-1)
        conv_here = lax.dynamic_slice_in_dim(
            conv_full.astype(jnp.float32), position * cols_here, cols_here, axis=2
        )
        beta_here = lax.dynamic_slice_in_dim(beta_full, position * heads_here, heads_here, axis=1)

        owned_rows, hidden_half = swiglu_gate.shape
        hidden_here = hidden_half // inner
        ff_owned = jnp.stack([swiglu_gate, swiglu_up, swiglu_down.T]).reshape(
            3, owned_rows, inner, hidden_here
        )
        lanes = hidden_here // 128 if hidden_here % 128 == 0 else 0
        first = (lanes + 1) // 2 * 128 if lanes > 1 else hidden_here // 2
        bounds = ((0, first), (first, hidden_here - first))
        ff_chunks = []
        for offset, size in bounds:
            swapped = exchange(ff_owned[..., offset : offset + size], INNER_AXES, 2, 1)
            ff_chunks.append(fsdp_gather(swapped.reshape(3, inner * owned_rows, size), 1))

        inputs = tokens.astype(jnp.float32).reshape(micro_count * slot, width)
        normed, norm_back = jax.vjp(rms_norm, inputs, gain_mixer.astype(jnp.float32))
        normed_low = normed.astype(jnp.bfloat16)
        group_tokens = micro_count * slot * tp
        normed_group = tp_gather(normed_low.reshape(micro_count, slot, width), 1).reshape(
            group_tokens, width
        )
        starts = tp_gather(group_start, 1).reshape(-1)

        query_lin = matmul_rows(normed_group, query_cols)
        key_lin = matmul_rows(normed_group, key_cols)
        value_lin = matmul_rows(normed_group, value_cols)
        gate_lin = matmul_rows(normed_group, gate_cols)
        beta_lin = matmul_rows(normed_group, beta_here)

        def core_at(query_in, key_in, value_in, gate_in, beta_in, conv_in, head_in):
            return mixer_core(
                query_in, key_in, value_in, gate_in, beta_in, conv_in, head_in, starts, reset_len
            )

        gated_out, core_back = jax.vjp(
            core_at, query_lin, key_lin, value_lin, gate_lin, beta_lin, conv_here, head_scale
        )
        gated_low = gated_out.astype(jnp.bfloat16)
        gated_rows = heads_to_rows(gated_low, tp, fsdp, rows)
        mixed_partial = matmul_rows(gated_rows, out_rows)
        residual = inputs + tp_scatter_low(
            mixed_partial.reshape(micro_count, slot * tp, width), 1
        ).reshape(micro_count * slot, width)

        inner_norm, inner_norm_back = jax.vjp(rms_norm, residual, gain_swiglu.astype(jnp.float32))
        inner_low = inner_norm.astype(jnp.bfloat16)
        inner_group = tp_gather(inner_low.reshape(micro_count, slot, width), 1).reshape(
            group_tokens, width
        )
        out_back = cotangent.astype(jnp.float32) * pad_mask.astype(jnp.float32)[:, :, None]
        out_back_low = out_back.astype(jnp.bfloat16)
        upstream_group = tp_gather(out_back_low, 1).reshape(group_tokens, width)
        partial_rows = None
        inner_part = None
        ff_reduced = []
        for index, chunk_weights in enumerate(ff_chunks):
            if index > 0:
                sums_low, chunk_weights = lax.optimization_barrier((sums_low, chunk_weights))
            gate_piece, up_piece, down_piece_t = chunk_weights[0], chunk_weights[1], chunk_weights[2]
            gate_act = matmul_rows(inner_group, gate_piece)
            up_act = matmul_rows(inner_group, up_piece)
            hidden, hidden_back = jax.vjp(swiglu_mix, gate_act, up_act)
            hidden_low = hidden.astype(jnp.bfloat16)
            piece_rows = back_product(hidden_low, down_piece_t)
            partial_rows = piece_rows if partial_rows is None else partial_rows + piece_rows
            gate_back, up_back = hidden_back(matmul_rows(upstream_group, down_piece_t))
            gate_back_low = gate_back.astype(jnp.bfloat16)
            up_back_low = up_back.astype(jnp.bfloat16)
            piece_part = back_product(gate_back_low, gate_piece) + back_product(up_back_low, up_piece)
            inner_part = piece_part if inner_part is None else inner_part + piece_part
            sums_low = jnp.stack(
                [
                    left_product(inner_group, gate_back_low),
                    left_product(inner_group, up_back_low),
                    left_product(upstream_group, hidden_low),
                ]
            ).astype(jnp.bfloat16)
            ff_reduced.append(fsdp_scatter_low(sums_low, 1))
        branch_rows = tp_scatter_low(partial_rows.reshape(micro_count, slot * tp, width), 1)
        block_out = (residual.reshape(micro_count, slot, width) + branch_rows).astype(jnp.bfloat16)
        inner_back = tp_scatter_low(inner_part.reshape(micro_count, slot * tp, width), 1)
        block_out, inner_back = lax.optimization_barrier((block_out, inner_back))

        residual_part, swiglu_gain_term = inner_norm_back(
            inner_back.reshape(micro_count * slot, width)
        )
        residual_back = out_back.reshape(micro_count * slot, width) + residual_part
        mixed_back = residual_back.astype(jnp.bfloat16)
        mixed_group = tp_gather(mixed_back.reshape(micro_count, slot, width), 1).reshape(
            group_tokens, width
        )
        gated_back_rows = back_product(mixed_group, out_rows)
        gated_back = rows_to_heads(gated_back_rows, tp, fsdp, rows)
        query_back, key_back, value_back, gate_lin_back, beta_back, conv_term, head_term = (
            core_back(gated_back)
        )
        query_low = query_back.astype(jnp.bfloat16)
        key_low = key_back.astype(jnp.bfloat16)
        value_low = value_back.astype(jnp.bfloat16)
        gate_low = gate_lin_back.astype(jnp.bfloat16)
        beta_low = beta_back.astype(jnp.bfloat16)
        mixer_sums = jnp.stack(
            [
                left_product(normed_group, query_low),
                left_product(normed_group, key_low),
                left_product(normed_group, value_low),
                left_product(normed_group, gate_low),
                left_product(gated_rows, mixed_group).reshape(width, cols_here),
            ]
        )
        ff_reduced, mixer_sums = lax.optimization_barrier((ff_reduced, mixer_sums))
        mixer_reduced = fsdp_scatter_low(mixer_sums, 1)
        ff_back = jnp.concatenate(
            [
                exchange(
                    piece.reshape(3, inner, owned_rows, 1, size), INNER_AXES, 1, 3
                ).reshape(3, owned_rows, inner, size)
                for piece, (offset, size) in zip(ff_reduced, bounds)
            ],
            axis=3,
        ).reshape(3, owned_rows, hidden_half).astype(jnp.float32)
        swiglu_gate_grad = ff_back[0]
        swiglu_up_grad = ff_back[1]
        swiglu_down_grad = ff_back[2].T

        normed_part = (
            back_product(query_low, query_cols)
            + back_product(key_low, key_cols)
            + back_product(value_low, value_cols)
            + back_product(gate_low, gate_cols)
            + back_product(beta_low, beta_here)
        )
        normed_back = tp_scatter_low(normed_part.reshape(micro_count, slot * tp, width), 1)
        input_part, mixer_gain_term = norm_back(normed_back.reshape(micro_count * slot, width))
        tokens_grad = (residual_back + input_part).reshape(micro_count, slot, width)

        beta_sum = left_product(normed_group, beta_low)
        beta_wide = lax.dynamic_update_slice_in_dim(
            jnp.zeros((width, head_count), jnp.float32), beta_sum, position * heads_here, axis=1
        )
        conv_wide = lax.dynamic_update_slice_in_dim(
            jnp.zeros(conv_full.shape, jnp.float32), conv_term, position * cols_here, axis=2
        )
        taps = conv_wide.shape[0] * conv_wide.shape[1]
        small_terms = jnp.concatenate(
            [
                conv_wide.reshape(taps, n_all, -1).transpose(1, 0, 2).reshape(n_all, -1),
                beta_wide.reshape(n_all, -1),
                mixer_gain_term.reshape(n_all, -1),
                swiglu_gain_term.reshape(n_all, -1),
                jnp.broadcast_to(head_term[None, :], (n_all, head_term.shape[0])),
            ],
            axis=1,
        )
        small_width = small_terms.shape[1]
        small_out = jnp.sum(exchange(small_terms, ALL_AXES, 0, 0), axis=0)
        column_back = exchange(
            mixer_reduced[:4].reshape(4, tp, rows, 1, cols_here), TP_AXES, 1, 3
        ).reshape(4, rows, width).astype(jnp.float32)
        query_grad, key_grad, value_grad, gate_grad = (column_back[index] for index in range(4))
        out_grad = mixer_reduced[4].reshape(rows, width).astype(jnp.float32)
        conv_grad = small_out[:conv_size].reshape(conv_weight.shape)
        beta_grad = small_out[conv_size : conv_size + beta_size].reshape(beta_weight.shape)
        mixer_gain_grad = small_out[conv_size + beta_size : conv_size + beta_size + rows]
        swiglu_gain_grad = small_out[conv_size + beta_size + rows : conv_size + beta_size + 2 * rows]
        head_total = small_out[conv_size + beta_size + 2 * rows :]
        return (
            block_out,
            tokens_grad,
            query_grad,
            key_grad,
            value_grad,
            gate_grad,
            beta_grad,
            out_grad,
            conv_grad,
            mixer_gain_grad,
            head_total,
            swiglu_gain_grad,
            swiglu_gate_grad,
            swiglu_up_grad,
            swiglu_down_grad,
        )

    return on_device


def solution(mesh):
    n_dp = mesh.shape["dp"]
    n_mlp = mesh.shape["mlp"]
    devices = np.asarray(mesh.devices).reshape(n_dp // 2, 2, n_mlp)
    split_mesh = Mesh(devices, ALL_AXES)
    sizes = dict(zip(ALL_AXES, devices.shape))
    tp = int(np.prod([sizes[name] for name in TP_AXES]))
    fsdp = int(np.prod([sizes[name] for name in FSDP_AXES]))
    inner = int(np.prod([sizes[name] for name in INNER_AXES]))
    rows_axes = ALL_AXES
    swiglu_rows = ("dq", "core")
    placed = (
        P(None, rows_axes, None),
        P(None, rows_axes, None),
        P(None, rows_axes),
        P(None, rows_axes),
        P(rows_axes, None),
        P(rows_axes, None),
        P(rows_axes, None),
        P(rows_axes, None),
        P(rows_axes, None),
        P(rows_axes, None),
        P(None, None, rows_axes),
        P(rows_axes),
        P(),
        P(rows_axes),
        P(swiglu_rows, "mlp"),
        P(swiglu_rows, "mlp"),
        P("mlp", swiglu_rows),
    )
    return jax.shard_map(
        make_on_device(tp, fsdp, inner),
        mesh=split_mesh,
        in_specs=placed,
        out_specs=(
            P(None, rows_axes, None),
            P(None, rows_axes, None),
            P(rows_axes, None),
            P(rows_axes, None),
            P(rows_axes, None),
            P(rows_axes, None),
            P(rows_axes, None),
            P(rows_axes, None),
            P(None, None, rows_axes),
            P(rows_axes),
            P(),
            P(rows_axes),
            P(swiglu_rows, "mlp"),
            P(swiglu_rows, "mlp"),
            P("mlp", swiglu_rows),
        ),
        check_vma=False,
    )
```

```python
import jax
import jax.numpy as jnp
import numpy as np
from jax import lax
from jax.sharding import Mesh
from jax.sharding import PartitionSpec as P

TP_AXES = ("core", "mlp")
ALL_AXES = ("dq", "core", "mlp")
FSDP_AXES = tuple(name for name in ALL_AXES if name not in TP_AXES)
INNER_AXES = tuple(name for name in TP_AXES if name != "mlp")


def rms_norm(values, scale_gain):
    return (
        values * lax.rsqrt(jnp.mean(values * values, axis=-1, keepdims=True) + 1e-06) * scale_gain
    )


def short_conv(linear, tap_weights, starts):
    length = linear.shape[0]
    block_len = length // starts.shape[0]
    position = jnp.arange(length)
    restart = jnp.repeat(starts, block_len)
    summed = linear * tap_weights[0]
    for offset in range(1, tap_weights.shape[0]):
        shifted = jnp.concatenate(
            [jnp.zeros((offset, linear.shape[1]), linear.dtype), linear[: length - offset]], axis=0
        )
        usable = ((position % block_len >= offset) | (restart == 0)).astype(linear.dtype)
        summed = summed + shifted * tap_weights[offset] * usable[:, None]
    return summed


def outer_product_result(form, first, second):
    return jnp.einsum(form, first, second, precision=lax.Precision.HIGHEST)


def delta_core(queries, keys, values, betas, starts):
    length, head_count, head_width = queries.shape
    value_width = values.shape[2]
    block_count = starts.shape[0]
    block_len = length // block_count

    def blocked(array):
        return array.reshape(block_count, block_len, head_count, -1).transpose(0, 2, 1, 3)

    query_blocks = blocked(queries)
    key_blocks = blocked(keys)
    value_blocks = blocked(values)
    beta_blocks = betas.reshape(block_count, block_len, head_count).transpose(0, 2, 1)[..., None]
    position = jnp.arange(block_len)
    strict = (position[:, None] > position[None, :]).astype(queries.dtype)
    causal = (position[:, None] >= position[None, :]).astype(queries.dtype)
    weighted = key_blocks * beta_blocks
    negative = -outer_product_result("nhik,nhjk->nhij", weighted, key_blocks) * strict
    inverse = jnp.eye(block_len, dtype=queries.dtype) + negative
    power_term = negative
    for doubling in range(5):
        power_term = outer_product_result("nhij,nhjk->nhik", power_term, power_term)
        inverse = inverse + outer_product_result("nhij,nhjk->nhik", inverse, power_term)
    key_mix = outer_product_result("nhij,nhjk->nhik", inverse, weighted)
    value_mix = outer_product_result("nhij,nhjk->nhik", inverse, value_blocks * beta_blocks)
    scores = outer_product_result("nhik,nhjk->nhij", query_blocks, key_blocks) * causal

    def advance(current_state, block_items):
        (
            query_slice,
            key_slice,
            key_mixture_slice,
            value_mixture_slice,
            attention_score_slice,
            restart,
        ) = block_items
        current_state = current_state * (1 - restart).astype(current_state.dtype)
        adjusted_result = value_mixture_slice - outer_product_result(
            "pzd,pde->pze", key_mixture_slice, current_state
        )
        produced_output = outer_product_result(
            "pzd,pde->pze", query_slice, current_state
        ) + outer_product_result("lqz,lzr->lqr", attention_score_slice, adjusted_result)
        current_state = current_state + outer_product_result(
            "ixl,ixr->ilr", key_slice, adjusted_result
        )
        return (current_state, produced_output)

    initial = jnp.zeros((head_count, head_width, value_width), queries.dtype)
    final_state, produced_output = lax.scan(
        advance, initial, (query_blocks, key_blocks, key_mix, value_mix, scores, starts)
    )
    return produced_output.transpose(0, 2, 1, 3).reshape(length, head_count, value_width)


def delta_core_reset(queries, keys, values, betas, block_len):
    length, head_count, head_width = queries.shape
    block_count = length // block_len

    def blocked(array):
        return array.reshape(block_count, block_len, head_count, -1).transpose(0, 2, 1, 3)

    query_blocks = blocked(queries)
    key_blocks = blocked(keys)
    value_blocks = blocked(values)
    beta_blocks = betas.reshape(block_count, block_len, head_count).transpose(0, 2, 1)[..., None]
    position = jnp.arange(block_len)
    strict = (position[:, None] > position[None, :]).astype(queries.dtype)
    causal = (position[:, None] >= position[None, :]).astype(queries.dtype)
    weighted = key_blocks * beta_blocks
    negative = -outer_product_result("nhik,nhjk->nhij", weighted, key_blocks) * strict
    inverse = jnp.eye(block_len, dtype=queries.dtype) + negative
    power_term = negative
    for doubling in range(5):
        power_term = outer_product_result("nhij,nhjk->nhik", power_term, power_term)
        inverse = inverse + outer_product_result("nhij,nhjk->nhik", inverse, power_term)
    value_mix = outer_product_result("nhij,nhjk->nhik", inverse, value_blocks * beta_blocks)
    scores = outer_product_result("nhik,nhjk->nhij", query_blocks, key_blocks) * causal
    produced_output = outer_product_result("nhqz,nhzr->nhqr", scores, value_mix)
    return produced_output.transpose(0, 2, 1, 3).reshape(length, head_count, -1)


def mixer_core(
    query_lin, key_lin, value_lin, gate_lin, beta_lin, conv_taps, head_scale, starts, reset_len
):
    length = query_lin.shape[0]
    head_count = beta_lin.shape[1]
    head_width = query_lin.shape[1] // head_count
    queries = jax.nn.silu(short_conv(query_lin, conv_taps[0], starts)).reshape(
        length, head_count, head_width
    )
    keys = jax.nn.silu(short_conv(key_lin, conv_taps[1], starts)).reshape(
        length, head_count, head_width
    )
    values = jax.nn.silu(short_conv(value_lin, conv_taps[2], starts)).reshape(
        length, head_count, head_width
    )
    queries = (
        queries
        * lax.rsqrt(jnp.sum(queries * queries, axis=-1, keepdims=True) + 1e-06)
        * head_width ** (-0.5)
    )
    keys = keys * lax.rsqrt(jnp.sum(keys * keys, axis=-1, keepdims=True) + 1e-06)
    if reset_len:
        recurrent = delta_core_reset(queries, keys, values, jax.nn.sigmoid(beta_lin), reset_len)
    else:
        recurrent = delta_core(queries, keys, values, jax.nn.sigmoid(beta_lin), starts)
    normed = (
        recurrent
        * lax.rsqrt(jnp.mean(recurrent * recurrent, axis=-1, keepdims=True) + 1e-05)
        * head_scale
    )
    gated_out = normed * jax.nn.silu(gate_lin.reshape(length, head_count, head_width))
    return gated_out.reshape(length, head_count * head_width)


def swiglu_mix(gate_act, up_act):
    return jax.nn.silu(gate_act) * up_act


def matmul_rows(left, right):
    return jnp.dot(left, right, preferred_element_type=jnp.float32)


def left_product(first, second):
    return jnp.einsum("tf,tg->fg", first, second, preferred_element_type=jnp.float32)


def back_product(gradient, weight):
    return jnp.einsum("tg,fg->tf", gradient, weight, preferred_element_type=jnp.float32)


def tp_gather(value, axis):
    tp = lax.psum(1, TP_AXES)
    spread = jnp.broadcast_to(
        jnp.expand_dims(value, axis), value.shape[:axis] + (tp,) + value.shape[axis:]
    )
    moved = lax.all_to_all(spread, TP_AXES, axis, axis, tiled=True)
    shape = list(value.shape)
    shape[axis] *= tp
    return moved.reshape(shape)


def tp_scatter_low(value, axis):
    tp = lax.psum(1, TP_AXES)
    shape = list(value.shape)
    staged = value.astype(jnp.bfloat16).reshape(
        shape[:axis] + [tp, shape[axis] // tp] + shape[axis + 1 :]
    )
    moved = lax.all_to_all(staged, TP_AXES, axis, axis, tiled=True)
    return jnp.sum(moved.astype(jnp.float32), axis=axis)


def fsdp_gather(value, axis):
    return lax.all_gather(value, FSDP_AXES, axis=axis, tiled=True)


def fsdp_scatter_low(value, axis):
    return lax.psum_scatter(
        value.astype(jnp.bfloat16), FSDP_AXES, scatter_dimension=axis, tiled=True
    )


def exchange(value, axes, split_axis, concat_axis):
    if not axes:
        return value
    return lax.all_to_all(value, axes, split_axis, concat_axis, tiled=True)


def heads_to_rows(values, tp, fsdp, rows):
    count = values.shape[0]
    staged = values.reshape(count, 1, fsdp // tp, tp, rows)
    moved = exchange(staged, TP_AXES, 3, 1)
    return moved.reshape(count, fsdp * rows)


def rows_to_heads(values, tp, fsdp, rows):
    count = values.shape[0]
    staged = values.reshape(count, tp, fsdp // tp, 1, rows)
    moved = exchange(staged, TP_AXES, 1, 3)
    return moved.reshape(count, fsdp * rows)


def padded_rows(flat, slices, width):
    extra = -(-flat.shape[0] // (slices * width))
    extra = -(-extra // 16) * 16
    filled = jnp.pad(flat, (0, slices * extra * width - flat.shape[0]))
    return filled.reshape(slices, extra, width)


def make_on_device(tp, fsdp, inner):
    def on_device(
        tokens,
        cotangent,
        group_start,
        pad_mask,
        query_weight,
        key_weight,
        value_weight,
        gate_weight,
        beta_weight,
        out_weight,
        conv_weight,
        mixer_gain,
        head_gain,
        swiglu_gain,
        swiglu_gate,
        swiglu_up,
        swiglu_down,
    ):
        micro_count, slot, width = tokens.shape
        n_all = tp * fsdp
        rows = query_weight.shape[0]
        head_count = beta_weight.shape[1]
        heads_here = head_count // tp
        cols_here = width // tp
        group_rows = tp * rows
        position = lax.axis_index(TP_AXES)
        head_scale = head_gain.astype(jnp.float32)
        reset_len = slot if group_start.shape[1] == 1 else 0

        out_rows = fsdp_gather(out_weight, 0)
        column_owned = jnp.stack([query_weight, key_weight, value_weight, gate_weight])
        column_swapped = exchange(
            column_owned.reshape(4, rows, tp, cols_here), TP_AXES, 2, 1
        ).reshape(4, group_rows, cols_here)
        column_all = fsdp_gather(column_swapped, 1)
        query_cols, key_cols, value_cols, gate_cols = (column_all[index] for index in range(4))
        small_pack = jnp.concatenate(
            [
                conv_weight.reshape(-1),
                beta_weight.reshape(-1),
                mixer_gain.reshape(-1),
                swiglu_gain.reshape(-1),
            ]
        )
        small_size = small_pack.shape[0]
        small_all = exchange(
            jnp.broadcast_to(small_pack[None, :], (n_all, small_size)), ALL_AXES, 0, 0
        )
        conv_size = conv_weight.size
        beta_size = beta_weight.size
        conv_full = (
            small_all[:, :conv_size]
            .reshape((n_all,) + conv_weight.shape)
            .transpose(1, 2, 0, 3)
            .reshape(conv_weight.shape[0], conv_weight.shape[1], -1)
        )
        beta_full = small_all[:, conv_size : conv_size + beta_size].reshape(-1, head_count)
        gain_mixer = small_all[:, conv_size + beta_size : conv_size + beta_size + rows].reshape(-1)
        gain_swiglu = small_all[:, conv_size + beta_size + rows :].reshape(-1)
        conv_here = lax.dynamic_slice_in_dim(
            conv_full.astype(jnp.float32), position * cols_here, cols_here, axis=2
        )
        beta_here = lax.dynamic_slice_in_dim(beta_full, position * heads_here, heads_here, axis=1)

        owned_rows, hidden_half = swiglu_gate.shape
        hidden_here = hidden_half // inner
        ff_owned = jnp.stack([swiglu_gate, swiglu_up, swiglu_down.T]).reshape(
            3, owned_rows, inner, hidden_here
        )
        lanes = hidden_here // 128 if hidden_here % 128 == 0 else 0
        first = (lanes + 1) // 2 * 128 if lanes > 1 else hidden_here // 2
        bounds = ((0, first), (first, hidden_here - first))
        ff_chunks = []
        for offset, size in bounds:
            swapped = exchange(ff_owned[..., offset : offset + size], INNER_AXES, 2, 1)
            ff_chunks.append(fsdp_gather(swapped.reshape(3, inner * owned_rows, size), 1))

        inputs = tokens.astype(jnp.float32).reshape(micro_count * slot, width)
        normed, norm_back = jax.vjp(rms_norm, inputs, gain_mixer.astype(jnp.float32))
        normed_low = normed.astype(jnp.bfloat16)
        group_tokens = micro_count * slot * tp
        normed_group = tp_gather(normed_low.reshape(micro_count, slot, width), 1).reshape(
            group_tokens, width
        )
        starts = tp_gather(group_start, 1).reshape(-1)

        query_lin = matmul_rows(normed_group, query_cols)
        key_lin = matmul_rows(normed_group, key_cols)
        value_lin = matmul_rows(normed_group, value_cols)
        gate_lin = matmul_rows(normed_group, gate_cols)
        beta_lin = matmul_rows(normed_group, beta_here)

        def core_at(query_in, key_in, value_in, gate_in, beta_in, conv_in, head_in):
            return mixer_core(
                query_in, key_in, value_in, gate_in, beta_in, conv_in, head_in, starts, reset_len
            )

        gated_out, core_back = jax.vjp(
            core_at, query_lin, key_lin, value_lin, gate_lin, beta_lin, conv_here, head_scale
        )
        gated_low = gated_out.astype(jnp.bfloat16)
        gated_rows = heads_to_rows(gated_low, tp, fsdp, rows)
        mixed_partial = matmul_rows(gated_rows, out_rows)
        residual = inputs + tp_scatter_low(
            mixed_partial.reshape(micro_count, slot * tp, width), 1
        ).reshape(micro_count * slot, width)

        inner_norm, inner_norm_back = jax.vjp(rms_norm, residual, gain_swiglu.astype(jnp.float32))
        inner_low = inner_norm.astype(jnp.bfloat16)
        inner_group = tp_gather(inner_low.reshape(micro_count, slot, width), 1).reshape(
            group_tokens, width
        )
        out_back = cotangent.astype(jnp.float32) * pad_mask.astype(jnp.float32)[:, :, None]
        out_back_low = out_back.astype(jnp.bfloat16)
        upstream_group = tp_gather(out_back_low, 1).reshape(group_tokens, width)
        partial_rows = None
        inner_part = None
        ff_reduced = []
        for index, chunk_weights in enumerate(ff_chunks):
            if index > 0:
                sums_low, chunk_weights = lax.optimization_barrier((sums_low, chunk_weights))
            gate_piece, up_piece, down_piece_t = chunk_weights[0], chunk_weights[1], chunk_weights[2]
            gate_act = matmul_rows(inner_group, gate_piece)
            up_act = matmul_rows(inner_group, up_piece)
            hidden, hidden_back = jax.vjp(swiglu_mix, gate_act, up_act)
            hidden_low = hidden.astype(jnp.bfloat16)
            piece_rows = back_product(hidden_low, down_piece_t)
            partial_rows = piece_rows if partial_rows is None else partial_rows + piece_rows
            gate_back, up_back = hidden_back(matmul_rows(upstream_group, down_piece_t))
            gate_back_low = gate_back.astype(jnp.bfloat16)
            up_back_low = up_back.astype(jnp.bfloat16)
            piece_part = back_product(gate_back_low, gate_piece) + back_product(up_back_low, up_piece)
            inner_part = piece_part if inner_part is None else inner_part + piece_part
            sums_low = jnp.stack(
                [
                    left_product(inner_group, gate_back_low),
                    left_product(inner_group, up_back_low),
                    left_product(upstream_group, hidden_low),
                ]
            ).astype(jnp.bfloat16)
            ff_reduced.append(fsdp_scatter_low(sums_low, 1))
        branch_rows = tp_scatter_low(partial_rows.reshape(micro_count, slot * tp, width), 1)
        block_out = (residual.reshape(micro_count, slot, width) + branch_rows).astype(jnp.bfloat16)
        inner_back = tp_scatter_low(inner_part.reshape(micro_count, slot * tp, width), 1)
        block_out, inner_back = lax.optimization_barrier((block_out, inner_back))

        residual_part, swiglu_gain_term = inner_norm_back(
            inner_back.reshape(micro_count * slot, width)
        )
        residual_back = out_back.reshape(micro_count * slot, width) + residual_part
        mixed_back = residual_back.astype(jnp.bfloat16)
        mixed_group = tp_gather(mixed_back.reshape(micro_count, slot, width), 1).reshape(
            group_tokens, width
        )
        gated_back_rows = back_product(mixed_group, out_rows)
        gated_back = rows_to_heads(gated_back_rows, tp, fsdp, rows)
        query_back, key_back, value_back, gate_lin_back, beta_back, conv_term, head_term = (
            core_back(gated_back)
        )
        query_low = query_back.astype(jnp.bfloat16)
        key_low = key_back.astype(jnp.bfloat16)
        value_low = value_back.astype(jnp.bfloat16)
        gate_low = gate_lin_back.astype(jnp.bfloat16)
        beta_low = beta_back.astype(jnp.bfloat16)
        mixer_sums = jnp.stack(
            [
                left_product(normed_group, query_low),
                left_product(normed_group, key_low),
                left_product(normed_group, value_low),
                left_product(normed_group, gate_low),
                left_product(gated_rows, mixed_group).reshape(width, cols_here),
            ]
        )
        ff_reduced, mixer_sums = lax.optimization_barrier((ff_reduced, mixer_sums))
        mixer_reduced = fsdp_scatter_low(mixer_sums, 1)
        ff_back = jnp.concatenate(
            [
                exchange(
                    piece.reshape(3, inner, owned_rows, 1, size), INNER_AXES, 1, 3
                ).reshape(3, owned_rows, inner, size)
                for piece, (offset, size) in zip(ff_reduced, bounds)
            ],
            axis=3,
        ).reshape(3, owned_rows, hidden_half).astype(jnp.float32)
        swiglu_gate_grad = ff_back[0]
        swiglu_up_grad = ff_back[1]
        swiglu_down_grad = ff_back[2].T

        normed_part = (
            back_product(query_low, query_cols)
            + back_product(key_low, key_cols)
            + back_product(value_low, value_cols)
            + back_product(gate_low, gate_cols)
            + back_product(beta_low, beta_here)
        )
        normed_back = tp_scatter_low(normed_part.reshape(micro_count, slot * tp, width), 1)
        input_part, mixer_gain_term = norm_back(normed_back.reshape(micro_count * slot, width))
        tokens_grad = (residual_back + input_part).reshape(micro_count, slot, width)

        beta_sum = left_product(normed_group, beta_low)
        beta_wide = lax.dynamic_update_slice_in_dim(
            jnp.zeros((width, head_count), jnp.float32), beta_sum, position * heads_here, axis=1
        )
        conv_wide = lax.dynamic_update_slice_in_dim(
            jnp.zeros(conv_full.shape, jnp.float32), conv_term, position * cols_here, axis=2
        )
        taps = conv_wide.shape[0] * conv_wide.shape[1]
        small_terms = jnp.concatenate(
            [
                conv_wide.reshape(taps, n_all, -1).transpose(1, 0, 2).reshape(n_all, -1),
                beta_wide.reshape(n_all, -1),
                mixer_gain_term.reshape(n_all, -1),
                swiglu_gain_term.reshape(n_all, -1),
                jnp.broadcast_to(head_term[None, :], (n_all, head_term.shape[0])),
            ],
            axis=1,
        )
        small_width = small_terms.shape[1]
        small_out = jnp.sum(exchange(small_terms, ALL_AXES, 0, 0), axis=0)
        column_back = exchange(
            mixer_reduced[:4].reshape(4, tp, rows, 1, cols_here), TP_AXES, 1, 3
        ).reshape(4, rows, width).astype(jnp.float32)
        query_grad, key_grad, value_grad, gate_grad = (column_back[index] for index in range(4))
        out_grad = mixer_reduced[4].reshape(rows, width).astype(jnp.float32)
        conv_grad = small_out[:conv_size].reshape(conv_weight.shape)
        beta_grad = small_out[conv_size : conv_size + beta_size].reshape(beta_weight.shape)
        mixer_gain_grad = small_out[conv_size + beta_size : conv_size + beta_size + rows]
        swiglu_gain_grad = small_out[conv_size + beta_size + rows : conv_size + beta_size + 2 * rows]
        head_total = small_out[conv_size + beta_size + 2 * rows :]
        return (
            block_out,
            tokens_grad,
            query_grad,
            key_grad,
            value_grad,
            gate_grad,
            beta_grad,
            out_grad,
            conv_grad,
            mixer_gain_grad,
            head_total,
            swiglu_gain_grad,
            swiglu_gate_grad,
            swiglu_up_grad,
            swiglu_down_grad,
        )

    return on_device


def solution(mesh):
    n_dp = mesh.shape["dp"]
    n_mlp = mesh.shape["mlp"]
    devices = np.asarray(mesh.devices).reshape(n_dp // 2, 2, n_mlp)
    split_mesh = Mesh(devices, ALL_AXES)
    sizes = dict(zip(ALL_AXES, devices.shape))
    tp = int(np.prod([sizes[name] for name in TP_AXES]))
    fsdp = int(np.prod([sizes[name] for name in FSDP_AXES]))
    inner = int(np.prod([sizes[name] for name in INNER_AXES]))
    rows_axes = ALL_AXES
    swiglu_rows = ("dq", "core")
    placed = (
        P(None, rows_axes, None),
        P(None, rows_axes, None),
        P(None, rows_axes),
        P(None, rows_axes),
        P(rows_axes, None),
        P(rows_axes, None),
        P(rows_axes, None),
        P(rows_axes, None),
        P(rows_axes, None),
        P(rows_axes, None),
        P(None, None, rows_axes),
        P(rows_axes),
        P(),
        P(rows_axes),
        P(swiglu_rows, "mlp"),
        P(swiglu_rows, "mlp"),
        P("mlp", swiglu_rows),
    )
    return jax.shard_map(
        make_on_device(tp, fsdp, inner),
        mesh=split_mesh,
        in_specs=placed,
        out_specs=(
            P(None, rows_axes, None),
            P(None, rows_axes, None),
            P(rows_axes, None),
            P(rows_axes, None),
            P(rows_axes, None),
            P(rows_axes, None),
            P(rows_axes, None),
            P(rows_axes, None),
            P(None, None, rows_axes),
            P(rows_axes),
            P(),
            P(rows_axes),
            P(swiglu_rows, "mlp"),
            P(swiglu_rows, "mlp"),
            P("mlp", swiglu_rows),
        ),
        check_vma=False,
    )
```

```python
import jax
import jax.numpy as jnp
import numpy as np
from jax import lax
from jax.sharding import Mesh
from jax.sharding import PartitionSpec as P

TP_AXES = ("core", "mlp")
ALL_AXES = ("dq", "core", "mlp")
FSDP_AXES = tuple(name for name in ALL_AXES if name not in TP_AXES)
INNER_AXES = tuple(name for name in TP_AXES if name != "mlp")


def rms_norm(values, scale_gain):
    return (
        values * lax.rsqrt(jnp.mean(values * values, axis=-1, keepdims=True) + 1e-06) * scale_gain
    )


def short_conv(linear, tap_weights, starts):
    length = linear.shape[0]
    block_len = length // starts.shape[0]
    position = jnp.arange(length)
    restart = jnp.repeat(starts, block_len)
    summed = linear * tap_weights[0]
    for offset in range(1, tap_weights.shape[0]):
        shifted = jnp.concatenate(
            [jnp.zeros((offset, linear.shape[1]), linear.dtype), linear[: length - offset]], axis=0
        )
        usable = ((position % block_len >= offset) | (restart == 0)).astype(linear.dtype)
        summed = summed + shifted * tap_weights[offset] * usable[:, None]
    return summed


def outer_product_result(form, first, second):
    return jnp.einsum(form, first, second, precision=lax.Precision.HIGHEST)


def delta_core(queries, keys, values, betas, starts):
    length, head_count, head_width = queries.shape
    value_width = values.shape[2]
    block_count = starts.shape[0]
    block_len = length // block_count

    def blocked(array):
        return array.reshape(block_count, block_len, head_count, -1).transpose(0, 2, 1, 3)

    query_blocks = blocked(queries)
    key_blocks = blocked(keys)
    value_blocks = blocked(values)
    beta_blocks = betas.reshape(block_count, block_len, head_count).transpose(0, 2, 1)[..., None]
    position = jnp.arange(block_len)
    strict = (position[:, None] > position[None, :]).astype(queries.dtype)
    causal = (position[:, None] >= position[None, :]).astype(queries.dtype)
    weighted = key_blocks * beta_blocks
    negative = -outer_product_result("nhik,nhjk->nhij", weighted, key_blocks) * strict
    inverse = jnp.eye(block_len, dtype=queries.dtype) + negative
    power_term = negative
    for doubling in range(5):
        power_term = outer_product_result("nhij,nhjk->nhik", power_term, power_term)
        inverse = inverse + outer_product_result("nhij,nhjk->nhik", inverse, power_term)
    key_mix = outer_product_result("nhij,nhjk->nhik", inverse, weighted)
    value_mix = outer_product_result("nhij,nhjk->nhik", inverse, value_blocks * beta_blocks)
    scores = outer_product_result("nhik,nhjk->nhij", query_blocks, key_blocks) * causal

    def advance(current_state, block_items):
        (
            query_slice,
            key_slice,
            key_mixture_slice,
            value_mixture_slice,
            attention_score_slice,
            restart,
        ) = block_items
        current_state = current_state * (1 - restart).astype(current_state.dtype)
        adjusted_result = value_mixture_slice - outer_product_result(
            "pzd,pde->pze", key_mixture_slice, current_state
        )
        produced_output = outer_product_result(
            "pzd,pde->pze", query_slice, current_state
        ) + outer_product_result("lqz,lzr->lqr", attention_score_slice, adjusted_result)
        current_state = current_state + outer_product_result(
            "ixl,ixr->ilr", key_slice, adjusted_result
        )
        return (current_state, produced_output)

    initial = jnp.zeros((head_count, head_width, value_width), queries.dtype)
    final_state, produced_output = lax.scan(
        advance, initial, (query_blocks, key_blocks, key_mix, value_mix, scores, starts)
    )
    return produced_output.transpose(0, 2, 1, 3).reshape(length, head_count, value_width)


def delta_core_reset(queries, keys, values, betas, block_len):
    length, head_count, head_width = queries.shape
    block_count = length // block_len

    def blocked(array):
        return array.reshape(block_count, block_len, head_count, -1).transpose(0, 2, 1, 3)

    query_blocks = blocked(queries)
    key_blocks = blocked(keys)
    value_blocks = blocked(values)
    beta_blocks = betas.reshape(block_count, block_len, head_count).transpose(0, 2, 1)[..., None]
    position = jnp.arange(block_len)
    strict = (position[:, None] > position[None, :]).astype(queries.dtype)
    causal = (position[:, None] >= position[None, :]).astype(queries.dtype)
    weighted = key_blocks * beta_blocks
    negative = -outer_product_result("nhik,nhjk->nhij", weighted, key_blocks) * strict
    inverse = jnp.eye(block_len, dtype=queries.dtype) + negative
    power_term = negative
    for doubling in range(5):
        power_term = outer_product_result("nhij,nhjk->nhik", power_term, power_term)
        inverse = inverse + outer_product_result("nhij,nhjk->nhik", inverse, power_term)
    value_mix = outer_product_result("nhij,nhjk->nhik", inverse, value_blocks * beta_blocks)
    scores = outer_product_result("nhik,nhjk->nhij", query_blocks, key_blocks) * causal
    produced_output = outer_product_result("nhqz,nhzr->nhqr", scores, value_mix)
    return produced_output.transpose(0, 2, 1, 3).reshape(length, head_count, -1)


def mixer_core(
    query_lin, key_lin, value_lin, gate_lin, beta_lin, conv_taps, head_scale, starts, reset_len
):
    length = query_lin.shape[0]
    head_count = beta_lin.shape[1]
    head_width = query_lin.shape[1] // head_count
    queries = jax.nn.silu(short_conv(query_lin, conv_taps[0], starts)).reshape(
        length, head_count, head_width
    )
    keys = jax.nn.silu(short_conv(key_lin, conv_taps[1], starts)).reshape(
        length, head_count, head_width
    )
    values = jax.nn.silu(short_conv(value_lin, conv_taps[2], starts)).reshape(
        length, head_count, head_width
    )
    queries = (
        queries
        * lax.rsqrt(jnp.sum(queries * queries, axis=-1, keepdims=True) + 1e-06)
        * head_width ** (-0.5)
    )
    keys = keys * lax.rsqrt(jnp.sum(keys * keys, axis=-1, keepdims=True) + 1e-06)
    if reset_len:
        recurrent = delta_core_reset(queries, keys, values, jax.nn.sigmoid(beta_lin), reset_len)
    else:
        recurrent = delta_core(queries, keys, values, jax.nn.sigmoid(beta_lin), starts)
    normed = (
        recurrent
        * lax.rsqrt(jnp.mean(recurrent * recurrent, axis=-1, keepdims=True) + 1e-05)
        * head_scale
    )
    gated_out = normed * jax.nn.silu(gate_lin.reshape(length, head_count, head_width))
    return gated_out.reshape(length, head_count * head_width)


def swiglu_mix(gate_act, up_act):
    return jax.nn.silu(gate_act) * up_act


def matmul_rows(left, right):
    return jnp.dot(left, right, preferred_element_type=jnp.float32)


def left_product(first, second):
    return jnp.einsum("tf,tg->fg", first, second, preferred_element_type=jnp.float32)


def back_product(gradient, weight):
    return jnp.einsum("tg,fg->tf", gradient, weight, preferred_element_type=jnp.float32)


def tp_gather(value, axis):
    tp = lax.psum(1, TP_AXES)
    spread = jnp.broadcast_to(
        jnp.expand_dims(value, axis), value.shape[:axis] + (tp,) + value.shape[axis:]
    )
    moved = lax.all_to_all(spread, TP_AXES, axis, axis, tiled=True)
    shape = list(value.shape)
    shape[axis] *= tp
    return moved.reshape(shape)


def tp_scatter_low(value, axis):
    tp = lax.psum(1, TP_AXES)
    shape = list(value.shape)
    staged = value.astype(jnp.bfloat16).reshape(
        shape[:axis] + [tp, shape[axis] // tp] + shape[axis + 1 :]
    )
    moved = lax.all_to_all(staged, TP_AXES, axis, axis, tiled=True)
    return jnp.sum(moved.astype(jnp.float32), axis=axis)


def fsdp_gather(value, axis):
    return lax.all_gather(value, FSDP_AXES, axis=axis, tiled=True)


def fsdp_scatter_low(value, axis):
    return lax.psum_scatter(
        value.astype(jnp.bfloat16), FSDP_AXES, scatter_dimension=axis, tiled=True
    )


def exchange(value, axes, split_axis, concat_axis):
    if not axes:
        return value
    return lax.all_to_all(value, axes, split_axis, concat_axis, tiled=True)


def heads_to_rows(values, tp, fsdp, rows):
    count = values.shape[0]
    staged = values.reshape(count, 1, fsdp // tp, tp, rows)
    moved = exchange(staged, TP_AXES, 3, 1)
    return moved.reshape(count, fsdp * rows)


def rows_to_heads(values, tp, fsdp, rows):
    count = values.shape[0]
    staged = values.reshape(count, tp, fsdp // tp, 1, rows)
    moved = exchange(staged, TP_AXES, 1, 3)
    return moved.reshape(count, fsdp * rows)


def padded_rows(flat, slices, width):
    extra = -(-flat.shape[0] // (slices * width))
    extra = -(-extra // 16) * 16
    filled = jnp.pad(flat, (0, slices * extra * width - flat.shape[0]))
    return filled.reshape(slices, extra, width)


def make_on_device(tp, fsdp, inner):
    def on_device(
        tokens,
        cotangent,
        group_start,
        pad_mask,
        query_weight,
        key_weight,
        value_weight,
        gate_weight,
        beta_weight,
        out_weight,
        conv_weight,
        mixer_gain,
        head_gain,
        swiglu_gain,
        swiglu_gate,
        swiglu_up,
        swiglu_down,
    ):
        micro_count, slot, width = tokens.shape
        n_all = tp * fsdp
        rows = query_weight.shape[0]
        head_count = beta_weight.shape[1]
        heads_here = head_count // tp
        cols_here = width // tp
        group_rows = tp * rows
        position = lax.axis_index(TP_AXES)
        head_scale = head_gain.astype(jnp.float32)
        reset_len = slot if group_start.shape[1] == 1 else 0

        column_owned = jnp.stack([query_weight, key_weight, value_weight, gate_weight])
        column_swapped = exchange(
            column_owned.reshape(4, rows, tp, cols_here), TP_AXES, 2, 1
        ).reshape(4, group_rows, cols_here)
        mixer_stack = jnp.concatenate(
            [column_swapped, out_weight.reshape(1, group_rows, cols_here)], axis=0
        )
        weight_all = fsdp_gather(mixer_stack, 1)
        query_cols, key_cols, value_cols, gate_cols = (weight_all[index] for index in range(4))
        out_rows = weight_all[4].reshape(fsdp * rows, width)
        small_pack = jnp.concatenate(
            [
                conv_weight.reshape(-1),
                beta_weight.reshape(-1),
                mixer_gain.reshape(-1),
                swiglu_gain.reshape(-1),
            ]
        )
        small_size = small_pack.shape[0]
        small_all = exchange(
            jnp.broadcast_to(small_pack[None, :], (n_all, small_size)), ALL_AXES, 0, 0
        )
        conv_size = conv_weight.size
        beta_size = beta_weight.size
        conv_full = (
            small_all[:, :conv_size]
            .reshape((n_all,) + conv_weight.shape)
            .transpose(1, 2, 0, 3)
            .reshape(conv_weight.shape[0], conv_weight.shape[1], -1)
        )
        beta_full = small_all[:, conv_size : conv_size + beta_size].reshape(-1, head_count)
        gain_mixer = small_all[:, conv_size + beta_size : conv_size + beta_size + rows].reshape(-1)
        gain_swiglu = small_all[:, conv_size + beta_size + rows :].reshape(-1)
        conv_here = lax.dynamic_slice_in_dim(
            conv_full.astype(jnp.float32), position * cols_here, cols_here, axis=2
        )
        beta_here = lax.dynamic_slice_in_dim(beta_full, position * heads_here, heads_here, axis=1)

        owned_rows, hidden_half = swiglu_gate.shape
        hidden_here = hidden_half // inner
        ff_owned = jnp.stack([swiglu_gate, swiglu_up, swiglu_down.T]).reshape(
            3, owned_rows, inner, hidden_here
        )
        lanes = hidden_here // 128 if hidden_here % 128 == 0 else 0
        first = (lanes + 1) // 2 * 128 if lanes > 1 else hidden_here // 2
        bounds = ((0, first), (first, hidden_here - first))
        ff_chunks = []
        for offset, size in bounds:
            swapped = exchange(ff_owned[..., offset : offset + size], INNER_AXES, 2, 1)
            ff_chunks.append(fsdp_gather(swapped.reshape(3, inner * owned_rows, size), 1))

        inputs = tokens.astype(jnp.float32).reshape(micro_count * slot, width)
        normed, norm_back = jax.vjp(rms_norm, inputs, gain_mixer.astype(jnp.float32))
        normed_low = normed.astype(jnp.bfloat16)
        group_tokens = micro_count * slot * tp
        normed_group = tp_gather(normed_low.reshape(micro_count, slot, width), 1).reshape(
            group_tokens, width
        )
        starts = tp_gather(group_start, 1).reshape(-1)

        query_lin = matmul_rows(normed_group, query_cols)
        key_lin = matmul_rows(normed_group, key_cols)
        value_lin = matmul_rows(normed_group, value_cols)
        gate_lin = matmul_rows(normed_group, gate_cols)
        beta_lin = matmul_rows(normed_group, beta_here)

        def core_at(query_in, key_in, value_in, gate_in, beta_in, conv_in, head_in):
            return mixer_core(
                query_in, key_in, value_in, gate_in, beta_in, conv_in, head_in, starts, reset_len
            )

        gated_out, core_back = jax.vjp(
            core_at, query_lin, key_lin, value_lin, gate_lin, beta_lin, conv_here, head_scale
        )
        gated_low = gated_out.astype(jnp.bfloat16)
        gated_rows = heads_to_rows(gated_low, tp, fsdp, rows)
        mixed_partial = matmul_rows(gated_rows, out_rows)
        residual = inputs + tp_scatter_low(
            mixed_partial.reshape(micro_count, slot * tp, width), 1
        ).reshape(micro_count * slot, width)

        inner_norm, inner_norm_back = jax.vjp(rms_norm, residual, gain_swiglu.astype(jnp.float32))
        inner_low = inner_norm.astype(jnp.bfloat16)
        inner_group = tp_gather(inner_low.reshape(micro_count, slot, width), 1).reshape(
            group_tokens, width
        )
        out_back = cotangent.astype(jnp.float32) * pad_mask.astype(jnp.float32)[:, :, None]
        out_back_low = out_back.astype(jnp.bfloat16)
        upstream_group = tp_gather(out_back_low, 1).reshape(group_tokens, width)
        partial_rows = None
        inner_part = None
        ff_reduced = []
        for index, chunk_weights in enumerate(ff_chunks):
            if index > 0:
                sums_low, chunk_weights = lax.optimization_barrier((sums_low, chunk_weights))
            gate_piece, up_piece, down_piece_t = chunk_weights[0], chunk_weights[1], chunk_weights[2]
            gate_act = matmul_rows(inner_group, gate_piece)
            up_act = matmul_rows(inner_group, up_piece)
            hidden, hidden_back = jax.vjp(swiglu_mix, gate_act, up_act)
            hidden_low = hidden.astype(jnp.bfloat16)
            piece_rows = back_product(hidden_low, down_piece_t)
            partial_rows = piece_rows if partial_rows is None else partial_rows + piece_rows
            gate_back, up_back = hidden_back(matmul_rows(upstream_group, down_piece_t))
            gate_back_low = gate_back.astype(jnp.bfloat16)
            up_back_low = up_back.astype(jnp.bfloat16)
            piece_part = back_product(gate_back_low, gate_piece) + back_product(up_back_low, up_piece)
            inner_part = piece_part if inner_part is None else inner_part + piece_part
            sums_low = jnp.stack(
                [
                    left_product(inner_group, gate_back_low),
                    left_product(inner_group, up_back_low),
                    left_product(upstream_group, hidden_low),
                ]
            ).astype(jnp.bfloat16)
            ff_reduced.append(fsdp_scatter_low(sums_low, 1))
        branch_rows = tp_scatter_low(partial_rows.reshape(micro_count, slot * tp, width), 1)
        block_out = (residual.reshape(micro_count, slot, width) + branch_rows).astype(jnp.bfloat16)
        inner_back = tp_scatter_low(inner_part.reshape(micro_count, slot * tp, width), 1)
        block_out, inner_back = lax.optimization_barrier((block_out, inner_back))

        residual_part, swiglu_gain_term = inner_norm_back(
            inner_back.reshape(micro_count * slot, width)
        )
        residual_back = out_back.reshape(micro_count * slot, width) + residual_part
        mixed_back = residual_back.astype(jnp.bfloat16)
        mixed_group = tp_gather(mixed_back.reshape(micro_count, slot, width), 1).reshape(
            group_tokens, width
        )
        gated_back_rows = back_product(mixed_group, out_rows)
        gated_back = rows_to_heads(gated_back_rows, tp, fsdp, rows)
        query_back, key_back, value_back, gate_lin_back, beta_back, conv_term, head_term = (
            core_back(gated_back)
        )
        query_low = query_back.astype(jnp.bfloat16)
        key_low = key_back.astype(jnp.bfloat16)
        value_low = value_back.astype(jnp.bfloat16)
        gate_low = gate_lin_back.astype(jnp.bfloat16)
        beta_low = beta_back.astype(jnp.bfloat16)
        mixer_sums = jnp.stack(
            [
                left_product(normed_group, query_low),
                left_product(normed_group, key_low),
                left_product(normed_group, value_low),
                left_product(normed_group, gate_low),
                left_product(gated_rows, mixed_group).reshape(width, cols_here),
            ]
        )
        ff_reduced, mixer_sums = lax.optimization_barrier((ff_reduced, mixer_sums))
        mixer_reduced = fsdp_scatter_low(mixer_sums, 1)
        ff_back = jnp.concatenate(
            [
                exchange(
                    piece.reshape(3, inner, owned_rows, 1, size), INNER_AXES, 1, 3
                ).reshape(3, owned_rows, inner, size)
                for piece, (offset, size) in zip(ff_reduced, bounds)
            ],
            axis=3,
        ).reshape(3, owned_rows, hidden_half).astype(jnp.float32)
        swiglu_gate_grad = ff_back[0]
        swiglu_up_grad = ff_back[1]
        swiglu_down_grad = ff_back[2].T

        normed_part = (
            back_product(query_low, query_cols)
            + back_product(key_low, key_cols)
            + back_product(value_low, value_cols)
            + back_product(gate_low, gate_cols)
            + back_product(beta_low, beta_here)
        )
        normed_back = tp_scatter_low(normed_part.reshape(micro_count, slot * tp, width), 1)
        input_part, mixer_gain_term = norm_back(normed_back.reshape(micro_count * slot, width))
        tokens_grad = (residual_back + input_part).reshape(micro_count, slot, width)

        beta_sum = left_product(normed_group, beta_low)
        beta_wide = lax.dynamic_update_slice_in_dim(
            jnp.zeros((width, head_count), jnp.float32), beta_sum, position * heads_here, axis=1
        )
        conv_wide = lax.dynamic_update_slice_in_dim(
            jnp.zeros(conv_full.shape, jnp.float32), conv_term, position * cols_here, axis=2
        )
        taps = conv_wide.shape[0] * conv_wide.shape[1]
        small_terms = jnp.concatenate(
            [
                conv_wide.reshape(taps, n_all, -1).transpose(1, 0, 2).reshape(n_all, -1),
                beta_wide.reshape(n_all, -1),
                mixer_gain_term.reshape(n_all, -1),
                swiglu_gain_term.reshape(n_all, -1),
                jnp.broadcast_to(head_term[None, :], (n_all, head_term.shape[0])),
            ],
            axis=1,
        )
        small_width = small_terms.shape[1]
        small_out = jnp.sum(exchange(small_terms, ALL_AXES, 0, 0), axis=0)
        column_back = exchange(
            mixer_reduced[:4].reshape(4, tp, rows, 1, cols_here), TP_AXES, 1, 3
        ).reshape(4, rows, width).astype(jnp.float32)
        query_grad, key_grad, value_grad, gate_grad = (column_back[index] for index in range(4))
        out_grad = mixer_reduced[4].reshape(rows, width).astype(jnp.float32)
        conv_grad = small_out[:conv_size].reshape(conv_weight.shape)
        beta_grad = small_out[conv_size : conv_size + beta_size].reshape(beta_weight.shape)
        mixer_gain_grad = small_out[conv_size + beta_size : conv_size + beta_size + rows]
        swiglu_gain_grad = small_out[conv_size + beta_size + rows : conv_size + beta_size + 2 * rows]
        head_total = small_out[conv_size + beta_size + 2 * rows :]
        return (
            block_out,
            tokens_grad,
            query_grad,
            key_grad,
            value_grad,
            gate_grad,
            beta_grad,
            out_grad,
            conv_grad,
            mixer_gain_grad,
            head_total,
            swiglu_gain_grad,
            swiglu_gate_grad,
            swiglu_up_grad,
            swiglu_down_grad,
        )

    return on_device


def solution(mesh):
    n_dp = mesh.shape["dp"]
    n_mlp = mesh.shape["mlp"]
    devices = np.asarray(mesh.devices).reshape(n_dp // 2, 2, n_mlp)
    split_mesh = Mesh(devices, ALL_AXES)
    sizes = dict(zip(ALL_AXES, devices.shape))
    tp = int(np.prod([sizes[name] for name in TP_AXES]))
    fsdp = int(np.prod([sizes[name] for name in FSDP_AXES]))
    inner = int(np.prod([sizes[name] for name in INNER_AXES]))
    rows_axes = ALL_AXES
    swiglu_rows = ("dq", "core")
    placed = (
        P(None, rows_axes, None),
        P(None, rows_axes, None),
        P(None, rows_axes),
        P(None, rows_axes),
        P(rows_axes, None),
        P(rows_axes, None),
        P(rows_axes, None),
        P(rows_axes, None),
        P(rows_axes, None),
        P(rows_axes, None),
        P(None, None, rows_axes),
        P(rows_axes),
        P(),
        P(rows_axes),
        P(swiglu_rows, "mlp"),
        P(swiglu_rows, "mlp"),
        P("mlp", swiglu_rows),
    )
    return jax.shard_map(
        make_on_device(tp, fsdp, inner),
        mesh=split_mesh,
        in_specs=placed,
        out_specs=(
            P(None, rows_axes, None),
            P(None, rows_axes, None),
            P(rows_axes, None),
            P(rows_axes, None),
            P(rows_axes, None),
            P(rows_axes, None),
            P(rows_axes, None),
            P(rows_axes, None),
            P(None, None, rows_axes),
            P(rows_axes),
            P(),
            P(rows_axes),
            P(swiglu_rows, "mlp"),
            P(swiglu_rows, "mlp"),
            P("mlp", swiglu_rows),
        ),
        check_vma=False,
    )
```

```python
import jax
import jax.numpy as jnp
import numpy as np
from jax import lax
from jax.sharding import Mesh
from jax.sharding import PartitionSpec as P

TP_AXES = ("core", "mlp")
ALL_AXES = ("dq", "core", "mlp")
FSDP_AXES = tuple(name for name in ALL_AXES if name not in TP_AXES)
INNER_AXES = tuple(name for name in TP_AXES if name != "mlp")


def rms_norm(values, scale_gain):
    return (
        values * lax.rsqrt(jnp.mean(values * values, axis=-1, keepdims=True) + 1e-06) * scale_gain
    )


def short_conv(linear, tap_weights, starts):
    length = linear.shape[0]
    block_len = length // starts.shape[0]
    position = jnp.arange(length)
    restart = jnp.repeat(starts, block_len)
    summed = linear * tap_weights[0]
    for offset in range(1, tap_weights.shape[0]):
        shifted = jnp.concatenate(
            [jnp.zeros((offset, linear.shape[1]), linear.dtype), linear[: length - offset]], axis=0
        )
        usable = ((position % block_len >= offset) | (restart == 0)).astype(linear.dtype)
        summed = summed + shifted * tap_weights[offset] * usable[:, None]
    return summed


def outer_product_result(form, first, second):
    return jnp.einsum(form, first, second, precision=lax.Precision.HIGHEST)


def delta_core(queries, keys, values, betas, starts):
    length, head_count, head_width = queries.shape
    value_width = values.shape[2]
    block_count = starts.shape[0]
    block_len = length // block_count

    def blocked(array):
        return array.reshape(block_count, block_len, head_count, -1).transpose(0, 2, 1, 3)

    query_blocks = blocked(queries)
    key_blocks = blocked(keys)
    value_blocks = blocked(values)
    beta_blocks = betas.reshape(block_count, block_len, head_count).transpose(0, 2, 1)[..., None]
    position = jnp.arange(block_len)
    strict = (position[:, None] > position[None, :]).astype(queries.dtype)
    causal = (position[:, None] >= position[None, :]).astype(queries.dtype)
    weighted = key_blocks * beta_blocks
    negative = -outer_product_result("nhik,nhjk->nhij", weighted, key_blocks) * strict
    inverse = jnp.eye(block_len, dtype=queries.dtype) + negative
    power_term = negative
    for doubling in range(5):
        power_term = outer_product_result("nhij,nhjk->nhik", power_term, power_term)
        inverse = inverse + outer_product_result("nhij,nhjk->nhik", inverse, power_term)
    key_mix = outer_product_result("nhij,nhjk->nhik", inverse, weighted)
    value_mix = outer_product_result("nhij,nhjk->nhik", inverse, value_blocks * beta_blocks)
    scores = outer_product_result("nhik,nhjk->nhij", query_blocks, key_blocks) * causal

    def advance(current_state, block_items):
        (
            query_slice,
            key_slice,
            key_mixture_slice,
            value_mixture_slice,
            attention_score_slice,
            restart,
        ) = block_items
        current_state = current_state * (1 - restart).astype(current_state.dtype)
        adjusted_result = value_mixture_slice - outer_product_result(
            "pzd,pde->pze", key_mixture_slice, current_state
        )
        produced_output = outer_product_result(
            "pzd,pde->pze", query_slice, current_state
        ) + outer_product_result("lqz,lzr->lqr", attention_score_slice, adjusted_result)
        current_state = current_state + outer_product_result(
            "ixl,ixr->ilr", key_slice, adjusted_result
        )
        return (current_state, produced_output)

    initial = jnp.zeros((head_count, head_width, value_width), queries.dtype)
    final_state, produced_output = lax.scan(
        advance, initial, (query_blocks, key_blocks, key_mix, value_mix, scores, starts)
    )
    return produced_output.transpose(0, 2, 1, 3).reshape(length, head_count, value_width)


def delta_core_reset(queries, keys, values, betas, block_len):
    length, head_count, head_width = queries.shape
    block_count = length // block_len

    def blocked(array):
        return array.reshape(block_count, block_len, head_count, -1).transpose(0, 2, 1, 3)

    query_blocks = blocked(queries)
    key_blocks = blocked(keys)
    value_blocks = blocked(values)
    beta_blocks = betas.reshape(block_count, block_len, head_count).transpose(0, 2, 1)[..., None]
    position = jnp.arange(block_len)
    strict = (position[:, None] > position[None, :]).astype(queries.dtype)
    causal = (position[:, None] >= position[None, :]).astype(queries.dtype)
    weighted = key_blocks * beta_blocks
    negative = -outer_product_result("nhik,nhjk->nhij", weighted, key_blocks) * strict
    inverse = jnp.eye(block_len, dtype=queries.dtype) + negative
    power_term = negative
    for doubling in range(5):
        power_term = outer_product_result("nhij,nhjk->nhik", power_term, power_term)
        inverse = inverse + outer_product_result("nhij,nhjk->nhik", inverse, power_term)
    value_mix = outer_product_result("nhij,nhjk->nhik", inverse, value_blocks * beta_blocks)
    scores = outer_product_result("nhik,nhjk->nhij", query_blocks, key_blocks) * causal
    produced_output = outer_product_result("nhqz,nhzr->nhqr", scores, value_mix)
    return produced_output.transpose(0, 2, 1, 3).reshape(length, head_count, -1)


def mixer_core(
    query_lin, key_lin, value_lin, gate_lin, beta_lin, conv_taps, head_scale, starts, reset_len
):
    length = query_lin.shape[0]
    head_count = beta_lin.shape[1]
    head_width = query_lin.shape[1] // head_count
    queries = jax.nn.silu(short_conv(query_lin, conv_taps[0], starts)).reshape(
        length, head_count, head_width
    )
    keys = jax.nn.silu(short_conv(key_lin, conv_taps[1], starts)).reshape(
        length, head_count, head_width
    )
    values = jax.nn.silu(short_conv(value_lin, conv_taps[2], starts)).reshape(
        length, head_count, head_width
    )
    queries = (
        queries
        * lax.rsqrt(jnp.sum(queries * queries, axis=-1, keepdims=True) + 1e-06)
        * head_width ** (-0.5)
    )
    keys = keys * lax.rsqrt(jnp.sum(keys * keys, axis=-1, keepdims=True) + 1e-06)
    if reset_len:
        recurrent = delta_core_reset(queries, keys, values, jax.nn.sigmoid(beta_lin), reset_len)
    else:
        recurrent = delta_core(queries, keys, values, jax.nn.sigmoid(beta_lin), starts)
    normed = (
        recurrent
        * lax.rsqrt(jnp.mean(recurrent * recurrent, axis=-1, keepdims=True) + 1e-05)
        * head_scale
    )
    gated_out = normed * jax.nn.silu(gate_lin.reshape(length, head_count, head_width))
    return gated_out.reshape(length, head_count * head_width)


def swiglu_mix(gate_act, up_act):
    return jax.nn.silu(gate_act) * up_act


def matmul_rows(left, right):
    return jnp.dot(left, right, preferred_element_type=jnp.float32)


def left_product(first, second):
    return jnp.einsum("tf,tg->fg", first, second, preferred_element_type=jnp.float32)


def back_product(gradient, weight):
    return jnp.einsum("tg,fg->tf", gradient, weight, preferred_element_type=jnp.float32)


def tp_gather(value, axis):
    tp = lax.psum(1, TP_AXES)
    spread = jnp.broadcast_to(
        jnp.expand_dims(value, axis), value.shape[:axis] + (tp,) + value.shape[axis:]
    )
    moved = lax.all_to_all(spread, TP_AXES, axis, axis, tiled=True)
    shape = list(value.shape)
    shape[axis] *= tp
    return moved.reshape(shape)


def tp_scatter_low(value, axis):
    tp = lax.psum(1, TP_AXES)
    shape = list(value.shape)
    staged = value.astype(jnp.bfloat16).reshape(
        shape[:axis] + [tp, shape[axis] // tp] + shape[axis + 1 :]
    )
    moved = lax.all_to_all(staged, TP_AXES, axis, axis, tiled=True)
    return jnp.sum(moved.astype(jnp.float32), axis=axis)


def fsdp_gather(value, axis):
    return lax.all_gather(value, FSDP_AXES, axis=axis, tiled=True)


def fsdp_scatter_low(value, axis):
    return lax.psum_scatter(
        value.astype(jnp.bfloat16), FSDP_AXES, scatter_dimension=axis, tiled=True
    )


def exchange(value, axes, split_axis, concat_axis):
    if not axes:
        return value
    return lax.all_to_all(value, axes, split_axis, concat_axis, tiled=True)


def heads_to_rows(values, tp, fsdp, rows):
    count = values.shape[0]
    staged = values.reshape(count, 1, fsdp // tp, tp, rows)
    moved = exchange(staged, TP_AXES, 3, 1)
    return moved.reshape(count, fsdp * rows)


def rows_to_heads(values, tp, fsdp, rows):
    count = values.shape[0]
    staged = values.reshape(count, tp, fsdp // tp, 1, rows)
    moved = exchange(staged, TP_AXES, 1, 3)
    return moved.reshape(count, fsdp * rows)


def padded_rows(flat, slices, width):
    extra = -(-flat.shape[0] // (slices * width))
    extra = -(-extra // 16) * 16
    filled = jnp.pad(flat, (0, slices * extra * width - flat.shape[0]))
    return filled.reshape(slices, extra, width)


def make_on_device(tp, fsdp, inner):
    def on_device(
        tokens,
        cotangent,
        group_start,
        pad_mask,
        query_weight,
        key_weight,
        value_weight,
        gate_weight,
        beta_weight,
        out_weight,
        conv_weight,
        mixer_gain,
        head_gain,
        swiglu_gain,
        swiglu_gate,
        swiglu_up,
        swiglu_down,
    ):
        micro_count, slot, width = tokens.shape
        n_all = tp * fsdp
        rows = query_weight.shape[0]
        head_count = beta_weight.shape[1]
        heads_here = head_count // tp
        cols_here = width // tp
        group_rows = tp * rows
        position = lax.axis_index(TP_AXES)
        head_scale = head_gain.astype(jnp.float32)
        reset_len = slot if group_start.shape[1] == 1 else 0

        column_owned = jnp.stack([query_weight, key_weight, value_weight, gate_weight])
        column_swapped = exchange(
            column_owned.reshape(4, rows, tp, cols_here), TP_AXES, 2, 1
        ).reshape(4, group_rows, cols_here)
        mixer_stack = jnp.concatenate(
            [column_swapped, out_weight.reshape(1, group_rows, cols_here)], axis=0
        )
        weight_all = fsdp_gather(mixer_stack, 1)
        query_cols, key_cols, value_cols, gate_cols = (weight_all[index] for index in range(4))
        out_rows = weight_all[4].reshape(fsdp * rows, width)
        small_pack = jnp.concatenate(
            [
                conv_weight.reshape(-1),
                beta_weight.reshape(-1),
                mixer_gain.reshape(-1),
                swiglu_gain.reshape(-1),
            ]
        )
        small_size = small_pack.shape[0]
        small_all = exchange(
            jnp.broadcast_to(small_pack[None, :], (n_all, small_size)), ALL_AXES, 0, 0
        )
        conv_size = conv_weight.size
        beta_size = beta_weight.size
        conv_full = (
            small_all[:, :conv_size]
            .reshape((n_all,) + conv_weight.shape)
            .transpose(1, 2, 0, 3)
            .reshape(conv_weight.shape[0], conv_weight.shape[1], -1)
        )
        beta_full = small_all[:, conv_size : conv_size + beta_size].reshape(-1, head_count)
        gain_mixer = small_all[:, conv_size + beta_size : conv_size + beta_size + rows].reshape(-1)
        gain_swiglu = small_all[:, conv_size + beta_size + rows :].reshape(-1)
        conv_here = lax.dynamic_slice_in_dim(
            conv_full.astype(jnp.float32), position * cols_here, cols_here, axis=2
        )
        beta_here = lax.dynamic_slice_in_dim(beta_full, position * heads_here, heads_here, axis=1)

        owned_rows, hidden_half = swiglu_gate.shape
        hidden_here = hidden_half // inner
        ff_owned = jnp.stack([swiglu_gate, swiglu_up, swiglu_down.T]).reshape(
            3, owned_rows, inner, hidden_here
        )
        lanes = hidden_here // 128 if hidden_here % 128 == 0 else 0
        if lanes >= 3:
            sizes = [(lanes + 2) // 3 * 128, (lanes + 2) // 3 * 128]
            sizes.append(hidden_here - sum(sizes))
        else:
            sizes = [hidden_here // 2, hidden_here - hidden_here // 2]
        starts_at = [sum(sizes[:index]) for index in range(len(sizes))]
        bounds = tuple(zip(starts_at, sizes))
        ff_chunks = []
        for offset, size in bounds:
            swapped = exchange(ff_owned[..., offset : offset + size], INNER_AXES, 2, 1)
            ff_chunks.append(fsdp_gather(swapped.reshape(3, inner * owned_rows, size), 1))

        inputs = tokens.astype(jnp.float32).reshape(micro_count * slot, width)
        normed, norm_back = jax.vjp(rms_norm, inputs, gain_mixer.astype(jnp.float32))
        normed_low = normed.astype(jnp.bfloat16)
        group_tokens = micro_count * slot * tp
        normed_group = tp_gather(normed_low.reshape(micro_count, slot, width), 1).reshape(
            group_tokens, width
        )
        starts = tp_gather(group_start, 1).reshape(-1)

        query_lin = matmul_rows(normed_group, query_cols)
        key_lin = matmul_rows(normed_group, key_cols)
        value_lin = matmul_rows(normed_group, value_cols)
        gate_lin = matmul_rows(normed_group, gate_cols)
        beta_lin = matmul_rows(normed_group, beta_here)

        def core_at(query_in, key_in, value_in, gate_in, beta_in, conv_in, head_in):
            return mixer_core(
                query_in, key_in, value_in, gate_in, beta_in, conv_in, head_in, starts, reset_len
            )

        gated_out, core_back = jax.vjp(
            core_at, query_lin, key_lin, value_lin, gate_lin, beta_lin, conv_here, head_scale
        )
        gated_low = gated_out.astype(jnp.bfloat16)
        gated_rows = heads_to_rows(gated_low, tp, fsdp, rows)
        mixed_partial = matmul_rows(gated_rows, out_rows)
        residual = inputs + tp_scatter_low(
            mixed_partial.reshape(micro_count, slot * tp, width), 1
        ).reshape(micro_count * slot, width)

        inner_norm, inner_norm_back = jax.vjp(rms_norm, residual, gain_swiglu.astype(jnp.float32))
        inner_low = inner_norm.astype(jnp.bfloat16)
        inner_group = tp_gather(inner_low.reshape(micro_count, slot, width), 1).reshape(
            group_tokens, width
        )
        out_back = cotangent.astype(jnp.float32) * pad_mask.astype(jnp.float32)[:, :, None]
        out_back_low = out_back.astype(jnp.bfloat16)
        upstream_group = tp_gather(out_back_low, 1).reshape(group_tokens, width)
        partial_rows = None
        inner_part = None
        ff_reduced = []
        for index, chunk_weights in enumerate(ff_chunks):
            if index > 0:
                sums_low, chunk_weights = lax.optimization_barrier((sums_low, chunk_weights))
            gate_piece, up_piece, down_piece_t = chunk_weights[0], chunk_weights[1], chunk_weights[2]
            gate_act = matmul_rows(inner_group, gate_piece)
            up_act = matmul_rows(inner_group, up_piece)
            hidden, hidden_back = jax.vjp(swiglu_mix, gate_act, up_act)
            hidden_low = hidden.astype(jnp.bfloat16)
            piece_rows = back_product(hidden_low, down_piece_t)
            partial_rows = piece_rows if partial_rows is None else partial_rows + piece_rows
            gate_back, up_back = hidden_back(matmul_rows(upstream_group, down_piece_t))
            gate_back_low = gate_back.astype(jnp.bfloat16)
            up_back_low = up_back.astype(jnp.bfloat16)
            piece_part = back_product(gate_back_low, gate_piece) + back_product(up_back_low, up_piece)
            inner_part = piece_part if inner_part is None else inner_part + piece_part
            sums_low = jnp.stack(
                [
                    left_product(inner_group, gate_back_low),
                    left_product(inner_group, up_back_low),
                    left_product(upstream_group, hidden_low),
                ]
            ).astype(jnp.bfloat16)
            ff_reduced.append(fsdp_scatter_low(sums_low, 1))
        branch_rows = tp_scatter_low(partial_rows.reshape(micro_count, slot * tp, width), 1)
        block_out = (residual.reshape(micro_count, slot, width) + branch_rows).astype(jnp.bfloat16)
        inner_back = tp_scatter_low(inner_part.reshape(micro_count, slot * tp, width), 1)
        block_out, inner_back = lax.optimization_barrier((block_out, inner_back))

        residual_part, swiglu_gain_term = inner_norm_back(
            inner_back.reshape(micro_count * slot, width)
        )
        residual_back = out_back.reshape(micro_count * slot, width) + residual_part
        mixed_back = residual_back.astype(jnp.bfloat16)
        mixed_group = tp_gather(mixed_back.reshape(micro_count, slot, width), 1).reshape(
            group_tokens, width
        )
        gated_back_rows = back_product(mixed_group, out_rows)
        gated_back = rows_to_heads(gated_back_rows, tp, fsdp, rows)
        query_back, key_back, value_back, gate_lin_back, beta_back, conv_term, head_term = (
            core_back(gated_back)
        )
        query_low = query_back.astype(jnp.bfloat16)
        key_low = key_back.astype(jnp.bfloat16)
        value_low = value_back.astype(jnp.bfloat16)
        gate_low = gate_lin_back.astype(jnp.bfloat16)
        beta_low = beta_back.astype(jnp.bfloat16)
        mixer_sums = jnp.stack(
            [
                left_product(normed_group, query_low),
                left_product(normed_group, key_low),
                left_product(normed_group, value_low),
                left_product(normed_group, gate_low),
                left_product(gated_rows, mixed_group).reshape(width, cols_here),
            ]
        )
        ff_reduced, mixer_sums = lax.optimization_barrier((ff_reduced, mixer_sums))
        mixer_reduced = fsdp_scatter_low(mixer_sums, 1)
        ff_back = jnp.concatenate(
            [
                exchange(
                    piece.reshape(3, inner, owned_rows, 1, size), INNER_AXES, 1, 3
                ).reshape(3, owned_rows, inner, size)
                for piece, (offset, size) in zip(ff_reduced, bounds)
            ],
            axis=3,
        ).reshape(3, owned_rows, hidden_half).astype(jnp.float32)
        swiglu_gate_grad = ff_back[0]
        swiglu_up_grad = ff_back[1]
        swiglu_down_grad = ff_back[2].T

        normed_part = (
            back_product(query_low, query_cols)
            + back_product(key_low, key_cols)
            + back_product(value_low, value_cols)
            + back_product(gate_low, gate_cols)
            + back_product(beta_low, beta_here)
        )
        normed_back = tp_scatter_low(normed_part.reshape(micro_count, slot * tp, width), 1)
        input_part, mixer_gain_term = norm_back(normed_back.reshape(micro_count * slot, width))
        tokens_grad = (residual_back + input_part).reshape(micro_count, slot, width)

        beta_sum = left_product(normed_group, beta_low)
        beta_wide = lax.dynamic_update_slice_in_dim(
            jnp.zeros((width, head_count), jnp.float32), beta_sum, position * heads_here, axis=1
        )
        conv_wide = lax.dynamic_update_slice_in_dim(
            jnp.zeros(conv_full.shape, jnp.float32), conv_term, position * cols_here, axis=2
        )
        taps = conv_wide.shape[0] * conv_wide.shape[1]
        small_terms = jnp.concatenate(
            [
                conv_wide.reshape(taps, n_all, -1).transpose(1, 0, 2).reshape(n_all, -1),
                beta_wide.reshape(n_all, -1),
                mixer_gain_term.reshape(n_all, -1),
                swiglu_gain_term.reshape(n_all, -1),
                jnp.broadcast_to(head_term[None, :], (n_all, head_term.shape[0])),
            ],
            axis=1,
        )
        small_width = small_terms.shape[1]
        small_out = jnp.sum(exchange(small_terms, ALL_AXES, 0, 0), axis=0)
        column_back = exchange(
            mixer_reduced[:4].reshape(4, tp, rows, 1, cols_here), TP_AXES, 1, 3
        ).reshape(4, rows, width).astype(jnp.float32)
        query_grad, key_grad, value_grad, gate_grad = (column_back[index] for index in range(4))
        out_grad = mixer_reduced[4].reshape(rows, width).astype(jnp.float32)
        conv_grad = small_out[:conv_size].reshape(conv_weight.shape)
        beta_grad = small_out[conv_size : conv_size + beta_size].reshape(beta_weight.shape)
        mixer_gain_grad = small_out[conv_size + beta_size : conv_size + beta_size + rows]
        swiglu_gain_grad = small_out[conv_size + beta_size + rows : conv_size + beta_size + 2 * rows]
        head_total = small_out[conv_size + beta_size + 2 * rows :]
        return (
            block_out,
            tokens_grad,
            query_grad,
            key_grad,
            value_grad,
            gate_grad,
            beta_grad,
            out_grad,
            conv_grad,
            mixer_gain_grad,
            head_total,
            swiglu_gain_grad,
            swiglu_gate_grad,
            swiglu_up_grad,
            swiglu_down_grad,
        )

    return on_device


def solution(mesh):
    n_dp = mesh.shape["dp"]
    n_mlp = mesh.shape["mlp"]
    devices = np.asarray(mesh.devices).reshape(n_dp // 2, 2, n_mlp)
    split_mesh = Mesh(devices, ALL_AXES)
    sizes = dict(zip(ALL_AXES, devices.shape))
    tp = int(np.prod([sizes[name] for name in TP_AXES]))
    fsdp = int(np.prod([sizes[name] for name in FSDP_AXES]))
    inner = int(np.prod([sizes[name] for name in INNER_AXES]))
    rows_axes = ALL_AXES
    swiglu_rows = ("dq", "core")
    placed = (
        P(None, rows_axes, None),
        P(None, rows_axes, None),
        P(None, rows_axes),
        P(None, rows_axes),
        P(rows_axes, None),
        P(rows_axes, None),
        P(rows_axes, None),
        P(rows_axes, None),
        P(rows_axes, None),
        P(rows_axes, None),
        P(None, None, rows_axes),
        P(rows_axes),
        P(),
        P(rows_axes),
        P(swiglu_rows, "mlp"),
        P(swiglu_rows, "mlp"),
        P("mlp", swiglu_rows),
    )
    return jax.shard_map(
        make_on_device(tp, fsdp, inner),
        mesh=split_mesh,
        in_specs=placed,
        out_specs=(
            P(None, rows_axes, None),
            P(None, rows_axes, None),
            P(rows_axes, None),
            P(rows_axes, None),
            P(rows_axes, None),
            P(rows_axes, None),
            P(rows_axes, None),
            P(rows_axes, None),
            P(None, None, rows_axes),
            P(rows_axes),
            P(),
            P(rows_axes),
            P(swiglu_rows, "mlp"),
            P(swiglu_rows, "mlp"),
            P("mlp", swiglu_rows),
        ),
        check_vma=False,
    )
```

```python
import jax
import jax.numpy as jnp
import numpy as np
from jax import lax
from jax.sharding import Mesh
from jax.sharding import PartitionSpec as P

TP_AXES = ("core", "mlp")
ALL_AXES = ("dq", "core", "mlp")
FSDP_AXES = tuple(name for name in ALL_AXES if name not in TP_AXES)
INNER_AXES = tuple(name for name in TP_AXES if name != "mlp")


def rms_norm(values, scale_gain):
    return (
        values * lax.rsqrt(jnp.mean(values * values, axis=-1, keepdims=True) + 1e-06) * scale_gain
    )


def short_conv(linear, tap_weights, starts):
    length = linear.shape[0]
    block_len = length // starts.shape[0]
    position = jnp.arange(length)
    restart = jnp.repeat(starts, block_len)
    summed = linear * tap_weights[0]
    for offset in range(1, tap_weights.shape[0]):
        shifted = jnp.concatenate(
            [jnp.zeros((offset, linear.shape[1]), linear.dtype), linear[: length - offset]], axis=0
        )
        usable = ((position % block_len >= offset) | (restart == 0)).astype(linear.dtype)
        summed = summed + shifted * tap_weights[offset] * usable[:, None]
    return summed


def outer_product_result(form, first, second):
    return jnp.einsum(form, first, second, precision=lax.Precision.HIGHEST)


def delta_core(queries, keys, values, betas, starts):
    length, head_count, head_width = queries.shape
    value_width = values.shape[2]
    block_count = starts.shape[0]
    block_len = length // block_count

    def blocked(array):
        return array.reshape(block_count, block_len, head_count, -1).transpose(0, 2, 1, 3)

    query_blocks = blocked(queries)
    key_blocks = blocked(keys)
    value_blocks = blocked(values)
    beta_blocks = betas.reshape(block_count, block_len, head_count).transpose(0, 2, 1)[..., None]
    position = jnp.arange(block_len)
    strict = (position[:, None] > position[None, :]).astype(queries.dtype)
    causal = (position[:, None] >= position[None, :]).astype(queries.dtype)
    weighted = key_blocks * beta_blocks
    negative = -outer_product_result("nhik,nhjk->nhij", weighted, key_blocks) * strict
    inverse = jnp.eye(block_len, dtype=queries.dtype) + negative
    power_term = negative
    for doubling in range(5):
        power_term = outer_product_result("nhij,nhjk->nhik", power_term, power_term)
        inverse = inverse + outer_product_result("nhij,nhjk->nhik", inverse, power_term)
    key_mix = outer_product_result("nhij,nhjk->nhik", inverse, weighted)
    value_mix = outer_product_result("nhij,nhjk->nhik", inverse, value_blocks * beta_blocks)
    scores = outer_product_result("nhik,nhjk->nhij", query_blocks, key_blocks) * causal

    def advance(current_state, block_items):
        (
            query_slice,
            key_slice,
            key_mixture_slice,
            value_mixture_slice,
            attention_score_slice,
            restart,
        ) = block_items
        current_state = current_state * (1 - restart).astype(current_state.dtype)
        adjusted_result = value_mixture_slice - outer_product_result(
            "pzd,pde->pze", key_mixture_slice, current_state
        )
        produced_output = outer_product_result(
            "pzd,pde->pze", query_slice, current_state
        ) + outer_product_result("lqz,lzr->lqr", attention_score_slice, adjusted_result)
        current_state = current_state + outer_product_result(
            "ixl,ixr->ilr", key_slice, adjusted_result
        )
        return (current_state, produced_output)

    initial = jnp.zeros((head_count, head_width, value_width), queries.dtype)
    final_state, produced_output = lax.scan(
        advance, initial, (query_blocks, key_blocks, key_mix, value_mix, scores, starts)
    )
    return produced_output.transpose(0, 2, 1, 3).reshape(length, head_count, value_width)


def delta_core_reset(queries, keys, values, betas, block_len):
    length, head_count, head_width = queries.shape
    block_count = length // block_len

    def blocked(array):
        return array.reshape(block_count, block_len, head_count, -1).transpose(0, 2, 1, 3)

    query_blocks = blocked(queries)
    key_blocks = blocked(keys)
    value_blocks = blocked(values)
    beta_blocks = betas.reshape(block_count, block_len, head_count).transpose(0, 2, 1)[..., None]
    position = jnp.arange(block_len)
    strict = (position[:, None] > position[None, :]).astype(queries.dtype)
    causal = (position[:, None] >= position[None, :]).astype(queries.dtype)
    weighted = key_blocks * beta_blocks
    negative = -outer_product_result("nhik,nhjk->nhij", weighted, key_blocks) * strict
    inverse = jnp.eye(block_len, dtype=queries.dtype) + negative
    power_term = negative
    for doubling in range(5):
        power_term = outer_product_result("nhij,nhjk->nhik", power_term, power_term)
        inverse = inverse + outer_product_result("nhij,nhjk->nhik", inverse, power_term)
    value_mix = outer_product_result("nhij,nhjk->nhik", inverse, value_blocks * beta_blocks)
    scores = outer_product_result("nhik,nhjk->nhij", query_blocks, key_blocks) * causal
    produced_output = outer_product_result("nhqz,nhzr->nhqr", scores, value_mix)
    return produced_output.transpose(0, 2, 1, 3).reshape(length, head_count, -1)


def mixer_core(
    query_lin, key_lin, value_lin, gate_lin, beta_lin, conv_taps, head_scale, starts, reset_len
):
    length = query_lin.shape[0]
    head_count = beta_lin.shape[1]
    head_width = query_lin.shape[1] // head_count
    queries = jax.nn.silu(short_conv(query_lin, conv_taps[0], starts)).reshape(
        length, head_count, head_width
    )
    keys = jax.nn.silu(short_conv(key_lin, conv_taps[1], starts)).reshape(
        length, head_count, head_width
    )
    values = jax.nn.silu(short_conv(value_lin, conv_taps[2], starts)).reshape(
        length, head_count, head_width
    )
    queries = (
        queries
        * lax.rsqrt(jnp.sum(queries * queries, axis=-1, keepdims=True) + 1e-06)
        * head_width ** (-0.5)
    )
    keys = keys * lax.rsqrt(jnp.sum(keys * keys, axis=-1, keepdims=True) + 1e-06)
    if reset_len:
        recurrent = delta_core_reset(queries, keys, values, jax.nn.sigmoid(beta_lin), reset_len)
    else:
        recurrent = delta_core(queries, keys, values, jax.nn.sigmoid(beta_lin), starts)
    normed = (
        recurrent
        * lax.rsqrt(jnp.mean(recurrent * recurrent, axis=-1, keepdims=True) + 1e-05)
        * head_scale
    )
    gated_out = normed * jax.nn.silu(gate_lin.reshape(length, head_count, head_width))
    return gated_out.reshape(length, head_count * head_width)


def swiglu_mix(gate_act, up_act):
    return jax.nn.silu(gate_act) * up_act


def matmul_rows(left, right):
    return jnp.dot(left, right, preferred_element_type=jnp.float32)


def left_product(first, second):
    return jnp.einsum("tf,tg->fg", first, second, preferred_element_type=jnp.float32)


def back_product(gradient, weight):
    return jnp.einsum("tg,fg->tf", gradient, weight, preferred_element_type=jnp.float32)


def tp_gather(value, axis):
    tp = lax.psum(1, TP_AXES)
    spread = jnp.broadcast_to(
        jnp.expand_dims(value, axis), value.shape[:axis] + (tp,) + value.shape[axis:]
    )
    moved = lax.all_to_all(spread, TP_AXES, axis, axis, tiled=True)
    shape = list(value.shape)
    shape[axis] *= tp
    return moved.reshape(shape)


def tp_scatter_low(value, axis):
    tp = lax.psum(1, TP_AXES)
    shape = list(value.shape)
    staged = value.astype(jnp.bfloat16).reshape(
        shape[:axis] + [tp, shape[axis] // tp] + shape[axis + 1 :]
    )
    moved = lax.all_to_all(staged, TP_AXES, axis, axis, tiled=True)
    return jnp.sum(moved.astype(jnp.float32), axis=axis)


def fsdp_gather(value, axis):
    return lax.all_gather(value, FSDP_AXES, axis=axis, tiled=True)


def fsdp_scatter_low(value, axis):
    return lax.psum_scatter(
        value.astype(jnp.bfloat16), FSDP_AXES, scatter_dimension=axis, tiled=True
    )


def exchange(value, axes, split_axis, concat_axis):
    if not axes:
        return value
    return lax.all_to_all(value, axes, split_axis, concat_axis, tiled=True)


def heads_to_rows(values, tp, fsdp, rows):
    count = values.shape[0]
    staged = values.reshape(count, 1, fsdp // tp, tp, rows)
    moved = exchange(staged, TP_AXES, 3, 1)
    return moved.reshape(count, fsdp * rows)


def rows_to_heads(values, tp, fsdp, rows):
    count = values.shape[0]
    staged = values.reshape(count, tp, fsdp // tp, 1, rows)
    moved = exchange(staged, TP_AXES, 1, 3)
    return moved.reshape(count, fsdp * rows)


def padded_rows(flat, slices, width):
    extra = -(-flat.shape[0] // (slices * width))
    extra = -(-extra // 16) * 16
    filled = jnp.pad(flat, (0, slices * extra * width - flat.shape[0]))
    return filled.reshape(slices, extra, width)


def make_on_device(tp, fsdp, inner):
    def on_device(
        tokens,
        cotangent,
        group_start,
        pad_mask,
        query_weight,
        key_weight,
        value_weight,
        gate_weight,
        beta_weight,
        out_weight,
        conv_weight,
        mixer_gain,
        head_gain,
        swiglu_gain,
        swiglu_gate,
        swiglu_up,
        swiglu_down,
    ):
        micro_count, slot, width = tokens.shape
        n_all = tp * fsdp
        rows = query_weight.shape[0]
        head_count = beta_weight.shape[1]
        heads_here = head_count // tp
        cols_here = width // tp
        group_rows = tp * rows
        position = lax.axis_index(TP_AXES)
        head_scale = head_gain.astype(jnp.float32)
        reset_len = slot if group_start.shape[1] == 1 else 0

        column_owned = jnp.stack([query_weight, key_weight, value_weight, gate_weight])
        column_swapped = exchange(
            column_owned.reshape(4, rows, tp, cols_here), TP_AXES, 2, 1
        ).reshape(4, group_rows, cols_here)
        mixer_stack = jnp.concatenate(
            [column_swapped, out_weight.reshape(1, group_rows, cols_here)], axis=0
        )
        weight_all = fsdp_gather(mixer_stack, 1)
        query_cols, key_cols, value_cols, gate_cols = (weight_all[index] for index in range(4))
        out_rows = weight_all[4].reshape(fsdp * rows, width)
        small_pack = jnp.concatenate(
            [
                conv_weight.reshape(-1),
                beta_weight.reshape(-1),
                mixer_gain.reshape(-1),
                swiglu_gain.reshape(-1),
            ]
        )
        small_size = small_pack.shape[0]
        small_all = exchange(
            jnp.broadcast_to(small_pack[None, :], (n_all, small_size)), ALL_AXES, 0, 0
        )
        conv_size = conv_weight.size
        beta_size = beta_weight.size
        conv_full = (
            small_all[:, :conv_size]
            .reshape((n_all,) + conv_weight.shape)
            .transpose(1, 2, 0, 3)
            .reshape(conv_weight.shape[0], conv_weight.shape[1], -1)
        )
        beta_full = small_all[:, conv_size : conv_size + beta_size].reshape(-1, head_count)
        gain_mixer = small_all[:, conv_size + beta_size : conv_size + beta_size + rows].reshape(-1)
        gain_swiglu = small_all[:, conv_size + beta_size + rows :].reshape(-1)
        conv_here = lax.dynamic_slice_in_dim(
            conv_full.astype(jnp.float32), position * cols_here, cols_here, axis=2
        )
        beta_here = lax.dynamic_slice_in_dim(beta_full, position * heads_here, heads_here, axis=1)

        owned_rows, hidden_half = swiglu_gate.shape
        hidden_here = hidden_half // inner
        ff_owned = jnp.stack([swiglu_gate, swiglu_up, swiglu_down.T]).reshape(
            3, owned_rows, inner, hidden_here
        )
        lanes = hidden_here // 128 if hidden_here % 128 == 0 else 0
        first = (lanes - lanes * 3 // 11) * 128 if lanes > 1 else hidden_here // 2
        bounds = ((0, first), (first, hidden_here - first))
        ff_chunks = []
        for offset, size in bounds:
            swapped = exchange(ff_owned[..., offset : offset + size], INNER_AXES, 2, 1)
            ff_chunks.append(fsdp_gather(swapped.reshape(3, inner * owned_rows, size), 1))

        inputs = tokens.astype(jnp.float32).reshape(micro_count * slot, width)
        normed, norm_back = jax.vjp(rms_norm, inputs, gain_mixer.astype(jnp.float32))
        normed_low = normed.astype(jnp.bfloat16)
        group_tokens = micro_count * slot * tp
        normed_group = tp_gather(normed_low.reshape(micro_count, slot, width), 1).reshape(
            group_tokens, width
        )
        starts = tp_gather(group_start, 1).reshape(-1)

        query_lin = matmul_rows(normed_group, query_cols)
        key_lin = matmul_rows(normed_group, key_cols)
        value_lin = matmul_rows(normed_group, value_cols)
        gate_lin = matmul_rows(normed_group, gate_cols)
        beta_lin = matmul_rows(normed_group, beta_here)

        def core_at(query_in, key_in, value_in, gate_in, beta_in, conv_in, head_in):
            return mixer_core(
                query_in, key_in, value_in, gate_in, beta_in, conv_in, head_in, starts, reset_len
            )

        gated_out, core_back = jax.vjp(
            core_at, query_lin, key_lin, value_lin, gate_lin, beta_lin, conv_here, head_scale
        )
        gated_low = gated_out.astype(jnp.bfloat16)
        gated_rows = heads_to_rows(gated_low, tp, fsdp, rows)
        mixed_partial = matmul_rows(gated_rows, out_rows)
        residual = inputs + tp_scatter_low(
            mixed_partial.reshape(micro_count, slot * tp, width), 1
        ).reshape(micro_count * slot, width)

        inner_norm, inner_norm_back = jax.vjp(rms_norm, residual, gain_swiglu.astype(jnp.float32))
        inner_low = inner_norm.astype(jnp.bfloat16)
        inner_group = tp_gather(inner_low.reshape(micro_count, slot, width), 1).reshape(
            group_tokens, width
        )
        out_back = cotangent.astype(jnp.float32) * pad_mask.astype(jnp.float32)[:, :, None]
        out_back_low = out_back.astype(jnp.bfloat16)
        upstream_group = tp_gather(out_back_low, 1).reshape(group_tokens, width)
        partial_rows = None
        inner_part = None
        ff_reduced = []
        for index, chunk_weights in enumerate(ff_chunks):
            if index > 0:
                sums_low, chunk_weights = lax.optimization_barrier((sums_low, chunk_weights))
            gate_piece, up_piece, down_piece_t = chunk_weights[0], chunk_weights[1], chunk_weights[2]
            gate_act = matmul_rows(inner_group, gate_piece)
            up_act = matmul_rows(inner_group, up_piece)
            hidden, hidden_back = jax.vjp(swiglu_mix, gate_act, up_act)
            hidden_low = hidden.astype(jnp.bfloat16)
            piece_rows = back_product(hidden_low, down_piece_t)
            partial_rows = piece_rows if partial_rows is None else partial_rows + piece_rows
            gate_back, up_back = hidden_back(matmul_rows(upstream_group, down_piece_t))
            gate_back_low = gate_back.astype(jnp.bfloat16)
            up_back_low = up_back.astype(jnp.bfloat16)
            piece_part = back_product(gate_back_low, gate_piece) + back_product(up_back_low, up_piece)
            inner_part = piece_part if inner_part is None else inner_part + piece_part
            sums_low = jnp.stack(
                [
                    left_product(inner_group, gate_back_low),
                    left_product(inner_group, up_back_low),
                    left_product(upstream_group, hidden_low),
                ]
            ).astype(jnp.bfloat16)
            ff_reduced.append(fsdp_scatter_low(sums_low, 1))
        branch_rows = tp_scatter_low(partial_rows.reshape(micro_count, slot * tp, width), 1)
        block_out = (residual.reshape(micro_count, slot, width) + branch_rows).astype(jnp.bfloat16)
        inner_back = tp_scatter_low(inner_part.reshape(micro_count, slot * tp, width), 1)
        block_out, inner_back = lax.optimization_barrier((block_out, inner_back))

        residual_part, swiglu_gain_term = inner_norm_back(
            inner_back.reshape(micro_count * slot, width)
        )
        residual_back = out_back.reshape(micro_count * slot, width) + residual_part
        mixed_back = residual_back.astype(jnp.bfloat16)
        mixed_group = tp_gather(mixed_back.reshape(micro_count, slot, width), 1).reshape(
            group_tokens, width
        )
        gated_back_rows = back_product(mixed_group, out_rows)
        gated_back = rows_to_heads(gated_back_rows, tp, fsdp, rows)
        query_back, key_back, value_back, gate_lin_back, beta_back, conv_term, head_term = (
            core_back(gated_back)
        )
        query_low = query_back.astype(jnp.bfloat16)
        key_low = key_back.astype(jnp.bfloat16)
        value_low = value_back.astype(jnp.bfloat16)
        gate_low = gate_lin_back.astype(jnp.bfloat16)
        beta_low = beta_back.astype(jnp.bfloat16)
        mixer_sums = jnp.stack(
            [
                left_product(normed_group, query_low),
                left_product(normed_group, key_low),
                left_product(normed_group, value_low),
                left_product(normed_group, gate_low),
                left_product(gated_rows, mixed_group).reshape(width, cols_here),
            ]
        )
        ff_reduced, mixer_sums = lax.optimization_barrier((ff_reduced, mixer_sums))
        mixer_reduced = fsdp_scatter_low(mixer_sums, 1)
        ff_back = jnp.concatenate(
            [
                exchange(
                    piece.reshape(3, inner, owned_rows, 1, size), INNER_AXES, 1, 3
                ).reshape(3, owned_rows, inner, size)
                for piece, (offset, size) in zip(ff_reduced, bounds)
            ],
            axis=3,
        ).reshape(3, owned_rows, hidden_half).astype(jnp.float32)
        swiglu_gate_grad = ff_back[0]
        swiglu_up_grad = ff_back[1]
        swiglu_down_grad = ff_back[2].T

        normed_part = (
            back_product(query_low, query_cols)
            + back_product(key_low, key_cols)
            + back_product(value_low, value_cols)
            + back_product(gate_low, gate_cols)
            + back_product(beta_low, beta_here)
        )
        normed_back = tp_scatter_low(normed_part.reshape(micro_count, slot * tp, width), 1)
        input_part, mixer_gain_term = norm_back(normed_back.reshape(micro_count * slot, width))
        tokens_grad = (residual_back + input_part).reshape(micro_count, slot, width)

        beta_sum = left_product(normed_group, beta_low)
        beta_wide = lax.dynamic_update_slice_in_dim(
            jnp.zeros((width, head_count), jnp.float32), beta_sum, position * heads_here, axis=1
        )
        conv_wide = lax.dynamic_update_slice_in_dim(
            jnp.zeros(conv_full.shape, jnp.float32), conv_term, position * cols_here, axis=2
        )
        taps = conv_wide.shape[0] * conv_wide.shape[1]
        small_terms = jnp.concatenate(
            [
                conv_wide.reshape(taps, n_all, -1).transpose(1, 0, 2).reshape(n_all, -1),
                beta_wide.reshape(n_all, -1),
                mixer_gain_term.reshape(n_all, -1),
                swiglu_gain_term.reshape(n_all, -1),
                jnp.broadcast_to(head_term[None, :], (n_all, head_term.shape[0])),
            ],
            axis=1,
        )
        small_width = small_terms.shape[1]
        small_out = jnp.sum(exchange(small_terms, ALL_AXES, 0, 0), axis=0)
        column_back = exchange(
            mixer_reduced[:4].reshape(4, tp, rows, 1, cols_here), TP_AXES, 1, 3
        ).reshape(4, rows, width).astype(jnp.float32)
        query_grad, key_grad, value_grad, gate_grad = (column_back[index] for index in range(4))
        out_grad = mixer_reduced[4].reshape(rows, width).astype(jnp.float32)
        conv_grad = small_out[:conv_size].reshape(conv_weight.shape)
        beta_grad = small_out[conv_size : conv_size + beta_size].reshape(beta_weight.shape)
        mixer_gain_grad = small_out[conv_size + beta_size : conv_size + beta_size + rows]
        swiglu_gain_grad = small_out[conv_size + beta_size + rows : conv_size + beta_size + 2 * rows]
        head_total = small_out[conv_size + beta_size + 2 * rows :]
        return (
            block_out,
            tokens_grad,
            query_grad,
            key_grad,
            value_grad,
            gate_grad,
            beta_grad,
            out_grad,
            conv_grad,
            mixer_gain_grad,
            head_total,
            swiglu_gain_grad,
            swiglu_gate_grad,
            swiglu_up_grad,
            swiglu_down_grad,
        )

    return on_device


def solution(mesh):
    n_dp = mesh.shape["dp"]
    n_mlp = mesh.shape["mlp"]
    devices = np.asarray(mesh.devices).reshape(n_dp // 2, 2, n_mlp)
    split_mesh = Mesh(devices, ALL_AXES)
    sizes = dict(zip(ALL_AXES, devices.shape))
    tp = int(np.prod([sizes[name] for name in TP_AXES]))
    fsdp = int(np.prod([sizes[name] for name in FSDP_AXES]))
    inner = int(np.prod([sizes[name] for name in INNER_AXES]))
    rows_axes = ALL_AXES
    swiglu_rows = ("dq", "core")
    placed = (
        P(None, rows_axes, None),
        P(None, rows_axes, None),
        P(None, rows_axes),
        P(None, rows_axes),
        P(rows_axes, None),
        P(rows_axes, None),
        P(rows_axes, None),
        P(rows_axes, None),
        P(rows_axes, None),
        P(rows_axes, None),
        P(None, None, rows_axes),
        P(rows_axes),
        P(),
        P(rows_axes),
        P(swiglu_rows, "mlp"),
        P(swiglu_rows, "mlp"),
        P("mlp", swiglu_rows),
    )
    return jax.shard_map(
        make_on_device(tp, fsdp, inner),
        mesh=split_mesh,
        in_specs=placed,
        out_specs=(
            P(None, rows_axes, None),
            P(None, rows_axes, None),
            P(rows_axes, None),
            P(rows_axes, None),
            P(rows_axes, None),
            P(rows_axes, None),
            P(rows_axes, None),
            P(rows_axes, None),
            P(None, None, rows_axes),
            P(rows_axes),
            P(),
            P(rows_axes),
            P(swiglu_rows, "mlp"),
            P(swiglu_rows, "mlp"),
            P("mlp", swiglu_rows),
        ),
        check_vma=False,
    )
```

```python
import jax
import jax.numpy as jnp
import numpy as np
from jax import lax
from jax.sharding import Mesh
from jax.sharding import PartitionSpec as P

TP_AXES = ("core", "mlp")
ALL_AXES = ("dq", "core", "mlp")
FSDP_AXES = tuple(name for name in ALL_AXES if name not in TP_AXES)
INNER_AXES = tuple(name for name in TP_AXES if name != "mlp")


def rms_norm(values, scale_gain):
    return (
        values * lax.rsqrt(jnp.mean(values * values, axis=-1, keepdims=True) + 1e-06) * scale_gain
    )


def short_conv(linear, tap_weights, starts):
    length = linear.shape[0]
    block_len = length // starts.shape[0]
    position = jnp.arange(length)
    restart = jnp.repeat(starts, block_len)
    summed = linear * tap_weights[0]
    for offset in range(1, tap_weights.shape[0]):
        shifted = jnp.concatenate(
            [jnp.zeros((offset, linear.shape[1]), linear.dtype), linear[: length - offset]], axis=0
        )
        usable = ((position % block_len >= offset) | (restart == 0)).astype(linear.dtype)
        summed = summed + shifted * tap_weights[offset] * usable[:, None]
    return summed


def outer_product_result(form, first, second):
    return jnp.einsum(form, first, second, precision=lax.Precision.HIGHEST)


def delta_core(queries, keys, values, betas, starts):
    length, head_count, head_width = queries.shape
    value_width = values.shape[2]
    block_count = starts.shape[0]
    block_len = length // block_count

    def blocked(array):
        return array.reshape(block_count, block_len, head_count, -1).transpose(0, 2, 1, 3)

    query_blocks = blocked(queries)
    key_blocks = blocked(keys)
    value_blocks = blocked(values)
    beta_blocks = betas.reshape(block_count, block_len, head_count).transpose(0, 2, 1)[..., None]
    position = jnp.arange(block_len)
    strict = (position[:, None] > position[None, :]).astype(queries.dtype)
    causal = (position[:, None] >= position[None, :]).astype(queries.dtype)
    weighted = key_blocks * beta_blocks
    negative = -outer_product_result("nhik,nhjk->nhij", weighted, key_blocks) * strict
    inverse = jnp.eye(block_len, dtype=queries.dtype) + negative
    power_term = negative
    for doubling in range(5):
        power_term = outer_product_result("nhij,nhjk->nhik", power_term, power_term)
        inverse = inverse + outer_product_result("nhij,nhjk->nhik", inverse, power_term)
    key_mix = outer_product_result("nhij,nhjk->nhik", inverse, weighted)
    value_mix = outer_product_result("nhij,nhjk->nhik", inverse, value_blocks * beta_blocks)
    scores = outer_product_result("nhik,nhjk->nhij", query_blocks, key_blocks) * causal

    def advance(current_state, block_items):
        (
            query_slice,
            key_slice,
            key_mixture_slice,
            value_mixture_slice,
            attention_score_slice,
            restart,
        ) = block_items
        current_state = current_state * (1 - restart).astype(current_state.dtype)
        adjusted_result = value_mixture_slice - outer_product_result(
            "pzd,pde->pze", key_mixture_slice, current_state
        )
        produced_output = outer_product_result(
            "pzd,pde->pze", query_slice, current_state
        ) + outer_product_result("lqz,lzr->lqr", attention_score_slice, adjusted_result)
        current_state = current_state + outer_product_result(
            "ixl,ixr->ilr", key_slice, adjusted_result
        )
        return (current_state, produced_output)

    initial = jnp.zeros((head_count, head_width, value_width), queries.dtype)
    final_state, produced_output = lax.scan(
        advance, initial, (query_blocks, key_blocks, key_mix, value_mix, scores, starts)
    )
    return produced_output.transpose(0, 2, 1, 3).reshape(length, head_count, value_width)


def delta_core_reset(queries, keys, values, betas, block_len):
    length, head_count, head_width = queries.shape
    block_count = length // block_len

    def blocked(array):
        return array.reshape(block_count, block_len, head_count, -1).transpose(0, 2, 1, 3)

    query_blocks = blocked(queries)
    key_blocks = blocked(keys)
    value_blocks = blocked(values)
    beta_blocks = betas.reshape(block_count, block_len, head_count).transpose(0, 2, 1)[..., None]
    position = jnp.arange(block_len)
    strict = (position[:, None] > position[None, :]).astype(queries.dtype)
    causal = (position[:, None] >= position[None, :]).astype(queries.dtype)
    weighted = key_blocks * beta_blocks
    negative = -outer_product_result("nhik,nhjk->nhij", weighted, key_blocks) * strict
    inverse = jnp.eye(block_len, dtype=queries.dtype) + negative
    power_term = negative
    for doubling in range(5):
        power_term = outer_product_result("nhij,nhjk->nhik", power_term, power_term)
        inverse = inverse + outer_product_result("nhij,nhjk->nhik", inverse, power_term)
    value_mix = outer_product_result("nhij,nhjk->nhik", inverse, value_blocks * beta_blocks)
    scores = outer_product_result("nhik,nhjk->nhij", query_blocks, key_blocks) * causal
    produced_output = outer_product_result("nhqz,nhzr->nhqr", scores, value_mix)
    return produced_output.transpose(0, 2, 1, 3).reshape(length, head_count, -1)


def mixer_core(
    query_lin, key_lin, value_lin, gate_lin, beta_lin, conv_taps, head_scale, starts, reset_len
):
    length = query_lin.shape[0]
    head_count = beta_lin.shape[1]
    head_width = query_lin.shape[1] // head_count
    queries = jax.nn.silu(short_conv(query_lin, conv_taps[0], starts)).reshape(
        length, head_count, head_width
    )
    keys = jax.nn.silu(short_conv(key_lin, conv_taps[1], starts)).reshape(
        length, head_count, head_width
    )
    values = jax.nn.silu(short_conv(value_lin, conv_taps[2], starts)).reshape(
        length, head_count, head_width
    )
    queries = (
        queries
        * lax.rsqrt(jnp.sum(queries * queries, axis=-1, keepdims=True) + 1e-06)
        * head_width ** (-0.5)
    )
    keys = keys * lax.rsqrt(jnp.sum(keys * keys, axis=-1, keepdims=True) + 1e-06)
    if reset_len:
        recurrent = delta_core_reset(queries, keys, values, jax.nn.sigmoid(beta_lin), reset_len)
    else:
        recurrent = delta_core(queries, keys, values, jax.nn.sigmoid(beta_lin), starts)
    normed = (
        recurrent
        * lax.rsqrt(jnp.mean(recurrent * recurrent, axis=-1, keepdims=True) + 1e-05)
        * head_scale
    )
    gated_out = normed * jax.nn.silu(gate_lin.reshape(length, head_count, head_width))
    return gated_out.reshape(length, head_count * head_width)


def swiglu_mix(gate_act, up_act):
    return jax.nn.silu(gate_act) * up_act


def matmul_rows(left, right):
    return jnp.dot(left, right, preferred_element_type=jnp.float32)


def left_product(first, second):
    return jnp.einsum("tf,tg->fg", first, second, preferred_element_type=jnp.float32)


def back_product(gradient, weight):
    return jnp.einsum("tg,fg->tf", gradient, weight, preferred_element_type=jnp.float32)


def tp_gather(value, axis):
    tp = lax.psum(1, TP_AXES)
    spread = jnp.broadcast_to(
        jnp.expand_dims(value, axis), value.shape[:axis] + (tp,) + value.shape[axis:]
    )
    moved = lax.all_to_all(spread, TP_AXES, axis, axis, tiled=True)
    shape = list(value.shape)
    shape[axis] *= tp
    return moved.reshape(shape)


def tp_scatter_low(value, axis):
    tp = lax.psum(1, TP_AXES)
    shape = list(value.shape)
    staged = value.astype(jnp.bfloat16).reshape(
        shape[:axis] + [tp, shape[axis] // tp] + shape[axis + 1 :]
    )
    moved = lax.all_to_all(staged, TP_AXES, axis, axis, tiled=True)
    return jnp.sum(moved.astype(jnp.float32), axis=axis)


def fsdp_gather(value, axis):
    return lax.all_gather(value, FSDP_AXES, axis=axis, tiled=True)


def fsdp_scatter_low(value, axis):
    return lax.psum_scatter(
        value.astype(jnp.bfloat16), FSDP_AXES, scatter_dimension=axis, tiled=True
    )


def fsdp_scatter_direct(value, fsdp, axis):
    shape = list(value.shape)
    staged = value.astype(jnp.bfloat16).reshape(
        shape[:axis] + [fsdp, shape[axis] // fsdp] + shape[axis + 1 :]
    )
    moved = lax.all_to_all(staged, FSDP_AXES, axis, axis, tiled=True)
    return jnp.sum(moved.astype(jnp.float32), axis=axis)


def exchange(value, axes, split_axis, concat_axis):
    if not axes:
        return value
    return lax.all_to_all(value, axes, split_axis, concat_axis, tiled=True)


def heads_to_rows(values, tp, fsdp, rows):
    count = values.shape[0]
    staged = values.reshape(count, 1, fsdp // tp, tp, rows)
    moved = exchange(staged, TP_AXES, 3, 1)
    return moved.reshape(count, fsdp * rows)


def rows_to_heads(values, tp, fsdp, rows):
    count = values.shape[0]
    staged = values.reshape(count, tp, fsdp // tp, 1, rows)
    moved = exchange(staged, TP_AXES, 1, 3)
    return moved.reshape(count, fsdp * rows)


def padded_rows(flat, slices, width):
    extra = -(-flat.shape[0] // (slices * width))
    extra = -(-extra // 16) * 16
    filled = jnp.pad(flat, (0, slices * extra * width - flat.shape[0]))
    return filled.reshape(slices, extra, width)


def make_on_device(tp, fsdp, inner):
    def on_device(
        tokens,
        cotangent,
        group_start,
        pad_mask,
        query_weight,
        key_weight,
        value_weight,
        gate_weight,
        beta_weight,
        out_weight,
        conv_weight,
        mixer_gain,
        head_gain,
        swiglu_gain,
        swiglu_gate,
        swiglu_up,
        swiglu_down,
    ):
        micro_count, slot, width = tokens.shape
        n_all = tp * fsdp
        rows = query_weight.shape[0]
        head_count = beta_weight.shape[1]
        heads_here = head_count // tp
        cols_here = width // tp
        group_rows = tp * rows
        position = lax.axis_index(TP_AXES)
        head_scale = head_gain.astype(jnp.float32)
        reset_len = slot if group_start.shape[1] == 1 else 0

        column_owned = jnp.stack([query_weight, key_weight, value_weight, gate_weight])
        column_swapped = exchange(
            column_owned.reshape(4, rows, tp, cols_here), TP_AXES, 2, 1
        ).reshape(4, group_rows, cols_here)
        mixer_stack = jnp.concatenate(
            [column_swapped, out_weight.reshape(1, group_rows, cols_here)], axis=0
        )
        weight_all = fsdp_gather(mixer_stack, 1)
        query_cols, key_cols, value_cols, gate_cols = (weight_all[index] for index in range(4))
        out_rows = weight_all[4].reshape(fsdp * rows, width)
        small_pack = jnp.concatenate(
            [
                conv_weight.reshape(-1),
                beta_weight.reshape(-1),
                mixer_gain.reshape(-1),
                swiglu_gain.reshape(-1),
            ]
        )
        small_size = small_pack.shape[0]
        small_all = exchange(
            jnp.broadcast_to(small_pack[None, :], (n_all, small_size)), ALL_AXES, 0, 0
        )
        conv_size = conv_weight.size
        beta_size = beta_weight.size
        conv_full = (
            small_all[:, :conv_size]
            .reshape((n_all,) + conv_weight.shape)
            .transpose(1, 2, 0, 3)
            .reshape(conv_weight.shape[0], conv_weight.shape[1], -1)
        )
        beta_full = small_all[:, conv_size : conv_size + beta_size].reshape(-1, head_count)
        gain_mixer = small_all[:, conv_size + beta_size : conv_size + beta_size + rows].reshape(-1)
        gain_swiglu = small_all[:, conv_size + beta_size + rows :].reshape(-1)
        conv_here = lax.dynamic_slice_in_dim(
            conv_full.astype(jnp.float32), position * cols_here, cols_here, axis=2
        )
        beta_here = lax.dynamic_slice_in_dim(beta_full, position * heads_here, heads_here, axis=1)

        owned_rows, hidden_half = swiglu_gate.shape
        hidden_here = hidden_half // inner
        ff_owned = jnp.stack([swiglu_gate, swiglu_up, swiglu_down.T]).reshape(
            3, owned_rows, inner, hidden_here
        )
        lanes = hidden_here // 128 if hidden_here % 128 == 0 else 0
        first = (lanes - lanes * 3 // 11) * 128 if lanes > 1 else hidden_here // 2
        bounds = ((0, first), (first, hidden_here - first))
        ff_chunks = []
        for offset, size in bounds:
            swapped = exchange(ff_owned[..., offset : offset + size], INNER_AXES, 2, 1)
            ff_chunks.append(fsdp_gather(swapped.reshape(3, inner * owned_rows, size), 1))

        inputs = tokens.astype(jnp.float32).reshape(micro_count * slot, width)
        normed, norm_back = jax.vjp(rms_norm, inputs, gain_mixer.astype(jnp.float32))
        normed_low = normed.astype(jnp.bfloat16)
        group_tokens = micro_count * slot * tp
        normed_group = tp_gather(normed_low.reshape(micro_count, slot, width), 1).reshape(
            group_tokens, width
        )
        starts = tp_gather(group_start, 1).reshape(-1)

        query_lin = matmul_rows(normed_group, query_cols)
        key_lin = matmul_rows(normed_group, key_cols)
        value_lin = matmul_rows(normed_group, value_cols)
        gate_lin = matmul_rows(normed_group, gate_cols)
        beta_lin = matmul_rows(normed_group, beta_here)

        def core_at(query_in, key_in, value_in, gate_in, beta_in, conv_in, head_in):
            return mixer_core(
                query_in, key_in, value_in, gate_in, beta_in, conv_in, head_in, starts, reset_len
            )

        gated_out, core_back = jax.vjp(
            core_at, query_lin, key_lin, value_lin, gate_lin, beta_lin, conv_here, head_scale
        )
        gated_low = gated_out.astype(jnp.bfloat16)
        gated_rows = heads_to_rows(gated_low, tp, fsdp, rows)
        mixed_partial = matmul_rows(gated_rows, out_rows)
        residual = inputs + tp_scatter_low(
            mixed_partial.reshape(micro_count, slot * tp, width), 1
        ).reshape(micro_count * slot, width)

        inner_norm, inner_norm_back = jax.vjp(rms_norm, residual, gain_swiglu.astype(jnp.float32))
        inner_low = inner_norm.astype(jnp.bfloat16)
        inner_group = tp_gather(inner_low.reshape(micro_count, slot, width), 1).reshape(
            group_tokens, width
        )
        out_back = cotangent.astype(jnp.float32) * pad_mask.astype(jnp.float32)[:, :, None]
        out_back_low = out_back.astype(jnp.bfloat16)
        upstream_group = tp_gather(out_back_low, 1).reshape(group_tokens, width)
        partial_rows = None
        inner_part = None
        ff_reduced = []
        for index, chunk_weights in enumerate(ff_chunks):
            if index > 0:
                sums_low, chunk_weights = lax.optimization_barrier((sums_low, chunk_weights))
            gate_piece, up_piece, down_piece_t = chunk_weights[0], chunk_weights[1], chunk_weights[2]
            gate_act = matmul_rows(inner_group, gate_piece)
            up_act = matmul_rows(inner_group, up_piece)
            hidden, hidden_back = jax.vjp(swiglu_mix, gate_act, up_act)
            hidden_low = hidden.astype(jnp.bfloat16)
            piece_rows = back_product(hidden_low, down_piece_t)
            partial_rows = piece_rows if partial_rows is None else partial_rows + piece_rows
            gate_back, up_back = hidden_back(matmul_rows(upstream_group, down_piece_t))
            gate_back_low = gate_back.astype(jnp.bfloat16)
            up_back_low = up_back.astype(jnp.bfloat16)
            piece_part = back_product(gate_back_low, gate_piece) + back_product(up_back_low, up_piece)
            inner_part = piece_part if inner_part is None else inner_part + piece_part
            sums_low = jnp.stack(
                [
                    left_product(inner_group, gate_back_low),
                    left_product(inner_group, up_back_low),
                    left_product(upstream_group, hidden_low),
                ]
            ).astype(jnp.bfloat16)
            ff_reduced.append(fsdp_scatter_low(sums_low, 1))
        branch_rows = tp_scatter_low(partial_rows.reshape(micro_count, slot * tp, width), 1)
        block_out = (residual.reshape(micro_count, slot, width) + branch_rows).astype(jnp.bfloat16)
        inner_back = tp_scatter_low(inner_part.reshape(micro_count, slot * tp, width), 1)
        block_out, inner_back = lax.optimization_barrier((block_out, inner_back))

        residual_part, swiglu_gain_term = inner_norm_back(
            inner_back.reshape(micro_count * slot, width)
        )
        residual_back = out_back.reshape(micro_count * slot, width) + residual_part
        mixed_back = residual_back.astype(jnp.bfloat16)
        mixed_group = tp_gather(mixed_back.reshape(micro_count, slot, width), 1).reshape(
            group_tokens, width
        )
        gated_back_rows = back_product(mixed_group, out_rows)
        gated_back = rows_to_heads(gated_back_rows, tp, fsdp, rows)
        query_back, key_back, value_back, gate_lin_back, beta_back, conv_term, head_term = (
            core_back(gated_back)
        )
        query_low = query_back.astype(jnp.bfloat16)
        key_low = key_back.astype(jnp.bfloat16)
        value_low = value_back.astype(jnp.bfloat16)
        gate_low = gate_lin_back.astype(jnp.bfloat16)
        beta_low = beta_back.astype(jnp.bfloat16)
        mixer_sums = jnp.stack(
            [
                left_product(normed_group, query_low),
                left_product(normed_group, key_low),
                left_product(normed_group, value_low),
                left_product(normed_group, gate_low),
                left_product(gated_rows, mixed_group).reshape(width, cols_here),
            ]
        )
        ff_reduced, mixer_sums = lax.optimization_barrier((ff_reduced, mixer_sums))
        mixer_reduced = jnp.concatenate(
            [
                fsdp_scatter_low(mixer_sums[:3], 1),
                fsdp_scatter_direct(mixer_sums[3:], fsdp, 1).astype(jnp.bfloat16),
            ],
            axis=0,
        )
        ff_back = jnp.concatenate(
            [
                exchange(
                    piece.reshape(3, inner, owned_rows, 1, size), INNER_AXES, 1, 3
                ).reshape(3, owned_rows, inner, size)
                for piece, (offset, size) in zip(ff_reduced, bounds)
            ],
            axis=3,
        ).reshape(3, owned_rows, hidden_half).astype(jnp.float32)
        swiglu_gate_grad = ff_back[0]
        swiglu_up_grad = ff_back[1]
        swiglu_down_grad = ff_back[2].T

        normed_part = (
            back_product(query_low, query_cols)
            + back_product(key_low, key_cols)
            + back_product(value_low, value_cols)
            + back_product(gate_low, gate_cols)
            + back_product(beta_low, beta_here)
        )
        normed_back = tp_scatter_low(normed_part.reshape(micro_count, slot * tp, width), 1)
        input_part, mixer_gain_term = norm_back(normed_back.reshape(micro_count * slot, width))
        tokens_grad = (residual_back + input_part).reshape(micro_count, slot, width)

        beta_sum = left_product(normed_group, beta_low)
        beta_wide = lax.dynamic_update_slice_in_dim(
            jnp.zeros((width, head_count), jnp.float32), beta_sum, position * heads_here, axis=1
        )
        conv_wide = lax.dynamic_update_slice_in_dim(
            jnp.zeros(conv_full.shape, jnp.float32), conv_term, position * cols_here, axis=2
        )
        taps = conv_wide.shape[0] * conv_wide.shape[1]
        small_terms = jnp.concatenate(
            [
                conv_wide.reshape(taps, n_all, -1).transpose(1, 0, 2).reshape(n_all, -1),
                beta_wide.reshape(n_all, -1),
                mixer_gain_term.reshape(n_all, -1),
                swiglu_gain_term.reshape(n_all, -1),
                jnp.broadcast_to(head_term[None, :], (n_all, head_term.shape[0])),
            ],
            axis=1,
        )
        small_width = small_terms.shape[1]
        small_out = jnp.sum(exchange(small_terms, ALL_AXES, 0, 0), axis=0)
        column_back = exchange(
            mixer_reduced[:4].reshape(4, tp, rows, 1, cols_here), TP_AXES, 1, 3
        ).reshape(4, rows, width).astype(jnp.float32)
        query_grad, key_grad, value_grad, gate_grad = (column_back[index] for index in range(4))
        out_grad = mixer_reduced[4].reshape(rows, width).astype(jnp.float32)
        conv_grad = small_out[:conv_size].reshape(conv_weight.shape)
        beta_grad = small_out[conv_size : conv_size + beta_size].reshape(beta_weight.shape)
        mixer_gain_grad = small_out[conv_size + beta_size : conv_size + beta_size + rows]
        swiglu_gain_grad = small_out[conv_size + beta_size + rows : conv_size + beta_size + 2 * rows]
        head_total = small_out[conv_size + beta_size + 2 * rows :]
        return (
            block_out,
            tokens_grad,
            query_grad,
            key_grad,
            value_grad,
            gate_grad,
            beta_grad,
            out_grad,
            conv_grad,
            mixer_gain_grad,
            head_total,
            swiglu_gain_grad,
            swiglu_gate_grad,
            swiglu_up_grad,
            swiglu_down_grad,
        )

    return on_device


def solution(mesh):
    n_dp = mesh.shape["dp"]
    n_mlp = mesh.shape["mlp"]
    devices = np.asarray(mesh.devices).reshape(n_dp // 2, 2, n_mlp)
    split_mesh = Mesh(devices, ALL_AXES)
    sizes = dict(zip(ALL_AXES, devices.shape))
    tp = int(np.prod([sizes[name] for name in TP_AXES]))
    fsdp = int(np.prod([sizes[name] for name in FSDP_AXES]))
    inner = int(np.prod([sizes[name] for name in INNER_AXES]))
    rows_axes = ALL_AXES
    swiglu_rows = ("dq", "core")
    placed = (
        P(None, rows_axes, None),
        P(None, rows_axes, None),
        P(None, rows_axes),
        P(None, rows_axes),
        P(rows_axes, None),
        P(rows_axes, None),
        P(rows_axes, None),
        P(rows_axes, None),
        P(rows_axes, None),
        P(rows_axes, None),
        P(None, None, rows_axes),
        P(rows_axes),
        P(),
        P(rows_axes),
        P(swiglu_rows, "mlp"),
        P(swiglu_rows, "mlp"),
        P("mlp", swiglu_rows),
    )
    return jax.shard_map(
        make_on_device(tp, fsdp, inner),
        mesh=split_mesh,
        in_specs=placed,
        out_specs=(
            P(None, rows_axes, None),
            P(None, rows_axes, None),
            P(rows_axes, None),
            P(rows_axes, None),
            P(rows_axes, None),
            P(rows_axes, None),
            P(rows_axes, None),
            P(rows_axes, None),
            P(None, None, rows_axes),
            P(rows_axes),
            P(),
            P(rows_axes),
            P(swiglu_rows, "mlp"),
            P(swiglu_rows, "mlp"),
            P("mlp", swiglu_rows),
        ),
        check_vma=False,
    )
```

```python
import jax
import jax.numpy as jnp
import numpy as np
from jax import lax
from jax.sharding import Mesh
from jax.sharding import PartitionSpec as P

TP_AXES = ("core", "mlp")
ALL_AXES = ("dq", "core", "mlp")
FSDP_AXES = tuple(name for name in ALL_AXES if name not in TP_AXES)
INNER_AXES = tuple(name for name in TP_AXES if name != "mlp")


def rms_norm(values, scale_gain):
    return (
        values * lax.rsqrt(jnp.mean(values * values, axis=-1, keepdims=True) + 1e-06) * scale_gain
    )


def short_conv(linear, tap_weights, starts):
    length = linear.shape[0]
    block_len = length // starts.shape[0]
    position = jnp.arange(length)
    restart = jnp.repeat(starts, block_len)
    summed = linear * tap_weights[0]
    for offset in range(1, tap_weights.shape[0]):
        shifted = jnp.concatenate(
            [jnp.zeros((offset, linear.shape[1]), linear.dtype), linear[: length - offset]], axis=0
        )
        usable = ((position % block_len >= offset) | (restart == 0)).astype(linear.dtype)
        summed = summed + shifted * tap_weights[offset] * usable[:, None]
    return summed


def outer_product_result(form, first, second):
    return jnp.einsum(form, first, second, precision=lax.Precision.HIGHEST)


def delta_core(queries, keys, values, betas, starts):
    length, head_count, head_width = queries.shape
    value_width = values.shape[2]
    block_count = starts.shape[0]
    block_len = length // block_count

    def blocked(array):
        return array.reshape(block_count, block_len, head_count, -1).transpose(0, 2, 1, 3)

    query_blocks = blocked(queries)
    key_blocks = blocked(keys)
    value_blocks = blocked(values)
    beta_blocks = betas.reshape(block_count, block_len, head_count).transpose(0, 2, 1)[..., None]
    position = jnp.arange(block_len)
    strict = (position[:, None] > position[None, :]).astype(queries.dtype)
    causal = (position[:, None] >= position[None, :]).astype(queries.dtype)
    weighted = key_blocks * beta_blocks
    negative = -outer_product_result("nhik,nhjk->nhij", weighted, key_blocks) * strict
    inverse = jnp.eye(block_len, dtype=queries.dtype) + negative
    power_term = negative
    for doubling in range(5):
        power_term = outer_product_result("nhij,nhjk->nhik", power_term, power_term)
        inverse = inverse + outer_product_result("nhij,nhjk->nhik", inverse, power_term)
    key_mix = outer_product_result("nhij,nhjk->nhik", inverse, weighted)
    value_mix = outer_product_result("nhij,nhjk->nhik", inverse, value_blocks * beta_blocks)
    scores = outer_product_result("nhik,nhjk->nhij", query_blocks, key_blocks) * causal

    def advance(current_state, block_items):
        (
            query_slice,
            key_slice,
            key_mixture_slice,
            value_mixture_slice,
            attention_score_slice,
            restart,
        ) = block_items
        current_state = current_state * (1 - restart).astype(current_state.dtype)
        adjusted_result = value_mixture_slice - outer_product_result(
            "pzd,pde->pze", key_mixture_slice, current_state
        )
        produced_output = outer_product_result(
            "pzd,pde->pze", query_slice, current_state
        ) + outer_product_result("lqz,lzr->lqr", attention_score_slice, adjusted_result)
        current_state = current_state + outer_product_result(
            "ixl,ixr->ilr", key_slice, adjusted_result
        )
        return (current_state, produced_output)

    initial = jnp.zeros((head_count, head_width, value_width), queries.dtype)
    final_state, produced_output = lax.scan(
        advance, initial, (query_blocks, key_blocks, key_mix, value_mix, scores, starts)
    )
    return produced_output.transpose(0, 2, 1, 3).reshape(length, head_count, value_width)


def delta_core_reset(queries, keys, values, betas, block_len):
    length, head_count, head_width = queries.shape
    block_count = length // block_len

    def blocked(array):
        return array.reshape(block_count, block_len, head_count, -1).transpose(0, 2, 1, 3)

    query_blocks = blocked(queries)
    key_blocks = blocked(keys)
    value_blocks = blocked(values)
    beta_blocks = betas.reshape(block_count, block_len, head_count).transpose(0, 2, 1)[..., None]
    position = jnp.arange(block_len)
    strict = (position[:, None] > position[None, :]).astype(queries.dtype)
    causal = (position[:, None] >= position[None, :]).astype(queries.dtype)
    weighted = key_blocks * beta_blocks
    negative = -outer_product_result("nhik,nhjk->nhij", weighted, key_blocks) * strict
    inverse = jnp.eye(block_len, dtype=queries.dtype) + negative
    power_term = negative
    for doubling in range(5):
        power_term = outer_product_result("nhij,nhjk->nhik", power_term, power_term)
        inverse = inverse + outer_product_result("nhij,nhjk->nhik", inverse, power_term)
    value_mix = outer_product_result("nhij,nhjk->nhik", inverse, value_blocks * beta_blocks)
    scores = outer_product_result("nhik,nhjk->nhij", query_blocks, key_blocks) * causal
    produced_output = outer_product_result("nhqz,nhzr->nhqr", scores, value_mix)
    return produced_output.transpose(0, 2, 1, 3).reshape(length, head_count, -1)


def mixer_core(
    query_lin, key_lin, value_lin, gate_lin, beta_lin, conv_taps, head_scale, starts, reset_len
):
    length = query_lin.shape[0]
    head_count = beta_lin.shape[1]
    head_width = query_lin.shape[1] // head_count
    queries = jax.nn.silu(short_conv(query_lin, conv_taps[0], starts)).reshape(
        length, head_count, head_width
    )
    keys = jax.nn.silu(short_conv(key_lin, conv_taps[1], starts)).reshape(
        length, head_count, head_width
    )
    values = jax.nn.silu(short_conv(value_lin, conv_taps[2], starts)).reshape(
        length, head_count, head_width
    )
    queries = (
        queries
        * lax.rsqrt(jnp.sum(queries * queries, axis=-1, keepdims=True) + 1e-06)
        * head_width ** (-0.5)
    )
    keys = keys * lax.rsqrt(jnp.sum(keys * keys, axis=-1, keepdims=True) + 1e-06)
    if reset_len:
        recurrent = delta_core_reset(queries, keys, values, jax.nn.sigmoid(beta_lin), reset_len)
    else:
        recurrent = delta_core(queries, keys, values, jax.nn.sigmoid(beta_lin), starts)
    normed = (
        recurrent
        * lax.rsqrt(jnp.mean(recurrent * recurrent, axis=-1, keepdims=True) + 1e-05)
        * head_scale
    )
    gated_out = normed * jax.nn.silu(gate_lin.reshape(length, head_count, head_width))
    return gated_out.reshape(length, head_count * head_width)


def swiglu_mix(gate_act, up_act):
    return jax.nn.silu(gate_act) * up_act


def matmul_rows(left, right):
    return jnp.dot(left, right, preferred_element_type=jnp.float32)


def left_product(first, second):
    return jnp.einsum("tf,tg->fg", first, second, preferred_element_type=jnp.float32)


def back_product(gradient, weight):
    return jnp.einsum("tg,fg->tf", gradient, weight, preferred_element_type=jnp.float32)


def tp_gather(value, axis):
    tp = lax.psum(1, TP_AXES)
    spread = jnp.broadcast_to(
        jnp.expand_dims(value, axis), value.shape[:axis] + (tp,) + value.shape[axis:]
    )
    moved = lax.all_to_all(spread, TP_AXES, axis, axis, tiled=True)
    shape = list(value.shape)
    shape[axis] *= tp
    return moved.reshape(shape)


def tp_scatter_low(value, axis):
    tp = lax.psum(1, TP_AXES)
    shape = list(value.shape)
    staged = value.astype(jnp.bfloat16).reshape(
        shape[:axis] + [tp, shape[axis] // tp] + shape[axis + 1 :]
    )
    moved = lax.all_to_all(staged, TP_AXES, axis, axis, tiled=True)
    return jnp.sum(moved.astype(jnp.float32), axis=axis)


def fsdp_gather(value, axis):
    return lax.all_gather(value, FSDP_AXES, axis=axis, tiled=True)


def fsdp_scatter_low(value, axis):
    return lax.psum_scatter(
        value.astype(jnp.bfloat16), FSDP_AXES, scatter_dimension=axis, tiled=True
    )


def exchange(value, axes, split_axis, concat_axis):
    if not axes:
        return value
    return lax.all_to_all(value, axes, split_axis, concat_axis, tiled=True)


def heads_to_rows(values, tp, fsdp, rows):
    count = values.shape[0]
    staged = values.reshape(count, 1, fsdp // tp, tp, rows)
    moved = exchange(staged, TP_AXES, 3, 1)
    return moved.reshape(count, fsdp * rows)


def rows_to_heads(values, tp, fsdp, rows):
    count = values.shape[0]
    staged = values.reshape(count, tp, fsdp // tp, 1, rows)
    moved = exchange(staged, TP_AXES, 1, 3)
    return moved.reshape(count, fsdp * rows)


def padded_rows(flat, slices, width):
    extra = -(-flat.shape[0] // (slices * width))
    extra = -(-extra // 16) * 16
    filled = jnp.pad(flat, (0, slices * extra * width - flat.shape[0]))
    return filled.reshape(slices, extra, width)


def make_on_device(tp, fsdp, inner):
    def on_device(
        tokens,
        cotangent,
        group_start,
        pad_mask,
        query_weight,
        key_weight,
        value_weight,
        gate_weight,
        beta_weight,
        out_weight,
        conv_weight,
        mixer_gain,
        head_gain,
        swiglu_gain,
        swiglu_gate,
        swiglu_up,
        swiglu_down,
    ):
        micro_count, slot, width = tokens.shape
        n_all = tp * fsdp
        rows = query_weight.shape[0]
        head_count = beta_weight.shape[1]
        heads_here = head_count // tp
        cols_here = width // tp
        group_rows = tp * rows
        position = lax.axis_index(TP_AXES)
        head_scale = head_gain.astype(jnp.float32)
        reset_len = slot if group_start.shape[1] == 1 else 0

        column_owned = jnp.stack([query_weight, key_weight, value_weight, gate_weight])
        column_swapped = exchange(
            column_owned.reshape(4, rows, tp, cols_here), TP_AXES, 2, 1
        ).reshape(4, group_rows, cols_here)
        mixer_stack = jnp.concatenate(
            [column_swapped, out_weight.reshape(1, group_rows, cols_here)], axis=0
        )
        weight_all = fsdp_gather(mixer_stack, 1)
        query_cols, key_cols, value_cols, gate_cols = (weight_all[index] for index in range(4))
        out_rows = weight_all[4].reshape(fsdp * rows, width)
        small_pack = jnp.concatenate(
            [
                conv_weight.reshape(-1),
                beta_weight.reshape(-1),
                mixer_gain.reshape(-1),
                swiglu_gain.reshape(-1),
            ]
        )
        small_size = small_pack.shape[0]
        small_all = exchange(
            jnp.broadcast_to(small_pack[None, :], (n_all, small_size)), ALL_AXES, 0, 0
        )
        conv_size = conv_weight.size
        beta_size = beta_weight.size
        conv_full = (
            small_all[:, :conv_size]
            .reshape((n_all,) + conv_weight.shape)
            .transpose(1, 2, 0, 3)
            .reshape(conv_weight.shape[0], conv_weight.shape[1], -1)
        )
        beta_full = small_all[:, conv_size : conv_size + beta_size].reshape(-1, head_count)
        gain_mixer = small_all[:, conv_size + beta_size : conv_size + beta_size + rows].reshape(-1)
        gain_swiglu = small_all[:, conv_size + beta_size + rows :].reshape(-1)
        conv_here = lax.dynamic_slice_in_dim(
            conv_full.astype(jnp.float32), position * cols_here, cols_here, axis=2
        )
        beta_here = lax.dynamic_slice_in_dim(beta_full, position * heads_here, heads_here, axis=1)

        owned_rows, hidden_half = swiglu_gate.shape
        hidden_here = hidden_half // inner
        ff_owned = jnp.stack([swiglu_gate, swiglu_up, swiglu_down.T]).reshape(
            3, owned_rows, inner, hidden_here
        )
        lanes = hidden_here // 128 if hidden_here % 128 == 0 else 0
        first = (lanes - lanes * 2 // 11) * 128 if lanes > 1 else hidden_here // 2
        bounds = ((0, first), (first, hidden_here - first))
        ff_chunks = []
        for offset, size in bounds:
            swapped = exchange(ff_owned[..., offset : offset + size], INNER_AXES, 2, 1)
            ff_chunks.append(fsdp_gather(swapped.reshape(3, inner * owned_rows, size), 1))

        inputs = tokens.astype(jnp.float32).reshape(micro_count * slot, width)
        normed, norm_back = jax.vjp(rms_norm, inputs, gain_mixer.astype(jnp.float32))
        normed_low = normed.astype(jnp.bfloat16)
        group_tokens = micro_count * slot * tp
        normed_group = tp_gather(normed_low.reshape(micro_count, slot, width), 1).reshape(
            group_tokens, width
        )
        starts = tp_gather(group_start, 1).reshape(-1)

        query_lin = matmul_rows(normed_group, query_cols)
        key_lin = matmul_rows(normed_group, key_cols)
        value_lin = matmul_rows(normed_group, value_cols)
        gate_lin = matmul_rows(normed_group, gate_cols)
        beta_lin = matmul_rows(normed_group, beta_here)

        def core_at(query_in, key_in, value_in, gate_in, beta_in, conv_in, head_in):
            return mixer_core(
                query_in, key_in, value_in, gate_in, beta_in, conv_in, head_in, starts, reset_len
            )

        gated_out, core_back = jax.vjp(
            core_at, query_lin, key_lin, value_lin, gate_lin, beta_lin, conv_here, head_scale
        )
        gated_low = gated_out.astype(jnp.bfloat16)
        gated_rows = heads_to_rows(gated_low, tp, fsdp, rows)
        mixed_partial = matmul_rows(gated_rows, out_rows)
        residual = inputs + tp_scatter_low(
            mixed_partial.reshape(micro_count, slot * tp, width), 1
        ).reshape(micro_count * slot, width)

        inner_norm, inner_norm_back = jax.vjp(rms_norm, residual, gain_swiglu.astype(jnp.float32))
        inner_low = inner_norm.astype(jnp.bfloat16)
        inner_group = tp_gather(inner_low.reshape(micro_count, slot, width), 1).reshape(
            group_tokens, width
        )
        out_back = cotangent.astype(jnp.float32) * pad_mask.astype(jnp.float32)[:, :, None]
        out_back_low = out_back.astype(jnp.bfloat16)
        upstream_group = tp_gather(out_back_low, 1).reshape(group_tokens, width)
        partial_rows = None
        inner_part = None
        ff_reduced = []
        for index, chunk_weights in enumerate(ff_chunks):
            if index > 0:
                sums_low, chunk_weights = lax.optimization_barrier((sums_low, chunk_weights))
            gate_piece, up_piece, down_piece_t = chunk_weights[0], chunk_weights[1], chunk_weights[2]
            gate_act = matmul_rows(inner_group, gate_piece)
            up_act = matmul_rows(inner_group, up_piece)
            hidden, hidden_back = jax.vjp(swiglu_mix, gate_act, up_act)
            hidden_low = hidden.astype(jnp.bfloat16)
            piece_rows = back_product(hidden_low, down_piece_t)
            partial_rows = piece_rows if partial_rows is None else partial_rows + piece_rows
            gate_back, up_back = hidden_back(matmul_rows(upstream_group, down_piece_t))
            gate_back_low = gate_back.astype(jnp.bfloat16)
            up_back_low = up_back.astype(jnp.bfloat16)
            piece_part = back_product(gate_back_low, gate_piece) + back_product(up_back_low, up_piece)
            inner_part = piece_part if inner_part is None else inner_part + piece_part
            sums_low = jnp.stack(
                [
                    left_product(inner_group, gate_back_low),
                    left_product(inner_group, up_back_low),
                    left_product(upstream_group, hidden_low),
                ]
            ).astype(jnp.bfloat16)
            ff_reduced.append(fsdp_scatter_low(sums_low, 1))
        branch_rows = tp_scatter_low(partial_rows.reshape(micro_count, slot * tp, width), 1)
        block_out = (residual.reshape(micro_count, slot, width) + branch_rows).astype(jnp.bfloat16)
        inner_back = tp_scatter_low(inner_part.reshape(micro_count, slot * tp, width), 1)
        block_out, inner_back = lax.optimization_barrier((block_out, inner_back))

        residual_part, swiglu_gain_term = inner_norm_back(
            inner_back.reshape(micro_count * slot, width)
        )
        residual_back = out_back.reshape(micro_count * slot, width) + residual_part
        mixed_back = residual_back.astype(jnp.bfloat16)
        mixed_group = tp_gather(mixed_back.reshape(micro_count, slot, width), 1).reshape(
            group_tokens, width
        )
        gated_back_rows = back_product(mixed_group, out_rows)
        gated_back = rows_to_heads(gated_back_rows, tp, fsdp, rows)
        query_back, key_back, value_back, gate_lin_back, beta_back, conv_term, head_term = (
            core_back(gated_back)
        )
        query_low = query_back.astype(jnp.bfloat16)
        key_low = key_back.astype(jnp.bfloat16)
        value_low = value_back.astype(jnp.bfloat16)
        gate_low = gate_lin_back.astype(jnp.bfloat16)
        beta_low = beta_back.astype(jnp.bfloat16)
        mixer_sums = jnp.stack(
            [
                left_product(normed_group, query_low),
                left_product(normed_group, key_low),
                left_product(normed_group, value_low),
                left_product(normed_group, gate_low),
                left_product(gated_rows, mixed_group).reshape(width, cols_here),
            ]
        )
        ff_reduced, mixer_sums = lax.optimization_barrier((ff_reduced, mixer_sums))
        mixer_reduced = fsdp_scatter_low(mixer_sums, 1)
        ff_back = jnp.concatenate(
            [
                exchange(
                    piece.reshape(3, inner, owned_rows, 1, size), INNER_AXES, 1, 3
                ).reshape(3, owned_rows, inner, size)
                for piece, (offset, size) in zip(ff_reduced, bounds)
            ],
            axis=3,
        ).reshape(3, owned_rows, hidden_half).astype(jnp.float32)
        swiglu_gate_grad = ff_back[0]
        swiglu_up_grad = ff_back[1]
        swiglu_down_grad = ff_back[2].T

        normed_part = (
            back_product(query_low, query_cols)
            + back_product(key_low, key_cols)
            + back_product(value_low, value_cols)
            + back_product(gate_low, gate_cols)
            + back_product(beta_low, beta_here)
        )
        normed_back = tp_scatter_low(normed_part.reshape(micro_count, slot * tp, width), 1)
        input_part, mixer_gain_term = norm_back(normed_back.reshape(micro_count * slot, width))
        tokens_grad = (residual_back + input_part).reshape(micro_count, slot, width)

        beta_sum = left_product(normed_group, beta_low)
        beta_wide = lax.dynamic_update_slice_in_dim(
            jnp.zeros((width, head_count), jnp.float32), beta_sum, position * heads_here, axis=1
        )
        conv_wide = lax.dynamic_update_slice_in_dim(
            jnp.zeros(conv_full.shape, jnp.float32), conv_term, position * cols_here, axis=2
        )
        taps = conv_wide.shape[0] * conv_wide.shape[1]
        small_terms = jnp.concatenate(
            [
                conv_wide.reshape(taps, n_all, -1).transpose(1, 0, 2).reshape(n_all, -1),
                beta_wide.reshape(n_all, -1),
                mixer_gain_term.reshape(n_all, -1),
                swiglu_gain_term.reshape(n_all, -1),
                jnp.broadcast_to(head_term[None, :], (n_all, head_term.shape[0])),
            ],
            axis=1,
        )
        small_width = small_terms.shape[1]
        small_out = jnp.sum(exchange(small_terms, ALL_AXES, 0, 0), axis=0)
        column_back = exchange(
            mixer_reduced[:4].reshape(4, tp, rows, 1, cols_here), TP_AXES, 1, 3
        ).reshape(4, rows, width).astype(jnp.float32)
        query_grad, key_grad, value_grad, gate_grad = (column_back[index] for index in range(4))
        out_grad = mixer_reduced[4].reshape(rows, width).astype(jnp.float32)
        conv_grad = small_out[:conv_size].reshape(conv_weight.shape)
        beta_grad = small_out[conv_size : conv_size + beta_size].reshape(beta_weight.shape)
        mixer_gain_grad = small_out[conv_size + beta_size : conv_size + beta_size + rows]
        swiglu_gain_grad = small_out[conv_size + beta_size + rows : conv_size + beta_size + 2 * rows]
        head_total = small_out[conv_size + beta_size + 2 * rows :]
        return (
            block_out,
            tokens_grad,
            query_grad,
            key_grad,
            value_grad,
            gate_grad,
            beta_grad,
            out_grad,
            conv_grad,
            mixer_gain_grad,
            head_total,
            swiglu_gain_grad,
            swiglu_gate_grad,
            swiglu_up_grad,
            swiglu_down_grad,
        )

    return on_device


def solution(mesh):
    n_dp = mesh.shape["dp"]
    n_mlp = mesh.shape["mlp"]
    devices = np.asarray(mesh.devices).reshape(n_dp // 2, 2, n_mlp)
    split_mesh = Mesh(devices, ALL_AXES)
    sizes = dict(zip(ALL_AXES, devices.shape))
    tp = int(np.prod([sizes[name] for name in TP_AXES]))
    fsdp = int(np.prod([sizes[name] for name in FSDP_AXES]))
    inner = int(np.prod([sizes[name] for name in INNER_AXES]))
    rows_axes = ALL_AXES
    swiglu_rows = ("dq", "core")
    placed = (
        P(None, rows_axes, None),
        P(None, rows_axes, None),
        P(None, rows_axes),
        P(None, rows_axes),
        P(rows_axes, None),
        P(rows_axes, None),
        P(rows_axes, None),
        P(rows_axes, None),
        P(rows_axes, None),
        P(rows_axes, None),
        P(None, None, rows_axes),
        P(rows_axes),
        P(),
        P(rows_axes),
        P(swiglu_rows, "mlp"),
        P(swiglu_rows, "mlp"),
        P("mlp", swiglu_rows),
    )
    return jax.shard_map(
        make_on_device(tp, fsdp, inner),
        mesh=split_mesh,
        in_specs=placed,
        out_specs=(
            P(None, rows_axes, None),
            P(None, rows_axes, None),
            P(rows_axes, None),
            P(rows_axes, None),
            P(rows_axes, None),
            P(rows_axes, None),
            P(rows_axes, None),
            P(rows_axes, None),
            P(None, None, rows_axes),
            P(rows_axes),
            P(),
            P(rows_axes),
            P(swiglu_rows, "mlp"),
            P(swiglu_rows, "mlp"),
            P("mlp", swiglu_rows),
        ),
        check_vma=False,
    )
```

```python
import jax
import jax.numpy as jnp
import numpy as np
from jax import lax
from jax.sharding import Mesh
from jax.sharding import PartitionSpec as P

TP_AXES = ("core", "mlp")
ALL_AXES = ("dq", "core", "mlp")
FSDP_AXES = tuple(name for name in ALL_AXES if name not in TP_AXES)
INNER_AXES = tuple(name for name in TP_AXES if name != "mlp")


def rms_norm(values, scale_gain):
    return (
        values * lax.rsqrt(jnp.mean(values * values, axis=-1, keepdims=True) + 1e-06) * scale_gain
    )


def short_conv(linear, tap_weights, starts):
    length = linear.shape[0]
    block_len = length // starts.shape[0]
    position = jnp.arange(length)
    restart = jnp.repeat(starts, block_len)
    summed = linear * tap_weights[0]
    for offset in range(1, tap_weights.shape[0]):
        shifted = jnp.concatenate(
            [jnp.zeros((offset, linear.shape[1]), linear.dtype), linear[: length - offset]], axis=0
        )
        usable = ((position % block_len >= offset) | (restart == 0)).astype(linear.dtype)
        summed = summed + shifted * tap_weights[offset] * usable[:, None]
    return summed


def outer_product_result(form, first, second):
    return jnp.einsum(form, first, second, precision=lax.Precision.HIGHEST)


def delta_core(queries, keys, values, betas, starts):
    length, head_count, head_width = queries.shape
    value_width = values.shape[2]
    block_count = starts.shape[0]
    block_len = length // block_count

    def blocked(array):
        return array.reshape(block_count, block_len, head_count, -1).transpose(0, 2, 1, 3)

    query_blocks = blocked(queries)
    key_blocks = blocked(keys)
    value_blocks = blocked(values)
    beta_blocks = betas.reshape(block_count, block_len, head_count).transpose(0, 2, 1)[..., None]
    position = jnp.arange(block_len)
    strict = (position[:, None] > position[None, :]).astype(queries.dtype)
    causal = (position[:, None] >= position[None, :]).astype(queries.dtype)
    weighted = key_blocks * beta_blocks
    negative = -outer_product_result("nhik,nhjk->nhij", weighted, key_blocks) * strict
    inverse = jnp.eye(block_len, dtype=queries.dtype) + negative
    power_term = negative
    for doubling in range(5):
        power_term = outer_product_result("nhij,nhjk->nhik", power_term, power_term)
        inverse = inverse + outer_product_result("nhij,nhjk->nhik", inverse, power_term)
    key_mix = outer_product_result("nhij,nhjk->nhik", inverse, weighted)
    value_mix = outer_product_result("nhij,nhjk->nhik", inverse, value_blocks * beta_blocks)
    scores = outer_product_result("nhik,nhjk->nhij", query_blocks, key_blocks) * causal

    def advance(current_state, block_items):
        (
            query_slice,
            key_slice,
            key_mixture_slice,
            value_mixture_slice,
            attention_score_slice,
            restart,
        ) = block_items
        current_state = current_state * (1 - restart).astype(current_state.dtype)
        adjusted_result = value_mixture_slice - outer_product_result(
            "pzd,pde->pze", key_mixture_slice, current_state
        )
        produced_output = outer_product_result(
            "pzd,pde->pze", query_slice, current_state
        ) + outer_product_result("lqz,lzr->lqr", attention_score_slice, adjusted_result)
        current_state = current_state + outer_product_result(
            "ixl,ixr->ilr", key_slice, adjusted_result
        )
        return (current_state, produced_output)

    initial = jnp.zeros((head_count, head_width, value_width), queries.dtype)
    final_state, produced_output = lax.scan(
        advance, initial, (query_blocks, key_blocks, key_mix, value_mix, scores, starts)
    )
    return produced_output.transpose(0, 2, 1, 3).reshape(length, head_count, value_width)


def delta_core_reset(queries, keys, values, betas, block_len):
    length, head_count, head_width = queries.shape
    block_count = length // block_len

    def blocked(array):
        return array.reshape(block_count, block_len, head_count, -1).transpose(0, 2, 1, 3)

    query_blocks = blocked(queries)
    key_blocks = blocked(keys)
    value_blocks = blocked(values)
    beta_blocks = betas.reshape(block_count, block_len, head_count).transpose(0, 2, 1)[..., None]
    position = jnp.arange(block_len)
    strict = (position[:, None] > position[None, :]).astype(queries.dtype)
    causal = (position[:, None] >= position[None, :]).astype(queries.dtype)
    weighted = key_blocks * beta_blocks
    negative = -outer_product_result("nhik,nhjk->nhij", weighted, key_blocks) * strict
    inverse = jnp.eye(block_len, dtype=queries.dtype) + negative
    power_term = negative
    for doubling in range(5):
        power_term = outer_product_result("nhij,nhjk->nhik", power_term, power_term)
        inverse = inverse + outer_product_result("nhij,nhjk->nhik", inverse, power_term)
    value_mix = outer_product_result("nhij,nhjk->nhik", inverse, value_blocks * beta_blocks)
    scores = outer_product_result("nhik,nhjk->nhij", query_blocks, key_blocks) * causal
    produced_output = outer_product_result("nhqz,nhzr->nhqr", scores, value_mix)
    return produced_output.transpose(0, 2, 1, 3).reshape(length, head_count, -1)


def mixer_core(
    query_lin, key_lin, value_lin, gate_lin, beta_lin, conv_taps, head_scale, starts, reset_len
):
    length = query_lin.shape[0]
    head_count = beta_lin.shape[1]
    head_width = query_lin.shape[1] // head_count
    queries = jax.nn.silu(short_conv(query_lin, conv_taps[0], starts)).reshape(
        length, head_count, head_width
    )
    keys = jax.nn.silu(short_conv(key_lin, conv_taps[1], starts)).reshape(
        length, head_count, head_width
    )
    values = jax.nn.silu(short_conv(value_lin, conv_taps[2], starts)).reshape(
        length, head_count, head_width
    )
    queries = (
        queries
        * lax.rsqrt(jnp.sum(queries * queries, axis=-1, keepdims=True) + 1e-06)
        * head_width ** (-0.5)
    )
    keys = keys * lax.rsqrt(jnp.sum(keys * keys, axis=-1, keepdims=True) + 1e-06)
    if reset_len:
        recurrent = delta_core_reset(queries, keys, values, jax.nn.sigmoid(beta_lin), reset_len)
    else:
        recurrent = delta_core(queries, keys, values, jax.nn.sigmoid(beta_lin), starts)
    normed = (
        recurrent
        * lax.rsqrt(jnp.mean(recurrent * recurrent, axis=-1, keepdims=True) + 1e-05)
        * head_scale
    )
    gated_out = normed * jax.nn.silu(gate_lin.reshape(length, head_count, head_width))
    return gated_out.reshape(length, head_count * head_width)


def swiglu_mix(gate_act, up_act):
    return jax.nn.silu(gate_act) * up_act


def matmul_rows(left, right):
    return jnp.dot(left, right, preferred_element_type=jnp.float32)


def left_product(first, second):
    return jnp.einsum("tf,tg->fg", first, second, preferred_element_type=jnp.float32)


def back_product(gradient, weight):
    return jnp.einsum("tg,fg->tf", gradient, weight, preferred_element_type=jnp.float32)


def tp_gather(value, axis):
    tp = lax.psum(1, TP_AXES)
    spread = jnp.broadcast_to(
        jnp.expand_dims(value, axis), value.shape[:axis] + (tp,) + value.shape[axis:]
    )
    moved = lax.all_to_all(spread, TP_AXES, axis, axis, tiled=True)
    shape = list(value.shape)
    shape[axis] *= tp
    return moved.reshape(shape)


def tp_scatter_low(value, axis):
    tp = lax.psum(1, TP_AXES)
    shape = list(value.shape)
    staged = value.astype(jnp.bfloat16).reshape(
        shape[:axis] + [tp, shape[axis] // tp] + shape[axis + 1 :]
    )
    moved = lax.all_to_all(staged, TP_AXES, axis, axis, tiled=True)
    return jnp.sum(moved.astype(jnp.float32), axis=axis)


def fsdp_gather(value, axis):
    return lax.all_gather(value, FSDP_AXES, axis=axis, tiled=True)


def fsdp_scatter_low(value, axis):
    return lax.psum_scatter(
        value.astype(jnp.bfloat16), FSDP_AXES, scatter_dimension=axis, tiled=True
    )


def exchange(value, axes, split_axis, concat_axis):
    if not axes:
        return value
    return lax.all_to_all(value, axes, split_axis, concat_axis, tiled=True)


def heads_to_rows(values, tp, fsdp, rows):
    count = values.shape[0]
    staged = values.reshape(count, 1, fsdp // tp, tp, rows)
    moved = exchange(staged, TP_AXES, 3, 1)
    return moved.reshape(count, fsdp * rows)


def rows_to_heads(values, tp, fsdp, rows):
    count = values.shape[0]
    staged = values.reshape(count, tp, fsdp // tp, 1, rows)
    moved = exchange(staged, TP_AXES, 1, 3)
    return moved.reshape(count, fsdp * rows)


def padded_rows(flat, slices, width):
    extra = -(-flat.shape[0] // (slices * width))
    extra = -(-extra // 16) * 16
    filled = jnp.pad(flat, (0, slices * extra * width - flat.shape[0]))
    return filled.reshape(slices, extra, width)


def make_on_device(tp, fsdp, inner):
    def on_device(
        tokens,
        cotangent,
        group_start,
        pad_mask,
        query_weight,
        key_weight,
        value_weight,
        gate_weight,
        beta_weight,
        out_weight,
        conv_weight,
        mixer_gain,
        head_gain,
        swiglu_gain,
        swiglu_gate,
        swiglu_up,
        swiglu_down,
    ):
        micro_count, slot, width = tokens.shape
        n_all = tp * fsdp
        rows = query_weight.shape[0]
        head_count = beta_weight.shape[1]
        heads_here = head_count // tp
        cols_here = width // tp
        group_rows = tp * rows
        position = lax.axis_index(TP_AXES)
        head_scale = head_gain.astype(jnp.float32)
        reset_len = slot if group_start.shape[1] == 1 else 0

        column_owned = jnp.stack([query_weight, key_weight, value_weight, gate_weight])
        column_swapped = exchange(
            column_owned.reshape(4, rows, tp, cols_here), TP_AXES, 2, 1
        ).reshape(4, group_rows, cols_here)
        mixer_stack = jnp.concatenate(
            [column_swapped, out_weight.reshape(1, group_rows, cols_here)], axis=0
        )
        weight_all = fsdp_gather(mixer_stack, 1)
        query_cols, key_cols, value_cols, gate_cols = (weight_all[index] for index in range(4))
        out_rows = weight_all[4].reshape(fsdp * rows, width)
        small_pack = jnp.concatenate(
            [
                conv_weight.reshape(-1),
                beta_weight.reshape(-1),
                mixer_gain.reshape(-1),
                swiglu_gain.reshape(-1),
            ]
        )
        small_size = small_pack.shape[0]
        small_all = exchange(
            jnp.broadcast_to(small_pack[None, :], (n_all, small_size)), ALL_AXES, 0, 0
        )
        conv_size = conv_weight.size
        beta_size = beta_weight.size
        conv_full = (
            small_all[:, :conv_size]
            .reshape((n_all,) + conv_weight.shape)
            .transpose(1, 2, 0, 3)
            .reshape(conv_weight.shape[0], conv_weight.shape[1], -1)
        )
        beta_full = small_all[:, conv_size : conv_size + beta_size].reshape(-1, head_count)
        gain_mixer = small_all[:, conv_size + beta_size : conv_size + beta_size + rows].reshape(-1)
        gain_swiglu = small_all[:, conv_size + beta_size + rows :].reshape(-1)
        conv_here = lax.dynamic_slice_in_dim(
            conv_full.astype(jnp.float32), position * cols_here, cols_here, axis=2
        )
        beta_here = lax.dynamic_slice_in_dim(beta_full, position * heads_here, heads_here, axis=1)

        owned_rows, hidden_half = swiglu_gate.shape
        hidden_here = hidden_half // inner
        ff_owned = jnp.stack([swiglu_gate, swiglu_up, swiglu_down.T]).reshape(
            3, owned_rows, inner, hidden_here
        )
        lanes = hidden_here // 128 if hidden_here % 128 == 0 else 0
        first = (lanes - lanes * 2 // 11) * 128 if lanes > 1 else hidden_here // 2
        bounds = ((0, first), (first, hidden_here - first))
        ff_chunks = []
        for offset, size in bounds:
            swapped = exchange(ff_owned[..., offset : offset + size], INNER_AXES, 2, 1)
            ff_chunks.append(fsdp_gather(swapped.reshape(3, inner * owned_rows, size), 1))

        inputs = tokens.astype(jnp.float32).reshape(micro_count * slot, width)
        normed, norm_back = jax.vjp(rms_norm, inputs, gain_mixer.astype(jnp.float32))
        normed_low = normed.astype(jnp.bfloat16)
        group_tokens = micro_count * slot * tp
        normed_group = tp_gather(normed_low.reshape(micro_count, slot, width), 1).reshape(
            group_tokens, width
        )
        starts = tp_gather(group_start, 1).reshape(-1)

        query_lin = matmul_rows(normed_group, query_cols)
        key_lin = matmul_rows(normed_group, key_cols)
        value_lin = matmul_rows(normed_group, value_cols)
        gate_lin = matmul_rows(normed_group, gate_cols)
        beta_lin = matmul_rows(normed_group, beta_here)

        def core_at(query_in, key_in, value_in, gate_in, beta_in, conv_in, head_in):
            return mixer_core(
                query_in, key_in, value_in, gate_in, beta_in, conv_in, head_in, starts, reset_len
            )

        gated_out, core_back = jax.vjp(
            core_at, query_lin, key_lin, value_lin, gate_lin, beta_lin, conv_here, head_scale
        )
        gated_low = gated_out.astype(jnp.bfloat16)
        gated_rows = heads_to_rows(gated_low, tp, fsdp, rows)
        mixed_partial = matmul_rows(gated_rows, out_rows)
        residual = inputs + tp_scatter_low(
            mixed_partial.reshape(micro_count, slot * tp, width), 1
        ).reshape(micro_count * slot, width)

        inner_norm, inner_norm_back = jax.vjp(rms_norm, residual, gain_swiglu.astype(jnp.float32))
        inner_low = inner_norm.astype(jnp.bfloat16)
        inner_group = tp_gather(inner_low.reshape(micro_count, slot, width), 1).reshape(
            group_tokens, width
        )
        out_back = cotangent.astype(jnp.float32) * pad_mask.astype(jnp.float32)[:, :, None]
        out_back_low = out_back.astype(jnp.bfloat16)
        upstream_group = tp_gather(out_back_low, 1).reshape(group_tokens, width)
        partial_rows = None
        inner_part = None
        ff_reduced = []
        for index, chunk_weights in enumerate(ff_chunks):
            if index > 0:
                sums_low, chunk_weights = lax.optimization_barrier((sums_low, chunk_weights))
            gate_piece, up_piece, down_piece_t = chunk_weights[0], chunk_weights[1], chunk_weights[2]
            gate_act = matmul_rows(inner_group, gate_piece)
            up_act = matmul_rows(inner_group, up_piece)
            hidden, hidden_back = jax.vjp(swiglu_mix, gate_act, up_act)
            hidden_low = hidden.astype(jnp.bfloat16)
            piece_rows = back_product(hidden_low, down_piece_t)
            partial_rows = piece_rows if partial_rows is None else partial_rows + piece_rows
            gate_back, up_back = hidden_back(matmul_rows(upstream_group, down_piece_t))
            gate_back_low = gate_back.astype(jnp.bfloat16)
            up_back_low = up_back.astype(jnp.bfloat16)
            piece_part = back_product(gate_back_low, gate_piece) + back_product(up_back_low, up_piece)
            inner_part = piece_part if inner_part is None else inner_part + piece_part
            sums_low = jnp.stack(
                [
                    left_product(inner_group, gate_back_low),
                    left_product(inner_group, up_back_low),
                    left_product(upstream_group, hidden_low),
                ]
            ).astype(jnp.bfloat16)
            ff_reduced.append(fsdp_scatter_low(sums_low, 1))
        branch_rows = tp_scatter_low(partial_rows.reshape(micro_count, slot * tp, width), 1)
        block_out = (residual.reshape(micro_count, slot, width) + branch_rows).astype(jnp.bfloat16)
        inner_back = tp_scatter_low(inner_part.reshape(micro_count, slot * tp, width), 1)
        block_out, inner_back = lax.optimization_barrier((block_out, inner_back))

        residual_part, swiglu_gain_term = inner_norm_back(
            inner_back.reshape(micro_count * slot, width)
        )
        residual_back = out_back.reshape(micro_count * slot, width) + residual_part
        mixed_back = residual_back.astype(jnp.bfloat16)
        mixed_group = tp_gather(mixed_back.reshape(micro_count, slot, width), 1).reshape(
            group_tokens, width
        )
        gated_back_rows = back_product(mixed_group, out_rows)
        gated_back = rows_to_heads(gated_back_rows, tp, fsdp, rows)
        query_back, key_back, value_back, gate_lin_back, beta_back, conv_term, head_term = (
            core_back(gated_back)
        )
        query_low = query_back.astype(jnp.bfloat16)
        key_low = key_back.astype(jnp.bfloat16)
        value_low = value_back.astype(jnp.bfloat16)
        gate_low = gate_lin_back.astype(jnp.bfloat16)
        beta_low = beta_back.astype(jnp.bfloat16)
        column_sums = jnp.stack(
            [
                left_product(normed_group, query_low),
                left_product(normed_group, key_low),
                left_product(normed_group, value_low),
                left_product(normed_group, gate_low),
            ]
        ).astype(jnp.bfloat16)
        column_rows = exchange(
            column_sums.reshape(4, fsdp, tp, rows, 1, cols_here), TP_AXES, 2, 4
        ).reshape(4, fsdp * rows, width)
        mixer_sums = jnp.concatenate(
            [
                column_rows,
                left_product(gated_rows, mixed_group).astype(jnp.bfloat16)[None],
            ],
            axis=0,
        )
        ff_reduced, mixer_sums = lax.optimization_barrier((ff_reduced, mixer_sums))
        mixer_reduced = fsdp_scatter_low(mixer_sums, 1)
        ff_back = jnp.concatenate(
            [
                exchange(
                    piece.reshape(3, inner, owned_rows, 1, size), INNER_AXES, 1, 3
                ).reshape(3, owned_rows, inner, size)
                for piece, (offset, size) in zip(ff_reduced, bounds)
            ],
            axis=3,
        ).reshape(3, owned_rows, hidden_half).astype(jnp.float32)
        swiglu_gate_grad = ff_back[0]
        swiglu_up_grad = ff_back[1]
        swiglu_down_grad = ff_back[2].T

        normed_part = (
            back_product(query_low, query_cols)
            + back_product(key_low, key_cols)
            + back_product(value_low, value_cols)
            + back_product(gate_low, gate_cols)
            + back_product(beta_low, beta_here)
        )
        normed_back = tp_scatter_low(normed_part.reshape(micro_count, slot * tp, width), 1)
        input_part, mixer_gain_term = norm_back(normed_back.reshape(micro_count * slot, width))
        tokens_grad = (residual_back + input_part).reshape(micro_count, slot, width)

        beta_sum = left_product(normed_group, beta_low)
        beta_wide = lax.dynamic_update_slice_in_dim(
            jnp.zeros((width, head_count), jnp.float32), beta_sum, position * heads_here, axis=1
        )
        conv_wide = lax.dynamic_update_slice_in_dim(
            jnp.zeros(conv_full.shape, jnp.float32), conv_term, position * cols_here, axis=2
        )
        taps = conv_wide.shape[0] * conv_wide.shape[1]
        small_terms = jnp.concatenate(
            [
                conv_wide.reshape(taps, n_all, -1).transpose(1, 0, 2).reshape(n_all, -1),
                beta_wide.reshape(n_all, -1),
                mixer_gain_term.reshape(n_all, -1),
                swiglu_gain_term.reshape(n_all, -1),
                jnp.broadcast_to(head_term[None, :], (n_all, head_term.shape[0])),
            ],
            axis=1,
        )
        small_width = small_terms.shape[1]
        small_out = jnp.sum(exchange(small_terms, ALL_AXES, 0, 0), axis=0)
        mixer_grads = mixer_reduced.astype(jnp.float32)
        query_grad, key_grad, value_grad, gate_grad, out_grad = (
            mixer_grads[index] for index in range(5)
        )
        conv_grad = small_out[:conv_size].reshape(conv_weight.shape)
        beta_grad = small_out[conv_size : conv_size + beta_size].reshape(beta_weight.shape)
        mixer_gain_grad = small_out[conv_size + beta_size : conv_size + beta_size + rows]
        swiglu_gain_grad = small_out[conv_size + beta_size + rows : conv_size + beta_size + 2 * rows]
        head_total = small_out[conv_size + beta_size + 2 * rows :]
        return (
            block_out,
            tokens_grad,
            query_grad,
            key_grad,
            value_grad,
            gate_grad,
            beta_grad,
            out_grad,
            conv_grad,
            mixer_gain_grad,
            head_total,
            swiglu_gain_grad,
            swiglu_gate_grad,
            swiglu_up_grad,
            swiglu_down_grad,
        )

    return on_device


def solution(mesh):
    n_dp = mesh.shape["dp"]
    n_mlp = mesh.shape["mlp"]
    devices = np.asarray(mesh.devices).reshape(n_dp // 2, 2, n_mlp)
    split_mesh = Mesh(devices, ALL_AXES)
    sizes = dict(zip(ALL_AXES, devices.shape))
    tp = int(np.prod([sizes[name] for name in TP_AXES]))
    fsdp = int(np.prod([sizes[name] for name in FSDP_AXES]))
    inner = int(np.prod([sizes[name] for name in INNER_AXES]))
    rows_axes = ALL_AXES
    swiglu_rows = ("dq", "core")
    placed = (
        P(None, rows_axes, None),
        P(None, rows_axes, None),
        P(None, rows_axes),
        P(None, rows_axes),
        P(rows_axes, None),
        P(rows_axes, None),
        P(rows_axes, None),
        P(rows_axes, None),
        P(rows_axes, None),
        P(rows_axes, None),
        P(None, None, rows_axes),
        P(rows_axes),
        P(),
        P(rows_axes),
        P(swiglu_rows, "mlp"),
        P(swiglu_rows, "mlp"),
        P("mlp", swiglu_rows),
    )
    return jax.shard_map(
        make_on_device(tp, fsdp, inner),
        mesh=split_mesh,
        in_specs=placed,
        out_specs=(
            P(None, rows_axes, None),
            P(None, rows_axes, None),
            P(rows_axes, None),
            P(rows_axes, None),
            P(rows_axes, None),
            P(rows_axes, None),
            P(rows_axes, None),
            P(rows_axes, None),
            P(None, None, rows_axes),
            P(rows_axes),
            P(),
            P(rows_axes),
            P(swiglu_rows, "mlp"),
            P(swiglu_rows, "mlp"),
            P("mlp", swiglu_rows),
        ),
        check_vma=False,
    )
```

```python
import jax
import jax.numpy as jnp
import numpy as np
from jax import lax
from jax.sharding import Mesh
from jax.sharding import PartitionSpec as P

TP_AXES = ("core", "mlp")
ALL_AXES = ("dq", "core", "mlp")
FSDP_AXES = tuple(name for name in ALL_AXES if name not in TP_AXES)
INNER_AXES = tuple(name for name in TP_AXES if name != "mlp")


def rms_norm(values, scale_gain):
    return (
        values * lax.rsqrt(jnp.mean(values * values, axis=-1, keepdims=True) + 1e-06) * scale_gain
    )


def short_conv(linear, tap_weights, starts):
    length = linear.shape[0]
    block_len = length // starts.shape[0]
    position = jnp.arange(length)
    restart = jnp.repeat(starts, block_len)
    summed = linear * tap_weights[0]
    for offset in range(1, tap_weights.shape[0]):
        shifted = jnp.concatenate(
            [jnp.zeros((offset, linear.shape[1]), linear.dtype), linear[: length - offset]], axis=0
        )
        usable = ((position % block_len >= offset) | (restart == 0)).astype(linear.dtype)
        summed = summed + shifted * tap_weights[offset] * usable[:, None]
    return summed


def outer_product_result(form, first, second):
    return jnp.einsum(form, first, second, precision=lax.Precision.HIGHEST)


def delta_core(queries, keys, values, betas, starts):
    length, head_count, head_width = queries.shape
    value_width = values.shape[2]
    block_count = starts.shape[0]
    block_len = length // block_count

    def blocked(array):
        return array.reshape(block_count, block_len, head_count, -1).transpose(0, 2, 1, 3)

    query_blocks = blocked(queries)
    key_blocks = blocked(keys)
    value_blocks = blocked(values)
    beta_blocks = betas.reshape(block_count, block_len, head_count).transpose(0, 2, 1)[..., None]
    position = jnp.arange(block_len)
    strict = (position[:, None] > position[None, :]).astype(queries.dtype)
    causal = (position[:, None] >= position[None, :]).astype(queries.dtype)
    weighted = key_blocks * beta_blocks
    negative = -outer_product_result("nhik,nhjk->nhij", weighted, key_blocks) * strict
    inverse = jnp.eye(block_len, dtype=queries.dtype) + negative
    power_term = negative
    for doubling in range(5):
        power_term = outer_product_result("nhij,nhjk->nhik", power_term, power_term)
        inverse = inverse + outer_product_result("nhij,nhjk->nhik", inverse, power_term)
    key_mix = outer_product_result("nhij,nhjk->nhik", inverse, weighted)
    value_mix = outer_product_result("nhij,nhjk->nhik", inverse, value_blocks * beta_blocks)
    scores = outer_product_result("nhik,nhjk->nhij", query_blocks, key_blocks) * causal

    def advance(current_state, block_items):
        (
            query_slice,
            key_slice,
            key_mixture_slice,
            value_mixture_slice,
            attention_score_slice,
            restart,
        ) = block_items
        current_state = current_state * (1 - restart).astype(current_state.dtype)
        adjusted_result = value_mixture_slice - outer_product_result(
            "pzd,pde->pze", key_mixture_slice, current_state
        )
        produced_output = outer_product_result(
            "pzd,pde->pze", query_slice, current_state
        ) + outer_product_result("lqz,lzr->lqr", attention_score_slice, adjusted_result)
        current_state = current_state + outer_product_result(
            "ixl,ixr->ilr", key_slice, adjusted_result
        )
        return (current_state, produced_output)

    initial = jnp.zeros((head_count, head_width, value_width), queries.dtype)
    final_state, produced_output = lax.scan(
        advance, initial, (query_blocks, key_blocks, key_mix, value_mix, scores, starts)
    )
    return produced_output.transpose(0, 2, 1, 3).reshape(length, head_count, value_width)


def delta_core_reset(queries, keys, values, betas, block_len):
    length, head_count, head_width = queries.shape
    block_count = length // block_len

    def blocked(array):
        return array.reshape(block_count, block_len, head_count, -1).transpose(0, 2, 1, 3)

    query_blocks = blocked(queries)
    key_blocks = blocked(keys)
    value_blocks = blocked(values)
    beta_blocks = betas.reshape(block_count, block_len, head_count).transpose(0, 2, 1)[..., None]
    position = jnp.arange(block_len)
    strict = (position[:, None] > position[None, :]).astype(queries.dtype)
    causal = (position[:, None] >= position[None, :]).astype(queries.dtype)
    weighted = key_blocks * beta_blocks
    negative = -outer_product_result("nhik,nhjk->nhij", weighted, key_blocks) * strict
    inverse = jnp.eye(block_len, dtype=queries.dtype) + negative
    power_term = negative
    for doubling in range(5):
        power_term = outer_product_result("nhij,nhjk->nhik", power_term, power_term)
        inverse = inverse + outer_product_result("nhij,nhjk->nhik", inverse, power_term)
    value_mix = outer_product_result("nhij,nhjk->nhik", inverse, value_blocks * beta_blocks)
    scores = outer_product_result("nhik,nhjk->nhij", query_blocks, key_blocks) * causal
    produced_output = outer_product_result("nhqz,nhzr->nhqr", scores, value_mix)
    return produced_output.transpose(0, 2, 1, 3).reshape(length, head_count, -1)


def mixer_core(
    query_lin, key_lin, value_lin, gate_lin, beta_lin, conv_taps, head_scale, starts, reset_len
):
    length = query_lin.shape[0]
    head_count = beta_lin.shape[1]
    head_width = query_lin.shape[1] // head_count
    queries = jax.nn.silu(short_conv(query_lin, conv_taps[0], starts)).reshape(
        length, head_count, head_width
    )
    keys = jax.nn.silu(short_conv(key_lin, conv_taps[1], starts)).reshape(
        length, head_count, head_width
    )
    values = jax.nn.silu(short_conv(value_lin, conv_taps[2], starts)).reshape(
        length, head_count, head_width
    )
    queries = (
        queries
        * lax.rsqrt(jnp.sum(queries * queries, axis=-1, keepdims=True) + 1e-06)
        * head_width ** (-0.5)
    )
    keys = keys * lax.rsqrt(jnp.sum(keys * keys, axis=-1, keepdims=True) + 1e-06)
    if reset_len:
        recurrent = delta_core_reset(queries, keys, values, jax.nn.sigmoid(beta_lin), reset_len)
    else:
        recurrent = delta_core(queries, keys, values, jax.nn.sigmoid(beta_lin), starts)
    normed = (
        recurrent
        * lax.rsqrt(jnp.mean(recurrent * recurrent, axis=-1, keepdims=True) + 1e-05)
        * head_scale
    )
    gated_out = normed * jax.nn.silu(gate_lin.reshape(length, head_count, head_width))
    return gated_out.reshape(length, head_count * head_width)


def swiglu_mix(gate_act, up_act):
    return jax.nn.silu(gate_act) * up_act


def matmul_rows(left, right):
    return jnp.dot(left, right, preferred_element_type=jnp.float32)


def left_product(first, second):
    return jnp.einsum("tf,tg->fg", first, second, preferred_element_type=jnp.float32)


def back_product(gradient, weight):
    return jnp.einsum("tg,fg->tf", gradient, weight, preferred_element_type=jnp.float32)


def tp_gather(value, axis):
    tp = lax.psum(1, TP_AXES)
    spread = jnp.broadcast_to(
        jnp.expand_dims(value, axis), value.shape[:axis] + (tp,) + value.shape[axis:]
    )
    moved = lax.all_to_all(spread, TP_AXES, axis, axis, tiled=True)
    shape = list(value.shape)
    shape[axis] *= tp
    return moved.reshape(shape)


def tp_scatter_low(value, axis):
    tp = lax.psum(1, TP_AXES)
    shape = list(value.shape)
    staged = value.astype(jnp.bfloat16).reshape(
        shape[:axis] + [tp, shape[axis] // tp] + shape[axis + 1 :]
    )
    moved = lax.all_to_all(staged, TP_AXES, axis, axis, tiled=True)
    return jnp.sum(moved.astype(jnp.float32), axis=axis)


def fsdp_gather(value, axis):
    return lax.all_gather(value, FSDP_AXES, axis=axis, tiled=True)


def fsdp_scatter_low(value, axis):
    return lax.psum_scatter(
        value.astype(jnp.bfloat16), FSDP_AXES, scatter_dimension=axis, tiled=True
    )


def exchange(value, axes, split_axis, concat_axis):
    if not axes:
        return value
    return lax.all_to_all(value, axes, split_axis, concat_axis, tiled=True)


def heads_to_rows(values, tp, fsdp, rows):
    count = values.shape[0]
    staged = values.reshape(count, 1, fsdp // tp, tp, rows)
    moved = exchange(staged, TP_AXES, 3, 1)
    return moved.reshape(count, fsdp * rows)


def rows_to_heads(values, tp, fsdp, rows):
    count = values.shape[0]
    staged = values.reshape(count, tp, fsdp // tp, 1, rows)
    moved = exchange(staged, TP_AXES, 1, 3)
    return moved.reshape(count, fsdp * rows)


def padded_rows(flat, slices, width):
    extra = -(-flat.shape[0] // (slices * width))
    extra = -(-extra // 16) * 16
    filled = jnp.pad(flat, (0, slices * extra * width - flat.shape[0]))
    return filled.reshape(slices, extra, width)


def make_on_device(tp, fsdp, inner):
    def on_device(
        tokens,
        cotangent,
        group_start,
        pad_mask,
        query_weight,
        key_weight,
        value_weight,
        gate_weight,
        beta_weight,
        out_weight,
        conv_weight,
        mixer_gain,
        head_gain,
        swiglu_gain,
        swiglu_gate,
        swiglu_up,
        swiglu_down,
    ):
        micro_count, slot, width = tokens.shape
        n_all = tp * fsdp
        rows = query_weight.shape[0]
        head_count = beta_weight.shape[1]
        heads_here = head_count // tp
        cols_here = width // tp
        group_rows = tp * rows
        position = lax.axis_index(TP_AXES)
        head_scale = head_gain.astype(jnp.float32)
        reset_len = slot if group_start.shape[1] == 1 else 0

        column_owned = jnp.stack([query_weight, key_weight, value_weight, gate_weight])
        column_swapped = exchange(
            column_owned.reshape(4, rows, tp, cols_here), TP_AXES, 2, 1
        ).reshape(4, group_rows, cols_here)
        mixer_stack = jnp.concatenate(
            [column_swapped, out_weight.reshape(1, group_rows, cols_here)], axis=0
        )
        weight_all = fsdp_gather(mixer_stack, 1)
        query_cols, key_cols, value_cols, gate_cols = (weight_all[index] for index in range(4))
        out_rows = weight_all[4].reshape(fsdp * rows, width)
        small_pack = jnp.concatenate(
            [
                conv_weight.reshape(-1),
                beta_weight.reshape(-1),
                mixer_gain.reshape(-1),
                swiglu_gain.reshape(-1),
            ]
        )
        small_size = small_pack.shape[0]
        small_all = exchange(
            jnp.broadcast_to(small_pack[None, :], (n_all, small_size)), ALL_AXES, 0, 0
        )
        conv_size = conv_weight.size
        beta_size = beta_weight.size
        conv_full = (
            small_all[:, :conv_size]
            .reshape((n_all,) + conv_weight.shape)
            .transpose(1, 2, 0, 3)
            .reshape(conv_weight.shape[0], conv_weight.shape[1], -1)
        )
        beta_full = small_all[:, conv_size : conv_size + beta_size].reshape(-1, head_count)
        gain_mixer = small_all[:, conv_size + beta_size : conv_size + beta_size + rows].reshape(-1)
        gain_swiglu = small_all[:, conv_size + beta_size + rows :].reshape(-1)
        conv_here = lax.dynamic_slice_in_dim(
            conv_full.astype(jnp.float32), position * cols_here, cols_here, axis=2
        )
        beta_here = lax.dynamic_slice_in_dim(beta_full, position * heads_here, heads_here, axis=1)

        owned_rows, hidden_half = swiglu_gate.shape
        hidden_here = hidden_half // inner
        ff_owned = jnp.stack([swiglu_gate, swiglu_up, swiglu_down.T]).reshape(
            3, owned_rows, inner, hidden_here
        )
        lanes = hidden_here // 128 if hidden_here % 128 == 0 else 0
        first = (lanes - 1) * 128 if lanes > 1 else hidden_here // 2
        bounds = ((0, first), (first, hidden_here - first))
        ff_chunks = []
        for offset, size in bounds:
            swapped = exchange(ff_owned[..., offset : offset + size], INNER_AXES, 2, 1)
            ff_chunks.append(fsdp_gather(swapped.reshape(3, inner * owned_rows, size), 1))

        inputs = tokens.astype(jnp.float32).reshape(micro_count * slot, width)
        normed, norm_back = jax.vjp(rms_norm, inputs, gain_mixer.astype(jnp.float32))
        normed_low = normed.astype(jnp.bfloat16)
        group_tokens = micro_count * slot * tp
        normed_group = tp_gather(normed_low.reshape(micro_count, slot, width), 1).reshape(
            group_tokens, width
        )
        starts = tp_gather(group_start, 1).reshape(-1)

        query_lin = matmul_rows(normed_group, query_cols)
        key_lin = matmul_rows(normed_group, key_cols)
        value_lin = matmul_rows(normed_group, value_cols)
        gate_lin = matmul_rows(normed_group, gate_cols)
        beta_lin = matmul_rows(normed_group, beta_here)

        def core_at(query_in, key_in, value_in, gate_in, beta_in, conv_in, head_in):
            return mixer_core(
                query_in, key_in, value_in, gate_in, beta_in, conv_in, head_in, starts, reset_len
            )

        gated_out, core_back = jax.vjp(
            core_at, query_lin, key_lin, value_lin, gate_lin, beta_lin, conv_here, head_scale
        )
        gated_low = gated_out.astype(jnp.bfloat16)
        gated_rows = heads_to_rows(gated_low, tp, fsdp, rows)
        mixed_partial = matmul_rows(gated_rows, out_rows)
        residual = inputs + tp_scatter_low(
            mixed_partial.reshape(micro_count, slot * tp, width), 1
        ).reshape(micro_count * slot, width)

        inner_norm, inner_norm_back = jax.vjp(rms_norm, residual, gain_swiglu.astype(jnp.float32))
        inner_low = inner_norm.astype(jnp.bfloat16)
        inner_group = tp_gather(inner_low.reshape(micro_count, slot, width), 1).reshape(
            group_tokens, width
        )
        out_back = cotangent.astype(jnp.float32) * pad_mask.astype(jnp.float32)[:, :, None]
        out_back_low = out_back.astype(jnp.bfloat16)
        upstream_group = tp_gather(out_back_low, 1).reshape(group_tokens, width)
        partial_rows = None
        inner_part = None
        ff_reduced = []
        for index, chunk_weights in enumerate(ff_chunks):
            if index > 0:
                sums_low, chunk_weights = lax.optimization_barrier((sums_low, chunk_weights))
            gate_piece, up_piece, down_piece_t = chunk_weights[0], chunk_weights[1], chunk_weights[2]
            gate_act = matmul_rows(inner_group, gate_piece)
            up_act = matmul_rows(inner_group, up_piece)
            hidden, hidden_back = jax.vjp(swiglu_mix, gate_act, up_act)
            hidden_low = hidden.astype(jnp.bfloat16)
            piece_rows = back_product(hidden_low, down_piece_t)
            partial_rows = piece_rows if partial_rows is None else partial_rows + piece_rows
            gate_back, up_back = hidden_back(matmul_rows(upstream_group, down_piece_t))
            gate_back_low = gate_back.astype(jnp.bfloat16)
            up_back_low = up_back.astype(jnp.bfloat16)
            piece_part = back_product(gate_back_low, gate_piece) + back_product(up_back_low, up_piece)
            inner_part = piece_part if inner_part is None else inner_part + piece_part
            sums_low = jnp.stack(
                [
                    left_product(inner_group, gate_back_low),
                    left_product(inner_group, up_back_low),
                    left_product(upstream_group, hidden_low),
                ]
            ).astype(jnp.bfloat16)
            ff_reduced.append(fsdp_scatter_low(sums_low, 1))
        branch_rows = tp_scatter_low(partial_rows.reshape(micro_count, slot * tp, width), 1)
        block_out = (residual.reshape(micro_count, slot, width) + branch_rows).astype(jnp.bfloat16)
        inner_back = tp_scatter_low(inner_part.reshape(micro_count, slot * tp, width), 1)
        block_out, inner_back = lax.optimization_barrier((block_out, inner_back))

        residual_part, swiglu_gain_term = inner_norm_back(
            inner_back.reshape(micro_count * slot, width)
        )
        residual_back = out_back.reshape(micro_count * slot, width) + residual_part
        mixed_back = residual_back.astype(jnp.bfloat16)
        mixed_group = tp_gather(mixed_back.reshape(micro_count, slot, width), 1).reshape(
            group_tokens, width
        )
        gated_back_rows = back_product(mixed_group, out_rows)
        gated_back = rows_to_heads(gated_back_rows, tp, fsdp, rows)
        query_back, key_back, value_back, gate_lin_back, beta_back, conv_term, head_term = (
            core_back(gated_back)
        )
        query_low = query_back.astype(jnp.bfloat16)
        key_low = key_back.astype(jnp.bfloat16)
        value_low = value_back.astype(jnp.bfloat16)
        gate_low = gate_lin_back.astype(jnp.bfloat16)
        beta_low = beta_back.astype(jnp.bfloat16)
        mixer_sums = jnp.stack(
            [
                left_product(normed_group, query_low),
                left_product(normed_group, key_low),
                left_product(normed_group, value_low),
                left_product(normed_group, gate_low),
                left_product(gated_rows, mixed_group).reshape(width, cols_here),
            ]
        )
        ff_reduced, mixer_sums = lax.optimization_barrier((ff_reduced, mixer_sums))
        mixer_reduced = fsdp_scatter_low(mixer_sums, 1)
        ff_back = jnp.concatenate(
            [
                exchange(
                    piece.reshape(3, inner, owned_rows, 1, size), INNER_AXES, 1, 3
                ).reshape(3, owned_rows, inner, size)
                for piece, (offset, size) in zip(ff_reduced, bounds)
            ],
            axis=3,
        ).reshape(3, owned_rows, hidden_half).astype(jnp.float32)
        swiglu_gate_grad = ff_back[0]
        swiglu_up_grad = ff_back[1]
        swiglu_down_grad = ff_back[2].T

        normed_part = (
            back_product(query_low, query_cols)
            + back_product(key_low, key_cols)
            + back_product(value_low, value_cols)
            + back_product(gate_low, gate_cols)
            + back_product(beta_low, beta_here)
        )
        normed_back = tp_scatter_low(normed_part.reshape(micro_count, slot * tp, width), 1)
        input_part, mixer_gain_term = norm_back(normed_back.reshape(micro_count * slot, width))
        tokens_grad = (residual_back + input_part).reshape(micro_count, slot, width)

        beta_sum = left_product(normed_group, beta_low)
        beta_wide = lax.dynamic_update_slice_in_dim(
            jnp.zeros((width, head_count), jnp.float32), beta_sum, position * heads_here, axis=1
        )
        conv_wide = lax.dynamic_update_slice_in_dim(
            jnp.zeros(conv_full.shape, jnp.float32), conv_term, position * cols_here, axis=2
        )
        taps = conv_wide.shape[0] * conv_wide.shape[1]
        small_terms = jnp.concatenate(
            [
                conv_wide.reshape(taps, n_all, -1).transpose(1, 0, 2).reshape(n_all, -1),
                beta_wide.reshape(n_all, -1),
                mixer_gain_term.reshape(n_all, -1),
                swiglu_gain_term.reshape(n_all, -1),
                jnp.broadcast_to(head_term[None, :], (n_all, head_term.shape[0])),
            ],
            axis=1,
        )
        small_width = small_terms.shape[1]
        small_out = jnp.sum(exchange(small_terms, ALL_AXES, 0, 0), axis=0)
        column_back = exchange(
            mixer_reduced[:4].reshape(4, tp, rows, 1, cols_here), TP_AXES, 1, 3
        ).reshape(4, rows, width).astype(jnp.float32)
        query_grad, key_grad, value_grad, gate_grad = (column_back[index] for index in range(4))
        out_grad = mixer_reduced[4].reshape(rows, width).astype(jnp.float32)
        conv_grad = small_out[:conv_size].reshape(conv_weight.shape)
        beta_grad = small_out[conv_size : conv_size + beta_size].reshape(beta_weight.shape)
        mixer_gain_grad = small_out[conv_size + beta_size : conv_size + beta_size + rows]
        swiglu_gain_grad = small_out[conv_size + beta_size + rows : conv_size + beta_size + 2 * rows]
        head_total = small_out[conv_size + beta_size + 2 * rows :]
        return (
            block_out,
            tokens_grad,
            query_grad,
            key_grad,
            value_grad,
            gate_grad,
            beta_grad,
            out_grad,
            conv_grad,
            mixer_gain_grad,
            head_total,
            swiglu_gain_grad,
            swiglu_gate_grad,
            swiglu_up_grad,
            swiglu_down_grad,
        )

    return on_device


def solution(mesh):
    n_dp = mesh.shape["dp"]
    n_mlp = mesh.shape["mlp"]
    devices = np.asarray(mesh.devices).reshape(n_dp // 2, 2, n_mlp)
    split_mesh = Mesh(devices, ALL_AXES)
    sizes = dict(zip(ALL_AXES, devices.shape))
    tp = int(np.prod([sizes[name] for name in TP_AXES]))
    fsdp = int(np.prod([sizes[name] for name in FSDP_AXES]))
    inner = int(np.prod([sizes[name] for name in INNER_AXES]))
    rows_axes = ALL_AXES
    swiglu_rows = ("dq", "core")
    placed = (
        P(None, rows_axes, None),
        P(None, rows_axes, None),
        P(None, rows_axes),
        P(None, rows_axes),
        P(rows_axes, None),
        P(rows_axes, None),
        P(rows_axes, None),
        P(rows_axes, None),
        P(rows_axes, None),
        P(rows_axes, None),
        P(None, None, rows_axes),
        P(rows_axes),
        P(),
        P(rows_axes),
        P(swiglu_rows, "mlp"),
        P(swiglu_rows, "mlp"),
        P("mlp", swiglu_rows),
    )
    return jax.shard_map(
        make_on_device(tp, fsdp, inner),
        mesh=split_mesh,
        in_specs=placed,
        out_specs=(
            P(None, rows_axes, None),
            P(None, rows_axes, None),
            P(rows_axes, None),
            P(rows_axes, None),
            P(rows_axes, None),
            P(rows_axes, None),
            P(rows_axes, None),
            P(rows_axes, None),
            P(None, None, rows_axes),
            P(rows_axes),
            P(),
            P(rows_axes),
            P(swiglu_rows, "mlp"),
            P(swiglu_rows, "mlp"),
            P("mlp", swiglu_rows),
        ),
        check_vma=False,
    )
```

```python
import jax
import jax.numpy as jnp
import numpy as np
from jax import lax
from jax.sharding import Mesh
from jax.sharding import PartitionSpec as P

TP_AXES = ("core", "mlp")
ALL_AXES = ("dq", "core", "mlp")
FSDP_AXES = tuple(name for name in ALL_AXES if name not in TP_AXES)
INNER_AXES = tuple(name for name in TP_AXES if name != "mlp")


def rms_norm(values, scale_gain):
    return (
        values * lax.rsqrt(jnp.mean(values * values, axis=-1, keepdims=True) + 1e-06) * scale_gain
    )


def short_conv(linear, tap_weights, starts):
    length = linear.shape[0]
    block_len = length // starts.shape[0]
    position = jnp.arange(length)
    restart = jnp.repeat(starts, block_len)
    summed = linear * tap_weights[0]
    for offset in range(1, tap_weights.shape[0]):
        shifted = jnp.concatenate(
            [jnp.zeros((offset, linear.shape[1]), linear.dtype), linear[: length - offset]], axis=0
        )
        usable = ((position % block_len >= offset) | (restart == 0)).astype(linear.dtype)
        summed = summed + shifted * tap_weights[offset] * usable[:, None]
    return summed


def outer_product_result(form, first, second):
    return jnp.einsum(form, first, second, precision=lax.Precision.HIGHEST)


def delta_core(queries, keys, values, betas, starts):
    length, head_count, head_width = queries.shape
    value_width = values.shape[2]
    block_count = starts.shape[0]
    block_len = length // block_count

    def blocked(array):
        return array.reshape(block_count, block_len, head_count, -1).transpose(0, 2, 1, 3)

    query_blocks = blocked(queries)
    key_blocks = blocked(keys)
    value_blocks = blocked(values)
    beta_blocks = betas.reshape(block_count, block_len, head_count).transpose(0, 2, 1)[..., None]
    position = jnp.arange(block_len)
    strict = (position[:, None] > position[None, :]).astype(queries.dtype)
    causal = (position[:, None] >= position[None, :]).astype(queries.dtype)
    weighted = key_blocks * beta_blocks
    negative = -outer_product_result("nhik,nhjk->nhij", weighted, key_blocks) * strict
    inverse = jnp.eye(block_len, dtype=queries.dtype) + negative
    power_term = negative
    for doubling in range(5):
        power_term = outer_product_result("nhij,nhjk->nhik", power_term, power_term)
        inverse = inverse + outer_product_result("nhij,nhjk->nhik", inverse, power_term)
    key_mix = outer_product_result("nhij,nhjk->nhik", inverse, weighted)
    value_mix = outer_product_result("nhij,nhjk->nhik", inverse, value_blocks * beta_blocks)
    scores = outer_product_result("nhik,nhjk->nhij", query_blocks, key_blocks) * causal

    def advance(current_state, block_items):
        (
            query_slice,
            key_slice,
            key_mixture_slice,
            value_mixture_slice,
            attention_score_slice,
            restart,
        ) = block_items
        current_state = current_state * (1 - restart).astype(current_state.dtype)
        adjusted_result = value_mixture_slice - outer_product_result(
            "pzd,pde->pze", key_mixture_slice, current_state
        )
        produced_output = outer_product_result(
            "pzd,pde->pze", query_slice, current_state
        ) + outer_product_result("lqz,lzr->lqr", attention_score_slice, adjusted_result)
        current_state = current_state + outer_product_result(
            "ixl,ixr->ilr", key_slice, adjusted_result
        )
        return (current_state, produced_output)

    initial = jnp.zeros((head_count, head_width, value_width), queries.dtype)
    final_state, produced_output = lax.scan(
        advance, initial, (query_blocks, key_blocks, key_mix, value_mix, scores, starts)
    )
    return produced_output.transpose(0, 2, 1, 3).reshape(length, head_count, value_width)


def delta_core_reset(queries, keys, values, betas, block_len):
    length, head_count, head_width = queries.shape
    block_count = length // block_len

    def blocked(array):
        return array.reshape(block_count, block_len, head_count, -1).transpose(0, 2, 1, 3)

    query_blocks = blocked(queries)
    key_blocks = blocked(keys)
    value_blocks = blocked(values)
    beta_blocks = betas.reshape(block_count, block_len, head_count).transpose(0, 2, 1)[..., None]
    position = jnp.arange(block_len)
    strict = (position[:, None] > position[None, :]).astype(queries.dtype)
    causal = (position[:, None] >= position[None, :]).astype(queries.dtype)
    weighted = key_blocks * beta_blocks
    negative = -outer_product_result("nhik,nhjk->nhij", weighted, key_blocks) * strict
    inverse = jnp.eye(block_len, dtype=queries.dtype) + negative
    power_term = negative
    for doubling in range(5):
        power_term = outer_product_result("nhij,nhjk->nhik", power_term, power_term)
        inverse = inverse + outer_product_result("nhij,nhjk->nhik", inverse, power_term)
    value_mix = outer_product_result("nhij,nhjk->nhik", inverse, value_blocks * beta_blocks)
    scores = outer_product_result("nhik,nhjk->nhij", query_blocks, key_blocks) * causal
    produced_output = outer_product_result("nhqz,nhzr->nhqr", scores, value_mix)
    return produced_output.transpose(0, 2, 1, 3).reshape(length, head_count, -1)


def mixer_core(
    query_lin, key_lin, value_lin, gate_lin, beta_lin, conv_taps, head_scale, starts, reset_len
):
    length = query_lin.shape[0]
    head_count = beta_lin.shape[1]
    head_width = query_lin.shape[1] // head_count
    queries = jax.nn.silu(short_conv(query_lin, conv_taps[0], starts)).reshape(
        length, head_count, head_width
    )
    keys = jax.nn.silu(short_conv(key_lin, conv_taps[1], starts)).reshape(
        length, head_count, head_width
    )
    values = jax.nn.silu(short_conv(value_lin, conv_taps[2], starts)).reshape(
        length, head_count, head_width
    )
    queries = (
        queries
        * lax.rsqrt(jnp.sum(queries * queries, axis=-1, keepdims=True) + 1e-06)
        * head_width ** (-0.5)
    )
    keys = keys * lax.rsqrt(jnp.sum(keys * keys, axis=-1, keepdims=True) + 1e-06)
    if reset_len:
        recurrent = delta_core_reset(queries, keys, values, jax.nn.sigmoid(beta_lin), reset_len)
    else:
        recurrent = delta_core(queries, keys, values, jax.nn.sigmoid(beta_lin), starts)
    normed = (
        recurrent
        * lax.rsqrt(jnp.mean(recurrent * recurrent, axis=-1, keepdims=True) + 1e-05)
        * head_scale
    )
    gated_out = normed * jax.nn.silu(gate_lin.reshape(length, head_count, head_width))
    return gated_out.reshape(length, head_count * head_width)


def swiglu_mix(gate_act, up_act):
    return jax.nn.silu(gate_act) * up_act


def matmul_rows(left, right):
    return jnp.dot(left, right, preferred_element_type=jnp.float32)


def left_product(first, second):
    return jnp.einsum("tf,tg->fg", first, second, preferred_element_type=jnp.float32)


def back_product(gradient, weight):
    return jnp.einsum("tg,fg->tf", gradient, weight, preferred_element_type=jnp.float32)


def tp_gather(value, axis):
    tp = lax.psum(1, TP_AXES)
    spread = jnp.broadcast_to(
        jnp.expand_dims(value, axis), value.shape[:axis] + (tp,) + value.shape[axis:]
    )
    moved = lax.all_to_all(spread, TP_AXES, axis, axis, tiled=True)
    shape = list(value.shape)
    shape[axis] *= tp
    return moved.reshape(shape)


def tp_scatter_low(value, axis):
    tp = lax.psum(1, TP_AXES)
    shape = list(value.shape)
    staged = value.astype(jnp.bfloat16).reshape(
        shape[:axis] + [tp, shape[axis] // tp] + shape[axis + 1 :]
    )
    moved = lax.all_to_all(staged, TP_AXES, axis, axis, tiled=True)
    return jnp.sum(moved.astype(jnp.float32), axis=axis)


def fsdp_gather(value, axis):
    return lax.all_gather(value, FSDP_AXES, axis=axis, tiled=True)


def fsdp_scatter_low(value, axis):
    return lax.psum_scatter(
        value.astype(jnp.bfloat16), FSDP_AXES, scatter_dimension=axis, tiled=True
    )


def exchange(value, axes, split_axis, concat_axis):
    if not axes:
        return value
    return lax.all_to_all(value, axes, split_axis, concat_axis, tiled=True)


def heads_to_rows(values, tp, fsdp, rows):
    count = values.shape[0]
    staged = values.reshape(count, 1, fsdp // tp, tp, rows)
    moved = exchange(staged, TP_AXES, 3, 1)
    return moved.reshape(count, fsdp * rows)


def rows_to_heads(values, tp, fsdp, rows):
    count = values.shape[0]
    staged = values.reshape(count, tp, fsdp // tp, 1, rows)
    moved = exchange(staged, TP_AXES, 1, 3)
    return moved.reshape(count, fsdp * rows)


def padded_rows(flat, slices, width):
    extra = -(-flat.shape[0] // (slices * width))
    extra = -(-extra // 16) * 16
    filled = jnp.pad(flat, (0, slices * extra * width - flat.shape[0]))
    return filled.reshape(slices, extra, width)


def make_on_device(tp, fsdp, inner):
    def on_device(
        tokens,
        cotangent,
        group_start,
        pad_mask,
        query_weight,
        key_weight,
        value_weight,
        gate_weight,
        beta_weight,
        out_weight,
        conv_weight,
        mixer_gain,
        head_gain,
        swiglu_gain,
        swiglu_gate,
        swiglu_up,
        swiglu_down,
    ):
        micro_count, slot, width = tokens.shape
        n_all = tp * fsdp
        rows = query_weight.shape[0]
        head_count = beta_weight.shape[1]
        heads_here = head_count // tp
        cols_here = width // tp
        group_rows = tp * rows
        position = lax.axis_index(TP_AXES)
        head_scale = head_gain.astype(jnp.float32)
        reset_len = slot if group_start.shape[1] == 1 else 0

        column_owned = jnp.stack([query_weight, key_weight, value_weight, gate_weight])
        column_swapped = exchange(
            column_owned.reshape(4, rows, tp, cols_here), TP_AXES, 2, 1
        ).reshape(4, group_rows, cols_here)
        owned_rows, hidden_half = swiglu_gate.shape
        hidden_here = hidden_half // inner
        ff_owned = jnp.stack([swiglu_gate, swiglu_up, swiglu_down.T]).reshape(
            3, owned_rows, inner, hidden_here
        )
        lanes = hidden_here // 128 if hidden_here % 128 == 0 else 0
        first = (lanes - lanes * 2 // 11) * 128 if lanes > 1 else hidden_here // 2
        order = ((first, hidden_here - first), (0, first))
        ff_swapped = [
            exchange(ff_owned[..., offset : offset + size], INNER_AXES, 2, 1).reshape(
                3, inner * owned_rows, size
            )
            for offset, size in order
        ]
        small_chunk = fsdp_gather(ff_swapped[0], 1)
        mixer_stack = jnp.concatenate(
            [column_swapped, out_weight.reshape(1, group_rows, cols_here)], axis=0
        )
        small_chunk, mixer_stack = lax.optimization_barrier((small_chunk, mixer_stack))
        weight_all = fsdp_gather(mixer_stack, 1)
        weight_all, large_swapped = lax.optimization_barrier((weight_all, ff_swapped[1]))
        ff_chunks = [small_chunk, fsdp_gather(large_swapped, 1)]
        query_cols, key_cols, value_cols, gate_cols = (weight_all[index] for index in range(4))
        out_rows = weight_all[4].reshape(fsdp * rows, width)
        small_pack = jnp.concatenate(
            [
                conv_weight.reshape(-1),
                beta_weight.reshape(-1),
                mixer_gain.reshape(-1),
                swiglu_gain.reshape(-1),
            ]
        )
        small_size = small_pack.shape[0]
        small_all = exchange(
            jnp.broadcast_to(small_pack[None, :], (n_all, small_size)), ALL_AXES, 0, 0
        )
        conv_size = conv_weight.size
        beta_size = beta_weight.size
        conv_full = (
            small_all[:, :conv_size]
            .reshape((n_all,) + conv_weight.shape)
            .transpose(1, 2, 0, 3)
            .reshape(conv_weight.shape[0], conv_weight.shape[1], -1)
        )
        beta_full = small_all[:, conv_size : conv_size + beta_size].reshape(-1, head_count)
        gain_mixer = small_all[:, conv_size + beta_size : conv_size + beta_size + rows].reshape(-1)
        gain_swiglu = small_all[:, conv_size + beta_size + rows :].reshape(-1)
        conv_here = lax.dynamic_slice_in_dim(
            conv_full.astype(jnp.float32), position * cols_here, cols_here, axis=2
        )
        beta_here = lax.dynamic_slice_in_dim(beta_full, position * heads_here, heads_here, axis=1)

        inputs = tokens.astype(jnp.float32).reshape(micro_count * slot, width)
        normed, norm_back = jax.vjp(rms_norm, inputs, gain_mixer.astype(jnp.float32))
        normed_low = normed.astype(jnp.bfloat16)
        group_tokens = micro_count * slot * tp
        normed_group = tp_gather(normed_low.reshape(micro_count, slot, width), 1).reshape(
            group_tokens, width
        )
        starts = tp_gather(group_start, 1).reshape(-1)

        query_lin = matmul_rows(normed_group, query_cols)
        key_lin = matmul_rows(normed_group, key_cols)
        value_lin = matmul_rows(normed_group, value_cols)
        gate_lin = matmul_rows(normed_group, gate_cols)
        beta_lin = matmul_rows(normed_group, beta_here)

        def core_at(query_in, key_in, value_in, gate_in, beta_in, conv_in, head_in):
            return mixer_core(
                query_in, key_in, value_in, gate_in, beta_in, conv_in, head_in, starts, reset_len
            )

        gated_out, core_back = jax.vjp(
            core_at, query_lin, key_lin, value_lin, gate_lin, beta_lin, conv_here, head_scale
        )
        gated_low = gated_out.astype(jnp.bfloat16)
        gated_rows = heads_to_rows(gated_low, tp, fsdp, rows)
        mixed_partial = matmul_rows(gated_rows, out_rows)
        residual = inputs + tp_scatter_low(
            mixed_partial.reshape(micro_count, slot * tp, width), 1
        ).reshape(micro_count * slot, width)

        inner_norm, inner_norm_back = jax.vjp(rms_norm, residual, gain_swiglu.astype(jnp.float32))
        inner_low = inner_norm.astype(jnp.bfloat16)
        inner_group = tp_gather(inner_low.reshape(micro_count, slot, width), 1).reshape(
            group_tokens, width
        )
        out_back = cotangent.astype(jnp.float32) * pad_mask.astype(jnp.float32)[:, :, None]
        out_back_low = out_back.astype(jnp.bfloat16)
        upstream_group = tp_gather(out_back_low, 1).reshape(group_tokens, width)
        partial_rows = None
        inner_part = None
        ff_reduced = []
        for index, chunk_weights in enumerate(ff_chunks):
            if index > 0:
                sums_low, chunk_weights = lax.optimization_barrier((sums_low, chunk_weights))
            gate_piece, up_piece, down_piece_t = chunk_weights[0], chunk_weights[1], chunk_weights[2]
            gate_act = matmul_rows(inner_group, gate_piece)
            up_act = matmul_rows(inner_group, up_piece)
            hidden, hidden_back = jax.vjp(swiglu_mix, gate_act, up_act)
            hidden_low = hidden.astype(jnp.bfloat16)
            piece_rows = back_product(hidden_low, down_piece_t)
            partial_rows = piece_rows if partial_rows is None else partial_rows + piece_rows
            gate_back, up_back = hidden_back(matmul_rows(upstream_group, down_piece_t))
            gate_back_low = gate_back.astype(jnp.bfloat16)
            up_back_low = up_back.astype(jnp.bfloat16)
            piece_part = back_product(gate_back_low, gate_piece) + back_product(up_back_low, up_piece)
            inner_part = piece_part if inner_part is None else inner_part + piece_part
            sums_low = jnp.stack(
                [
                    left_product(inner_group, gate_back_low),
                    left_product(inner_group, up_back_low),
                    left_product(upstream_group, hidden_low),
                ]
            ).astype(jnp.bfloat16)
            ff_reduced.append(fsdp_scatter_low(sums_low, 1))
        branch_rows = tp_scatter_low(partial_rows.reshape(micro_count, slot * tp, width), 1)
        block_out = (residual.reshape(micro_count, slot, width) + branch_rows).astype(jnp.bfloat16)
        inner_back = tp_scatter_low(inner_part.reshape(micro_count, slot * tp, width), 1)
        block_out, inner_back = lax.optimization_barrier((block_out, inner_back))

        residual_part, swiglu_gain_term = inner_norm_back(
            inner_back.reshape(micro_count * slot, width)
        )
        residual_back = out_back.reshape(micro_count * slot, width) + residual_part
        mixed_back = residual_back.astype(jnp.bfloat16)
        mixed_group = tp_gather(mixed_back.reshape(micro_count, slot, width), 1).reshape(
            group_tokens, width
        )
        gated_back_rows = back_product(mixed_group, out_rows)
        gated_back = rows_to_heads(gated_back_rows, tp, fsdp, rows)
        query_back, key_back, value_back, gate_lin_back, beta_back, conv_term, head_term = (
            core_back(gated_back)
        )
        query_low = query_back.astype(jnp.bfloat16)
        key_low = key_back.astype(jnp.bfloat16)
        value_low = value_back.astype(jnp.bfloat16)
        gate_low = gate_lin_back.astype(jnp.bfloat16)
        beta_low = beta_back.astype(jnp.bfloat16)
        mixer_sums = jnp.stack(
            [
                left_product(normed_group, query_low),
                left_product(normed_group, key_low),
                left_product(normed_group, value_low),
                left_product(normed_group, gate_low),
                left_product(gated_rows, mixed_group).reshape(width, cols_here),
            ]
        )
        ff_reduced, mixer_sums = lax.optimization_barrier((ff_reduced, mixer_sums))
        mixer_reduced = fsdp_scatter_low(mixer_sums, 1)
        ff_back = jnp.concatenate(
            [
                exchange(
                    piece.reshape(3, inner, owned_rows, 1, size), INNER_AXES, 1, 3
                ).reshape(3, owned_rows, inner, size)
                for piece, (offset, size) in sorted(zip(ff_reduced, order), key=lambda pair: pair[1][0])
            ],
            axis=3,
        ).reshape(3, owned_rows, hidden_half).astype(jnp.float32)
        swiglu_gate_grad = ff_back[0]
        swiglu_up_grad = ff_back[1]
        swiglu_down_grad = ff_back[2].T

        normed_part = (
            back_product(query_low, query_cols)
            + back_product(key_low, key_cols)
            + back_product(value_low, value_cols)
            + back_product(gate_low, gate_cols)
            + back_product(beta_low, beta_here)
        )
        normed_back = tp_scatter_low(normed_part.reshape(micro_count, slot * tp, width), 1)
        input_part, mixer_gain_term = norm_back(normed_back.reshape(micro_count * slot, width))
        tokens_grad = (residual_back + input_part).reshape(micro_count, slot, width)

        beta_sum = left_product(normed_group, beta_low)
        beta_wide = lax.dynamic_update_slice_in_dim(
            jnp.zeros((width, head_count), jnp.float32), beta_sum, position * heads_here, axis=1
        )
        conv_wide = lax.dynamic_update_slice_in_dim(
            jnp.zeros(conv_full.shape, jnp.float32), conv_term, position * cols_here, axis=2
        )
        taps = conv_wide.shape[0] * conv_wide.shape[1]
        small_terms = jnp.concatenate(
            [
                conv_wide.reshape(taps, n_all, -1).transpose(1, 0, 2).reshape(n_all, -1),
                beta_wide.reshape(n_all, -1),
                mixer_gain_term.reshape(n_all, -1),
                swiglu_gain_term.reshape(n_all, -1),
                jnp.broadcast_to(head_term[None, :], (n_all, head_term.shape[0])),
            ],
            axis=1,
        )
        small_width = small_terms.shape[1]
        small_out = jnp.sum(exchange(small_terms, ALL_AXES, 0, 0), axis=0)
        column_back = exchange(
            mixer_reduced[:4].reshape(4, tp, rows, 1, cols_here), TP_AXES, 1, 3
        ).reshape(4, rows, width).astype(jnp.float32)
        query_grad, key_grad, value_grad, gate_grad = (column_back[index] for index in range(4))
        out_grad = mixer_reduced[4].reshape(rows, width).astype(jnp.float32)
        conv_grad = small_out[:conv_size].reshape(conv_weight.shape)
        beta_grad = small_out[conv_size : conv_size + beta_size].reshape(beta_weight.shape)
        mixer_gain_grad = small_out[conv_size + beta_size : conv_size + beta_size + rows]
        swiglu_gain_grad = small_out[conv_size + beta_size + rows : conv_size + beta_size + 2 * rows]
        head_total = small_out[conv_size + beta_size + 2 * rows :]
        return (
            block_out,
            tokens_grad,
            query_grad,
            key_grad,
            value_grad,
            gate_grad,
            beta_grad,
            out_grad,
            conv_grad,
            mixer_gain_grad,
            head_total,
            swiglu_gain_grad,
            swiglu_gate_grad,
            swiglu_up_grad,
            swiglu_down_grad,
        )

    return on_device


def solution(mesh):
    n_dp = mesh.shape["dp"]
    n_mlp = mesh.shape["mlp"]
    devices = np.asarray(mesh.devices).reshape(n_dp // 2, 2, n_mlp)
    split_mesh = Mesh(devices, ALL_AXES)
    sizes = dict(zip(ALL_AXES, devices.shape))
    tp = int(np.prod([sizes[name] for name in TP_AXES]))
    fsdp = int(np.prod([sizes[name] for name in FSDP_AXES]))
    inner = int(np.prod([sizes[name] for name in INNER_AXES]))
    rows_axes = ALL_AXES
    swiglu_rows = ("dq", "core")
    placed = (
        P(None, rows_axes, None),
        P(None, rows_axes, None),
        P(None, rows_axes),
        P(None, rows_axes),
        P(rows_axes, None),
        P(rows_axes, None),
        P(rows_axes, None),
        P(rows_axes, None),
        P(rows_axes, None),
        P(rows_axes, None),
        P(None, None, rows_axes),
        P(rows_axes),
        P(),
        P(rows_axes),
        P(swiglu_rows, "mlp"),
        P(swiglu_rows, "mlp"),
        P("mlp", swiglu_rows),
    )
    return jax.shard_map(
        make_on_device(tp, fsdp, inner),
        mesh=split_mesh,
        in_specs=placed,
        out_specs=(
            P(None, rows_axes, None),
            P(None, rows_axes, None),
            P(rows_axes, None),
            P(rows_axes, None),
            P(rows_axes, None),
            P(rows_axes, None),
            P(rows_axes, None),
            P(rows_axes, None),
            P(None, None, rows_axes),
            P(rows_axes),
            P(),
            P(rows_axes),
            P(swiglu_rows, "mlp"),
            P(swiglu_rows, "mlp"),
            P("mlp", swiglu_rows),
        ),
        check_vma=False,
    )
```

```python
import jax
import jax.numpy as jnp
import numpy as np
from jax import lax
from jax.sharding import Mesh
from jax.sharding import PartitionSpec as P

TP_AXES = ("core", "mlp")
ALL_AXES = ("dq", "core", "mlp")
FSDP_AXES = tuple(name for name in ALL_AXES if name not in TP_AXES)
INNER_AXES = tuple(name for name in TP_AXES if name != "mlp")


def rms_norm(values, scale_gain):
    return (
        values * lax.rsqrt(jnp.mean(values * values, axis=-1, keepdims=True) + 1e-06) * scale_gain
    )


def short_conv(linear, tap_weights, starts):
    length = linear.shape[0]
    block_len = length // starts.shape[0]
    position = jnp.arange(length)
    restart = jnp.repeat(starts, block_len)
    summed = linear * tap_weights[0]
    for offset in range(1, tap_weights.shape[0]):
        shifted = jnp.concatenate(
            [jnp.zeros((offset, linear.shape[1]), linear.dtype), linear[: length - offset]], axis=0
        )
        usable = ((position % block_len >= offset) | (restart == 0)).astype(linear.dtype)
        summed = summed + shifted * tap_weights[offset] * usable[:, None]
    return summed


def outer_product_result(form, first, second):
    return jnp.einsum(form, first, second, precision=lax.Precision.HIGHEST)


def delta_core(queries, keys, values, betas, starts):
    length, head_count, head_width = queries.shape
    value_width = values.shape[2]
    block_count = starts.shape[0]
    block_len = length // block_count

    def blocked(array):
        return array.reshape(block_count, block_len, head_count, -1).transpose(0, 2, 1, 3)

    query_blocks = blocked(queries)
    key_blocks = blocked(keys)
    value_blocks = blocked(values)
    beta_blocks = betas.reshape(block_count, block_len, head_count).transpose(0, 2, 1)[..., None]
    position = jnp.arange(block_len)
    strict = (position[:, None] > position[None, :]).astype(queries.dtype)
    causal = (position[:, None] >= position[None, :]).astype(queries.dtype)
    weighted = key_blocks * beta_blocks
    negative = -outer_product_result("nhik,nhjk->nhij", weighted, key_blocks) * strict
    inverse = jnp.eye(block_len, dtype=queries.dtype) + negative
    power_term = negative
    for doubling in range(5):
        power_term = outer_product_result("nhij,nhjk->nhik", power_term, power_term)
        inverse = inverse + outer_product_result("nhij,nhjk->nhik", inverse, power_term)
    key_mix = outer_product_result("nhij,nhjk->nhik", inverse, weighted)
    value_mix = outer_product_result("nhij,nhjk->nhik", inverse, value_blocks * beta_blocks)
    scores = outer_product_result("nhik,nhjk->nhij", query_blocks, key_blocks) * causal

    def advance(current_state, block_items):
        (
            query_slice,
            key_slice,
            key_mixture_slice,
            value_mixture_slice,
            attention_score_slice,
            restart,
        ) = block_items
        current_state = current_state * (1 - restart).astype(current_state.dtype)
        adjusted_result = value_mixture_slice - outer_product_result(
            "pzd,pde->pze", key_mixture_slice, current_state
        )
        produced_output = outer_product_result(
            "pzd,pde->pze", query_slice, current_state
        ) + outer_product_result("lqz,lzr->lqr", attention_score_slice, adjusted_result)
        current_state = current_state + outer_product_result(
            "ixl,ixr->ilr", key_slice, adjusted_result
        )
        return (current_state, produced_output)

    initial = jnp.zeros((head_count, head_width, value_width), queries.dtype)
    final_state, produced_output = lax.scan(
        advance, initial, (query_blocks, key_blocks, key_mix, value_mix, scores, starts)
    )
    return produced_output.transpose(0, 2, 1, 3).reshape(length, head_count, value_width)


def delta_core_reset(queries, keys, values, betas, block_len):
    length, head_count, head_width = queries.shape
    block_count = length // block_len

    def blocked(array):
        return array.reshape(block_count, block_len, head_count, -1).transpose(0, 2, 1, 3)

    query_blocks = blocked(queries)
    key_blocks = blocked(keys)
    value_blocks = blocked(values)
    beta_blocks = betas.reshape(block_count, block_len, head_count).transpose(0, 2, 1)[..., None]
    position = jnp.arange(block_len)
    strict = (position[:, None] > position[None, :]).astype(queries.dtype)
    causal = (position[:, None] >= position[None, :]).astype(queries.dtype)
    weighted = key_blocks * beta_blocks
    negative = -outer_product_result("nhik,nhjk->nhij", weighted, key_blocks) * strict
    inverse = jnp.eye(block_len, dtype=queries.dtype) + negative
    power_term = negative
    for doubling in range(5):
        power_term = outer_product_result("nhij,nhjk->nhik", power_term, power_term)
        inverse = inverse + outer_product_result("nhij,nhjk->nhik", inverse, power_term)
    value_mix = outer_product_result("nhij,nhjk->nhik", inverse, value_blocks * beta_blocks)
    scores = outer_product_result("nhik,nhjk->nhij", query_blocks, key_blocks) * causal
    produced_output = outer_product_result("nhqz,nhzr->nhqr", scores, value_mix)
    return produced_output.transpose(0, 2, 1, 3).reshape(length, head_count, -1)


def mixer_core(
    query_lin, key_lin, value_lin, gate_lin, beta_lin, conv_taps, head_scale, starts, reset_len
):
    length = query_lin.shape[0]
    head_count = beta_lin.shape[1]
    head_width = query_lin.shape[1] // head_count
    queries = jax.nn.silu(short_conv(query_lin, conv_taps[0], starts)).reshape(
        length, head_count, head_width
    )
    keys = jax.nn.silu(short_conv(key_lin, conv_taps[1], starts)).reshape(
        length, head_count, head_width
    )
    values = jax.nn.silu(short_conv(value_lin, conv_taps[2], starts)).reshape(
        length, head_count, head_width
    )
    queries = (
        queries
        * lax.rsqrt(jnp.sum(queries * queries, axis=-1, keepdims=True) + 1e-06)
        * head_width ** (-0.5)
    )
    keys = keys * lax.rsqrt(jnp.sum(keys * keys, axis=-1, keepdims=True) + 1e-06)
    if reset_len:
        recurrent = delta_core_reset(queries, keys, values, jax.nn.sigmoid(beta_lin), reset_len)
    else:
        recurrent = delta_core(queries, keys, values, jax.nn.sigmoid(beta_lin), starts)
    normed = (
        recurrent
        * lax.rsqrt(jnp.mean(recurrent * recurrent, axis=-1, keepdims=True) + 1e-05)
        * head_scale
    )
    gated_out = normed * jax.nn.silu(gate_lin.reshape(length, head_count, head_width))
    return gated_out.reshape(length, head_count * head_width)


def swiglu_mix(gate_act, up_act):
    return jax.nn.silu(gate_act) * up_act


def matmul_rows(left, right):
    return jnp.dot(left, right, preferred_element_type=jnp.float32)


def left_product(first, second):
    return jnp.einsum("tf,tg->fg", first, second, preferred_element_type=jnp.float32)


def back_product(gradient, weight):
    return jnp.einsum("tg,fg->tf", gradient, weight, preferred_element_type=jnp.float32)


def tp_gather(value, axis):
    tp = lax.psum(1, TP_AXES)
    spread = jnp.broadcast_to(
        jnp.expand_dims(value, axis), value.shape[:axis] + (tp,) + value.shape[axis:]
    )
    moved = lax.all_to_all(spread, TP_AXES, axis, axis, tiled=True)
    shape = list(value.shape)
    shape[axis] *= tp
    return moved.reshape(shape)


def tp_scatter_low(value, axis):
    tp = lax.psum(1, TP_AXES)
    shape = list(value.shape)
    staged = value.astype(jnp.bfloat16).reshape(
        shape[:axis] + [tp, shape[axis] // tp] + shape[axis + 1 :]
    )
    moved = lax.all_to_all(staged, TP_AXES, axis, axis, tiled=True)
    return jnp.sum(moved.astype(jnp.float32), axis=axis)


def fsdp_gather(value, axis):
    return lax.all_gather(value, FSDP_AXES, axis=axis, tiled=True)


def fsdp_scatter_low(value, axis):
    return lax.psum_scatter(
        value.astype(jnp.bfloat16), FSDP_AXES, scatter_dimension=axis, tiled=True
    )


def exchange(value, axes, split_axis, concat_axis):
    if not axes:
        return value
    return lax.all_to_all(value, axes, split_axis, concat_axis, tiled=True)


def heads_to_rows(values, tp, fsdp, rows):
    count = values.shape[0]
    staged = values.reshape(count, 1, fsdp // tp, tp, rows)
    moved = exchange(staged, TP_AXES, 3, 1)
    return moved.reshape(count, fsdp * rows)


def rows_to_heads(values, tp, fsdp, rows):
    count = values.shape[0]
    staged = values.reshape(count, tp, fsdp // tp, 1, rows)
    moved = exchange(staged, TP_AXES, 1, 3)
    return moved.reshape(count, fsdp * rows)


def padded_rows(flat, slices, width):
    extra = -(-flat.shape[0] // (slices * width))
    extra = -(-extra // 16) * 16
    filled = jnp.pad(flat, (0, slices * extra * width - flat.shape[0]))
    return filled.reshape(slices, extra, width)


def make_on_device(tp, fsdp, inner):
    def on_device(
        tokens,
        cotangent,
        group_start,
        pad_mask,
        query_weight,
        key_weight,
        value_weight,
        gate_weight,
        beta_weight,
        out_weight,
        conv_weight,
        mixer_gain,
        head_gain,
        swiglu_gain,
        swiglu_gate,
        swiglu_up,
        swiglu_down,
    ):
        micro_count, slot, width = tokens.shape
        n_all = tp * fsdp
        rows = query_weight.shape[0]
        head_count = beta_weight.shape[1]
        heads_here = head_count // tp
        cols_here = width // tp
        group_rows = tp * rows
        position = lax.axis_index(TP_AXES)
        head_scale = head_gain.astype(jnp.float32)
        reset_len = slot if group_start.shape[1] == 1 else 0

        column_owned = jnp.stack([query_weight, key_weight, value_weight, gate_weight])
        column_swapped = exchange(
            column_owned.reshape(4, rows, tp, cols_here), TP_AXES, 2, 1
        ).reshape(4, group_rows, cols_here)
        owned_rows, hidden_half = swiglu_gate.shape
        hidden_here = hidden_half // inner
        ff_owned = jnp.stack([swiglu_gate, swiglu_up, swiglu_down.T]).reshape(
            3, owned_rows, inner, hidden_here
        )
        lanes = hidden_here // 128 if hidden_here % 128 == 0 else 0
        first = (lanes - lanes * 2 // 11) * 128 if lanes > 1 else hidden_here // 2
        order = ((first, hidden_here - first), (0, first))
        ff_swapped = [
            exchange(ff_owned[..., offset : offset + size], INNER_AXES, 2, 1).reshape(
                3, inner * owned_rows, size
            )
            for offset, size in order
        ]
        mixer_stack = jnp.concatenate(
            [column_swapped, out_weight.reshape(1, group_rows, cols_here)], axis=0
        )
        weight_all = fsdp_gather(mixer_stack, 1)
        weight_all, small_swapped, large_swapped = lax.optimization_barrier(
            (weight_all, ff_swapped[0], ff_swapped[1])
        )
        ff_chunks = [fsdp_gather(small_swapped, 1), fsdp_gather(large_swapped, 1)]
        query_cols, key_cols, value_cols, gate_cols = (weight_all[index] for index in range(4))
        out_rows = weight_all[4].reshape(fsdp * rows, width)
        small_pack = jnp.concatenate(
            [
                conv_weight.reshape(-1),
                beta_weight.reshape(-1),
                mixer_gain.reshape(-1),
                swiglu_gain.reshape(-1),
            ]
        )
        small_size = small_pack.shape[0]
        small_all = exchange(
            jnp.broadcast_to(small_pack[None, :], (n_all, small_size)), ALL_AXES, 0, 0
        )
        conv_size = conv_weight.size
        beta_size = beta_weight.size
        conv_full = (
            small_all[:, :conv_size]
            .reshape((n_all,) + conv_weight.shape)
            .transpose(1, 2, 0, 3)
            .reshape(conv_weight.shape[0], conv_weight.shape[1], -1)
        )
        beta_full = small_all[:, conv_size : conv_size + beta_size].reshape(-1, head_count)
        gain_mixer = small_all[:, conv_size + beta_size : conv_size + beta_size + rows].reshape(-1)
        gain_swiglu = small_all[:, conv_size + beta_size + rows :].reshape(-1)
        conv_here = lax.dynamic_slice_in_dim(
            conv_full.astype(jnp.float32), position * cols_here, cols_here, axis=2
        )
        beta_here = lax.dynamic_slice_in_dim(beta_full, position * heads_here, heads_here, axis=1)

        inputs = tokens.astype(jnp.float32).reshape(micro_count * slot, width)
        normed, norm_back = jax.vjp(rms_norm, inputs, gain_mixer.astype(jnp.float32))
        normed_low = normed.astype(jnp.bfloat16)
        group_tokens = micro_count * slot * tp
        normed_group = tp_gather(normed_low.reshape(micro_count, slot, width), 1).reshape(
            group_tokens, width
        )
        starts = tp_gather(group_start, 1).reshape(-1)

        query_lin = matmul_rows(normed_group, query_cols)
        key_lin = matmul_rows(normed_group, key_cols)
        value_lin = matmul_rows(normed_group, value_cols)
        gate_lin = matmul_rows(normed_group, gate_cols)
        beta_lin = matmul_rows(normed_group, beta_here)

        def core_at(query_in, key_in, value_in, gate_in, beta_in, conv_in, head_in):
            return mixer_core(
                query_in, key_in, value_in, gate_in, beta_in, conv_in, head_in, starts, reset_len
            )

        gated_out, core_back = jax.vjp(
            core_at, query_lin, key_lin, value_lin, gate_lin, beta_lin, conv_here, head_scale
        )
        gated_low = gated_out.astype(jnp.bfloat16)
        gated_rows = heads_to_rows(gated_low, tp, fsdp, rows)
        mixed_partial = matmul_rows(gated_rows, out_rows)
        residual = inputs + tp_scatter_low(
            mixed_partial.reshape(micro_count, slot * tp, width), 1
        ).reshape(micro_count * slot, width)

        inner_norm, inner_norm_back = jax.vjp(rms_norm, residual, gain_swiglu.astype(jnp.float32))
        inner_low = inner_norm.astype(jnp.bfloat16)
        inner_group = tp_gather(inner_low.reshape(micro_count, slot, width), 1).reshape(
            group_tokens, width
        )
        out_back = cotangent.astype(jnp.float32) * pad_mask.astype(jnp.float32)[:, :, None]
        out_back_low = out_back.astype(jnp.bfloat16)
        upstream_group = tp_gather(out_back_low, 1).reshape(group_tokens, width)
        partial_rows = None
        inner_part = None
        ff_reduced = []
        for index, chunk_weights in enumerate(ff_chunks):
            if index > 0:
                sums_low, chunk_weights = lax.optimization_barrier((sums_low, chunk_weights))
            gate_piece, up_piece, down_piece_t = chunk_weights[0], chunk_weights[1], chunk_weights[2]
            gate_act = matmul_rows(inner_group, gate_piece)
            up_act = matmul_rows(inner_group, up_piece)
            hidden, hidden_back = jax.vjp(swiglu_mix, gate_act, up_act)
            hidden_low = hidden.astype(jnp.bfloat16)
            piece_rows = back_product(hidden_low, down_piece_t)
            partial_rows = piece_rows if partial_rows is None else partial_rows + piece_rows
            gate_back, up_back = hidden_back(matmul_rows(upstream_group, down_piece_t))
            gate_back_low = gate_back.astype(jnp.bfloat16)
            up_back_low = up_back.astype(jnp.bfloat16)
            piece_part = back_product(gate_back_low, gate_piece) + back_product(up_back_low, up_piece)
            inner_part = piece_part if inner_part is None else inner_part + piece_part
            sums_low = jnp.stack(
                [
                    left_product(inner_group, gate_back_low),
                    left_product(inner_group, up_back_low),
                    left_product(upstream_group, hidden_low),
                ]
            ).astype(jnp.bfloat16)
            ff_reduced.append(fsdp_scatter_low(sums_low, 1))
        branch_rows = tp_scatter_low(partial_rows.reshape(micro_count, slot * tp, width), 1)
        block_out = (residual.reshape(micro_count, slot, width) + branch_rows).astype(jnp.bfloat16)
        inner_back = tp_scatter_low(inner_part.reshape(micro_count, slot * tp, width), 1)
        block_out, inner_back = lax.optimization_barrier((block_out, inner_back))

        residual_part, swiglu_gain_term = inner_norm_back(
            inner_back.reshape(micro_count * slot, width)
        )
        residual_back = out_back.reshape(micro_count * slot, width) + residual_part
        mixed_back = residual_back.astype(jnp.bfloat16)
        mixed_group = tp_gather(mixed_back.reshape(micro_count, slot, width), 1).reshape(
            group_tokens, width
        )
        gated_back_rows = back_product(mixed_group, out_rows)
        gated_back = rows_to_heads(gated_back_rows, tp, fsdp, rows)
        query_back, key_back, value_back, gate_lin_back, beta_back, conv_term, head_term = (
            core_back(gated_back)
        )
        query_low = query_back.astype(jnp.bfloat16)
        key_low = key_back.astype(jnp.bfloat16)
        value_low = value_back.astype(jnp.bfloat16)
        gate_low = gate_lin_back.astype(jnp.bfloat16)
        beta_low = beta_back.astype(jnp.bfloat16)
        mixer_sums = jnp.stack(
            [
                left_product(normed_group, query_low),
                left_product(normed_group, key_low),
                left_product(normed_group, value_low),
                left_product(normed_group, gate_low),
                left_product(gated_rows, mixed_group).reshape(width, cols_here),
            ]
        )
        ff_reduced, mixer_sums = lax.optimization_barrier((ff_reduced, mixer_sums))
        mixer_reduced = fsdp_scatter_low(mixer_sums, 1)
        ff_back = jnp.concatenate(
            [
                exchange(
                    piece.reshape(3, inner, owned_rows, 1, size), INNER_AXES, 1, 3
                ).reshape(3, owned_rows, inner, size)
                for piece, (offset, size) in sorted(zip(ff_reduced, order), key=lambda pair: pair[1][0])
            ],
            axis=3,
        ).reshape(3, owned_rows, hidden_half).astype(jnp.float32)
        swiglu_gate_grad = ff_back[0]
        swiglu_up_grad = ff_back[1]
        swiglu_down_grad = ff_back[2].T

        normed_part = (
            back_product(query_low, query_cols)
            + back_product(key_low, key_cols)
            + back_product(value_low, value_cols)
            + back_product(gate_low, gate_cols)
            + back_product(beta_low, beta_here)
        )
        normed_back = tp_scatter_low(normed_part.reshape(micro_count, slot * tp, width), 1)
        input_part, mixer_gain_term = norm_back(normed_back.reshape(micro_count * slot, width))
        tokens_grad = (residual_back + input_part).reshape(micro_count, slot, width)

        beta_sum = left_product(normed_group, beta_low)
        beta_wide = lax.dynamic_update_slice_in_dim(
            jnp.zeros((width, head_count), jnp.float32), beta_sum, position * heads_here, axis=1
        )
        conv_wide = lax.dynamic_update_slice_in_dim(
            jnp.zeros(conv_full.shape, jnp.float32), conv_term, position * cols_here, axis=2
        )
        taps = conv_wide.shape[0] * conv_wide.shape[1]
        small_terms = jnp.concatenate(
            [
                conv_wide.reshape(taps, n_all, -1).transpose(1, 0, 2).reshape(n_all, -1),
                beta_wide.reshape(n_all, -1),
                mixer_gain_term.reshape(n_all, -1),
                swiglu_gain_term.reshape(n_all, -1),
                jnp.broadcast_to(head_term[None, :], (n_all, head_term.shape[0])),
            ],
            axis=1,
        )
        small_width = small_terms.shape[1]
        small_out = jnp.sum(exchange(small_terms, ALL_AXES, 0, 0), axis=0)
        column_back = exchange(
            mixer_reduced[:4].reshape(4, tp, rows, 1, cols_here), TP_AXES, 1, 3
        ).reshape(4, rows, width).astype(jnp.float32)
        query_grad, key_grad, value_grad, gate_grad = (column_back[index] for index in range(4))
        out_grad = mixer_reduced[4].reshape(rows, width).astype(jnp.float32)
        conv_grad = small_out[:conv_size].reshape(conv_weight.shape)
        beta_grad = small_out[conv_size : conv_size + beta_size].reshape(beta_weight.shape)
        mixer_gain_grad = small_out[conv_size + beta_size : conv_size + beta_size + rows]
        swiglu_gain_grad = small_out[conv_size + beta_size + rows : conv_size + beta_size + 2 * rows]
        head_total = small_out[conv_size + beta_size + 2 * rows :]
        return (
            block_out,
            tokens_grad,
            query_grad,
            key_grad,
            value_grad,
            gate_grad,
            beta_grad,
            out_grad,
            conv_grad,
            mixer_gain_grad,
            head_total,
            swiglu_gain_grad,
            swiglu_gate_grad,
            swiglu_up_grad,
            swiglu_down_grad,
        )

    return on_device


def solution(mesh):
    n_dp = mesh.shape["dp"]
    n_mlp = mesh.shape["mlp"]
    devices = np.asarray(mesh.devices).reshape(n_dp // 2, 2, n_mlp)
    split_mesh = Mesh(devices, ALL_AXES)
    sizes = dict(zip(ALL_AXES, devices.shape))
    tp = int(np.prod([sizes[name] for name in TP_AXES]))
    fsdp = int(np.prod([sizes[name] for name in FSDP_AXES]))
    inner = int(np.prod([sizes[name] for name in INNER_AXES]))
    rows_axes = ALL_AXES
    swiglu_rows = ("dq", "core")
    placed = (
        P(None, rows_axes, None),
        P(None, rows_axes, None),
        P(None, rows_axes),
        P(None, rows_axes),
        P(rows_axes, None),
        P(rows_axes, None),
        P(rows_axes, None),
        P(rows_axes, None),
        P(rows_axes, None),
        P(rows_axes, None),
        P(None, None, rows_axes),
        P(rows_axes),
        P(),
        P(rows_axes),
        P(swiglu_rows, "mlp"),
        P(swiglu_rows, "mlp"),
        P("mlp", swiglu_rows),
    )
    return jax.shard_map(
        make_on_device(tp, fsdp, inner),
        mesh=split_mesh,
        in_specs=placed,
        out_specs=(
            P(None, rows_axes, None),
            P(None, rows_axes, None),
            P(rows_axes, None),
            P(rows_axes, None),
            P(rows_axes, None),
            P(rows_axes, None),
            P(rows_axes, None),
            P(rows_axes, None),
            P(None, None, rows_axes),
            P(rows_axes),
            P(),
            P(rows_axes),
            P(swiglu_rows, "mlp"),
            P(swiglu_rows, "mlp"),
            P("mlp", swiglu_rows),
        ),
        check_vma=False,
    )
```

```python
import jax
import jax.numpy as jnp
import numpy as np
from jax import lax
from jax.sharding import Mesh
from jax.sharding import PartitionSpec as P

TP_AXES = ("core", "mlp")
ALL_AXES = ("dq", "core", "mlp")
FSDP_AXES = tuple(name for name in ALL_AXES if name not in TP_AXES)
INNER_AXES = tuple(name for name in TP_AXES if name != "mlp")


def rms_norm(values, scale_gain):
    return (
        values * lax.rsqrt(jnp.mean(values * values, axis=-1, keepdims=True) + 1e-06) * scale_gain
    )


def short_conv(linear, tap_weights, starts):
    length = linear.shape[0]
    block_len = length // starts.shape[0]
    position = jnp.arange(length)
    restart = jnp.repeat(starts, block_len)
    summed = linear * tap_weights[0]
    for offset in range(1, tap_weights.shape[0]):
        shifted = jnp.concatenate(
            [jnp.zeros((offset, linear.shape[1]), linear.dtype), linear[: length - offset]], axis=0
        )
        usable = ((position % block_len >= offset) | (restart == 0)).astype(linear.dtype)
        summed = summed + shifted * tap_weights[offset] * usable[:, None]
    return summed


def outer_product_result(form, first, second):
    return jnp.einsum(form, first, second, precision=lax.Precision.HIGHEST)


def delta_core(queries, keys, values, betas, starts):
    length, head_count, head_width = queries.shape
    value_width = values.shape[2]
    block_count = starts.shape[0]
    block_len = length // block_count

    def blocked(array):
        return array.reshape(block_count, block_len, head_count, -1).transpose(0, 2, 1, 3)

    query_blocks = blocked(queries)
    key_blocks = blocked(keys)
    value_blocks = blocked(values)
    beta_blocks = betas.reshape(block_count, block_len, head_count).transpose(0, 2, 1)[..., None]
    position = jnp.arange(block_len)
    strict = (position[:, None] > position[None, :]).astype(queries.dtype)
    causal = (position[:, None] >= position[None, :]).astype(queries.dtype)
    weighted = key_blocks * beta_blocks
    negative = -outer_product_result("nhik,nhjk->nhij", weighted, key_blocks) * strict
    inverse = jnp.eye(block_len, dtype=queries.dtype) + negative
    power_term = negative
    for doubling in range(5):
        power_term = outer_product_result("nhij,nhjk->nhik", power_term, power_term)
        inverse = inverse + outer_product_result("nhij,nhjk->nhik", inverse, power_term)
    key_mix = outer_product_result("nhij,nhjk->nhik", inverse, weighted)
    value_mix = outer_product_result("nhij,nhjk->nhik", inverse, value_blocks * beta_blocks)
    scores = outer_product_result("nhik,nhjk->nhij", query_blocks, key_blocks) * causal

    def advance(current_state, block_items):
        (
            query_slice,
            key_slice,
            key_mixture_slice,
            value_mixture_slice,
            attention_score_slice,
            restart,
        ) = block_items
        current_state = current_state * (1 - restart).astype(current_state.dtype)
        adjusted_result = value_mixture_slice - outer_product_result(
            "pzd,pde->pze", key_mixture_slice, current_state
        )
        produced_output = outer_product_result(
            "pzd,pde->pze", query_slice, current_state
        ) + outer_product_result("lqz,lzr->lqr", attention_score_slice, adjusted_result)
        current_state = current_state + outer_product_result(
            "ixl,ixr->ilr", key_slice, adjusted_result
        )
        return (current_state, produced_output)

    initial = jnp.zeros((head_count, head_width, value_width), queries.dtype)
    final_state, produced_output = lax.scan(
        advance, initial, (query_blocks, key_blocks, key_mix, value_mix, scores, starts)
    )
    return produced_output.transpose(0, 2, 1, 3).reshape(length, head_count, value_width)


def delta_core_reset(queries, keys, values, betas, block_len):
    length, head_count, head_width = queries.shape
    block_count = length // block_len

    def blocked(array):
        return array.reshape(block_count, block_len, head_count, -1).transpose(0, 2, 1, 3)

    query_blocks = blocked(queries)
    key_blocks = blocked(keys)
    value_blocks = blocked(values)
    beta_blocks = betas.reshape(block_count, block_len, head_count).transpose(0, 2, 1)[..., None]
    position = jnp.arange(block_len)
    strict = (position[:, None] > position[None, :]).astype(queries.dtype)
    causal = (position[:, None] >= position[None, :]).astype(queries.dtype)
    weighted = key_blocks * beta_blocks
    negative = -outer_product_result("nhik,nhjk->nhij", weighted, key_blocks) * strict
    inverse = jnp.eye(block_len, dtype=queries.dtype) + negative
    power_term = negative
    for doubling in range(5):
        power_term = outer_product_result("nhij,nhjk->nhik", power_term, power_term)
        inverse = inverse + outer_product_result("nhij,nhjk->nhik", inverse, power_term)
    value_mix = outer_product_result("nhij,nhjk->nhik", inverse, value_blocks * beta_blocks)
    scores = outer_product_result("nhik,nhjk->nhij", query_blocks, key_blocks) * causal
    produced_output = outer_product_result("nhqz,nhzr->nhqr", scores, value_mix)
    return produced_output.transpose(0, 2, 1, 3).reshape(length, head_count, -1)


def mixer_core(
    query_lin, key_lin, value_lin, gate_lin, beta_lin, conv_taps, head_scale, starts, reset_len
):
    length = query_lin.shape[0]
    head_count = beta_lin.shape[1]
    head_width = query_lin.shape[1] // head_count
    queries = jax.nn.silu(short_conv(query_lin, conv_taps[0], starts)).reshape(
        length, head_count, head_width
    )
    keys = jax.nn.silu(short_conv(key_lin, conv_taps[1], starts)).reshape(
        length, head_count, head_width
    )
    values = jax.nn.silu(short_conv(value_lin, conv_taps[2], starts)).reshape(
        length, head_count, head_width
    )
    queries = (
        queries
        * lax.rsqrt(jnp.sum(queries * queries, axis=-1, keepdims=True) + 1e-06)
        * head_width ** (-0.5)
    )
    keys = keys * lax.rsqrt(jnp.sum(keys * keys, axis=-1, keepdims=True) + 1e-06)
    if reset_len:
        recurrent = delta_core_reset(queries, keys, values, jax.nn.sigmoid(beta_lin), reset_len)
    else:
        recurrent = delta_core(queries, keys, values, jax.nn.sigmoid(beta_lin), starts)
    normed = (
        recurrent
        * lax.rsqrt(jnp.mean(recurrent * recurrent, axis=-1, keepdims=True) + 1e-05)
        * head_scale
    )
    gated_out = normed * jax.nn.silu(gate_lin.reshape(length, head_count, head_width))
    return gated_out.reshape(length, head_count * head_width)


def swiglu_mix(gate_act, up_act):
    return jax.nn.silu(gate_act) * up_act


def matmul_rows(left, right):
    return jnp.dot(left, right, preferred_element_type=jnp.float32)


def left_product(first, second):
    return jnp.einsum("tf,tg->fg", first, second, preferred_element_type=jnp.float32)


def back_product(gradient, weight):
    return jnp.einsum("tg,fg->tf", gradient, weight, preferred_element_type=jnp.float32)


def tp_gather(value, axis):
    tp = lax.psum(1, TP_AXES)
    spread = jnp.broadcast_to(
        jnp.expand_dims(value, axis), value.shape[:axis] + (tp,) + value.shape[axis:]
    )
    moved = lax.all_to_all(spread, TP_AXES, axis, axis, tiled=True)
    shape = list(value.shape)
    shape[axis] *= tp
    return moved.reshape(shape)


def tp_scatter_low(value, axis):
    tp = lax.psum(1, TP_AXES)
    shape = list(value.shape)
    staged = value.astype(jnp.bfloat16).reshape(
        shape[:axis] + [tp, shape[axis] // tp] + shape[axis + 1 :]
    )
    moved = lax.all_to_all(staged, TP_AXES, axis, axis, tiled=True)
    return jnp.sum(moved.astype(jnp.float32), axis=axis)


def fsdp_gather(value, axis):
    return lax.all_gather(value, FSDP_AXES, axis=axis, tiled=True)


def fsdp_scatter_low(value, axis):
    return lax.psum_scatter(
        value.astype(jnp.bfloat16), FSDP_AXES, scatter_dimension=axis, tiled=True
    )


def exchange(value, axes, split_axis, concat_axis):
    if not axes:
        return value
    return lax.all_to_all(value, axes, split_axis, concat_axis, tiled=True)


def heads_to_rows(values, tp, fsdp, rows):
    count = values.shape[0]
    staged = values.reshape(count, 1, fsdp // tp, tp, rows)
    moved = exchange(staged, TP_AXES, 3, 1)
    return moved.reshape(count, fsdp * rows)


def rows_to_heads(values, tp, fsdp, rows):
    count = values.shape[0]
    staged = values.reshape(count, tp, fsdp // tp, 1, rows)
    moved = exchange(staged, TP_AXES, 1, 3)
    return moved.reshape(count, fsdp * rows)


def padded_rows(flat, slices, width):
    extra = -(-flat.shape[0] // (slices * width))
    extra = -(-extra // 16) * 16
    filled = jnp.pad(flat, (0, slices * extra * width - flat.shape[0]))
    return filled.reshape(slices, extra, width)


def make_on_device(tp, fsdp, inner):
    def on_device(
        tokens,
        cotangent,
        group_start,
        pad_mask,
        query_weight,
        key_weight,
        value_weight,
        gate_weight,
        beta_weight,
        out_weight,
        conv_weight,
        mixer_gain,
        head_gain,
        swiglu_gain,
        swiglu_gate,
        swiglu_up,
        swiglu_down,
    ):
        micro_count, slot, width = tokens.shape
        n_all = tp * fsdp
        rows = query_weight.shape[0]
        head_count = beta_weight.shape[1]
        heads_here = head_count // tp
        cols_here = width // tp
        group_rows = tp * rows
        position = lax.axis_index(TP_AXES)
        head_scale = head_gain.astype(jnp.float32)
        reset_len = slot if group_start.shape[1] == 1 else 0

        column_owned = jnp.stack([query_weight, key_weight, value_weight, gate_weight])
        column_swapped = exchange(
            column_owned.reshape(4, rows, tp, cols_here), TP_AXES, 2, 1
        ).reshape(4, group_rows, cols_here)
        owned_rows, hidden_half = swiglu_gate.shape
        hidden_here = hidden_half // inner
        ff_owned = jnp.stack([swiglu_gate, swiglu_up, swiglu_down.T]).reshape(
            3, owned_rows, inner, hidden_here
        )
        lanes = hidden_here // 128 if hidden_here % 128 == 0 else 0
        first = (lanes - lanes * 3 // 11) * 128 if lanes > 1 else hidden_here // 2
        order = ((first, hidden_here - first), (0, first))
        ff_swapped = [
            exchange(ff_owned[..., offset : offset + size], INNER_AXES, 2, 1).reshape(
                3, inner * owned_rows, size
            )
            for offset, size in order
        ]
        mixer_stack = jnp.concatenate(
            [column_swapped, out_weight.reshape(1, group_rows, cols_here)], axis=0
        )
        weight_all = fsdp_gather(mixer_stack, 1)
        weight_all, small_swapped, large_swapped = lax.optimization_barrier(
            (weight_all, ff_swapped[0], ff_swapped[1])
        )
        ff_chunks = [fsdp_gather(small_swapped, 1), fsdp_gather(large_swapped, 1)]
        query_cols, key_cols, value_cols, gate_cols = (weight_all[index] for index in range(4))
        out_rows = weight_all[4].reshape(fsdp * rows, width)
        small_pack = jnp.concatenate(
            [
                conv_weight.reshape(-1),
                beta_weight.reshape(-1),
                mixer_gain.reshape(-1),
                swiglu_gain.reshape(-1),
            ]
        )
        small_size = small_pack.shape[0]
        small_all = exchange(
            jnp.broadcast_to(small_pack[None, :], (n_all, small_size)), ALL_AXES, 0, 0
        )
        conv_size = conv_weight.size
        beta_size = beta_weight.size
        conv_full = (
            small_all[:, :conv_size]
            .reshape((n_all,) + conv_weight.shape)
            .transpose(1, 2, 0, 3)
            .reshape(conv_weight.shape[0], conv_weight.shape[1], -1)
        )
        beta_full = small_all[:, conv_size : conv_size + beta_size].reshape(-1, head_count)
        gain_mixer = small_all[:, conv_size + beta_size : conv_size + beta_size + rows].reshape(-1)
        gain_swiglu = small_all[:, conv_size + beta_size + rows :].reshape(-1)
        conv_here = lax.dynamic_slice_in_dim(
            conv_full.astype(jnp.float32), position * cols_here, cols_here, axis=2
        )
        beta_here = lax.dynamic_slice_in_dim(beta_full, position * heads_here, heads_here, axis=1)

        inputs = tokens.astype(jnp.float32).reshape(micro_count * slot, width)
        normed, norm_back = jax.vjp(rms_norm, inputs, gain_mixer.astype(jnp.float32))
        normed_low = normed.astype(jnp.bfloat16)
        group_tokens = micro_count * slot * tp
        normed_group = tp_gather(normed_low.reshape(micro_count, slot, width), 1).reshape(
            group_tokens, width
        )
        starts = tp_gather(group_start, 1).reshape(-1)

        query_lin = matmul_rows(normed_group, query_cols)
        key_lin = matmul_rows(normed_group, key_cols)
        value_lin = matmul_rows(normed_group, value_cols)
        gate_lin = matmul_rows(normed_group, gate_cols)
        beta_lin = matmul_rows(normed_group, beta_here)

        def core_at(query_in, key_in, value_in, gate_in, beta_in, conv_in, head_in):
            return mixer_core(
                query_in, key_in, value_in, gate_in, beta_in, conv_in, head_in, starts, reset_len
            )

        gated_out, core_back = jax.vjp(
            core_at, query_lin, key_lin, value_lin, gate_lin, beta_lin, conv_here, head_scale
        )
        gated_low = gated_out.astype(jnp.bfloat16)
        gated_rows = heads_to_rows(gated_low, tp, fsdp, rows)
        mixed_partial = matmul_rows(gated_rows, out_rows)
        residual = inputs + tp_scatter_low(
            mixed_partial.reshape(micro_count, slot * tp, width), 1
        ).reshape(micro_count * slot, width)

        inner_norm, inner_norm_back = jax.vjp(rms_norm, residual, gain_swiglu.astype(jnp.float32))
        inner_low = inner_norm.astype(jnp.bfloat16)
        inner_group = tp_gather(inner_low.reshape(micro_count, slot, width), 1).reshape(
            group_tokens, width
        )
        out_back = cotangent.astype(jnp.float32) * pad_mask.astype(jnp.float32)[:, :, None]
        out_back_low = out_back.astype(jnp.bfloat16)
        upstream_group = tp_gather(out_back_low, 1).reshape(group_tokens, width)
        partial_rows = None
        inner_part = None
        ff_reduced = []
        for index, chunk_weights in enumerate(ff_chunks):
            if index > 0:
                sums_low, chunk_weights = lax.optimization_barrier((sums_low, chunk_weights))
            gate_piece, up_piece, down_piece_t = chunk_weights[0], chunk_weights[1], chunk_weights[2]
            gate_act = matmul_rows(inner_group, gate_piece)
            up_act = matmul_rows(inner_group, up_piece)
            hidden, hidden_back = jax.vjp(swiglu_mix, gate_act, up_act)
            hidden_low = hidden.astype(jnp.bfloat16)
            piece_rows = back_product(hidden_low, down_piece_t)
            partial_rows = piece_rows if partial_rows is None else partial_rows + piece_rows
            gate_back, up_back = hidden_back(matmul_rows(upstream_group, down_piece_t))
            gate_back_low = gate_back.astype(jnp.bfloat16)
            up_back_low = up_back.astype(jnp.bfloat16)
            piece_part = back_product(gate_back_low, gate_piece) + back_product(up_back_low, up_piece)
            inner_part = piece_part if inner_part is None else inner_part + piece_part
            sums_low = jnp.stack(
                [
                    left_product(inner_group, gate_back_low),
                    left_product(inner_group, up_back_low),
                    left_product(upstream_group, hidden_low),
                ]
            ).astype(jnp.bfloat16)
            ff_reduced.append(fsdp_scatter_low(sums_low, 1))
        branch_rows = tp_scatter_low(partial_rows.reshape(micro_count, slot * tp, width), 1)
        block_out = (residual.reshape(micro_count, slot, width) + branch_rows).astype(jnp.bfloat16)
        inner_back = tp_scatter_low(inner_part.reshape(micro_count, slot * tp, width), 1)
        block_out, inner_back = lax.optimization_barrier((block_out, inner_back))

        residual_part, swiglu_gain_term = inner_norm_back(
            inner_back.reshape(micro_count * slot, width)
        )
        residual_back = out_back.reshape(micro_count * slot, width) + residual_part
        mixed_back = residual_back.astype(jnp.bfloat16)
        mixed_group = tp_gather(mixed_back.reshape(micro_count, slot, width), 1).reshape(
            group_tokens, width
        )
        gated_back_rows = back_product(mixed_group, out_rows)
        gated_back = rows_to_heads(gated_back_rows, tp, fsdp, rows)
        query_back, key_back, value_back, gate_lin_back, beta_back, conv_term, head_term = (
            core_back(gated_back)
        )
        query_low = query_back.astype(jnp.bfloat16)
        key_low = key_back.astype(jnp.bfloat16)
        value_low = value_back.astype(jnp.bfloat16)
        gate_low = gate_lin_back.astype(jnp.bfloat16)
        beta_low = beta_back.astype(jnp.bfloat16)
        mixer_sums = jnp.stack(
            [
                left_product(normed_group, query_low),
                left_product(normed_group, key_low),
                left_product(normed_group, value_low),
                left_product(normed_group, gate_low),
                left_product(gated_rows, mixed_group).reshape(width, cols_here),
            ]
        )
        ff_reduced, mixer_sums = lax.optimization_barrier((ff_reduced, mixer_sums))
        mixer_reduced = fsdp_scatter_low(mixer_sums, 1)
        ff_back = jnp.concatenate(
            [
                exchange(
                    piece.reshape(3, inner, owned_rows, 1, size), INNER_AXES, 1, 3
                ).reshape(3, owned_rows, inner, size)
                for piece, (offset, size) in sorted(zip(ff_reduced, order), key=lambda pair: pair[1][0])
            ],
            axis=3,
        ).reshape(3, owned_rows, hidden_half).astype(jnp.float32)
        swiglu_gate_grad = ff_back[0]
        swiglu_up_grad = ff_back[1]
        swiglu_down_grad = ff_back[2].T

        normed_part = (
            back_product(query_low, query_cols)
            + back_product(key_low, key_cols)
            + back_product(value_low, value_cols)
            + back_product(gate_low, gate_cols)
            + back_product(beta_low, beta_here)
        )
        normed_back = tp_scatter_low(normed_part.reshape(micro_count, slot * tp, width), 1)
        input_part, mixer_gain_term = norm_back(normed_back.reshape(micro_count * slot, width))
        tokens_grad = (residual_back + input_part).reshape(micro_count, slot, width)

        beta_sum = left_product(normed_group, beta_low)
        beta_wide = lax.dynamic_update_slice_in_dim(
            jnp.zeros((width, head_count), jnp.float32), beta_sum, position * heads_here, axis=1
        )
        conv_wide = lax.dynamic_update_slice_in_dim(
            jnp.zeros(conv_full.shape, jnp.float32), conv_term, position * cols_here, axis=2
        )
        taps = conv_wide.shape[0] * conv_wide.shape[1]
        small_terms = jnp.concatenate(
            [
                conv_wide.reshape(taps, n_all, -1).transpose(1, 0, 2).reshape(n_all, -1),
                beta_wide.reshape(n_all, -1),
                mixer_gain_term.reshape(n_all, -1),
                swiglu_gain_term.reshape(n_all, -1),
                jnp.broadcast_to(head_term[None, :], (n_all, head_term.shape[0])),
            ],
            axis=1,
        )
        small_width = small_terms.shape[1]
        small_out = jnp.sum(exchange(small_terms, ALL_AXES, 0, 0), axis=0)
        column_back = exchange(
            mixer_reduced[:4].reshape(4, tp, rows, 1, cols_here), TP_AXES, 1, 3
        ).reshape(4, rows, width).astype(jnp.float32)
        query_grad, key_grad, value_grad, gate_grad = (column_back[index] for index in range(4))
        out_grad = mixer_reduced[4].reshape(rows, width).astype(jnp.float32)
        conv_grad = small_out[:conv_size].reshape(conv_weight.shape)
        beta_grad = small_out[conv_size : conv_size + beta_size].reshape(beta_weight.shape)
        mixer_gain_grad = small_out[conv_size + beta_size : conv_size + beta_size + rows]
        swiglu_gain_grad = small_out[conv_size + beta_size + rows : conv_size + beta_size + 2 * rows]
        head_total = small_out[conv_size + beta_size + 2 * rows :]
        return (
            block_out,
            tokens_grad,
            query_grad,
            key_grad,
            value_grad,
            gate_grad,
            beta_grad,
            out_grad,
            conv_grad,
            mixer_gain_grad,
            head_total,
            swiglu_gain_grad,
            swiglu_gate_grad,
            swiglu_up_grad,
            swiglu_down_grad,
        )

    return on_device


def solution(mesh):
    n_dp = mesh.shape["dp"]
    n_mlp = mesh.shape["mlp"]
    devices = np.asarray(mesh.devices).reshape(n_dp // 2, 2, n_mlp)
    split_mesh = Mesh(devices, ALL_AXES)
    sizes = dict(zip(ALL_AXES, devices.shape))
    tp = int(np.prod([sizes[name] for name in TP_AXES]))
    fsdp = int(np.prod([sizes[name] for name in FSDP_AXES]))
    inner = int(np.prod([sizes[name] for name in INNER_AXES]))
    rows_axes = ALL_AXES
    swiglu_rows = ("dq", "core")
    placed = (
        P(None, rows_axes, None),
        P(None, rows_axes, None),
        P(None, rows_axes),
        P(None, rows_axes),
        P(rows_axes, None),
        P(rows_axes, None),
        P(rows_axes, None),
        P(rows_axes, None),
        P(rows_axes, None),
        P(rows_axes, None),
        P(None, None, rows_axes),
        P(rows_axes),
        P(),
        P(rows_axes),
        P(swiglu_rows, "mlp"),
        P(swiglu_rows, "mlp"),
        P("mlp", swiglu_rows),
    )
    return jax.shard_map(
        make_on_device(tp, fsdp, inner),
        mesh=split_mesh,
        in_specs=placed,
        out_specs=(
            P(None, rows_axes, None),
            P(None, rows_axes, None),
            P(rows_axes, None),
            P(rows_axes, None),
            P(rows_axes, None),
            P(rows_axes, None),
            P(rows_axes, None),
            P(rows_axes, None),
            P(None, None, rows_axes),
            P(rows_axes),
            P(),
            P(rows_axes),
            P(swiglu_rows, "mlp"),
            P(swiglu_rows, "mlp"),
            P("mlp", swiglu_rows),
        ),
        check_vma=False,
    )
```
